32 devices in a mesh: wide: 8 (over z, x), narrow: 4 (over y, core).
Axes of the slice: x: 2, y: 2, z: 4, core: 2. Of those that a mesh axis runs over, the one named last changes fastest.
Arguments:
- tokens: bfloat16 [32768, 768], P(('wide', 'narrow')), may hold values from -6 to 6
- norm1_gain: bfloat16 [768], P(('wide', 'narrow')), may hold values from 0.25 to 1.75
- norm1_bias: bfloat16 [768], P(('wide', 'narrow')), may hold values from -2.5 to 2.5
- qkv_weight: bfloat16 [768, 2304], P(('wide', 'narrow')), may hold values from -0.21875 to 0.21875
- qkv_bias: bfloat16 [1536], P(('wide', 'narrow')), may hold values from -2.5 to 2.5
- out_weight: bfloat16 [768, 768], P(('wide', 'narrow')), may hold values from -9 to 9
- out_bias: bfloat16 [768], P(('wide', 'narrow')), may hold values from -12 to 12
- norm2_gain: bfloat16 [768], P(('wide', 'narrow')), may hold values from 0.25 to 1.75
- norm2_bias: bfloat16 [768], P(('wide', 'narrow')), may hold values from -2.5 to 2.5
- fc_weight: bfloat16 [768, 3072], P(('wide', 'narrow')), may hold values from -0.21875 to 0.21875
- fc_bias: bfloat16 [3072], P(('wide', 'narrow')), may hold values from -3 to 3
- proj_weight: bfloat16 [3072, 768], P(('wide', 'narrow')), may hold values from -2.5 to 2.5
- proj_bias: bfloat16 [768], P(('wide', 'narrow')), may hold values from -12 to 12
- seq_lengths: int32 [32], P(('wide', 'narrow')), may hold values from 64 to 1024, as said below
- out_cotangent: bfloat16 [32768, 768], P(('wide', 'narrow')), may hold values from -6 to 6
Outputs:
- layer_out: bfloat16 [32768, 768], P(('wide', 'narrow'))
- input_grad: bfloat16 [32768, 768], P(('wide', 'narrow'))
- norm1_gain_grad: float32 [768], P(('wide', 'narrow'))
- norm1_bias_grad: float32 [768], P(('wide', 'narrow'))
- qkv_weight_grad: float32 [768, 2304], P(('wide', 'narrow'))
- qkv_bias_grad: float32 [1536], P(('wide', 'narrow'))
- out_weight_grad: float32 [768, 768], P(('wide', 'narrow'))
- out_bias_grad: float32 [768], P(('wide', 'narrow'))
- norm2_gain_grad: float32 [768], P(('wide', 'narrow'))
- norm2_bias_grad: float32 [768], P(('wide', 'narrow'))
- fc_weight_grad: float32 [768, 3072], P(('wide', 'narrow'))
- fc_bias_grad: float32 [3072], P(('wide', 'narrow'))
- proj_weight_grad: float32 [3072, 768], P(('wide', 'narrow'))
- proj_bias_grad: float32 [768], P(('wide', 'narrow'))
The draws below stay inside these ranges and needn't reach their ends.
Inputs may be any that keep to these rules, and one draw needn't show every extreme that they name: Each slot holds one sequence of seq_lengths tokens from its first position on; the rest of the slot is padding. Some slot is full in every draw.
All inputs are finite; a program needn't handle non-finite values.
Results may differ from the reference program's by a relative error of at most 0.013.
Values may be sent and summed in bfloat16 or wider, within the bound.
No kernel may reach another device: no remote copies, remote signals or barrier semaphores. Data moves between devices by JAX's collectives and lax.ppermute only.
A program may use at most 256 MiB of HBM per device.

```python
import math
import jax
import jax.numpy as jnp
from jax import lax

D = 768
H = 12
HD = 64
FF = 3072
SLOT = 1024
MIN_LEN = 64
SLOTS = 32
TOKENS = 32768


def draw_seq_lengths(key, part):
    first_key, second_key = jax.random.split(key)
    drawn = jax.random.randint(first_key, (SLOTS,), MIN_LEN, SLOT + 1, dtype=jnp.int32)
    chosen = jax.random.randint(second_key, (), 0, SLOTS, dtype=jnp.int32)
    return jnp.where(jnp.arange(SLOTS) == chosen, SLOT, drawn).astype(jnp.int32)


def shard_levels(rng, shape, cuts, low, largest):
    level, own = 1.0, jax.random.fold_in(rng, 6)
    for axis_at, blocks in cuts:
        draws = jnp.exp(jax.random.uniform(jax.random.fold_in(own, axis_at), (blocks,), jnp.float32, low / len(cuts), largest / len(cuts)))
        level = level * jnp.repeat(draws, shape[axis_at] // blocks).reshape([-1 if axis == axis_at else 1 for axis in range(len(shape))])
    return level


def bell_draw(stream_key, shape, spread, reach, pieces=(), kind=jnp.bfloat16):
    values = jax.random.normal(stream_key, shape, jnp.float32) * spread
    if len(pieces) > 0:
        values = shard_levels(stream_key, shape, pieces, -0.22, 0.18) * values
    return jnp.clip(values, min=-reach, max=reach).astype(kind)


def setup_inputs(seed: int = 0) -> dict:
    arg_keys = jax.random.split(jax.random.key(seed), 16)
    tokens = bell_draw(arg_keys[0], (TOKENS, D), 1.0, 6.0, ((0, 32),))
    norm1_gain = jnp.clip(1.0 + 0.15 * jax.random.normal(arg_keys[1], (D,), jnp.float32), 0.25, 1.75).astype(jnp.bfloat16)
    norm1_bias = bell_draw(arg_keys[2], (D,), 0.3, 2.5, ((0, 32),))
    qkv_weight = bell_draw(arg_keys[3], (D, 3 * D), D ** -0.5, 0.21875, ((0, 32),))
    qkv_bias = bell_draw(arg_keys[4], (2 * D,), 0.3, 2.5, ((0, 32),))
    out_weight = bell_draw(arg_keys[5], (D, D), 1.5, 9.0, ((0, 32),))
    out_bias = bell_draw(arg_keys[6], (D,), 2.0, 12.0, ((0, 32),))
    norm2_gain = jnp.clip(1.0 + 0.15 * jax.random.normal(arg_keys[7], (D,), jnp.float32), 0.25, 1.75).astype(jnp.bfloat16)
    norm2_bias = bell_draw(arg_keys[8], (D,), 0.3, 2.5, ((0, 32),))
    fc_weight = bell_draw(arg_keys[9], (D, FF), D ** -0.5, 0.21875, ((0, 32),))
    fc_bias = bell_draw(arg_keys[10], (FF,), 0.5, 3.0, ((0, 32),))
    proj_weight = bell_draw(arg_keys[11], (FF, D), 0.2, 2.5, ((0, 32),))
    proj_bias = bell_draw(arg_keys[12], (D,), 2.0, 12.0, ((0, 32),))
    seq_lengths = draw_seq_lengths(jax.random.fold_in(arg_keys[15], 71), 0)
    out_cotangent = bell_draw(arg_keys[14], (TOKENS, D), 1.0, 6.0, ((0, 32),))
    return dict(tokens=tokens, norm1_gain=norm1_gain, norm1_bias=norm1_bias, qkv_weight=qkv_weight, qkv_bias=qkv_bias, out_weight=out_weight, out_bias=out_bias, norm2_gain=norm2_gain, norm2_bias=norm2_bias, fc_weight=fc_weight, fc_bias=fc_bias, proj_weight=proj_weight, proj_bias=proj_bias, seq_lengths=seq_lengths, out_cotangent=out_cotangent)


@jax.custom_vjp
def low(v):
    return lax.optimization_barrier(v.astype(jnp.bfloat16)).astype(jnp.float32)

@jax.custom_vjp
def low_back(v):
    return v

def low_keep(v):
    return (low(v), None)

def low_pass(kept, grad):
    return (grad,)

def back_keep(v):
    return (v, None)

def back_low(kept, grad):
    return (low(grad),)
low.defvjp(low_keep, low_pass)
low_back.defvjp(back_keep, back_low)
branch_scale = 1.0 / math.sqrt(48.0)
norm_epsilon = 1e-05
masked_value = -1e+30

def layer_norm(values_in, gain_vec, shift_vec):
    row_mean = lax.optimization_barrier(jnp.mean(values_in, axis=-1, keepdims=True))
    centred = values_in - row_mean
    row_var = lax.optimization_barrier(jnp.mean(centred * centred, axis=-1, keepdims=True))
    return centred * lax.rsqrt(row_var + norm_epsilon) * gain_vec + shift_vec

def gelu_tanh(pre_act):
    inner = 0.7978845608028654 * (pre_act + 0.044715 * pre_act * pre_act * pre_act)
    return 0.5 * pre_act * (1.0 + jnp.tanh(inner))

def matmul(left, right):
    return jnp.dot(left, right, precision=lax.Precision.HIGHEST, preferred_element_type=jnp.float32)

def slot_attention(item):
    packed_slot, seq_length = item
    slot_size = packed_slot.shape[0]
    query_rows = packed_slot[:, :D].reshape(slot_size, H, HD)
    key_rows = packed_slot[:, D:2 * D].reshape(slot_size, H, HD)
    value_rows = packed_slot[:, 2 * D:].reshape(slot_size, H, HD)
    raw_scores = jnp.einsum('qhd,khd->hqk', query_rows, key_rows, precision=lax.Precision.HIGHEST) * (1.0 / math.sqrt(HD))
    raw_scores = low_back(raw_scores)
    position = jnp.arange(slot_size)
    causal = position[None, :] <= position[:, None]
    soft_probs = low(jax.nn.softmax(jnp.where(causal[None], raw_scores, masked_value), axis=-1))
    mixed_rows = jnp.einsum('hqk,khd->qhd', soft_probs, value_rows, precision=lax.Precision.HIGHEST)
    valid_rows = (position < seq_length)[:, None, None]
    return jnp.where(valid_rows, mixed_rows, 0.0).reshape(slot_size, D)

def forward(param_set, input_rows, block_lengths):
    gain_one, shift_one, qkv_weight, qkv_bias, out_weight, out_bias, gain_two, shift_two, fc_weight, fc_bias, proj_weight, proj_bias = param_set
    norm_one = low(layer_norm(input_rows, gain_one, shift_one))
    bias_full = jnp.concatenate([qkv_bias[:D], jnp.zeros((D,), jnp.float32), qkv_bias[D:]])
    packed = low(low_back(matmul(norm_one, qkv_weight) + bias_full))
    slot_packed = packed.reshape(-1, SLOT, 3 * D)
    mixed_all = lax.map(jax.checkpoint(slot_attention), (slot_packed, block_lengths))
    mixed_all = low(low_back(mixed_all.reshape(-1, D)))
    branch = low_back(matmul(mixed_all, out_weight) + out_bias)
    middle = input_rows + branch_scale * branch
    norm_two = low(layer_norm(middle, gain_two, shift_two))
    hidden = low_back(matmul(norm_two, fc_weight) + fc_bias)
    active = low(gelu_tanh(hidden))
    second = low_back(matmul(active, proj_weight) + proj_bias)
    return middle + branch_scale * second

def reference(tokens, norm1_gain, norm1_bias, qkv_weight, qkv_bias, out_weight, out_bias, norm2_gain, norm2_bias, fc_weight, fc_bias, proj_weight, proj_bias, seq_lengths, out_cotangent):
    params = tuple((item.astype(jnp.float32) for item in (norm1_gain, norm1_bias, qkv_weight, qkv_bias, out_weight, out_bias, norm2_gain, norm2_bias, fc_weight, fc_bias, proj_weight, proj_bias)))
    group_slots = max(1, min(SLOTS, 4096 // SLOT))
    while SLOTS % group_slots != 0:
        group_slots = group_slots - 1
    group_count = SLOTS // group_slots
    rows_all = tokens.astype(jnp.float32).reshape(group_count, group_slots * SLOT, D)
    cot_all = out_cotangent.astype(jnp.float32).reshape(group_count, group_slots * SLOT, D)
    length_all = seq_lengths.reshape(group_count, group_slots)
    position = jnp.arange(SLOT)

    def group_step(running, item):
        group_rows, group_lengths, group_cot = item
        valid_rows = (position[None, :] < group_lengths[:, None]).reshape(-1, 1).astype(jnp.float32)

        def layer_fn(param_set, input_rows):
            return forward(param_set, input_rows, group_lengths)
        layer_value, pull_back = jax.vjp(layer_fn, params, group_rows)
        param_grads, input_grads = pull_back(group_cot * valid_rows)
        running = jax.tree.map(jnp.add, running, param_grads)
        return (running, (layer_value.astype(jnp.bfloat16), input_grads.astype(jnp.bfloat16)))
    zero_grads = jax.tree.map(jnp.zeros_like, params)
    grad_sums, (layer_all, input_all) = lax.scan(group_step, zero_grads, (rows_all, length_all, cot_all))
    layer_out = layer_all.reshape(TOKENS, D)
    input_grad = input_all.reshape(TOKENS, D)
    return (layer_out, input_grad, grad_sums[0], grad_sums[1], grad_sums[2], grad_sums[3], grad_sums[4], grad_sums[5], grad_sums[6], grad_sums[7], grad_sums[8], grad_sums[9], grad_sums[10], grad_sums[11])
```

```python
import functools
import math

import jax
import jax.numpy as jnp
import numpy as np
from jax import lax
from jax.experimental import pallas as pl
from jax.experimental.pallas import tpu as pltpu
from jax.sharding import PartitionSpec as P

AXES = ("wide", "narrow")
BF, F32 = jnp.bfloat16, jnp.float32
VMEM_CAP = 58 << 20
LOG2E = 1.4426950408889634

def params(n=1, cap=VMEM_CAP):
    return pltpu.CompilerParams(dimension_semantics=("arbitrary",) * n, vmem_limit_bytes=cap)

def cost(flops, bytes_accessed, trans=0):
    return pl.CostEstimate(flops=int(flops), bytes_accessed=int(bytes_accessed), transcendentals=int(trans))

def mm(a, b):
    return jnp.dot(a, b, preferred_element_type=F32)

def diagonal_mask(rows, cols):
    key_at = lax.broadcasted_iota(jnp.int32, (rows, cols), 0)
    query_at = lax.broadcasted_iota(jnp.int32, (rows, cols), 1)
    return key_at <= query_at

def attend_kernel(qb, len_ref, qkv_ref, out_t_ref, out_ref, stat_ref, v_t, q_t):
    slot = qkv_ref.shape[1]
    q_t[...] = (qkv_ref[0] * jnp.asarray(0.125, BF)).T
    v_t[...] = qkv_ref[2].T
    half = lax.broadcasted_iota(jnp.int32, (128, 1), 0) < 64
    causal = diagonal_mask(qb, qb)
    length = len_ref[0]
    for i in range(slot // qb):
        cols = slice(i * qb, (i + 1) * qb)
        parts = []
        for head in range(2):
            mine = half if head == 0 else jnp.logical_not(half)
            qh = jnp.where(mine, q_t[:, cols], jnp.zeros((), BF))
            s_low = mm(qkv_ref[1, : i * qb, :], qh) if i else None
            s_dia = jnp.where(causal, mm(qkv_ref[1, cols, :], qh), -1e30)
            top = jnp.max(s_dia, axis=0, keepdims=True)
            if i:
                top = jnp.maximum(top, jnp.max(s_low, axis=0, keepdims=True))
            e_dia = jnp.exp(s_dia - top)
            total = jnp.sum(e_dia, axis=0, keepdims=True)
            vh = v_t[head * 64 : head * 64 + 64, :]
            acc = mm(vh[:, cols], e_dia.astype(BF))
            if i:
                e_low = jnp.exp(s_low - top)
                total = total + jnp.sum(e_low, axis=0, keepdims=True)
                acc = acc + mm(vh[:, : i * qb], e_low.astype(BF))
            stat_ref[0, head : head + 1, cols] = top + jnp.log(total)
            parts.append(acc / total)
        both = jnp.concatenate(parts, axis=0)
        seen = (i * qb + lax.broadcasted_iota(jnp.int32, (1, qb), 1)) < length
        both = jnp.where(seen, both, 0.0)
        out_t_ref[:, cols] = both
        out_ref[cols, :] = both.T.astype(BF)

def attend(lengths, qkv, pairs, first, qb=256):
    slot, width = qkv.shape[1], qkv.shape[2]
    return pl.pallas_call(
        functools.partial(attend_kernel, qb),
        name="attend",
        grid=(pairs,),
        in_specs=[
            pl.BlockSpec(memory_space=pltpu.SMEM),
            pl.BlockSpec((3, slot, 128), lambda j: (0, 0, j + first)),
        ],
        out_specs=[
            pl.BlockSpec((128, slot), lambda j: (j, 0)),
            pl.BlockSpec((slot, 128), lambda j: (0, j)),
            pl.BlockSpec((1, 2, slot), lambda j: (j, 0, 0)),
        ],
        out_shape=[
            jax.ShapeDtypeStruct((pairs * 128, slot), F32),
            jax.ShapeDtypeStruct((slot, pairs * 128), BF),
            jax.ShapeDtypeStruct((pairs, 2, slot), F32),
        ],
        scratch_shapes=[pltpu.VMEM((128, slot), BF), pltpu.VMEM((128, slot), BF)],
        compiler_params=params(),
        cost_estimate=cost(pairs * 2 * slot * slot * 256, 8e6 * pairs / 6, pairs * slot * slot),
    )(lengths, qkv)

def attend_grad_kernel(qb, qkv_ref, grad_ref, out_t_ref, stat_ref, g_ref, q_t, do_t, k_t, qs, dq_t, dk_s, dv_s):
    slot = qkv_ref.shape[1]
    qs[...] = qkv_ref[0] * jnp.asarray(0.125, BF)
    q_t[...] = qs[...].T
    k_t[...] = qkv_ref[1].T
    do_t[...] = grad_ref[...].T
    half = lax.broadcasted_iota(jnp.int32, (128, 1), 0) < 64
    half_lane = lax.broadcasted_iota(jnp.int32, (1, 128), 1) < 64
    causal = diagonal_mask(qb, qb)
    zero = jnp.zeros((), BF)
    prod = do_t[...].astype(F32) * out_t_ref[...]
    delta = [jnp.sum(prod[h * 64 : h * 64 + 64], axis=0, keepdims=True) for h in range(2)]
    for i in range(slot // qb):
        cols = slice(i * qb, (i + 1) * qb)
        end = (i + 1) * qb
        dv_new = dk_new = None
        for head in range(2):
            mine = half if head == 0 else jnp.logical_not(half)
            mine_lane = half_lane if head == 0 else jnp.logical_not(half_lane)
            qh_t = jnp.where(mine, q_t[:, cols], zero)
            doh_t = jnp.where(mine, do_t[:, cols], zero)
            qh = jnp.where(mine_lane, qs[cols, :], zero)
            doh = jnp.where(mine_lane, grad_ref[cols, :], zero)
            stat = stat_ref[0, head : head + 1, cols]
            dl = delta[head][:, cols]
            s = mm(qkv_ref[1, :end, :], qh_t)
            dp = mm(qkv_ref[2, :end, :], doh_t)
            p = jnp.exp(s - stat)
            p_dia = jnp.where(causal, p[i * qb :], 0.0)
            p = jnp.concatenate([p[: i * qb], p_dia], axis=0) if i else p_dia
            ds = (p * (dp - dl)).astype(BF)
            pb = p.astype(BF)
            dv_h = mm(pb, doh)
            dk_h = mm(ds, qh)
            dv_new = dv_h if head == 0 else dv_new + dv_h
            dk_new = dk_h if head == 0 else dk_new + dk_h
            dq_t[head * 64 : head * 64 + 64, cols] = mm(k_t[head * 64 : head * 64 + 64, :end], ds)
        if i:
            dv_s[: i * qb] += dv_new[: i * qb]
            dk_s[: i * qb] += dk_new[: i * qb]
        dv_s[cols] = dv_new[i * qb :]
        dk_s[cols] = dk_new[i * qb :]
    g_ref[0] = (dq_t[...] * 0.125).T.astype(BF)
    g_ref[1] = dk_s[...].astype(BF)
    g_ref[2] = dv_s[...].astype(BF)

def attend_grad(qkv, grad, out_t, stat, qb=256):
    slot, width = qkv.shape[1], qkv.shape[2]
    pairs = width // 128
    return pl.pallas_call(
        functools.partial(attend_grad_kernel, qb),
        name="attend_grad",
        grid=(pairs,),
        in_specs=[
            pl.BlockSpec((3, slot, 128), lambda j: (0, 0, j)),
            pl.BlockSpec((slot, 128), lambda j: (0, j)),
            pl.BlockSpec((128, slot), lambda j: (j, 0)),
            pl.BlockSpec((1, 2, slot), lambda j: (j, 0, 0)),
        ],
        out_specs=pl.BlockSpec((3, slot, 128), lambda j: (0, 0, j)),
        out_shape=jax.ShapeDtypeStruct((3, slot, width), BF),
        scratch_shapes=[
            pltpu.VMEM((128, slot), BF),
            pltpu.VMEM((128, slot), BF),
            pltpu.VMEM((128, slot), BF),
            pltpu.VMEM((slot, 128), BF),
            pltpu.VMEM((128, slot), F32),
            pltpu.VMEM((slot, 128), F32),
            pltpu.VMEM((slot, 128), F32),
        ],
        compiler_params=params(),
        cost_estimate=cost(pairs * 5 * slot * slot * 256, 16e6, pairs * 2 * slot * slot),
    )(qkv, grad, out_t, stat)
branch_scale = 1.0 / math.sqrt(48.0)
norm_epsilon = 1e-05
WHOLE = dict(pipeline_mode=pl.Buffered(1))

def mm_nt(a, b):
    return lax.dot_general(a, b, (((1,), (1,)), ((), ())), preferred_element_type=F32)

def mm_tn(a, b):
    return lax.dot_general(a, b, (((0,), (0,)), ((), ())), preferred_element_type=F32)

def normalised(v):
    mean = jnp.mean(v, axis=-1, keepdims=True)
    centred = v - mean
    var = jnp.mean(centred * centred, axis=-1, keepdims=True)
    scale = lax.rsqrt(var + norm_epsilon)
    return centred * scale, scale

def norm_pull(n, scale, gain, u):
    ug = u * gain
    a = jnp.mean(ug, axis=-1, keepdims=True)
    b = jnp.mean(ug * n, axis=-1, keepdims=True)
    return (ug - a - n * b) * scale

def whole(shape, index=None):
    zeros = (0,) * len(shape)
    return pl.BlockSpec(shape, (lambda *_: index or zeros), **WHOLE)

def assemble(place, sources, target, at=0):
    wide = sources[0].shape[2]
    for s, source in enumerate(sources):
        for half in range(2):
            @pl.when(place[s, 0] == half)
            def _():
                for p in range(source.shape[0]):
                    target[place[s, 1 + p], :, half * wide : (half + 1) * wide] = source[p]

def assemble_chunks(place, sources, target):
    wide = sources[0].shape[2] // 4
    for s, source in enumerate(sources):
        for half in range(2):
            @pl.when(place[s, 0] == half)
            def _():
                for p in range(source.shape[0]):
                    for j in range(4):
                        target[place[s, 1 + p], j, :, half * wide : (half + 1) * wide] = source[p, :, j * wide : (j + 1) * wide]

def project_kernel(n_src, place, x_ref, gain_ref, shift_ref, bias_ref, *rest):
    sources, (qkv_ref, low_ref, w_ref) = rest[:n_src], rest[n_src:]
    @pl.when(pl.program_id(0) == 0)
    def _():
        assemble(place, sources, w_ref)
    n, _ = normalised(x_ref[...].astype(F32))
    low = (n * gain_ref[...] + shift_ref[...]).astype(BF)
    low_ref[...] = low
    d = low.shape[1]
    for part in range(3):
        w = w_ref[:, :, part * d : (part + 1) * d].reshape(d, d)
        qkv_ref[part] = (mm(low, w) + bias_ref[part : part + 1]).astype(BF)

def project(place, x, gain, shift, bias, sources, blocks, rows=256):
    t, d = x.shape
    r, wide = d // blocks, sources[0].shape[2]
    return pl.pallas_call(
        functools.partial(project_kernel, len(sources)),
        name="project",
        grid_spec=pltpu.PrefetchScalarGridSpec(
            num_scalar_prefetch=1,
            grid=(t // rows,),
            in_specs=[
                pl.BlockSpec((rows, d), lambda i, p: (i, 0)),
                whole((1, d)), whole((1, d)), whole((3, d)),
                *[whole(s.shape) for s in sources],
            ],
            out_specs=[
                pl.BlockSpec((3, rows, d), lambda i, p: (0, i, 0)),
                pl.BlockSpec((rows, d), lambda i, p: (i, 0)),
                whole((blocks, r, 2 * wide)),
            ],
        ),
        out_shape=[
            jax.ShapeDtypeStruct((3, t, d), BF),
            jax.ShapeDtypeStruct((t, d), BF),
            jax.ShapeDtypeStruct((blocks, r, 2 * wide), BF),
        ],
        compiler_params=params(),
        cost_estimate=cost(2 * t * d * 3 * d, 18e6),
    )(place, x, gain, shift, bias, *sources)

def mix_kernel(n_src, place, attn_ref, x_ref, bias_ref, gain_ref, shift_ref, *rest):
    sources, (mid_ref, low_ref, w_ref) = rest[:n_src], rest[n_src:]
    @pl.when(pl.program_id(0) == 0)
    def _():
        assemble(place, sources, w_ref)
    d = x_ref.shape[1]
    w = w_ref[...].reshape(d, d)
    mid = x_ref[...].astype(F32) + branch_scale * (mm(attn_ref[...], w) + bias_ref[...])
    mid_ref[...] = mid
    n, _ = normalised(mid)
    low_ref[...] = (n * gain_ref[...] + shift_ref[...]).astype(BF)

def mix(place, attn, x, bias, gain, shift, sources, blocks, column, rows=256):
    t, d = x.shape
    r, np_ = d // blocks, sources[0].shape[0]
    return pl.pallas_call(
        functools.partial(mix_kernel, len(sources)),
        name="mix",
        grid_spec=pltpu.PrefetchScalarGridSpec(
            num_scalar_prefetch=1,
            grid=(t // rows,),
            in_specs=[
                pl.BlockSpec((rows, d), lambda i, p: (i, 0)),
                pl.BlockSpec((rows, d), lambda i, p: (i, 0)),
                whole((1, d)), whole((1, d)), whole((1, d)),
                *[whole((np_, r, d // 2), (0, 0, column)) for s in sources],
            ],
            out_specs=[
                pl.BlockSpec((rows, d), lambda i, p: (i, 0)),
                pl.BlockSpec((rows, d), lambda i, p: (i, 0)),
                whole((blocks, r, d)),
            ],
        ),
        out_shape=[
            jax.ShapeDtypeStruct((t, d), F32),
            jax.ShapeDtypeStruct((t, d), BF),
            jax.ShapeDtypeStruct((blocks, r, d), BF),
        ],
        compiler_params=params(),
        cost_estimate=cost(2 * t * d * d, 9e6),
    )(place, attn, x, bias, gain, shift, *sources)

def mlp_kernel(n_src, blocks, rb, core, place, lens, mid_ref, low_ref, cot_ref, fb_ref, pb_ref, gain_ref, *rest):
    fcs, projs, rest = rest[:n_src], rest[n_src : 2 * n_src], rest[2 * n_src :]
    (out_ref, gmid_ref, gbr_ref, fsend_ref, fkeep_ref, psend_ref, pkeep_ref, fbg_ref, vec_ref,
     fc_s, proj_s, low_t, g2_s, second_s, gh_s, act_s, gpre_s) = rest
    t, d = mid_ref.shape
    r = d // blocks
    step = pl.program_id(0)
    mine = core[0]
    chunk = lax.rem(step + 2 * (1 - mine), 4)
    def valid_rows(at):
        return (at * rb + lax.broadcasted_iota(jnp.int32, (rb, 1), 0)) < lens[0]
    @pl.when(step == 0)
    def _():
        assemble(place, fcs, fc_s)
        assemble_chunks(place, projs, proj_s)
        low_t[...] = low_ref[...].T
        def begin(i, total):
            at = pl.ds(pl.multiple_of(i * rb, rb), rb)
            g = jnp.where(valid_rows(i), branch_scale * cot_ref[at, :].astype(F32), 0.0).astype(BF)
            g2_s[at, :] = g
            second_s[at, :] = jnp.zeros((rb, d), F32)
            gh_s[at, :] = jnp.zeros((rb, d), F32)
            return total + jnp.sum(g.astype(F32), axis=0, keepdims=True)
        vec_ref[0:1] = lax.fori_loop(0, t // rb, begin, jnp.zeros((1, d), F32))
    fcol = pl.ds(pl.multiple_of(chunk * d, d), d)
    fc = fc_s.at[:, :, fcol]
    bias = fb_ref[pl.ds(chunk, 1), :]
    if blocks % 4 == 0:
        per = blocks // 4
        proj = proj_s.at[pl.ds(chunk * per, per)]
    else:
        proj = proj_s.at[:, pl.ds(chunk, 1)]
    def rows_step(i, total):
        at = pl.ds(pl.multiple_of(i * rb, rb), rb)
        u = mm(low_ref[at, :], fc[...].reshape(d, d)) + bias
        sq = u * u
        th = jnp.tanh(0.7978845608028654 * u * (1.0 + 0.044715 * sq))
        up = 0.5 * (1.0 + th)
        act = (u * up).astype(BF)
        act_s[at, :] = act
        slope = up + u * (0.5 * 0.7978845608028654) * (1.0 - th * th) * (1.0 + 3 * 0.044715 * sq)
        w = proj[...].reshape(d, d)
        second_s[at, :] += mm(act, w)
        gp = mm_nt(g2_s[at, :], w) * slope
        gpb = gp.astype(BF)
        gpre_s[at, :] = gpb
        gh_s[at, :] += mm_nt(gpb, fc[...].reshape(d, d))
        return total + jnp.sum(gpb.astype(F32), axis=0, keepdims=True)
    fbg_ref[pl.ds(chunk, 1), :] = lax.fori_loop(0, t // rb, rows_step, jnp.zeros((1, d), F32))
    dfc = mm(low_t[...], gpre_s[...]).astype(BF).reshape(blocks, r, d)
    @pl.when(step < 2)
    def _():
        fsend_ref[...] = dfc
    @pl.when(step >= 2)
    def _():
        fkeep_ref[...] = dfc
    dproj = mm_tn(act_s[...], g2_s[...]).astype(BF)
    h = d // 2
    for half in range(2):
        @pl.when(mine == half)
        def _():
            for ref, cols in ((pkeep_ref, half), (psend_ref, 1 - half)):
                piece = dproj[:, cols * h : (cols + 1) * h]
                if blocks % 4 == 0:
                    for b in range(blocks // 4):
                        for j in range(4):
                            ref[b, :, j * h : (j + 1) * h] = piece[(b * 4 + j) * r : (b * 4 + j + 1) * r]
                else:
                    ref[0] = piece
    @pl.when(step == 3)
    def _():
        def finish(i, carry):
            at = pl.ds(pl.multiple_of(i * rb, rb), rb)
            mid = mid_ref[at, :]
            out_ref[at, :] = (mid + branch_scale * (second_s[at, :] + pb_ref[...])).astype(BF)
            n, scale = normalised(mid)
            gh = gh_s[at, :]
            cot = jnp.where(valid_rows(i), cot_ref[at, :].astype(F32), 0.0)
            gm = cot + norm_pull(n, scale, gain_ref[...], gh)
            gmid_ref[at, :] = gm
            gb = (branch_scale * gm).astype(BF)
            gbr_ref[at, :] = gb
            return (carry[0] + jnp.sum(gh * n, axis=0, keepdims=True),
                    carry[1] + jnp.sum(gh, axis=0, keepdims=True),
                    carry[2] + jnp.sum(gb.astype(F32), axis=0, keepdims=True))
        zero = jnp.zeros((1, d), F32)
        a, b, c = lax.fori_loop(0, t // rb, finish, (zero, zero, zero))
        vec_ref[1:2] = a
        vec_ref[2:3] = b
        vec_ref[3:4] = c

def mlp(core, place, lens, mid, low, cot, fb, pb, gain, fcs, projs, blocks, rb=256):
    t, d = mid.shape
    r, np_ = d // blocks, fcs[0][0].shape[0]
    smem = pl.BlockSpec(memory_space=pltpu.SMEM)
    if blocks % 4 == 0:
        pspec = pl.BlockSpec((blocks // 4, r, 2 * d), lambda i, c: (lax.rem(i + 2 * (1 - c[0]), 4), 0, 0))
    else:
        pspec = pl.BlockSpec((1, r, d // 2), lambda i, c: (0, 0, lax.rem(i + 2 * (1 - c[0]), 4)))
    big = jax.ShapeDtypeStruct((blocks, r, 2 * d), BF)
    return pl.pallas_call(
        functools.partial(mlp_kernel, len(fcs), blocks, rb),
        name="mlp",
        grid_spec=pltpu.PrefetchScalarGridSpec(
            num_scalar_prefetch=1,
            grid=(4,),
            in_specs=[
                smem, smem, whole((t, d)), whole((t, d)), whole((t, d)), whole((4, d)), whole((1, d)), whole((1, d)),
                *[whole((np_, r, 2 * d), (0, 0, at)) for _, at in fcs],
                *[whole((np_, r, 2 * d), (0, 0, at)) for _, at in projs],
            ],
            out_specs=[
                whole((t, d)), whole((t, d)), whole((t, d)),
                pl.BlockSpec((blocks, r, d), lambda i, c: (0, 0, jnp.minimum(i, 1))),
                pl.BlockSpec((blocks, r, d), lambda i, c: (0, 0, jnp.maximum(i - 2, 0))),
                pspec, pspec,
                whole((4, d)), whole((4, d)),
            ],
            scratch_shapes=[
                pltpu.VMEM((blocks, r, 4 * d), BF),
                pltpu.VMEM((blocks, 4, r, d), BF),
                pltpu.VMEM((d, t), BF),
                pltpu.VMEM((t, d), BF),
                pltpu.VMEM((t, d), F32),
                pltpu.VMEM((t, d), F32),
                pltpu.VMEM((t, d), BF),
                pltpu.VMEM((t, d), BF),
            ],
        ),
        out_shape=[
            jax.ShapeDtypeStruct((t, d), BF), jax.ShapeDtypeStruct((t, d), F32), jax.ShapeDtypeStruct((t, d), BF),
            big, big, big, big,
            jax.ShapeDtypeStruct((4, d), F32), jax.ShapeDtypeStruct((4, d), F32),
        ],
        compiler_params=params(),
        cost_estimate=cost(12 * t * d * 4 * d, 40e6, t * 4 * d),
    )(core, place, lens, mid, low, cot, fb, pb, gain, *[a for a, _ in fcs], *[a for a, _ in projs])

def unmix_kernel(blocks, core, lens, gbr_ref, attn_ref, w_ref, ga_ref, send_ref, keep_ref):
    t, d = gbr_ref.shape
    w = w_ref[...].reshape(d, d)
    seen = lax.broadcasted_iota(jnp.int32, (t, 1), 0) < lens[0]
    ga_ref[...] = jnp.where(seen, mm_nt(gbr_ref[...], w), 0.0).astype(BF)
    dw = mm_tn(attn_ref[...], gbr_ref[...]).astype(BF)
    h = d // 2
    for half in range(2):
        @pl.when(core[0] == half)
        def _():
            keep_ref[...] = dw[:, half * h : (half + 1) * h].reshape(keep_ref.shape)
            send_ref[...] = dw[:, (1 - half) * h : (2 - half) * h].reshape(send_ref.shape)

def unmix(core, lens, gbr, attn, w, blocks):
    t, d = gbr.shape
    smem = pl.BlockSpec(memory_space=pltpu.SMEM)
    piece = jax.ShapeDtypeStruct((blocks, d // blocks, d // 2), BF)
    return pl.pallas_call(
        functools.partial(unmix_kernel, blocks),
        name="unmix",
        in_specs=[smem, smem] + [pl.BlockSpec(memory_space=pltpu.VMEM)] * 3,
        out_shape=[jax.ShapeDtypeStruct((t, d), BF), piece, piece],
        compiler_params=params(0),
        cost_estimate=cost(4 * t * d * d, 9e6),
    )(core, lens, gbr, attn, w)

def unproject_kernel(blocks, core, low_ref, g_ref, send_ref, keep_ref, sums_ref):
    d = low_ref.shape[1]
    r = d // blocks
    low_t = low_ref[...].T
    q = mm(low_t, g_ref[0]).astype(BF).reshape(blocks, r, d)
    v = mm(low_t, g_ref[2]).astype(BF).reshape(blocks, r, d)
    k = mm(low_t, g_ref[1]).astype(BF).reshape(blocks, r, d)
    h = d // 2
    for half, refs in ((0, (keep_ref, send_ref)), (1, (send_ref, keep_ref))):
        @pl.when(core[0] == half)
        def _():
            refs[0][:, :, :d] = q
            refs[0][:, :, d:] = k[:, :, :h]
            refs[1][:, :, :h] = k[:, :, h:]
            refs[1][:, :, h:] = v
    for part in range(3):
        sums_ref[part : part + 1] = jnp.sum(g_ref[part].astype(F32), axis=0, keepdims=True)

def unproject(core, low, g, blocks):
    t, d = low.shape
    piece = jax.ShapeDtypeStruct((blocks, d // blocks, d // 2 * 3), BF)
    return pl.pallas_call(
        functools.partial(unproject_kernel, blocks),
        name="unproject",
        in_specs=[pl.BlockSpec(memory_space=pltpu.SMEM)] + [pl.BlockSpec(memory_space=pltpu.VMEM)] * 2,
        out_shape=[piece, piece, jax.ShapeDtypeStruct((3, d), F32)],
        compiler_params=params(0),
        cost_estimate=cost(6 * t * d * d, 10e6),
    )(core, low, g)

def final_kernel(x_ref, g_ref, w_ref, gmid_ref, gain_ref, out_ref, vec_ref):
    d = x_ref.shape[1]
    w = w_ref[...].reshape(d, 3 * d)
    gh = mm_nt(g_ref[0], w[:, :d]) + mm_nt(g_ref[1], w[:, d : 2 * d]) + mm_nt(g_ref[2], w[:, 2 * d :])
    n, scale = normalised(x_ref[...].astype(F32))
    out_ref[...] = (gmid_ref[...] + norm_pull(n, scale, gain_ref[...], gh)).astype(BF)
    @pl.when(pl.program_id(0) == 0)
    def _():
        vec_ref[...] = jnp.zeros_like(vec_ref)
    vec_ref[0:1] += jnp.sum(gh * n, axis=0, keepdims=True)
    vec_ref[1:2] += jnp.sum(gh, axis=0, keepdims=True)

def final(x, g, w, gmid, gain, rows=256):
    t, d = x.shape
    return pl.pallas_call(
        final_kernel,
        name="final",
        grid=(t // rows,),
        in_specs=[
            pl.BlockSpec((rows, d), lambda i: (i, 0)),
            pl.BlockSpec((3, rows, d), lambda i: (0, i, 0)),
            whole(w.shape),
            pl.BlockSpec((rows, d), lambda i: (i, 0)),
            whole((1, d)),
        ],
        out_specs=[pl.BlockSpec((rows, d), lambda i: (i, 0)), whole((2, d))],
        out_shape=[jax.ShapeDtypeStruct((t, d), BF), jax.ShapeDtypeStruct((2, d), F32)],
        compiler_params=params(),
        cost_estimate=cost(6 * t * d * d, 15e6),
    )(x, g, w, gmid, gain)


class Grid:
    def __init__(self, mesh, rows):
        wide, narrow = mesh.shape["wide"], mesh.shape["narrow"]
        self.count = wide * narrow
        self.paired = narrow == 4 and wide % 2 == 0 and rows % 8 == 0
        self.blocks = self.count // 2 if self.paired else 1
        self.z = wide // 2

    def index(self, z, x, y, c):
        return ((z * 2 + x) * 2 + y) * 2 + c

    def places(self):
        return [
            (z, x, y, c) for z in range(self.z) for x in range(2) for y in range(2) for c in range(2)
        ]

    def perm(self, target):
        return [(self.index(*at), self.index(*target(*at))) for at in self.places()]

    def here(self):
        w, n = lax.axis_index("wide"), lax.axis_index("narrow")
        return w // 2, w % 2, n // 2, n % 2

    def table(self):
        rows = []
        for z0, x0, y0, c0 in self.places():
            mine = []
            for half in (c0, 1 - c0):
                for kb in range(2):
                    line = [half]
                    for ka in range(2):
                        for kz in range(self.z):
                            kx, ky = (ka, kb) if half == 0 else (kb, ka)
                            line.append((((z0 - kz) % self.z) * 2 + (x0 ^ kx)) * 2 + (y0 ^ ky))
                    mine.append(line)
            rows.append(mine)
        return np.array(rows, np.int32)

    def send(self, value, target):
        return lax.ppermute(value, AXES, self.perm(target))

    def other_core(self, value):
        return self.send(value, lambda z, x, y, c: (z, x, y, 1 - c))

    def along(self, value, turn):
        return self.send(
            value,
            lambda z, x, y, c: (z, 1 - x, y, c) if c == turn else (z, x, 1 - y, c),
        )

    def up(self, value, k):
        return self.send(value, lambda z, x, y, c: ((z + k) % self.z, x, y, c))


def both(first, own, other, axis):
    return jnp.where(
        first, jnp.concatenate([own, other], axis), jnp.concatenate([other, own], axis)
    )


def pair_rows(grid, shard):
    c = grid.here()[3]
    h = shard.shape[1] // 2
    other = grid.other_core(lax.dynamic_slice_in_dim(shard, (1 - c) * h, h, 1))
    return both(c == 0, lax.dynamic_slice_in_dim(shard, c * h, h, 1), other, 0)


def spread_z(grid, pair):
    return jnp.stack([pair] + [grid.up(pair, k) for k in range(1, grid.z)])


def spread_rest(grid, stack):
    two = jnp.concatenate([stack, grid.along(stack, 0)], 0)
    far = grid.along(two, 1)
    return [two, far, grid.other_core(two), grid.other_core(far)]


def after(value, *earlier):
    return lax.optimization_barrier((value, *earlier))[0]


def add(a, b):
    return (a.astype(F32) + b.astype(F32)).astype(BF)


def collect(grid, sends, keeps):
    z, x, y, c = grid.here()
    got = [grid.other_core(s) for s in sends]
    own = jnp.concatenate([add(k, g) for k, g in zip(keeps, got)], 2)
    blocks, r, w = own.shape
    own = own.reshape(grid.z, 2, 2, r, w)
    pick = lambda v, at, axis: lax.dynamic_index_in_dim(v, at, axis, keepdims=False)
    away = jnp.where(c == 0, pick(own, 1 - x, 1), pick(own, 1 - y, 2))
    stay = jnp.where(c == 0, pick(own, x, 1), pick(own, y, 2))
    own = add(stay, grid.along(away, 0))
    left = jnp.where(c == 0, y, x)
    own = add(pick(own, left, 1), grid.along(pick(own, 1 - left, 1), 1))
    total = pick(own, z, 0).astype(F32)
    for k in range(1, grid.z):
        total = total + grid.up(pick(own, (z + k) % grid.z, 0), k).astype(F32)
    return total


def own_rows(grid, total):
    c = grid.here()[3]
    r = total.shape[0] // 2
    other = grid.other_core(lax.dynamic_slice_in_dim(total, (1 - c) * r, r, 0))
    return both(c == 0, lax.dynamic_slice_in_dim(total, c * r, r, 0), other, 1)


def to_chunks(pair):
    r = pair.shape[0] // 4
    return jnp.concatenate([pair[j * r : (j + 1) * r] for j in range(4)], 1)


def from_chunks(total):
    w = total.shape[1] // 4
    return jnp.concatenate([total[:, j * w : (j + 1) * w] for j in range(4)], 0)


def gather_small(vectors):
    flat = jnp.concatenate([v.astype(F32) for v in vectors]).astype(BF)
    full = lax.all_gather(flat, AXES, axis=0, tiled=False).astype(F32)
    out, at = [], 0
    for v in vectors:
        out.append(full[:, at : at + v.shape[0]].reshape(-1))
        at += v.shape[0]
    return out


def scatter_small(count, vectors):
    parts = [v.reshape(count, -1) for v in vectors]
    got = lax.all_to_all(jnp.concatenate(parts, 1), AXES, 0, 0, tiled=True)
    total = jnp.sum(got, axis=0)
    out, at = [], 0
    for p in parts:
        out.append(total[at : at + p.shape[1]])
        at += p.shape[1]
    return out


def halves_of(weight):
    h = weight.shape[1] // 2
    return [weight[None, :, :h], weight[None, :, h:]]


def local(
    mesh,
    tokens,
    norm1_gain,
    norm1_bias,
    qkv_weight,
    qkv_bias,
    out_weight,
    out_bias,
    norm2_gain,
    norm2_bias,
    fc_weight,
    fc_bias,
    proj_weight,
    proj_bias,
    seq_lengths,
    out_cotangent,
):
    d = tokens.shape[1]
    grid = Grid(mesh, out_weight.shape[0])
    blocks = grid.blocks
    if grid.paired:
        place = jnp.asarray(grid.table())[lax.axis_index(AXES)]
        core = grid.here()[3].reshape(1).astype(jnp.int32)
        stack_qkv = spread_z(grid, pair_rows(grid, qkv_weight))
        first = jnp.concatenate([pair_rows(grid, fc_weight), pair_rows(grid, out_weight)], 1)
        second = to_chunks(pair_rows(grid, proj_weight))
        stack_qkv, first, second = lax.optimization_barrier((stack_qkv, first, second))
        stack_first = spread_z(grid, first)
        qkv_sources = spread_rest(grid, stack_qkv)
        first_sources = spread_rest(grid, stack_first)
        second_sources = spread_rest(grid, spread_z(grid, after(second, stack_first)))
        fcs, outs = [(s, 0) for s in first_sources], first_sources
        out_at = 4
        projs = [(s, 0) for s in second_sources]
    else:
        place = jnp.asarray(np.array([[0, 0], [1, 0]], np.int32))
        core = jnp.zeros((1,), jnp.int32)
        full = lambda v: lax.all_gather(v, AXES, axis=0, tiled=True)
        qkv_sources = halves_of(full(qkv_weight))
        fcs = [(s, 0) for s in halves_of(full(fc_weight))]
        outs, out_at = halves_of(full(out_weight)), 0
        wide = full(proj_weight)
        projs = [(to_chunks(s[0])[None], 0) for s in halves_of(wide)]
    gain_one, shift_one, bias_qv, bias_out, gain_two, shift_two, bias_fc, bias_proj = gather_small(
        [norm1_gain, norm1_bias, qkv_bias, out_bias, norm2_gain, norm2_bias, fc_bias, proj_bias]
    )
    row = lambda v: v.reshape(1, d)
    bias_qkv = jnp.stack([bias_qv[:d], jnp.zeros((d,), F32), bias_qv[d:]])
    qkv, low_one, qkv_full = project(
        place, tokens, row(gain_one), row(shift_one), bias_qkv, qkv_sources, blocks
    )
    mixed_t, mixed, stats = attend(seq_lengths, qkv, d // 128, 0, 512)
    middle, low_two, out_full = mix(
        place, mixed, tokens, row(bias_out), row(gain_two), row(shift_two), outs, blocks, out_at
    )
    (layer_out, grad_middle, grad_branch, fc_send, fc_keep, proj_send, proj_keep, fc_bias_term, sums) = mlp(
        core, place, seq_lengths, middle, low_two, out_cotangent, bias_fc.reshape(4, d), row(bias_proj),
        row(gain_two), fcs, projs, blocks,
    )
    grad_mixed, out_send, out_keep = unmix(core, seq_lengths, grad_branch, mixed, out_full, blocks)
    grad_qkv = attend_grad(qkv, grad_mixed, mixed_t, stats)
    qkv_send, qkv_keep, qkv_sums = unproject(core, low_one, grad_qkv, blocks)
    input_grad, first_sums = final(tokens, grad_qkv, qkv_full, grad_middle, row(gain_one))
    if grid.paired:
        total = collect(grid, [fc_send, proj_send, out_send], [fc_keep, proj_keep, out_keep])
        fc_wide, out_wide = fc_keep.shape[2], out_keep.shape[2]
        fc_weight_grad = own_rows(grid, total[:, :fc_wide])
        proj_weight_grad = own_rows(grid, from_chunks(total[:, fc_wide : 2 * fc_wide]))
        out_weight_grad = own_rows(grid, total[:, 2 * fc_wide :])
        qkv_weight_grad = own_rows(grid, collect(grid, [qkv_send], [qkv_keep]))
    else:
        reduce = lambda v: lax.psum_scatter(v.astype(F32), AXES, scatter_dimension=0, tiled=True)
        side = lambda k, s: jnp.concatenate([k[0], s[0]], 1)
        fc_weight_grad = reduce(side(fc_keep, fc_send))
        out_weight_grad = reduce(side(out_keep, out_send))
        qkv_weight_grad = reduce(side(qkv_keep, qkv_send))
        proj_weight_grad = reduce(
            jnp.concatenate([from_chunks(proj_keep[0]), from_chunks(proj_send[0])], 1)
        )
    small = scatter_small(
        grid.count,
        [
            first_sums[0], first_sums[1], jnp.concatenate([qkv_sums[0], qkv_sums[2]]), sums[3],
            sums[1], sums[2], fc_bias_term.reshape(-1), sums[0],
        ],
    )
    return (
        layer_out,
        input_grad,
        small[0],
        small[1],
        qkv_weight_grad,
        small[2],
        out_weight_grad,
        small[3],
        small[4],
        small[5],
        fc_weight_grad,
        small[6],
        proj_weight_grad,
        small[7],
    )


def solution(mesh):
    matrix, vector = P(AXES, None), P(AXES)
    ins = (
        matrix, vector, vector, matrix, vector, matrix, vector, vector,
        vector, matrix, vector, matrix, vector, vector, matrix,
    )
    outs = (
        matrix, matrix, vector, vector, matrix, vector, matrix, vector,
        vector, vector, matrix, vector, matrix, vector,
    )
    return jax.shard_map(
        functools.partial(local, mesh), mesh=mesh, in_specs=ins, out_specs=outs, check_vma=False
    )
```

```python
import functools
import math

import jax
import jax.numpy as jnp
import numpy as np
from jax import lax
from jax.experimental import pallas as pl
from jax.experimental.pallas import tpu as pltpu
from jax.sharding import PartitionSpec as P

AXES = ("wide", "narrow")
BF, F32 = jnp.bfloat16, jnp.float32
VMEM_CAP = 58 << 20
LOG2E = 1.4426950408889634

def params(n=1, cap=VMEM_CAP):
    return pltpu.CompilerParams(dimension_semantics=("arbitrary",) * n, vmem_limit_bytes=cap)

def cost(flops, bytes_accessed, trans=0):
    return pl.CostEstimate(flops=int(flops), bytes_accessed=int(bytes_accessed), transcendentals=int(trans))

def mm(a, b):
    return jnp.dot(a, b, preferred_element_type=F32)

def diagonal_mask(rows, cols):
    key_at = lax.broadcasted_iota(jnp.int32, (rows, cols), 0)
    query_at = lax.broadcasted_iota(jnp.int32, (rows, cols), 1)
    return key_at <= query_at

def attend_kernel(qb, len_ref, qkv_ref, out_t_ref, out_ref, stat_ref, v_t, q_t):
    slot = qkv_ref.shape[1]
    q_t[...] = (qkv_ref[0] * jnp.asarray(0.125, BF)).T
    v_t[...] = qkv_ref[2].T
    half = lax.broadcasted_iota(jnp.int32, (128, 1), 0) < 64
    causal = diagonal_mask(qb, qb)
    length = len_ref[0]
    for i in range(slot // qb):
        cols = slice(i * qb, (i + 1) * qb)
        parts = []
        for head in range(2):
            mine = half if head == 0 else jnp.logical_not(half)
            qh = jnp.where(mine, q_t[:, cols], jnp.zeros((), BF))
            s_low = mm(qkv_ref[1, : i * qb, :], qh) if i else None
            s_dia = jnp.where(causal, mm(qkv_ref[1, cols, :], qh), -1e30)
            top = jnp.max(s_dia, axis=0, keepdims=True)
            if i:
                top = jnp.maximum(top, jnp.max(s_low, axis=0, keepdims=True))
            e_dia = jnp.exp(s_dia - top)
            total = jnp.sum(e_dia, axis=0, keepdims=True)
            vh = v_t[head * 64 : head * 64 + 64, :]
            acc = mm(vh[:, cols], e_dia.astype(BF))
            if i:
                e_low = jnp.exp(s_low - top)
                total = total + jnp.sum(e_low, axis=0, keepdims=True)
                acc = acc + mm(vh[:, : i * qb], e_low.astype(BF))
            stat_ref[0, head : head + 1, cols] = top + jnp.log(total)
            parts.append(acc / total)
        both = jnp.concatenate(parts, axis=0)
        seen = (i * qb + lax.broadcasted_iota(jnp.int32, (1, qb), 1)) < length
        both = jnp.where(seen, both, 0.0)
        out_t_ref[:, cols] = both
        out_ref[cols, :] = both.T.astype(BF)

def attend(lengths, qkv, pairs, first, qb=256):
    slot, width = qkv.shape[1], qkv.shape[2]
    return pl.pallas_call(
        functools.partial(attend_kernel, qb),
        name="attend",
        grid=(pairs,),
        in_specs=[
            pl.BlockSpec(memory_space=pltpu.SMEM),
            pl.BlockSpec((3, slot, 128), lambda j: (0, 0, j + first)),
        ],
        out_specs=[
            pl.BlockSpec((128, slot), lambda j: (j, 0)),
            pl.BlockSpec((slot, 128), lambda j: (0, j)),
            pl.BlockSpec((1, 2, slot), lambda j: (j, 0, 0)),
        ],
        out_shape=[
            jax.ShapeDtypeStruct((pairs * 128, slot), F32),
            jax.ShapeDtypeStruct((slot, pairs * 128), BF),
            jax.ShapeDtypeStruct((pairs, 2, slot), F32),
        ],
        scratch_shapes=[pltpu.VMEM((128, slot), BF), pltpu.VMEM((128, slot), BF)],
        compiler_params=params(),
        cost_estimate=cost(pairs * 2 * slot * slot * 256, 8e6 * pairs / 6, pairs * slot * slot),
    )(lengths, qkv)

def attend_grad_kernel(qb, qkv_ref, grad_ref, out_t_ref, stat_ref, g_ref, q_t, do_t, k_t, qs, dq_t, dk_s, dv_s):
    slot = qkv_ref.shape[1]
    qs[...] = qkv_ref[0] * jnp.asarray(0.125, BF)
    q_t[...] = qs[...].T
    k_t[...] = qkv_ref[1].T
    do_t[...] = grad_ref[...].T
    half = lax.broadcasted_iota(jnp.int32, (128, 1), 0) < 64
    half_lane = lax.broadcasted_iota(jnp.int32, (1, 128), 1) < 64
    causal = diagonal_mask(qb, qb)
    zero = jnp.zeros((), BF)
    prod = do_t[...].astype(F32) * out_t_ref[...]
    delta = [jnp.sum(prod[h * 64 : h * 64 + 64], axis=0, keepdims=True) for h in range(2)]
    for i in range(slot // qb):
        cols = slice(i * qb, (i + 1) * qb)
        end = (i + 1) * qb
        dv_new = dk_new = None
        for head in range(2):
            mine = half if head == 0 else jnp.logical_not(half)
            mine_lane = half_lane if head == 0 else jnp.logical_not(half_lane)
            qh_t = jnp.where(mine, q_t[:, cols], zero)
            doh_t = jnp.where(mine, do_t[:, cols], zero)
            qh = jnp.where(mine_lane, qs[cols, :], zero)
            doh = jnp.where(mine_lane, grad_ref[cols, :], zero)
            stat = stat_ref[0, head : head + 1, cols]
            dl = delta[head][:, cols]
            s = mm(qkv_ref[1, :end, :], qh_t)
            dp = mm(qkv_ref[2, :end, :], doh_t)
            p = jnp.exp(s - stat)
            p_dia = jnp.where(causal, p[i * qb :], 0.0)
            p = jnp.concatenate([p[: i * qb], p_dia], axis=0) if i else p_dia
            ds = (p * (dp - dl)).astype(BF)
            pb = p.astype(BF)
            dv_h = mm(pb, doh)
            dk_h = mm(ds, qh)
            dv_new = dv_h if head == 0 else dv_new + dv_h
            dk_new = dk_h if head == 0 else dk_new + dk_h
            dq_t[head * 64 : head * 64 + 64, cols] = mm(k_t[head * 64 : head * 64 + 64, :end], ds)
        if i:
            dv_s[: i * qb] += dv_new[: i * qb]
            dk_s[: i * qb] += dk_new[: i * qb]
        dv_s[cols] = dv_new[i * qb :]
        dk_s[cols] = dk_new[i * qb :]
    g_ref[0] = (dq_t[...] * 0.125).T.astype(BF)
    g_ref[1] = dk_s[...].astype(BF)
    g_ref[2] = dv_s[...].astype(BF)

def attend_grad(qkv, grad, out_t, stat, first, qb=256):
    slot = qkv.shape[1]
    pairs = out_t.shape[0] // 128
    width = pairs * 128
    return pl.pallas_call(
        functools.partial(attend_grad_kernel, qb),
        name="attend_grad",
        grid=(pairs,),
        in_specs=[
            pl.BlockSpec((3, slot, 128), lambda j: (0, 0, j + first)),
            pl.BlockSpec((slot, 128), lambda j: (0, j + first)),
            pl.BlockSpec((128, slot), lambda j: (j, 0)),
            pl.BlockSpec((1, 2, slot), lambda j: (j, 0, 0)),
        ],
        out_specs=pl.BlockSpec((3, slot, 128), lambda j: (0, 0, j)),
        out_shape=jax.ShapeDtypeStruct((3, slot, width), BF),
        scratch_shapes=[
            pltpu.VMEM((128, slot), BF),
            pltpu.VMEM((128, slot), BF),
            pltpu.VMEM((128, slot), BF),
            pltpu.VMEM((slot, 128), BF),
            pltpu.VMEM((128, slot), F32),
            pltpu.VMEM((slot, 128), F32),
            pltpu.VMEM((slot, 128), F32),
        ],
        compiler_params=params(),
        cost_estimate=cost(pairs * 5 * slot * slot * 256, 16e6 * pairs / 6, pairs * 2 * slot * slot),
    )(qkv, grad, out_t, stat)
branch_scale = 1.0 / math.sqrt(48.0)
norm_epsilon = 1e-05
WHOLE = dict(pipeline_mode=pl.Buffered(1))

def mm_nt(a, b):
    return lax.dot_general(a, b, (((1,), (1,)), ((), ())), preferred_element_type=F32)

def mm_tn(a, b):
    return lax.dot_general(a, b, (((0,), (0,)), ((), ())), preferred_element_type=F32)

def normalised(v):
    mean = jnp.mean(v, axis=-1, keepdims=True)
    centred = v - mean
    var = jnp.mean(centred * centred, axis=-1, keepdims=True)
    scale = lax.rsqrt(var + norm_epsilon)
    return centred * scale, scale

def norm_pull(n, scale, gain, u):
    ug = u * gain
    a = jnp.mean(ug, axis=-1, keepdims=True)
    b = jnp.mean(ug * n, axis=-1, keepdims=True)
    return (ug - a - n * b) * scale

def whole(shape, index=None):
    zeros = (0,) * len(shape)
    return pl.BlockSpec(shape, (lambda *_: index or zeros), **WHOLE)

def assemble(place, sources, target, at=0):
    wide = sources[0].shape[2]
    for s, source in enumerate(sources):
        for half in range(2):
            @pl.when(place[s, 0] == half)
            def _():
                for p in range(source.shape[0]):
                    target[place[s, 1 + p], :, half * wide : (half + 1) * wide] = source[p]

def assemble_chunks(place, sources, target):
    wide = sources[0].shape[2] // 4
    for s, source in enumerate(sources):
        for half in range(2):
            @pl.when(place[s, 0] == half)
            def _():
                for p in range(source.shape[0]):
                    for j in range(4):
                        target[place[s, 1 + p], j, :, half * wide : (half + 1) * wide] = source[p, :, j * wide : (j + 1) * wide]

def project_kernel(n_src, place, x_ref, gain_ref, shift_ref, bias_ref, *rest):
    sources, (qkv_ref, low_ref, w_ref) = rest[:n_src], rest[n_src:]
    @pl.when(pl.program_id(0) == 0)
    def _():
        assemble(place, sources, w_ref)
    n, _ = normalised(x_ref[...].astype(F32))
    low = (n * gain_ref[...] + shift_ref[...]).astype(BF)
    low_ref[...] = low
    d = low.shape[1]
    for part in range(3):
        w = w_ref[:, :, part * d : (part + 1) * d].reshape(d, d)
        qkv_ref[part] = (mm(low, w) + bias_ref[part : part + 1]).astype(BF)

def project(place, x, gain, shift, bias, sources, blocks, rows=256):
    t, d = x.shape
    r, wide = d // blocks, sources[0].shape[2]
    return pl.pallas_call(
        functools.partial(project_kernel, len(sources)),
        name="project",
        grid_spec=pltpu.PrefetchScalarGridSpec(
            num_scalar_prefetch=1,
            grid=(t // rows,),
            in_specs=[
                pl.BlockSpec((rows, d), lambda i, p: (i, 0)),
                whole((1, d)), whole((1, d)), whole((3, d)),
                *[whole(s.shape) for s in sources],
            ],
            out_specs=[
                pl.BlockSpec((3, rows, d), lambda i, p: (0, i, 0)),
                pl.BlockSpec((rows, d), lambda i, p: (i, 0)),
                whole((blocks, r, 2 * wide)),
            ],
        ),
        out_shape=[
            jax.ShapeDtypeStruct((3, t, d), BF),
            jax.ShapeDtypeStruct((t, d), BF),
            jax.ShapeDtypeStruct((blocks, r, 2 * wide), BF),
        ],
        compiler_params=params(),
        cost_estimate=cost(2 * t * d * 3 * d, 18e6),
    )(place, x, gain, shift, bias, *sources)

def mix_kernel(n_src, place, x_ref, bias_ref, gain_ref, shift_ref, *rest):
    sources, parts, (mid_ref, low_ref, w_ref) = rest[:n_src], rest[n_src:-3], rest[-3:]
    @pl.when(pl.program_id(0) == 0)
    def _():
        assemble(place, sources, w_ref)
    d = x_ref.shape[1]
    w = w_ref[...].reshape(d, d)
    mid = x_ref[...].astype(F32) + branch_scale * (mm(jnp.concatenate([p[...] for p in parts], 1), w) + bias_ref[...])
    mid_ref[...] = mid
    n, _ = normalised(mid)
    low_ref[...] = (n * gain_ref[...] + shift_ref[...]).astype(BF)

def mix(place, parts, x, bias, gain, shift, sources, blocks, column, rows=256):
    t, d = x.shape
    r, np_ = d // blocks, sources[0].shape[0]
    return pl.pallas_call(
        functools.partial(mix_kernel, len(sources)),
        name="mix",
        grid_spec=pltpu.PrefetchScalarGridSpec(
            num_scalar_prefetch=1,
            grid=(t // rows,),
            in_specs=[
                pl.BlockSpec((rows, d), lambda i, p: (i, 0)),
                whole((1, d)), whole((1, d)), whole((1, d)),
                *[whole((np_, r, d // 2), (0, 0, column)) for s in sources],
                *[pl.BlockSpec((rows, p.shape[1]), lambda i, p: (i, 0)) for p in parts],
            ],
            out_specs=[
                pl.BlockSpec((rows, d), lambda i, p: (i, 0)),
                pl.BlockSpec((rows, d), lambda i, p: (i, 0)),
                whole((blocks, r, d)),
            ],
        ),
        out_shape=[
            jax.ShapeDtypeStruct((t, d), F32),
            jax.ShapeDtypeStruct((t, d), BF),
            jax.ShapeDtypeStruct((blocks, r, d), BF),
        ],
        compiler_params=params(),
        cost_estimate=cost(2 * t * d * d, 9e6),
    )(place, x, bias, gain, shift, *sources, *parts)

def mlp_kernel(n_src, blocks, rb, core, place, lens, mid_ref, low_ref, cot_ref, fb_ref, pb_ref, gain_ref, *rest):
    fcs, projs, rest = rest[:n_src], rest[n_src : 2 * n_src], rest[2 * n_src :]
    (out_ref, gmid_ref, gbr_ref, fsend_ref, fkeep_ref, psend_ref, pkeep_ref, fbg_ref, vec_ref,
     fc_s, proj_s, low_t, g2_s, second_s, gh_s, act_s, gpre_s) = rest
    t, d = mid_ref.shape
    r = d // blocks
    step = pl.program_id(0)
    mine = core[0]
    chunk = lax.rem(step + 2 * (1 - mine), 4)
    def valid_rows(at):
        return (at * rb + lax.broadcasted_iota(jnp.int32, (rb, 1), 0)) < lens[0]
    @pl.when(step == 0)
    def _():
        assemble(place, fcs, fc_s)
        assemble_chunks(place, projs, proj_s)
        low_t[...] = low_ref[...].T
        def begin(i, total):
            at = pl.ds(pl.multiple_of(i * rb, rb), rb)
            g = jnp.where(valid_rows(i), branch_scale * cot_ref[at, :].astype(F32), 0.0).astype(BF)
            g2_s[at, :] = g
            second_s[at, :] = jnp.zeros((rb, d), F32)
            gh_s[at, :] = jnp.zeros((rb, d), F32)
            return total + jnp.sum(g.astype(F32), axis=0, keepdims=True)
        vec_ref[0:1] = lax.fori_loop(0, t // rb, begin, jnp.zeros((1, d), F32))
    fcol = pl.ds(pl.multiple_of(chunk * d, d), d)
    fc = fc_s.at[:, :, fcol]
    bias = fb_ref[pl.ds(chunk, 1), :]
    if blocks % 4 == 0:
        per = blocks // 4
        proj = proj_s.at[pl.ds(chunk * per, per)]
    else:
        proj = proj_s.at[:, pl.ds(chunk, 1)]
    def rows_step(i, total):
        at = pl.ds(pl.multiple_of(i * rb, rb), rb)
        u = mm(low_ref[at, :], fc[...].reshape(d, d)) + bias
        sq = u * u
        th = jnp.tanh(0.7978845608028654 * u * (1.0 + 0.044715 * sq))
        up = 0.5 * (1.0 + th)
        act = (u * up).astype(BF)
        act_s[at, :] = act
        slope = up + u * (0.5 * 0.7978845608028654) * (1.0 - th * th) * (1.0 + 3 * 0.044715 * sq)
        w = proj[...].reshape(d, d)
        second_s[at, :] += mm(act, w)
        gp = mm_nt(g2_s[at, :], w) * slope
        gpb = gp.astype(BF)
        gpre_s[at, :] = gpb
        gh_s[at, :] += mm_nt(gpb, fc[...].reshape(d, d))
        return total + jnp.sum(gpb.astype(F32), axis=0, keepdims=True)
    fbg_ref[pl.ds(chunk, 1), :] = lax.fori_loop(0, t // rb, rows_step, jnp.zeros((1, d), F32))
    dfc = mm(low_t[...], gpre_s[...]).astype(BF).reshape(blocks, r, d)
    @pl.when(step < 2)
    def _():
        fsend_ref[...] = dfc
    @pl.when(step >= 2)
    def _():
        fkeep_ref[...] = dfc
    dproj = mm_tn(act_s[...], g2_s[...]).astype(BF)
    h = d // 2
    for half in range(2):
        @pl.when(mine == half)
        def _():
            for ref, cols in ((pkeep_ref, half), (psend_ref, 1 - half)):
                piece = dproj[:, cols * h : (cols + 1) * h]
                if blocks % 4 == 0:
                    for b in range(blocks // 4):
                        for j in range(4):
                            ref[b, :, j * h : (j + 1) * h] = piece[(b * 4 + j) * r : (b * 4 + j + 1) * r]
                else:
                    ref[0] = piece
    @pl.when(step == 3)
    def _():
        def finish(i, carry):
            at = pl.ds(pl.multiple_of(i * rb, rb), rb)
            mid = mid_ref[at, :]
            out_ref[at, :] = (mid + branch_scale * (second_s[at, :] + pb_ref[...])).astype(BF)
            n, scale = normalised(mid)
            gh = gh_s[at, :]
            cot = jnp.where(valid_rows(i), cot_ref[at, :].astype(F32), 0.0)
            gm = cot + norm_pull(n, scale, gain_ref[...], gh)
            gmid_ref[at, :] = gm
            gb = (branch_scale * gm).astype(BF)
            gbr_ref[at, :] = gb
            return (carry[0] + jnp.sum(gh * n, axis=0, keepdims=True),
                    carry[1] + jnp.sum(gh, axis=0, keepdims=True),
                    carry[2] + jnp.sum(gb.astype(F32), axis=0, keepdims=True))
        zero = jnp.zeros((1, d), F32)
        a, b, c = lax.fori_loop(0, t // rb, finish, (zero, zero, zero))
        vec_ref[1:2] = a
        vec_ref[2:3] = b
        vec_ref[3:4] = c

def mlp(core, place, lens, mid, low, cot, fb, pb, gain, fcs, projs, blocks, rb=256):
    t, d = mid.shape
    r, np_ = d // blocks, fcs[0][0].shape[0]
    smem = pl.BlockSpec(memory_space=pltpu.SMEM)
    if blocks % 4 == 0:
        pspec = pl.BlockSpec((blocks // 4, r, 2 * d), lambda i, c: (lax.rem(i + 2 * (1 - c[0]), 4), 0, 0))
    else:
        pspec = pl.BlockSpec((1, r, d // 2), lambda i, c: (0, 0, lax.rem(i + 2 * (1 - c[0]), 4)))
    big = jax.ShapeDtypeStruct((blocks, r, 2 * d), BF)
    return pl.pallas_call(
        functools.partial(mlp_kernel, len(fcs), blocks, rb),
        name="mlp",
        grid_spec=pltpu.PrefetchScalarGridSpec(
            num_scalar_prefetch=1,
            grid=(4,),
            in_specs=[
                smem, smem, whole((t, d)), whole((t, d)), whole((t, d)), whole((4, d)), whole((1, d)), whole((1, d)),
                *[whole((np_, r, 2 * d), (0, 0, at)) for _, at in fcs],
                *[whole((np_, r, 2 * d), (0, 0, at)) for _, at in projs],
            ],
            out_specs=[
                whole((t, d)), whole((t, d)), whole((t, d)),
                pl.BlockSpec((blocks, r, d), lambda i, c: (0, 0, jnp.minimum(i, 1))),
                pl.BlockSpec((blocks, r, d), lambda i, c: (0, 0, jnp.maximum(i - 2, 0))),
                pspec, pspec,
                whole((4, d)), whole((4, d)),
            ],
            scratch_shapes=[
                pltpu.VMEM((blocks, r, 4 * d), BF),
                pltpu.VMEM((blocks, 4, r, d), BF),
                pltpu.VMEM((d, t), BF),
                pltpu.VMEM((t, d), BF),
                pltpu.VMEM((t, d), F32),
                pltpu.VMEM((t, d), F32),
                pltpu.VMEM((t, d), BF),
                pltpu.VMEM((t, d), BF),
            ],
        ),
        out_shape=[
            jax.ShapeDtypeStruct((t, d), BF), jax.ShapeDtypeStruct((t, d), F32), jax.ShapeDtypeStruct((t, d), BF),
            big, big, big, big,
            jax.ShapeDtypeStruct((4, d), F32), jax.ShapeDtypeStruct((4, d), F32),
        ],
        compiler_params=params(),
        cost_estimate=cost(12 * t * d * 4 * d, 40e6, t * 4 * d),
    )(core, place, lens, mid, low, cot, fb, pb, gain, *[a for a, _ in fcs], *[a for a, _ in projs])

def unmix_kernel(core, lens, gbr_ref, w_ref, *rest):
    parts, (ga_ref, send_ref, keep_ref) = rest[:-3], rest[-3:]
    t, d = gbr_ref.shape
    w = w_ref[...].reshape(d, d)
    seen = lax.broadcasted_iota(jnp.int32, (t, 1), 0) < lens[0]
    ga_ref[...] = jnp.where(seen, mm_nt(gbr_ref[...], w), 0.0).astype(BF)
    dw = jnp.concatenate([mm_tn(p[...], gbr_ref[...]).astype(BF) for p in parts], 0)
    h = d // 2
    for half in range(2):
        @pl.when(core[0] == half)
        def _():
            keep_ref[...] = dw[:, half * h : (half + 1) * h].reshape(keep_ref.shape)
            send_ref[...] = dw[:, (1 - half) * h : (2 - half) * h].reshape(send_ref.shape)

def unmix(core, lens, gbr, parts, w, blocks):
    t, d = gbr.shape
    smem = pl.BlockSpec(memory_space=pltpu.SMEM)
    piece = jax.ShapeDtypeStruct((blocks, d // blocks, d // 2), BF)
    return pl.pallas_call(
        unmix_kernel,
        name="unmix",
        in_specs=[smem, smem] + [pl.BlockSpec(memory_space=pltpu.VMEM)] * (2 + len(parts)),
        out_shape=[jax.ShapeDtypeStruct((t, d), BF), piece, piece],
        compiler_params=params(0),
        cost_estimate=cost(4 * t * d * d, 9e6),
    )(core, lens, gbr, w, *parts)

def unproject_kernel(blocks, core, low_ref, g_ref, send_ref, keep_ref, sums_ref):
    d, w = low_ref.shape[1], g_ref.shape[2]
    r, h = d // blocks, w // 2
    low_t = low_ref[...].T
    q, k, v = [mm(low_t, g_ref[part]).astype(BF).reshape(blocks, r, w) for part in range(3)]
    for half, refs in ((0, (keep_ref, send_ref)), (1, (send_ref, keep_ref))):
        @pl.when(core[0] == half)
        def _():
            refs[0][:, :, :w] = q
            refs[0][:, :, w:] = k[:, :, :h]
            refs[1][:, :, :h] = k[:, :, h:]
            refs[1][:, :, h:] = v
    for part in range(3):
        sums_ref[part : part + 1] = jnp.sum(g_ref[part].astype(F32), axis=0, keepdims=True)

def unproject(core, low, g, blocks):
    t, d = low.shape
    w = g.shape[2]
    piece = jax.ShapeDtypeStruct((blocks, d // blocks, w // 2 * 3), BF)
    return pl.pallas_call(
        functools.partial(unproject_kernel, blocks),
        name="unproject",
        in_specs=[pl.BlockSpec(memory_space=pltpu.SMEM)] + [pl.BlockSpec(memory_space=pltpu.VMEM)] * 2,
        out_shape=[piece, piece, jax.ShapeDtypeStruct((3, w), F32)],
        compiler_params=params(0),
        cost_estimate=cost(6 * t * d * w, 10e6 * w / d),
    )(core, low, g)

def final_kernel(x_ref, w_ref, gmid_ref, gain_ref, *rest):
    parts, (out_ref, vec_ref) = rest[:-2], rest[-2:]
    d = x_ref.shape[1]
    w = w_ref[...].reshape(d, 3 * d)
    gh = jnp.zeros(x_ref.shape, F32)
    at = 0
    for g in parts:
        for i in range(3):
            gh = gh + mm_nt(g[i], w[:, i * d + at : i * d + at + g.shape[2]])
        at += g.shape[2]
    n, scale = normalised(x_ref[...].astype(F32))
    out_ref[...] = (gmid_ref[...] + norm_pull(n, scale, gain_ref[...], gh)).astype(BF)
    @pl.when(pl.program_id(0) == 0)
    def _():
        vec_ref[...] = jnp.zeros_like(vec_ref)
    vec_ref[0:1] += jnp.sum(gh * n, axis=0, keepdims=True)
    vec_ref[1:2] += jnp.sum(gh, axis=0, keepdims=True)

def final(x, parts, w, gmid, gain, rows=256):
    t, d = x.shape
    return pl.pallas_call(
        final_kernel,
        name="final",
        grid=(t // rows,),
        in_specs=[
            pl.BlockSpec((rows, d), lambda i: (i, 0)),
            whole(w.shape),
            pl.BlockSpec((rows, d), lambda i: (i, 0)),
            whole((1, d)),
            *[pl.BlockSpec((3, rows, g.shape[2]), lambda i: (0, i, 0)) for g in parts],
        ],
        out_specs=[pl.BlockSpec((rows, d), lambda i: (i, 0)), whole((2, d))],
        out_shape=[jax.ShapeDtypeStruct((t, d), BF), jax.ShapeDtypeStruct((2, d), F32)],
        compiler_params=params(),
        cost_estimate=cost(6 * t * d * d, 15e6),
    )(x, w, gmid, gain, *parts)


class Grid:
    def __init__(self, mesh, rows):
        wide, narrow = mesh.shape["wide"], mesh.shape["narrow"]
        self.count = wide * narrow
        self.paired = narrow == 4 and wide % 2 == 0 and rows % 8 == 0
        self.blocks = self.count // 2 if self.paired else 1
        self.z = wide // 2

    def index(self, z, x, y, c):
        return ((z * 2 + x) * 2 + y) * 2 + c

    def places(self):
        return [
            (z, x, y, c) for z in range(self.z) for x in range(2) for y in range(2) for c in range(2)
        ]

    def perm(self, target):
        return [(self.index(*at), self.index(*target(*at))) for at in self.places()]

    def here(self):
        w, n = lax.axis_index("wide"), lax.axis_index("narrow")
        return w // 2, w % 2, n // 2, n % 2

    def table(self):
        rows = []
        for z0, x0, y0, c0 in self.places():
            mine = []
            for half in (c0, 1 - c0):
                for ka, kb in ((0, 0), (1, 0), (0, 1), (1, 1)):
                    kx, ky = (ka, kb) if half == 0 else (kb, ka)
                    blocks = [
                        (((z0 - kz) % self.z) * 2 + (x0 ^ kx)) * 2 + (y0 ^ ky) for kz in range(self.z)
                    ]
                    mine.append([half] + blocks)
            rows.append(mine)
        return np.array(rows, np.int32)

    def send(self, value, target):
        return lax.ppermute(value, AXES, self.perm(target))

    def other_core(self, value):
        return self.send(value, lambda z, x, y, c: (z, x, y, 1 - c))

    def along(self, value, turn):
        return self.send(
            value,
            lambda z, x, y, c: (z, 1 - x, y, c) if c == turn else (z, x, 1 - y, c),
        )

    def up(self, value, k):
        return self.send(value, lambda z, x, y, c: ((z + k) % self.z, x, y, c))


def both(first, own, other, axis):
    return jnp.where(
        first, jnp.concatenate([own, other], axis), jnp.concatenate([other, own], axis)
    )


def pair_rows(grid, shard):
    c = grid.here()[3]
    h = shard.shape[1] // 2
    other = grid.other_core(lax.dynamic_slice_in_dim(shard, (1 - c) * h, h, 1))
    return both(c == 0, lax.dynamic_slice_in_dim(shard, c * h, h, 1), other, 0)


def spread_z(grid, pair):
    return jnp.stack([pair] + [grid.up(pair, k) for k in range(1, grid.z)])


def with_other(grid, sources):
    return sources + [grid.other_core(s) for s in sources]


def stage(*values):
    return lax.optimization_barrier(values)


def after(value, *earlier):
    return lax.optimization_barrier((value, *earlier))[0]


def add(a, b):
    return (a.astype(F32) + b.astype(F32)).astype(BF)


def pick(v, at, axis):
    return lax.dynamic_index_in_dim(v, at, axis, keepdims=False)


class Sum:
    def __init__(self, grid, sends, keeps):
        self.grid, self.keeps = grid, keeps
        self.got = [grid.other_core(s) for s in sends]

    def core(self):
        grid = self.grid
        z, x, y, c = grid.here()
        own = jnp.concatenate([add(k, g) for k, g in zip(self.keeps, self.got)], 2)
        own = own.reshape(grid.z, 2, 2, *own.shape[1:])
        self.away = jnp.where(c == 0, pick(own, 1 - x, 1), pick(own, 1 - y, 2))
        self.stay = jnp.where(c == 0, pick(own, x, 1), pick(own, y, 2))
        return self.away

    def near(self, *earlier):
        self.got = self.grid.along(after(self.away, *earlier), 0)

    def middle(self):
        z, x, y, c = self.grid.here()
        own = add(self.stay, self.got)
        left = jnp.where(c == 0, y, x)
        self.away, self.stay = pick(own, 1 - left, 1), pick(own, left, 1)
        return self.away

    def far(self, *earlier):
        self.got = self.grid.along(after(self.away, *earlier), 1)

    def last(self):
        self.own = add(self.stay, self.got)
        return self.own

    def rows(self, *earlier):
        grid = self.grid
        z = grid.here()[0]
        own = after(self.own, *earlier)
        total = pick(own, z, 0).astype(F32)
        for k in range(1, grid.z):
            total = total + grid.up(pick(own, (z + k) % grid.z, 0), k).astype(F32)
        return total


def own_rows(grid, total):
    c = grid.here()[3]
    r = total.shape[0] // 2
    other = grid.other_core(lax.dynamic_slice_in_dim(total, (1 - c) * r, r, 0))
    return both(c == 0, lax.dynamic_slice_in_dim(total, c * r, r, 0), other, 1)


def to_chunks(pair):
    r = pair.shape[0] // 4
    return jnp.concatenate([pair[j * r : (j + 1) * r] for j in range(4)], 1)


def from_chunks(total):
    w = total.shape[1] // 4
    return jnp.concatenate([total[:, j * w : (j + 1) * w] for j in range(4)], 0)


def gather_small(count, vectors):
    flat = jnp.concatenate([v.astype(F32) for v in vectors]).astype(BF)
    full = jnp.broadcast_to(flat, (count, flat.shape[0]))
    return lax.all_to_all(full, AXES, 0, 0, tiled=True)


def split_small(full, vectors):
    full = full.astype(F32)
    out, at = [], 0
    for v in vectors:
        out.append(full[:, at : at + v.shape[0]].reshape(-1))
        at += v.shape[0]
    return out


def scatter_small(count, vectors):
    parts = [v.reshape(count, -1) for v in vectors]
    got = lax.all_to_all(jnp.concatenate(parts, 1), AXES, 0, 0, tiled=True)
    total = jnp.sum(got, axis=0)
    out, at = [], 0
    for p in parts:
        out.append(total[at : at + p.shape[1]])
        at += p.shape[1]
    return out


def halves_of(weight):
    h = weight.shape[1] // 2
    return [weight[None, :, :h], weight[None, :, h:]]


def local(
    mesh,
    tokens,
    norm1_gain,
    norm1_bias,
    qkv_weight,
    qkv_bias,
    out_weight,
    out_bias,
    norm2_gain,
    norm2_bias,
    fc_weight,
    fc_bias,
    proj_weight,
    proj_bias,
    seq_lengths,
    out_cotangent,
):
    d = tokens.shape[1]
    grid = Grid(mesh, out_weight.shape[0])
    blocks = grid.blocks
    vectors = [norm1_gain, norm1_bias, qkv_bias, out_bias, norm2_gain, norm2_bias, fc_bias, proj_bias]
    little_all = gather_small(grid.count, vectors)
    if grid.paired:
        place = jnp.asarray(grid.table())[lax.axis_index(AXES)]
        core = grid.here()[3].reshape(1).astype(jnp.int32)
        pair_qkv = pair_rows(grid, qkv_weight)
        first = jnp.concatenate([pair_rows(grid, fc_weight), pair_rows(grid, out_weight)], 1)
        second = to_chunks(pair_rows(grid, proj_weight))
        stack_qkv = spread_z(grid, pair_qkv)
        stack_qkv, first, second = stage(stack_qkv, first, second)
        near_qkv, far_qkv = grid.along(stack_qkv, 0), grid.along(stack_qkv, 1)
        stack_first = spread_z(grid, first)
        near_qkv, little_all = stage(near_qkv, little_all)
        last_qkv = grid.along(near_qkv, 1)
        last_qkv, stack_first, second, far_qkv = stage(last_qkv, stack_first, second, far_qkv)
        near_first, far_first = grid.along(stack_first, 0), grid.along(stack_first, 1)
        stack_second = spread_z(grid, second)
        qkv_sources = with_other(grid, [stack_qkv, near_qkv, far_qkv, last_qkv])
    else:
        place = jnp.asarray(np.array([[0, 0], [1, 0]], np.int32))
        core = jnp.zeros((1,), jnp.int32)
        full = lambda v: lax.all_gather(v, AXES, axis=0, tiled=True)
        qkv_sources = halves_of(full(qkv_weight))
    gain_one, shift_one, bias_qv, bias_out, gain_two, shift_two, bias_fc, bias_proj = split_small(
        little_all, vectors
    )
    row = lambda v: v.reshape(1, d)
    bias_qkv = jnp.stack([bias_qv[:d], jnp.zeros((d,), F32), bias_qv[d:]])
    qkv, low_one, qkv_full = project(
        place, tokens, row(gain_one), row(shift_one), bias_qkv, qkv_sources, blocks
    )
    if grid.paired:
        qkv, near_first, far_first, stack_second = stage(qkv, near_first, far_first, stack_second)
        last_first = grid.along(near_first, 1)
        near_second, far_second = grid.along(stack_second, 0), grid.along(stack_second, 1)
    attended = [attend(seq_lengths, qkv, 4, 0, 512)]
    if grid.paired:
        qkv, near_second, far_second, last_first, _ = stage(
            qkv, near_second, far_second, last_first, attended[0][2]
        )
        last_second = grid.along(near_second, 1)
        outs = with_other(grid, [stack_first, near_first, far_first, last_first])
        seconds = with_other(grid, [stack_second, near_second, far_second, last_second])
        fcs, out_at, projs = [(s, 0) for s in outs], 4, [(s, 0) for s in seconds]
    else:
        fcs = [(s, 0) for s in halves_of(full(fc_weight))]
        outs, out_at = halves_of(full(out_weight)), 0
        projs = [(to_chunks(s[0])[None], 0) for s in halves_of(full(proj_weight))]
    attended.append(attend(seq_lengths, qkv, 2, 4, 512))
    mixed = [a[1] for a in attended]
    middle, low_two, out_full = mix(
        place, mixed, tokens, row(bias_out), row(gain_two), row(shift_two), outs, blocks, out_at
    )
    (layer_out, grad_middle, grad_branch, fc_send, fc_keep, proj_send, proj_keep, fc_bias_term, sums) = mlp(
        core, place, seq_lengths, middle, low_two, out_cotangent, bias_fc.reshape(4, d), row(bias_proj),
        row(gain_two), fcs, projs, blocks,
    )
    grad_mixed, out_send, out_keep = unmix(core, seq_lengths, grad_branch, mixed, out_full, blocks)
    grads, dense, small_sums = [], [], []
    if grid.paired:
        block_sum = Sum(grid, [fc_send, proj_send, out_send], [fc_keep, proj_keep, out_keep])
        grad_mixed = after(grad_mixed, block_sum.core())
        block_sum.near()
    grads.append(attend_grad(qkv, grad_mixed, attended[0][0], attended[0][2], 0))
    dense.append(unproject(core, low_one, grads[0], blocks))
    if grid.paired:
        large = Sum(grid, [dense[0][0]], [dense[0][1]])
        grad_mixed = after(grad_mixed, block_sum.middle(), dense[0][2])
        block_sum.far()
    grads.append(attend_grad(qkv, grad_mixed, attended[1][0], attended[1][2], 4))
    dense.append(unproject(core, low_one, grads[1], blocks))
    if grid.paired:
        small = Sum(grid, [dense[1][0]], [dense[1][1]])
        large.core()
        large.near(block_sum.last())
        small.core()
        small.near(large.away)
        grad_middle = after(grad_middle, small.away, large.away)
    input_grad, first_sums = final(tokens, grads, qkv_full, grad_middle, row(gain_one))
    if grid.paired:
        total = block_sum.rows()
        large.middle()
        large.far()
        small.middle()
        small.far()
        large.last()
        small.last()
        fc_wide, out_wide = fc_keep.shape[2], out_keep.shape[2]
        fc_weight_grad = own_rows(grid, total[:, :fc_wide])
        proj_weight_grad = own_rows(grid, from_chunks(total[:, fc_wide : 2 * fc_wide]))
        out_weight_grad = own_rows(grid, total[:, 2 * fc_wide :])
        ends = [own_rows(grid, large.rows()), own_rows(grid, small.rows())]
    else:
        reduce = lambda v: lax.psum_scatter(v.astype(F32), AXES, scatter_dimension=0, tiled=True)
        side = lambda k, s: jnp.concatenate([k[0], s[0]], 1)
        fc_weight_grad = reduce(side(fc_keep, fc_send))
        out_weight_grad = reduce(side(out_keep, out_send))
        ends = [reduce(side(u[1], u[0])) for u in dense]
        proj_weight_grad = reduce(
            jnp.concatenate([from_chunks(proj_keep[0]), from_chunks(proj_send[0])], 1)
        )
    split = lambda e, i: e[:, i * e.shape[1] // 3 : (i + 1) * e.shape[1] // 3]
    qkv_weight_grad = jnp.concatenate([split(e, i) for i in range(3) for e in ends], 1)
    qkv_bias_term = jnp.concatenate([dense[p][2][i] for i in (0, 2) for p in range(2)])
    little = scatter_small(
        grid.count,
        [
            first_sums[0], first_sums[1], qkv_bias_term, sums[3],
            sums[1], sums[2], fc_bias_term.reshape(-1), sums[0],
        ],
    )
    return (
        layer_out,
        input_grad,
        little[0],
        little[1],
        qkv_weight_grad,
        little[2],
        out_weight_grad,
        little[3],
        little[4],
        little[5],
        fc_weight_grad,
        little[6],
        proj_weight_grad,
        little[7],
    )


def solution(mesh):
    matrix, vector = P(AXES, None), P(AXES)
    ins = (
        matrix, vector, vector, matrix, vector, matrix, vector, vector,
        vector, matrix, vector, matrix, vector, vector, matrix,
    )
    outs = (
        matrix, matrix, vector, vector, matrix, vector, matrix, vector,
        vector, vector, matrix, vector, matrix, vector,
    )
    return jax.shard_map(
        functools.partial(local, mesh), mesh=mesh, in_specs=ins, out_specs=outs, check_vma=False
    )
```

```python
import functools
import math

import jax
import jax.numpy as jnp
import numpy as np
from jax import lax
from jax.experimental import pallas as pl
from jax.experimental.pallas import tpu as pltpu
from jax.sharding import PartitionSpec as P

AXES = ("wide", "narrow")
BF, F32 = jnp.bfloat16, jnp.float32
VMEM_CAP = 58 << 20
LOG2E = 1.4426950408889634

def params(n=1, cap=VMEM_CAP):
    return pltpu.CompilerParams(dimension_semantics=("arbitrary",) * n, vmem_limit_bytes=cap)

def cost(flops, bytes_accessed, trans=0):
    return pl.CostEstimate(flops=int(flops), bytes_accessed=int(bytes_accessed), transcendentals=int(trans))

def mm(a, b):
    return jnp.dot(a, b, preferred_element_type=F32)

def diagonal_mask(rows, cols):
    key_at = lax.broadcasted_iota(jnp.int32, (rows, cols), 0)
    query_at = lax.broadcasted_iota(jnp.int32, (rows, cols), 1)
    return key_at <= query_at

def attend_kernel(qb, len_ref, qkv_ref, out_t_ref, out_ref, stat_ref, v_t, q_t):
    slot = qkv_ref.shape[1]
    q_t[...] = (qkv_ref[0] * jnp.asarray(0.125, BF)).T
    v_t[...] = qkv_ref[2].T
    half = lax.broadcasted_iota(jnp.int32, (128, 1), 0) < 64
    causal = diagonal_mask(qb, qb)
    length = len_ref[0]
    for i in range(slot // qb):
        cols = slice(i * qb, (i + 1) * qb)
        parts = []
        for head in range(2):
            mine = half if head == 0 else jnp.logical_not(half)
            qh = jnp.where(mine, q_t[:, cols], jnp.zeros((), BF))
            s_low = mm(qkv_ref[1, : i * qb, :], qh) if i else None
            s_dia = jnp.where(causal, mm(qkv_ref[1, cols, :], qh), -1e30)
            top = jnp.max(s_dia, axis=0, keepdims=True)
            if i:
                top = jnp.maximum(top, jnp.max(s_low, axis=0, keepdims=True))
            e_dia = jnp.exp(s_dia - top)
            total = jnp.sum(e_dia, axis=0, keepdims=True)
            vh = v_t[head * 64 : head * 64 + 64, :]
            acc = mm(vh[:, cols], e_dia.astype(BF))
            if i:
                e_low = jnp.exp(s_low - top)
                total = total + jnp.sum(e_low, axis=0, keepdims=True)
                acc = acc + mm(vh[:, : i * qb], e_low.astype(BF))
            stat_ref[0, head : head + 1, cols] = top + jnp.log(total)
            parts.append(acc / total)
        both = jnp.concatenate(parts, axis=0)
        seen = (i * qb + lax.broadcasted_iota(jnp.int32, (1, qb), 1)) < length
        both = jnp.where(seen, both, 0.0)
        out_t_ref[:, cols] = both
        out_ref[cols, :] = both.T.astype(BF)

def attend(lengths, qkv, pairs, first, qb=256):
    slot, width = qkv.shape[1], qkv.shape[2]
    return pl.pallas_call(
        functools.partial(attend_kernel, qb),
        name="attend",
        grid=(pairs,),
        in_specs=[
            pl.BlockSpec(memory_space=pltpu.SMEM),
            pl.BlockSpec((3, slot, 128), lambda j: (0, 0, j + first)),
        ],
        out_specs=[
            pl.BlockSpec((128, slot), lambda j: (j, 0)),
            pl.BlockSpec((slot, 128), lambda j: (0, j)),
            pl.BlockSpec((1, 2, slot), lambda j: (j, 0, 0)),
        ],
        out_shape=[
            jax.ShapeDtypeStruct((pairs * 128, slot), F32),
            jax.ShapeDtypeStruct((slot, pairs * 128), BF),
            jax.ShapeDtypeStruct((pairs, 2, slot), F32),
        ],
        scratch_shapes=[pltpu.VMEM((128, slot), BF), pltpu.VMEM((128, slot), BF)],
        compiler_params=params(),
        cost_estimate=cost(pairs * 2 * slot * slot * 256, 8e6 * pairs / 6, pairs * slot * slot),
    )(lengths, qkv)

def attend_grad_kernel(qb, qkv_ref, grad_ref, out_t_ref, stat_ref, g_ref, q_t, do_t, k_t, qs, dq_t, dk_s, dv_s):
    slot = qkv_ref.shape[1]
    qs[...] = qkv_ref[0] * jnp.asarray(0.125, BF)
    q_t[...] = qs[...].T
    k_t[...] = qkv_ref[1].T
    do_t[...] = grad_ref[...].T
    half = lax.broadcasted_iota(jnp.int32, (128, 1), 0) < 64
    half_lane = lax.broadcasted_iota(jnp.int32, (1, 128), 1) < 64
    causal = diagonal_mask(qb, qb)
    zero = jnp.zeros((), BF)
    prod = do_t[...].astype(F32) * out_t_ref[...]
    delta = [jnp.sum(prod[h * 64 : h * 64 + 64], axis=0, keepdims=True) for h in range(2)]
    for i in range(slot // qb):
        cols = slice(i * qb, (i + 1) * qb)
        end = (i + 1) * qb
        dv_new = dk_new = None
        for head in range(2):
            mine = half if head == 0 else jnp.logical_not(half)
            mine_lane = half_lane if head == 0 else jnp.logical_not(half_lane)
            qh_t = jnp.where(mine, q_t[:, cols], zero)
            doh_t = jnp.where(mine, do_t[:, cols], zero)
            qh = jnp.where(mine_lane, qs[cols, :], zero)
            doh = jnp.where(mine_lane, grad_ref[cols, :], zero)
            stat = stat_ref[0, head : head + 1, cols]
            dl = delta[head][:, cols]
            s = mm(qkv_ref[1, :end, :], qh_t)
            dp = mm(qkv_ref[2, :end, :], doh_t)
            p = jnp.exp(s - stat)
            p_dia = jnp.where(causal, p[i * qb :], 0.0)
            p = jnp.concatenate([p[: i * qb], p_dia], axis=0) if i else p_dia
            ds = (p * (dp - dl)).astype(BF)
            pb = p.astype(BF)
            dv_h = mm(pb, doh)
            dk_h = mm(ds, qh)
            dv_new = dv_h if head == 0 else dv_new + dv_h
            dk_new = dk_h if head == 0 else dk_new + dk_h
            dq_t[head * 64 : head * 64 + 64, cols] = mm(k_t[head * 64 : head * 64 + 64, :end], ds)
        if i:
            dv_s[: i * qb] += dv_new[: i * qb]
            dk_s[: i * qb] += dk_new[: i * qb]
        dv_s[cols] = dv_new[i * qb :]
        dk_s[cols] = dk_new[i * qb :]
    g_ref[0] = (dq_t[...] * 0.125).T.astype(BF)
    g_ref[1] = dk_s[...].astype(BF)
    g_ref[2] = dv_s[...].astype(BF)

def attend_grad(qkv, grad, out_t, stat, first, qb=256):
    slot = qkv.shape[1]
    pairs = out_t.shape[0] // 128
    width = pairs * 128
    return pl.pallas_call(
        functools.partial(attend_grad_kernel, qb),
        name="attend_grad",
        grid=(pairs,),
        in_specs=[
            pl.BlockSpec((3, slot, 128), lambda j: (0, 0, j + first)),
            pl.BlockSpec((slot, 128), lambda j: (0, j + first)),
            pl.BlockSpec((128, slot), lambda j: (j, 0)),
            pl.BlockSpec((1, 2, slot), lambda j: (j, 0, 0)),
        ],
        out_specs=pl.BlockSpec((3, slot, 128), lambda j: (0, 0, j)),
        out_shape=jax.ShapeDtypeStruct((3, slot, width), BF),
        scratch_shapes=[
            pltpu.VMEM((128, slot), BF),
            pltpu.VMEM((128, slot), BF),
            pltpu.VMEM((128, slot), BF),
            pltpu.VMEM((slot, 128), BF),
            pltpu.VMEM((128, slot), F32),
            pltpu.VMEM((slot, 128), F32),
            pltpu.VMEM((slot, 128), F32),
        ],
        compiler_params=params(),
        cost_estimate=cost(pairs * 5 * slot * slot * 256, 16e6 * pairs / 6, pairs * 2 * slot * slot),
    )(qkv, grad, out_t, stat)
branch_scale = 1.0 / math.sqrt(48.0)
norm_epsilon = 1e-05
WHOLE = dict(pipeline_mode=pl.Buffered(1))

def mm_nt(a, b):
    return lax.dot_general(a, b, (((1,), (1,)), ((), ())), preferred_element_type=F32)

def mm_tn(a, b):
    return lax.dot_general(a, b, (((0,), (0,)), ((), ())), preferred_element_type=F32)

def normalised(v):
    mean = jnp.mean(v, axis=-1, keepdims=True)
    centred = v - mean
    var = jnp.mean(centred * centred, axis=-1, keepdims=True)
    scale = lax.rsqrt(var + norm_epsilon)
    return centred * scale, scale

def norm_pull(n, scale, gain, u):
    ug = u * gain
    a = jnp.mean(ug, axis=-1, keepdims=True)
    b = jnp.mean(ug * n, axis=-1, keepdims=True)
    return (ug - a - n * b) * scale

def whole(shape, index=None):
    zeros = (0,) * len(shape)
    return pl.BlockSpec(shape, (lambda *_: index or zeros), **WHOLE)

def assemble(place, sources, target, at=0):
    wide = sources[0].shape[2]
    for s, source in enumerate(sources):
        for half in range(2):
            @pl.when(place[s, 0] == half)
            def _():
                for p in range(source.shape[0]):
                    target[place[s, 1 + p], :, half * wide : (half + 1) * wide] = source[p]

def assemble_chunks(place, sources, target):
    wide = sources[0].shape[2] // 4
    for s, source in enumerate(sources):
        for half in range(2):
            @pl.when(place[s, 0] == half)
            def _():
                for p in range(source.shape[0]):
                    for j in range(4):
                        target[place[s, 1 + p], j, :, half * wide : (half + 1) * wide] = source[p, :, j * wide : (j + 1) * wide]

def project_kernel(n_src, place, x_ref, gain_ref, shift_ref, bias_ref, *rest):
    sources, (qkv_ref, low_ref, w_ref) = rest[:n_src], rest[n_src:]
    @pl.when(pl.program_id(0) == 0)
    def _():
        assemble(place, sources, w_ref)
    n, _ = normalised(x_ref[...].astype(F32))
    low = (n * gain_ref[...] + shift_ref[...]).astype(BF)
    low_ref[...] = low
    d = low.shape[1]
    for part in range(3):
        w = w_ref[:, :, part * d : (part + 1) * d].reshape(d, d)
        qkv_ref[part] = (mm(low, w) + bias_ref[part : part + 1]).astype(BF)

def project(place, x, gain, shift, bias, sources, blocks, rows=256):
    t, d = x.shape
    r, wide = d // blocks, sources[0].shape[2]
    return pl.pallas_call(
        functools.partial(project_kernel, len(sources)),
        name="project",
        grid_spec=pltpu.PrefetchScalarGridSpec(
            num_scalar_prefetch=1,
            grid=(t // rows,),
            in_specs=[
                pl.BlockSpec((rows, d), lambda i, p: (i, 0)),
                whole((1, d)), whole((1, d)), whole((3, d)),
                *[whole(s.shape) for s in sources],
            ],
            out_specs=[
                pl.BlockSpec((3, rows, d), lambda i, p: (0, i, 0)),
                pl.BlockSpec((rows, d), lambda i, p: (i, 0)),
                whole((blocks, r, 2 * wide)),
            ],
        ),
        out_shape=[
            jax.ShapeDtypeStruct((3, t, d), BF),
            jax.ShapeDtypeStruct((t, d), BF),
            jax.ShapeDtypeStruct((blocks, r, 2 * wide), BF),
        ],
        compiler_params=params(),
        cost_estimate=cost(2 * t * d * 3 * d, 18e6),
    )(place, x, gain, shift, bias, *sources)

def mix_kernel(n_src, place, x_ref, bias_ref, gain_ref, shift_ref, *rest):
    sources, parts, (mid_ref, low_ref, w_ref) = rest[:n_src], rest[n_src:-3], rest[-3:]
    @pl.when(pl.program_id(0) == 0)
    def _():
        assemble(place, sources, w_ref)
    d = x_ref.shape[1]
    w = w_ref[...].reshape(d, d)
    mid = x_ref[...].astype(F32) + branch_scale * (mm(jnp.concatenate([p[...] for p in parts], 1), w) + bias_ref[...])
    mid_ref[...] = mid
    n, _ = normalised(mid)
    low_ref[...] = (n * gain_ref[...] + shift_ref[...]).astype(BF)

def mix(place, parts, x, bias, gain, shift, sources, blocks, column, rows=256):
    t, d = x.shape
    r, np_ = d // blocks, sources[0].shape[0]
    return pl.pallas_call(
        functools.partial(mix_kernel, len(sources)),
        name="mix",
        grid_spec=pltpu.PrefetchScalarGridSpec(
            num_scalar_prefetch=1,
            grid=(t // rows,),
            in_specs=[
                pl.BlockSpec((rows, d), lambda i, p: (i, 0)),
                whole((1, d)), whole((1, d)), whole((1, d)),
                *[whole((np_, r, d // 2), (0, 0, column)) for s in sources],
                *[pl.BlockSpec((rows, p.shape[1]), lambda i, p: (i, 0)) for p in parts],
            ],
            out_specs=[
                pl.BlockSpec((rows, d), lambda i, p: (i, 0)),
                pl.BlockSpec((rows, d), lambda i, p: (i, 0)),
                whole((blocks, r, d)),
            ],
        ),
        out_shape=[
            jax.ShapeDtypeStruct((t, d), F32),
            jax.ShapeDtypeStruct((t, d), BF),
            jax.ShapeDtypeStruct((blocks, r, d), BF),
        ],
        compiler_params=params(),
        cost_estimate=cost(2 * t * d * d, 9e6),
    )(place, x, bias, gain, shift, *sources, *parts)

def mlp_kernel(n_src, blocks, rb, core, place, lens, mid_ref, low_ref, cot_ref, fb_ref, pb_ref, gain_ref, *rest):
    fcs, projs, rest = rest[:n_src], rest[n_src : 2 * n_src], rest[2 * n_src :]
    (out_ref, gmid_ref, gbr_ref, fsend_ref, fkeep_ref, psend_ref, pkeep_ref, fbg_ref, vec_ref,
     fc_s, proj_s, low_t, g2_s, second_s, gh_s, act_s, gpre_s) = rest
    t, d = mid_ref.shape
    r = d // blocks
    step = pl.program_id(0)
    mine = core[0]
    chunk = lax.rem(step + 2 * (1 - mine), 4)
    def valid_rows(at):
        return (at * rb + lax.broadcasted_iota(jnp.int32, (rb, 1), 0)) < lens[0]
    @pl.when(step == 0)
    def _():
        assemble(place, fcs, fc_s)
        assemble_chunks(place, projs, proj_s)
        low_t[...] = low_ref[...].T
        def begin(i, total):
            at = pl.ds(pl.multiple_of(i * rb, rb), rb)
            g = jnp.where(valid_rows(i), branch_scale * cot_ref[at, :].astype(F32), 0.0).astype(BF)
            g2_s[at, :] = g
            second_s[at, :] = jnp.zeros((rb, d), F32)
            gh_s[at, :] = jnp.zeros((rb, d), F32)
            return total + jnp.sum(g.astype(F32), axis=0, keepdims=True)
        vec_ref[0:1] = lax.fori_loop(0, t // rb, begin, jnp.zeros((1, d), F32))
    fcol = pl.ds(pl.multiple_of(chunk * d, d), d)
    fc = fc_s.at[:, :, fcol]
    bias = fb_ref[pl.ds(chunk, 1), :]
    if blocks % 4 == 0:
        per = blocks // 4
        proj = proj_s.at[pl.ds(chunk * per, per)]
    else:
        proj = proj_s.at[:, pl.ds(chunk, 1)]
    def rows_step(i, total):
        at = pl.ds(pl.multiple_of(i * rb, rb), rb)
        u = mm(low_ref[at, :], fc[...].reshape(d, d)) + bias
        sq = u * u
        th = jnp.tanh(0.7978845608028654 * u * (1.0 + 0.044715 * sq))
        up = 0.5 * (1.0 + th)
        act = (u * up).astype(BF)
        act_s[at, :] = act
        slope = up + u * (0.5 * 0.7978845608028654) * (1.0 - th * th) * (1.0 + 3 * 0.044715 * sq)
        w = proj[...].reshape(d, d)
        second_s[at, :] += mm(act, w)
        gp = mm_nt(g2_s[at, :], w) * slope
        gpb = gp.astype(BF)
        gpre_s[at, :] = gpb
        gh_s[at, :] += mm_nt(gpb, fc[...].reshape(d, d))
        return total + jnp.sum(gpb.astype(F32), axis=0, keepdims=True)
    fbg_ref[pl.ds(chunk, 1), :] = lax.fori_loop(0, t // rb, rows_step, jnp.zeros((1, d), F32))
    dfc = mm(low_t[...], gpre_s[...]).astype(BF).reshape(blocks, r, d)
    @pl.when(step < 2)
    def _():
        fsend_ref[...] = dfc
    @pl.when(step >= 2)
    def _():
        fkeep_ref[...] = dfc
    dproj = mm_tn(act_s[...], g2_s[...]).astype(BF)
    h = d // 2
    for half in range(2):
        @pl.when(mine == half)
        def _():
            for ref, cols in ((pkeep_ref, half), (psend_ref, 1 - half)):
                piece = dproj[:, cols * h : (cols + 1) * h]
                if blocks % 4 == 0:
                    for b in range(blocks // 4):
                        for j in range(4):
                            ref[b, :, j * h : (j + 1) * h] = piece[(b * 4 + j) * r : (b * 4 + j + 1) * r]
                else:
                    ref[0] = piece
    @pl.when(step == 3)
    def _():
        def finish(i, carry):
            at = pl.ds(pl.multiple_of(i * rb, rb), rb)
            mid = mid_ref[at, :]
            out_ref[at, :] = (mid + branch_scale * (second_s[at, :] + pb_ref[...])).astype(BF)
            n, scale = normalised(mid)
            gh = gh_s[at, :]
            cot = jnp.where(valid_rows(i), cot_ref[at, :].astype(F32), 0.0)
            gm = cot + norm_pull(n, scale, gain_ref[...], gh)
            gmid_ref[at, :] = gm
            gb = (branch_scale * gm).astype(BF)
            gbr_ref[at, :] = gb
            return (carry[0] + jnp.sum(gh * n, axis=0, keepdims=True),
                    carry[1] + jnp.sum(gh, axis=0, keepdims=True),
                    carry[2] + jnp.sum(gb.astype(F32), axis=0, keepdims=True))
        zero = jnp.zeros((1, d), F32)
        a, b, c = lax.fori_loop(0, t // rb, finish, (zero, zero, zero))
        vec_ref[1:2] = a
        vec_ref[2:3] = b
        vec_ref[3:4] = c

def mlp(core, place, lens, mid, low, cot, fb, pb, gain, fcs, projs, blocks, rb=256):
    t, d = mid.shape
    r, np_ = d // blocks, fcs[0][0].shape[0]
    smem = pl.BlockSpec(memory_space=pltpu.SMEM)
    if blocks % 4 == 0:
        pspec = pl.BlockSpec((blocks // 4, r, 2 * d), lambda i, c: (lax.rem(i + 2 * (1 - c[0]), 4), 0, 0))
    else:
        pspec = pl.BlockSpec((1, r, d // 2), lambda i, c: (0, 0, lax.rem(i + 2 * (1 - c[0]), 4)))
    big = jax.ShapeDtypeStruct((blocks, r, 2 * d), BF)
    return pl.pallas_call(
        functools.partial(mlp_kernel, len(fcs), blocks, rb),
        name="mlp",
        grid_spec=pltpu.PrefetchScalarGridSpec(
            num_scalar_prefetch=1,
            grid=(4,),
            in_specs=[
                smem, smem, whole((t, d)), whole((t, d)), whole((t, d)), whole((4, d)), whole((1, d)), whole((1, d)),
                *[whole((np_, r, 2 * d), (0, 0, at)) for _, at in fcs],
                *[whole((np_, r, 2 * d), (0, 0, at)) for _, at in projs],
            ],
            out_specs=[
                whole((t, d)), whole((t, d)), whole((t, d)),
                pl.BlockSpec((blocks, r, d), lambda i, c: (0, 0, jnp.minimum(i, 1))),
                pl.BlockSpec((blocks, r, d), lambda i, c: (0, 0, jnp.maximum(i - 2, 0))),
                pspec, pspec,
                whole((4, d)), whole((4, d)),
            ],
            scratch_shapes=[
                pltpu.VMEM((blocks, r, 4 * d), BF),
                pltpu.VMEM((blocks, 4, r, d), BF),
                pltpu.VMEM((d, t), BF),
                pltpu.VMEM((t, d), BF),
                pltpu.VMEM((t, d), F32),
                pltpu.VMEM((t, d), F32),
                pltpu.VMEM((t, d), BF),
                pltpu.VMEM((t, d), BF),
            ],
        ),
        out_shape=[
            jax.ShapeDtypeStruct((t, d), BF), jax.ShapeDtypeStruct((t, d), F32), jax.ShapeDtypeStruct((t, d), BF),
            big, big, big, big,
            jax.ShapeDtypeStruct((4, d), F32), jax.ShapeDtypeStruct((4, d), F32),
        ],
        compiler_params=params(),
        cost_estimate=cost(12 * t * d * 4 * d, 40e6, t * 4 * d),
    )(core, place, lens, mid, low, cot, fb, pb, gain, *[a for a, _ in fcs], *[a for a, _ in projs])

def unmix_kernel(core, lens, gbr_ref, w_ref, *rest):
    parts, (ga_ref, send_ref, keep_ref) = rest[:-3], rest[-3:]
    t, d = gbr_ref.shape
    w = w_ref[...].reshape(d, d)
    seen = lax.broadcasted_iota(jnp.int32, (t, 1), 0) < lens[0]
    ga_ref[...] = jnp.where(seen, mm_nt(gbr_ref[...], w), 0.0).astype(BF)
    dw = jnp.concatenate([mm_tn(p[...], gbr_ref[...]).astype(BF) for p in parts], 0)
    h = d // 2
    for half in range(2):
        @pl.when(core[0] == half)
        def _():
            keep_ref[...] = dw[:, half * h : (half + 1) * h].reshape(keep_ref.shape)
            send_ref[...] = dw[:, (1 - half) * h : (2 - half) * h].reshape(send_ref.shape)

def unmix(core, lens, gbr, parts, w, blocks):
    t, d = gbr.shape
    smem = pl.BlockSpec(memory_space=pltpu.SMEM)
    piece = jax.ShapeDtypeStruct((blocks, d // blocks, d // 2), BF)
    return pl.pallas_call(
        unmix_kernel,
        name="unmix",
        in_specs=[smem, smem] + [pl.BlockSpec(memory_space=pltpu.VMEM)] * (2 + len(parts)),
        out_shape=[jax.ShapeDtypeStruct((t, d), BF), piece, piece],
        compiler_params=params(0),
        cost_estimate=cost(4 * t * d * d, 9e6),
    )(core, lens, gbr, w, *parts)

def unproject_kernel(blocks, core, low_ref, *rest):
    parts, (send_ref, keep_ref, sums_ref) = rest[:-3], rest[-3:]
    d = low_ref.shape[1]
    r, h = d // blocks, d // 2
    low_t = low_ref[...].T
    first, second = (keep_ref, send_ref), (send_ref, keep_ref)
    at = 0
    for g in parts:
        w = g.shape[2]
        for part in range(3):
            grad = mm(low_t, g[part]).astype(BF).reshape(blocks, r, w)
            sums_ref[part : part + 1, at : at + w] = jnp.sum(g[part].astype(F32), axis=0, keepdims=True)
            for half, refs in ((0, first), (1, second)):
                @pl.when(core[0] == half)
                def _():
                    for lo in range(0, w, 128):
                        to = part * d + at + lo
                        side, to = to // (d + h), to % (d + h)
                        refs[side][:, :, to : to + 128] = grad[:, :, lo : lo + 128]
        at += w

def unproject(core, low, parts, blocks):
    t, d = low.shape
    piece = jax.ShapeDtypeStruct((blocks, d // blocks, d // 2 * 3), BF)
    return pl.pallas_call(
        functools.partial(unproject_kernel, blocks),
        name="unproject",
        in_specs=[pl.BlockSpec(memory_space=pltpu.SMEM)] + [pl.BlockSpec(memory_space=pltpu.VMEM)] * (1 + len(parts)),
        out_shape=[piece, piece, jax.ShapeDtypeStruct((3, d), F32)],
        compiler_params=params(0),
        cost_estimate=cost(6 * t * d * d, 10e6),
    )(core, low, *parts)

def route_kernel(count, steps, table, *refs):
    keeps, gots, (away_ref, stay_ref) = refs[:count], refs[count : 2 * count], refs[2 * count :]
    def write(ref):
        at = 0
        for k, g in zip(keeps, gots):
            w = k.shape[-1]
            total = (k[...].astype(F32) + g[...].astype(F32)).astype(BF)
            ref[..., at : at + w] = total.reshape(ref.shape[:-1] + (w,))
            at += w
    @pl.when(pl.program_id(0) < steps)
    def _():
        write(away_ref)
    @pl.when(pl.program_id(0) >= steps)
    def _():
        write(stay_ref)

def route(table, keeps, gots):
    shape = keeps[0].shape
    z, r = (shape[0], shape[3]) if len(shape) == 5 else (shape[1], shape[2])
    steps = 2 if len(shape) == 5 else 1
    wide = sum(k.shape[-1] for k in keeps)
    def spec(w):
        if len(shape) == 5:
            return pl.BlockSpec((z, 1, 1, r, w), lambda i, t: (0, t[i, 0], t[i, 1], 0, 0))
        return pl.BlockSpec((1, z, r, w), lambda i, t: (t[i, 0], 0, 0, 0))
    out = jax.ShapeDtypeStruct((steps, z, r, wide), BF)
    return pl.pallas_call(
        functools.partial(route_kernel, len(keeps), steps),
        name="route",
        grid_spec=pltpu.PrefetchScalarGridSpec(
            num_scalar_prefetch=1,
            grid=(2 * steps,),
            in_specs=[spec(k.shape[-1]) for k in keeps] * 2,
            out_specs=[
                pl.BlockSpec((1, z, r, wide), lambda i, t: (jnp.minimum(i, steps - 1), 0, 0, 0)),
                pl.BlockSpec((1, z, r, wide), lambda i, t: (jnp.maximum(i - steps, 0), 0, 0, 0)),
            ],
        ),
        out_shape=[out, out],
        compiler_params=params(1, 24 << 20),
        cost_estimate=cost(1e6, steps * 2 * z * r * wide * 6),
    )(table, *keeps, *gots)

def final_kernel(x_ref, w_ref, gmid_ref, gain_ref, *rest):
    parts, (out_ref, vec_ref) = rest[:-2], rest[-2:]
    d = x_ref.shape[1]
    w = w_ref[...].reshape(d, 3 * d)
    gh = jnp.zeros(x_ref.shape, F32)
    at = 0
    for g in parts:
        for i in range(3):
            gh = gh + mm_nt(g[i], w[:, i * d + at : i * d + at + g.shape[2]])
        at += g.shape[2]
    n, scale = normalised(x_ref[...].astype(F32))
    out_ref[...] = (gmid_ref[...] + norm_pull(n, scale, gain_ref[...], gh)).astype(BF)
    @pl.when(pl.program_id(0) == 0)
    def _():
        vec_ref[...] = jnp.zeros_like(vec_ref)
    vec_ref[0:1] += jnp.sum(gh * n, axis=0, keepdims=True)
    vec_ref[1:2] += jnp.sum(gh, axis=0, keepdims=True)

def final(x, parts, w, gmid, gain, rows=256):
    t, d = x.shape
    return pl.pallas_call(
        final_kernel,
        name="final",
        grid=(t // rows,),
        in_specs=[
            pl.BlockSpec((rows, d), lambda i: (i, 0)),
            whole(w.shape),
            pl.BlockSpec((rows, d), lambda i: (i, 0)),
            whole((1, d)),
            *[pl.BlockSpec((3, rows, g.shape[2]), lambda i: (0, i, 0)) for g in parts],
        ],
        out_specs=[pl.BlockSpec((rows, d), lambda i: (i, 0)), whole((2, d))],
        out_shape=[jax.ShapeDtypeStruct((t, d), BF), jax.ShapeDtypeStruct((2, d), F32)],
        compiler_params=params(),
        cost_estimate=cost(6 * t * d * d, 15e6),
    )(x, w, gmid, gain, *parts)
def spread_matrix(size, width):
    row = lax.broadcasted_iota(jnp.int32, (128, width), 0).astype(F32)
    col = lax.broadcasted_iota(jnp.int32, (128, width), 1).astype(F32)
    inside = col - jnp.floor((col + 0.5) / size) * size
    return jnp.where(inside == row, 1.0, 0.0)

def own_columns(count, size, per, width):
    at = lax.broadcasted_iota(jnp.int32, (count, width), 0).astype(F32)
    at = at - jnp.floor((at + 0.5) / per) * per
    col = lax.broadcasted_iota(jnp.int32, (count, width), 1).astype(F32)
    return jnp.logical_and(col >= at * size, col < (at + 1) * size)

SMALL_ROWS = (1, 1, 1, 1, 1, 1, 2, 4)

def unfold_kernel(x_ref, *out_refs):
    count, d = x_ref.shape[1], out_refs[0].shape[1]
    for rows, slots in ((1, range(6)), (2, (6,)), (4, (7,))):
        size, per = d * rows // count, count // rows
        spread = spread_matrix(size, d).astype(BF)
        mine = own_columns(count, size, per, d)
        for s in slots:
            got = jnp.where(mine, mm(x_ref[s], spread), 0.0)
            for r in range(rows):
                to = 2 * r if rows == 2 else r
                out_refs[s][to : to + 1] = jnp.sum(got[r * per : (r + 1) * per], axis=0, keepdims=True)
    out_refs[6][1:2] = jnp.zeros((1, d), F32)

def unfold(x, d):
    return pl.pallas_call(
        unfold_kernel,
        name="unfold",
        in_specs=[pl.BlockSpec(memory_space=pltpu.VMEM)],
        out_shape=[jax.ShapeDtypeStruct((r if r != 2 else 3, d), F32) for r in SMALL_ROWS],
        compiler_params=params(0, 16 << 20),
        cost_estimate=cost(1e8, 1e6),
    )(x)

def fold_kernel(first_ref, sums_ref, qkv_ref, fc_ref, out_ref):
    count, d = out_ref.shape[1], first_ref.shape[1]
    singles = [
        first_ref[0:1], first_ref[1:2], sums_ref[3:4], sums_ref[1:2], sums_ref[2:3], sums_ref[0:1],
    ]
    pairs = [[v] for v in singles] + [[qkv_ref[0:1], qkv_ref[2:3]], [fc_ref[r : r + 1] for r in range(4)]]
    for rows, slots in ((1, range(6)), (2, (6,)), (4, (7,))):
        size, per = d * rows // count, count // rows
        spread = spread_matrix(size, d)
        mine = own_columns(count, size, per, d)
        full = jnp.concatenate(
            [
                jnp.where(mine, jnp.concatenate([jnp.broadcast_to(v, (per, d)) for v in pairs[s]], 0), 0.0)
                for s in slots
            ],
            0,
        )
        got = lax.dot_general(
            full, spread, (((1,), (1,)), ((), ())), precision=lax.Precision.HIGHEST, preferred_element_type=F32
        )
        for i, s in enumerate(slots):
            out_ref[s] = got[i * count : (i + 1) * count]

def fold(first, sums, qkv, fc, count):
    return pl.pallas_call(
        fold_kernel,
        name="fold",
        in_specs=[pl.BlockSpec(memory_space=pltpu.VMEM)] * 4,
        out_shape=jax.ShapeDtypeStruct((8, count, 128), F32),
        compiler_params=params(0, 32 << 20),
        cost_estimate=cost(1e8, 1e6),
    )(first, sums, qkv, fc)


class Grid:
    def __init__(self, mesh, rows):
        wide, narrow = mesh.shape["wide"], mesh.shape["narrow"]
        self.count = wide * narrow
        self.paired = narrow == 4 and wide % 2 == 0 and rows % 8 == 0
        self.blocks = self.count // 2 if self.paired else 1
        self.z = wide // 2

    def index(self, z, x, y, c):
        return ((z * 2 + x) * 2 + y) * 2 + c

    def places(self):
        return [
            (z, x, y, c) for z in range(self.z) for x in range(2) for y in range(2) for c in range(2)
        ]

    def perm(self, target):
        return [(self.index(*at), self.index(*target(*at))) for at in self.places()]

    def here(self):
        w, n = lax.axis_index("wide"), lax.axis_index("narrow")
        return w // 2, w % 2, n // 2, n % 2

    def table(self):
        rows = []
        for z0, x0, y0, c0 in self.places():
            mine = []
            for half in (c0, 1 - c0):
                for ka, kb in ((0, 0), (1, 0), (0, 1), (1, 1)):
                    kx, ky = (ka, kb) if half == 0 else (kb, ka)
                    blocks = [
                        (((z0 - kz) % self.z) * 2 + (x0 ^ kx)) * 2 + (y0 ^ ky) for kz in range(self.z)
                    ]
                    mine.append([half] + blocks)
            rows.append(mine)
        return np.array(rows, np.int32)

    def routes(self):
        near, far = [], []
        for z0, x0, y0, c0 in self.places():
            if c0 == 0:
                near.append([[1 - x0, 0], [1 - x0, 1], [x0, 0], [x0, 1]])
                far.append([[1 - y0], [y0]])
            else:
                near.append([[0, 1 - y0], [1, 1 - y0], [0, y0], [1, y0]])
                far.append([[1 - x0], [x0]])
        return np.array(near, np.int32), np.array(far, np.int32)

    def send(self, value, target):
        return lax.ppermute(value, AXES, self.perm(target))

    def other_core(self, value):
        return self.send(value, lambda z, x, y, c: (z, x, y, 1 - c))

    def along(self, value, turn):
        return self.send(
            value,
            lambda z, x, y, c: (z, 1 - x, y, c) if c == turn else (z, x, 1 - y, c),
        )

    def up(self, value, k):
        return self.send(value, lambda z, x, y, c: ((z + k) % self.z, x, y, c))


def both(first, own, other, axis):
    return jnp.where(
        first, jnp.concatenate([own, other], axis), jnp.concatenate([other, own], axis)
    )


def pair_rows(grid, shard):
    c = grid.here()[3]
    h = shard.shape[1] // 2
    other = grid.other_core(lax.dynamic_slice_in_dim(shard, (1 - c) * h, h, 1))
    return both(c == 0, lax.dynamic_slice_in_dim(shard, c * h, h, 1), other, 0)


def spread_z(grid, pair):
    return jnp.stack([pair] + [grid.up(pair, k) for k in range(1, grid.z)])


def with_other(grid, sources):
    return sources + [grid.other_core(s) for s in sources]


def stage(*values):
    return lax.optimization_barrier(values)


def after(value, *earlier):
    return lax.optimization_barrier((value, *earlier))[0]


def add(a, b):
    return (a.astype(F32) + b.astype(F32)).astype(BF)


def pick(v, at, axis):
    return lax.dynamic_index_in_dim(v, at, axis, keepdims=False)


class Sum:
    def __init__(self, grid, sends, keeps):
        self.grid = grid
        at = lax.axis_index(AXES)
        self.tables = [jnp.asarray(t)[at] for t in grid.routes()]
        self.shape = (grid.z, 2, 2)
        self.keeps = keeps
        self.got = [grid.other_core(s) for s in sends]

    def core(self):
        block = lambda v: v.reshape(*self.shape, *v.shape[1:])
        self.away, self.stay = route(
            self.tables[0], [block(k) for k in self.keeps], [block(g) for g in self.got]
        )
        return self.away

    def near(self):
        self.got = self.grid.along(self.away, 0)

    def middle(self):
        self.away, self.stay = route(self.tables[1], [self.stay], [self.got])
        return self.away

    def far(self):
        self.got = self.grid.along(self.away, 1)

    def last(self):
        self.own = add(self.stay, self.got)[0]
        return self.own

    def up(self):
        grid, z = self.grid, self.grid.here()[0]
        self.got = [
            grid.up(pick(self.own, (z + k) % grid.z, 0), k) for k in range(1, grid.z)
        ]

    def rows(self):
        total = pick(self.own, self.grid.here()[0], 0).astype(F32)
        for g in self.got:
            total = total + g.astype(F32)
        return total


def own_rows(grid, total):
    c = grid.here()[3]
    r = total.shape[0] // 2
    other = grid.other_core(lax.dynamic_slice_in_dim(total, (1 - c) * r, r, 0))
    return both(c == 0, lax.dynamic_slice_in_dim(total, c * r, r, 0), other, 1)


def to_chunks(pair):
    r = pair.shape[0] // 4
    return jnp.concatenate([pair[j * r : (j + 1) * r] for j in range(4)], 1)


def from_chunks(total):
    w = total.shape[1] // 4
    return jnp.concatenate([total[:, j * w : (j + 1) * w] for j in range(4)], 0)


def gather_small(count, vectors, first):
    rows = [jnp.pad(v, (0, 128 - v.shape[0])) for v in vectors]
    flat, _ = stage(jnp.stack(rows), first)
    return lax.all_to_all(jnp.broadcast_to(flat[:, None], (8, count, 128)), AXES, 1, 1, tiled=True)


def scatter_small(cut):
    return jnp.sum(lax.all_to_all(cut, AXES, 1, 1, tiled=True), axis=1)


def halves_of(weight):
    h = weight.shape[1] // 2
    return [weight[None, :, :h], weight[None, :, h:]]


def local(
    mesh,
    tokens,
    norm1_gain,
    norm1_bias,
    qkv_weight,
    qkv_bias,
    out_weight,
    out_bias,
    norm2_gain,
    norm2_bias,
    fc_weight,
    fc_bias,
    proj_weight,
    proj_bias,
    seq_lengths,
    out_cotangent,
):
    d = tokens.shape[1]
    grid = Grid(mesh, out_weight.shape[0])
    blocks = grid.blocks
    vectors = [norm1_gain, norm1_bias, out_bias, norm2_gain, norm2_bias, proj_bias, qkv_bias, fc_bias]
    if grid.paired:
        place = jnp.asarray(grid.table())[lax.axis_index(AXES)]
        core = grid.here()[3].reshape(1).astype(jnp.int32)
        pair_qkv = pair_rows(grid, qkv_weight)
        fc_shard, out_shard, proj_shard, pair_qkv = stage(fc_weight, out_weight, proj_weight, pair_qkv)
        stack_qkv = spread_z(grid, pair_qkv)
        first = jnp.concatenate([pair_rows(grid, fc_shard), pair_rows(grid, out_shard)], 1)
        second = to_chunks(pair_rows(grid, proj_shard))
        little_all = gather_small(grid.count, vectors, pair_qkv)
        stack_qkv, first, second = stage(stack_qkv, first, second)
        near_qkv, far_qkv = grid.along(stack_qkv, 0), grid.along(stack_qkv, 1)
        near_qkv, far_qkv, first, little_all = stage(near_qkv, far_qkv, first, little_all)
        last_qkv = grid.along(near_qkv, 1)
        stack_first = spread_z(grid, first)
        last_qkv, stack_first = stage(last_qkv, stack_first)
        qkv_sources = with_other(grid, [stack_qkv, near_qkv, far_qkv, last_qkv])
        near_first, far_first = grid.along(stack_first, 0), grid.along(stack_first, 1)
        *qkv_sources, second = stage(*qkv_sources, second)
        stack_second = spread_z(grid, second)
    else:
        place = jnp.asarray(np.array([[0, 0], [1, 0]], np.int32))
        core = jnp.zeros((1,), jnp.int32)
        full = lambda v: lax.all_gather(v, AXES, axis=0, tiled=True)
        qkv_sources = halves_of(full(qkv_weight))
        little_all = gather_small(grid.count, vectors, tokens)
    gain_one, shift_one, bias_out, gain_two, shift_two, bias_proj, bias_qkv, bias_fc = unfold(little_all, d)
    qkv, low_one, qkv_full = project(
        place, tokens, gain_one, shift_one, bias_qkv, qkv_sources, blocks
    )
    if grid.paired:
        qkv, near_first, far_first, stack_second = stage(qkv, near_first, far_first, stack_second)
        last_first = grid.along(near_first, 1)
        near_second, far_second = grid.along(stack_second, 0), grid.along(stack_second, 1)
    attended = [attend(seq_lengths, qkv, 4, 0, 512)]
    if grid.paired:
        qkv, near_second, far_second, last_first, _ = stage(
            qkv, near_second, far_second, last_first, attended[0][2]
        )
        last_second = grid.along(near_second, 1)
        outs = with_other(grid, [stack_first, near_first, far_first, last_first])
        seconds = with_other(grid, [stack_second, near_second, far_second, last_second])
        fcs, out_at, projs = [(s, 0) for s in outs], 4, [(s, 0) for s in seconds]
    else:
        fcs = [(s, 0) for s in halves_of(full(fc_weight))]
        outs, out_at = halves_of(full(out_weight)), 0
        projs = [(to_chunks(s[0])[None], 0) for s in halves_of(full(proj_weight))]
    attended.append(attend(seq_lengths, qkv, 2, 4, 512))
    mixed = [a[1] for a in attended]
    middle, low_two, out_full = mix(
        place, mixed, tokens, bias_out, gain_two, shift_two, outs, blocks, out_at
    )
    (layer_out, grad_middle, grad_branch, fc_send, fc_keep, proj_send, proj_keep, fc_bias_term, sums) = mlp(
        core, place, seq_lengths, middle, low_two, out_cotangent, bias_fc, bias_proj,
        gain_two, fcs, projs, blocks,
    )
    grad_mixed, out_send, out_keep = unmix(core, seq_lengths, grad_branch, mixed, out_full, blocks)
    if grid.paired:
        fc_sum = Sum(grid, [fc_send], [fc_keep])
        proj_sum = Sum(grid, [proj_send, out_send], [proj_keep, out_keep])
        grad_mixed, fc_sum.away, fc_sum.stay = stage(grad_mixed, fc_sum.core(), fc_sum.stay)
        fc_sum.near()
    grad_one = attend_grad(qkv, grad_mixed, attended[0][0], attended[0][2], 0)
    if grid.paired:
        fc_sum.got, grad_one, grad_mixed = stage(fc_sum.got, grad_one, grad_mixed)
        fc_sum.middle()
        proj_sum.core()
        grad_mixed, fc_sum.away, fc_sum.stay, proj_sum.away, proj_sum.stay = stage(
            grad_mixed, fc_sum.away, fc_sum.stay, proj_sum.away, proj_sum.stay
        )
        fc_sum.far()
        proj_sum.near()
    grad_two = attend_grad(qkv, grad_mixed, attended[1][0], attended[1][2], 4)
    if grid.paired:
        fc_sum.got, grad_two = stage(fc_sum.got, grad_two)
        fc_sum.own, grad_two = stage(fc_sum.last(), grad_two)
        fc_sum.up()
    grads = [grad_one, grad_two]
    qkv_send, qkv_keep, qkv_sums = unproject(core, low_one, grads, blocks)
    if grid.paired:
        qkv_send, proj_sum.got = stage(qkv_send, proj_sum.got)
        qkv_sum = Sum(grid, [qkv_send], [qkv_keep])
        proj_sum.away, proj_sum.stay, *qkv_sum.got = stage(proj_sum.middle(), proj_sum.stay, *qkv_sum.got)
        proj_sum.far()
        grad_middle, qkv_sum.away, qkv_sum.stay = stage(grad_middle, qkv_sum.core(), qkv_sum.stay)
        qkv_sum.near()
    input_grad, first_sums = final(tokens, grads, qkv_full, grad_middle, gain_one)
    cut = fold(first_sums, sums, qkv_sums, fc_bias_term, grid.count)
    if grid.paired:
        first_sums, proj_sum.got, fc_sum.got = stage(first_sums, proj_sum.got, fc_sum.got)
        first_sums, proj_sum.own, qkv_sum.got = stage(first_sums, proj_sum.last(), qkv_sum.got)
        proj_sum.up()
        cut, qkv_sum.away, qkv_sum.stay = stage(cut, qkv_sum.middle(), qkv_sum.stay)
        qkv_sum.far()
    little = scatter_small(cut)
    if grid.paired:
        little, qkv_sum.got = stage(little, qkv_sum.got)
        proj_sum.own = after(proj_sum.own, qkv_sum.last())
        qkv_sum.up()
        fc_weight_grad = own_rows(grid, fc_sum.rows())
        total = proj_sum.rows()
        proj_wide = proj_keep.shape[2]
        proj_weight_grad = own_rows(grid, from_chunks(total[:, :proj_wide]))
        out_weight_grad = own_rows(grid, total[:, proj_wide:])
        qkv_weight_grad = own_rows(grid, qkv_sum.rows())
    else:
        reduce = lambda v: lax.psum_scatter(v.astype(F32), AXES, scatter_dimension=0, tiled=True)
        side = lambda k, s: jnp.concatenate([k[0], s[0]], 1)
        fc_weight_grad = reduce(side(fc_keep, fc_send))
        out_weight_grad = reduce(side(out_keep, out_send))
        qkv_weight_grad = reduce(side(qkv_keep, qkv_send))
        proj_weight_grad = reduce(
            jnp.concatenate([from_chunks(proj_keep[0]), from_chunks(proj_send[0])], 1)
        )
    shard = lambda s: little[s, : vectors[s].shape[0]]
    return (
        layer_out,
        input_grad,
        shard(0),
        shard(1),
        qkv_weight_grad,
        shard(6),
        out_weight_grad,
        shard(2),
        shard(3),
        shard(4),
        fc_weight_grad,
        shard(7),
        proj_weight_grad,
        shard(5),
    )


def solution(mesh):
    matrix, vector = P(AXES, None), P(AXES)
    ins = (
        matrix, vector, vector, matrix, vector, matrix, vector, vector,
        vector, matrix, vector, matrix, vector, vector, matrix,
    )
    outs = (
        matrix, matrix, vector, vector, matrix, vector, matrix, vector,
        vector, vector, matrix, vector, matrix, vector,
    )
    return jax.shard_map(
        functools.partial(local, mesh), mesh=mesh, in_specs=ins, out_specs=outs, check_vma=False
    )
```

```python
import functools
import math

import jax
import jax.numpy as jnp
import numpy as np
from jax import lax
from jax.experimental import pallas as pl
from jax.experimental.pallas import tpu as pltpu
from jax.sharding import PartitionSpec as P

AXES = ("wide", "narrow")
BF, F32 = jnp.bfloat16, jnp.float32
VMEM_CAP = 58 << 20

def params(n=1, cap=VMEM_CAP):
    return pltpu.CompilerParams(dimension_semantics=("arbitrary",) * n, vmem_limit_bytes=cap)

def cost(flops, bytes_accessed, trans=0):
    return pl.CostEstimate(flops=int(flops), bytes_accessed=int(bytes_accessed), transcendentals=int(trans))

def mm(a, b):
    return jnp.dot(a, b, preferred_element_type=F32)

def diagonal_mask(rows, cols):
    key_at = lax.broadcasted_iota(jnp.int32, (rows, cols), 0)
    query_at = lax.broadcasted_iota(jnp.int32, (rows, cols), 1)
    return key_at <= query_at

def attend_kernel(qb, len_ref, qkv_ref, out_t_ref, out_ref, stat_ref, v_t, q_t):
    slot = qkv_ref.shape[1]
    q_t[...] = (qkv_ref[0] * jnp.asarray(0.125, BF)).T
    v_t[...] = qkv_ref[2].T
    half = lax.broadcasted_iota(jnp.int32, (128, 1), 0) < 64
    causal = diagonal_mask(qb, qb)
    length = len_ref[0]
    for i in range(slot // qb):
        cols = slice(i * qb, (i + 1) * qb)
        parts = []
        for head in range(2):
            mine = half if head == 0 else jnp.logical_not(half)
            qh = jnp.where(mine, q_t[:, cols], jnp.zeros((), BF))
            s_low = mm(qkv_ref[1, : i * qb, :], qh) if i else None
            s_dia = jnp.where(causal, mm(qkv_ref[1, cols, :], qh), -1e30)
            top = jnp.max(s_dia, axis=0, keepdims=True)
            if i:
                top = jnp.maximum(top, jnp.max(s_low, axis=0, keepdims=True))
            e_dia = jnp.exp(s_dia - top)
            total = jnp.sum(e_dia, axis=0, keepdims=True)
            vh = v_t[head * 64 : head * 64 + 64, :]
            acc = mm(vh[:, cols], e_dia.astype(BF))
            if i:
                e_low = jnp.exp(s_low - top)
                total = total + jnp.sum(e_low, axis=0, keepdims=True)
                acc = acc + mm(vh[:, : i * qb], e_low.astype(BF))
            stat_ref[0, head : head + 1, cols] = top + jnp.log(total)
            parts.append(acc / total)
        both = jnp.concatenate(parts, axis=0)
        seen = (i * qb + lax.broadcasted_iota(jnp.int32, (1, qb), 1)) < length
        both = jnp.where(seen, both, 0.0)
        out_t_ref[:, cols] = both
        out_ref[cols, :] = both.T.astype(BF)

def attend(lengths, qkv, pairs, first, qb=256):
    slot, width = qkv.shape[1], qkv.shape[2]
    return pl.pallas_call(
        functools.partial(attend_kernel, qb),
        name="attend",
        grid=(pairs,),
        in_specs=[
            pl.BlockSpec(memory_space=pltpu.SMEM),
            pl.BlockSpec((3, slot, 128), lambda j: (0, 0, j + first)),
        ],
        out_specs=[
            pl.BlockSpec((128, slot), lambda j: (j, 0)),
            pl.BlockSpec((slot, 128), lambda j: (0, j)),
            pl.BlockSpec((1, 2, slot), lambda j: (j, 0, 0)),
        ],
        out_shape=[
            jax.ShapeDtypeStruct((pairs * 128, slot), F32),
            jax.ShapeDtypeStruct((slot, pairs * 128), BF),
            jax.ShapeDtypeStruct((pairs, 2, slot), F32),
        ],
        scratch_shapes=[pltpu.VMEM((128, slot), BF), pltpu.VMEM((128, slot), BF)],
        compiler_params=params(),
        cost_estimate=cost(pairs * 2 * slot * slot * 256, 8e6 * pairs / 6, pairs * slot * slot),
    )(lengths, qkv)

def attend_grad_kernel(qb, qkv_ref, grad_ref, out_t_ref, stat_ref, g_ref, q_t, do_t, k_t, qs, dq_t, dk_s, dv_s):
    slot = qkv_ref.shape[1]
    qs[...] = qkv_ref[0] * jnp.asarray(0.125, BF)
    q_t[...] = qs[...].T
    k_t[...] = qkv_ref[1].T
    do_t[...] = grad_ref[...].T
    half = lax.broadcasted_iota(jnp.int32, (128, 1), 0) < 64
    half_lane = lax.broadcasted_iota(jnp.int32, (1, 128), 1) < 64
    causal = diagonal_mask(qb, qb)
    zero = jnp.zeros((), BF)
    prod = do_t[...].astype(F32) * out_t_ref[...]
    delta = [jnp.sum(prod[h * 64 : h * 64 + 64], axis=0, keepdims=True) for h in range(2)]
    for i in range(slot // qb):
        cols = slice(i * qb, (i + 1) * qb)
        end = (i + 1) * qb
        dv_new = dk_new = None
        for head in range(2):
            mine = half if head == 0 else jnp.logical_not(half)
            mine_lane = half_lane if head == 0 else jnp.logical_not(half_lane)
            qh_t = jnp.where(mine, q_t[:, cols], zero)
            doh_t = jnp.where(mine, do_t[:, cols], zero)
            qh = jnp.where(mine_lane, qs[cols, :], zero)
            doh = jnp.where(mine_lane, grad_ref[cols, :], zero)
            stat = stat_ref[0, head : head + 1, cols]
            dl = delta[head][:, cols]
            s = mm(qkv_ref[1, :end, :], qh_t)
            dp = mm(qkv_ref[2, :end, :], doh_t)
            p = jnp.exp(s - stat)
            p_dia = jnp.where(causal, p[i * qb :], 0.0)
            p = jnp.concatenate([p[: i * qb], p_dia], axis=0) if i else p_dia
            ds = (p * (dp - dl)).astype(BF)
            pb = p.astype(BF)
            dv_h = mm(pb, doh)
            dk_h = mm(ds, qh)
            dv_new = dv_h if head == 0 else dv_new + dv_h
            dk_new = dk_h if head == 0 else dk_new + dk_h
            dq_t[head * 64 : head * 64 + 64, cols] = mm(k_t[head * 64 : head * 64 + 64, :end], ds)
        if i:
            dv_s[: i * qb] += dv_new[: i * qb]
            dk_s[: i * qb] += dk_new[: i * qb]
        dv_s[cols] = dv_new[i * qb :]
        dk_s[cols] = dk_new[i * qb :]
    g_ref[0] = (dq_t[...] * 0.125).T.astype(BF)
    g_ref[1] = dk_s[...].astype(BF)
    g_ref[2] = dv_s[...].astype(BF)

def attend_grad(qkv, grad, out_t, stat, first, qb=256):
    slot = qkv.shape[1]
    pairs = out_t.shape[0] // 128
    width = pairs * 128
    return pl.pallas_call(
        functools.partial(attend_grad_kernel, qb),
        name="attend_grad",
        grid=(pairs,),
        in_specs=[
            pl.BlockSpec((3, slot, 128), lambda j: (0, 0, j + first)),
            pl.BlockSpec((slot, 128), lambda j: (0, j + first)),
            pl.BlockSpec((128, slot), lambda j: (j, 0)),
            pl.BlockSpec((1, 2, slot), lambda j: (j, 0, 0)),
        ],
        out_specs=pl.BlockSpec((3, slot, 128), lambda j: (0, 0, j)),
        out_shape=jax.ShapeDtypeStruct((3, slot, width), BF),
        scratch_shapes=[
            pltpu.VMEM((128, slot), BF),
            pltpu.VMEM((128, slot), BF),
            pltpu.VMEM((128, slot), BF),
            pltpu.VMEM((slot, 128), BF),
            pltpu.VMEM((128, slot), F32),
            pltpu.VMEM((slot, 128), F32),
            pltpu.VMEM((slot, 128), F32),
        ],
        compiler_params=params(),
        cost_estimate=cost(pairs * 5 * slot * slot * 256, 16e6 * pairs / 6, pairs * 2 * slot * slot),
    )(qkv, grad, out_t, stat)
branch_scale = 1.0 / math.sqrt(48.0)
norm_epsilon = 1e-05
WHOLE = dict(pipeline_mode=pl.Buffered(1))

def mm_nt(a, b):
    return lax.dot_general(a, b, (((1,), (1,)), ((), ())), preferred_element_type=F32)

def mm_tn(a, b):
    return lax.dot_general(a, b, (((0,), (0,)), ((), ())), preferred_element_type=F32)

def normalised(v):
    mean = jnp.mean(v, axis=-1, keepdims=True)
    centred = v - mean
    var = jnp.mean(centred * centred, axis=-1, keepdims=True)
    scale = lax.rsqrt(var + norm_epsilon)
    return centred * scale, scale

def norm_pull(n, scale, gain, u):
    ug = u * gain
    a = jnp.mean(ug, axis=-1, keepdims=True)
    b = jnp.mean(ug * n, axis=-1, keepdims=True)
    return (ug - a - n * b) * scale

def whole(shape, index=None):
    zeros = (0,) * len(shape)
    return pl.BlockSpec(shape, (lambda *_: index or zeros), **WHOLE)

def assemble(place, sources, target, at=0):
    wide = sources[0].shape[2]
    for s, source in enumerate(sources):
        for half in range(2):
            @pl.when(place[s, 0] == half)
            def _():
                for p in range(source.shape[0]):
                    target[place[s, 1 + p], :, half * wide : (half + 1) * wide] = source[p]

def assemble_chunks(place, sources, target):
    wide = sources[0].shape[2] // 4
    for s, source in enumerate(sources):
        for half in range(2):
            @pl.when(place[s, 0] == half)
            def _():
                for p in range(source.shape[0]):
                    for j in range(4):
                        target[place[s, 1 + p], j, :, half * wide : (half + 1) * wide] = source[p, :, j * wide : (j + 1) * wide]

def project_kernel(n_src, place, x_ref, gain_ref, shift_ref, bias_ref, *rest):
    sources, (qkv_ref, low_ref, w_ref) = rest[:n_src], rest[n_src:]
    @pl.when(pl.program_id(0) == 0)
    def _():
        assemble(place, sources, w_ref)
    n, _ = normalised(x_ref[...].astype(F32))
    low = (n * gain_ref[...] + shift_ref[...]).astype(BF)
    low_ref[...] = low
    d = low.shape[1]
    for part in range(3):
        w = w_ref[:, :, part * d : (part + 1) * d].reshape(d, d)
        qkv_ref[part] = (mm(low, w) + bias_ref[part : part + 1]).astype(BF)

def project(place, x, gain, shift, bias, sources, blocks, rows=256):
    t, d = x.shape
    r, wide = d // blocks, sources[0].shape[2]
    return pl.pallas_call(
        functools.partial(project_kernel, len(sources)),
        name="project",
        grid_spec=pltpu.PrefetchScalarGridSpec(
            num_scalar_prefetch=1,
            grid=(t // rows,),
            in_specs=[
                pl.BlockSpec((rows, d), lambda i, p: (i, 0)),
                whole((1, d)), whole((1, d)), whole((3, d)),
                *[whole(s.shape) for s in sources],
            ],
            out_specs=[
                pl.BlockSpec((3, rows, d), lambda i, p: (0, i, 0)),
                pl.BlockSpec((rows, d), lambda i, p: (i, 0)),
                whole((blocks, r, 2 * wide)),
            ],
        ),
        out_shape=[
            jax.ShapeDtypeStruct((3, t, d), BF),
            jax.ShapeDtypeStruct((t, d), BF),
            jax.ShapeDtypeStruct((blocks, r, 2 * wide), BF),
        ],
        compiler_params=params(),
        cost_estimate=cost(2 * t * d * 3 * d, 18e6),
    )(place, x, gain, shift, bias, *sources)

def mix_kernel(n_src, place, x_ref, bias_ref, gain_ref, shift_ref, *rest):
    sources, parts, (mid_ref, low_ref, w_ref) = rest[:n_src], rest[n_src:-3], rest[-3:]
    @pl.when(pl.program_id(0) == 0)
    def _():
        assemble(place, sources, w_ref)
    d = x_ref.shape[1]
    w = w_ref[...].reshape(d, d)
    mid = x_ref[...].astype(F32) + branch_scale * (mm(jnp.concatenate([p[...] for p in parts], 1), w) + bias_ref[...])
    mid_ref[...] = mid
    n, _ = normalised(mid)
    low_ref[...] = (n * gain_ref[...] + shift_ref[...]).astype(BF)

def mix(place, parts, x, bias, gain, shift, sources, blocks, column, rows=256):
    t, d = x.shape
    r, np_ = d // blocks, sources[0].shape[0]
    return pl.pallas_call(
        functools.partial(mix_kernel, len(sources)),
        name="mix",
        grid_spec=pltpu.PrefetchScalarGridSpec(
            num_scalar_prefetch=1,
            grid=(t // rows,),
            in_specs=[
                pl.BlockSpec((rows, d), lambda i, p: (i, 0)),
                whole((1, d)), whole((1, d)), whole((1, d)),
                *[whole((np_, r, d // 2), (0, 0, column)) for s in sources],
                *[pl.BlockSpec((rows, p.shape[1]), lambda i, p: (i, 0)) for p in parts],
            ],
            out_specs=[
                pl.BlockSpec((rows, d), lambda i, p: (i, 0)),
                pl.BlockSpec((rows, d), lambda i, p: (i, 0)),
                whole((blocks, r, d)),
            ],
        ),
        out_shape=[
            jax.ShapeDtypeStruct((t, d), F32),
            jax.ShapeDtypeStruct((t, d), BF),
            jax.ShapeDtypeStruct((blocks, r, d), BF),
        ],
        compiler_params=params(),
        cost_estimate=cost(2 * t * d * d, 9e6),
    )(place, x, bias, gain, shift, *sources, *parts)

def mlp_kernel(n_src, blocks, rb, core, place, lens, mid_ref, low_ref, cot_ref, fb_ref, pb_ref, gain_ref, *rest):
    fcs, projs, rest = rest[:n_src], rest[n_src : 2 * n_src], rest[2 * n_src :]
    (out_ref, gmid_ref, gbr_ref, fsend_ref, fkeep_ref, psend_ref, pkeep_ref, fbg_ref, vec_ref,
     fc_s, proj_s, low_t, g2_s, second_s, gh_s, act_s, gpre_s) = rest
    t, d = mid_ref.shape
    r = d // blocks
    step = pl.program_id(0)
    mine = core[0]
    chunk = lax.rem(step + 2 * (1 - mine), 4)
    def valid_rows(at):
        return (at * rb + lax.broadcasted_iota(jnp.int32, (rb, 1), 0)) < lens[0]
    @pl.when(step == 0)
    def _():
        assemble(place, fcs, fc_s)
        assemble_chunks(place, projs, proj_s)
        low_t[...] = low_ref[...].T
        def begin(i, total):
            at = pl.ds(pl.multiple_of(i * rb, rb), rb)
            g = jnp.where(valid_rows(i), branch_scale * cot_ref[at, :].astype(F32), 0.0).astype(BF)
            g2_s[at, :] = g
            second_s[at, :] = jnp.zeros((rb, d), F32)
            gh_s[at, :] = jnp.zeros((rb, d), F32)
            return total + jnp.sum(g.astype(F32), axis=0, keepdims=True)
        vec_ref[0:1] = lax.fori_loop(0, t // rb, begin, jnp.zeros((1, d), F32))
    fcol = pl.ds(pl.multiple_of(chunk * d, d), d)
    fc = fc_s.at[:, :, fcol]
    bias = fb_ref[pl.ds(chunk, 1), :]
    if blocks % 4 == 0:
        per = blocks // 4
        proj = proj_s.at[pl.ds(chunk * per, per)]
    else:
        proj = proj_s.at[:, pl.ds(chunk, 1)]
    def rows_step(i, total):
        at = pl.ds(pl.multiple_of(i * rb, rb), rb)
        u = mm(low_ref[at, :], fc[...].reshape(d, d)) + bias
        sq = u * u
        th = jnp.tanh(0.7978845608028654 * u * (1.0 + 0.044715 * sq))
        up = 0.5 * (1.0 + th)
        act = (u * up).astype(BF)
        act_s[at, :] = act
        slope = up + u * (0.5 * 0.7978845608028654) * (1.0 - th * th) * (1.0 + 3 * 0.044715 * sq)
        w = proj[...].reshape(d, d)
        second_s[at, :] += mm(act, w)
        gp = mm_nt(g2_s[at, :], w) * slope
        gpb = gp.astype(BF)
        gpre_s[at, :] = gpb
        gh_s[at, :] += mm_nt(gpb, fc[...].reshape(d, d))
        return total + jnp.sum(gpb.astype(F32), axis=0, keepdims=True)
    fbg_ref[pl.ds(chunk, 1), :] = lax.fori_loop(0, t // rb, rows_step, jnp.zeros((1, d), F32))
    dfc = mm(low_t[...], gpre_s[...]).astype(BF).reshape(blocks, r, d)
    @pl.when(step < 2)
    def _():
        fsend_ref[...] = dfc
    @pl.when(step >= 2)
    def _():
        fkeep_ref[...] = dfc
    dproj = mm_tn(act_s[...], g2_s[...]).astype(BF)
    h = d // 2
    for half in range(2):
        @pl.when(mine == half)
        def _():
            for ref, cols in ((pkeep_ref, half), (psend_ref, 1 - half)):
                piece = dproj[:, cols * h : (cols + 1) * h]
                if blocks % 4 == 0:
                    for b in range(blocks // 4):
                        for j in range(4):
                            ref[b, :, j * h : (j + 1) * h] = piece[(b * 4 + j) * r : (b * 4 + j + 1) * r]
                else:
                    ref[0] = piece
    @pl.when(step == 3)
    def _():
        def finish(i, carry):
            at = pl.ds(pl.multiple_of(i * rb, rb), rb)
            mid = mid_ref[at, :]
            out_ref[at, :] = (mid + branch_scale * (second_s[at, :] + pb_ref[...])).astype(BF)
            n, scale = normalised(mid)
            gh = gh_s[at, :]
            cot = jnp.where(valid_rows(i), cot_ref[at, :].astype(F32), 0.0)
            gm = cot + norm_pull(n, scale, gain_ref[...], gh)
            gmid_ref[at, :] = gm
            gb = (branch_scale * gm).astype(BF)
            gbr_ref[at, :] = gb
            return (carry[0] + jnp.sum(gh * n, axis=0, keepdims=True),
                    carry[1] + jnp.sum(gh, axis=0, keepdims=True),
                    carry[2] + jnp.sum(gb.astype(F32), axis=0, keepdims=True))
        zero = jnp.zeros((1, d), F32)
        a, b, c = lax.fori_loop(0, t // rb, finish, (zero, zero, zero))
        vec_ref[1:2] = a
        vec_ref[2:3] = b
        vec_ref[3:4] = c

def mlp(core, place, lens, mid, low, cot, fb, pb, gain, fcs, projs, blocks, rb=256):
    t, d = mid.shape
    r, np_ = d // blocks, fcs[0][0].shape[0]
    smem = pl.BlockSpec(memory_space=pltpu.SMEM)
    if blocks % 4 == 0:
        pspec = pl.BlockSpec((blocks // 4, r, 2 * d), lambda i, c: (lax.rem(i + 2 * (1 - c[0]), 4), 0, 0))
    else:
        pspec = pl.BlockSpec((1, r, d // 2), lambda i, c: (0, 0, lax.rem(i + 2 * (1 - c[0]), 4)))
    big = jax.ShapeDtypeStruct((blocks, r, 2 * d), BF)
    return pl.pallas_call(
        functools.partial(mlp_kernel, len(fcs), blocks, rb),
        name="mlp",
        grid_spec=pltpu.PrefetchScalarGridSpec(
            num_scalar_prefetch=1,
            grid=(4,),
            in_specs=[
                smem, smem, whole((t, d)), whole((t, d)), whole((t, d)), whole((4, d)), whole((1, d)), whole((1, d)),
                *[whole((np_, r, 2 * d), (0, 0, at)) for _, at in fcs],
                *[whole((np_, r, 2 * d), (0, 0, at)) for _, at in projs],
            ],
            out_specs=[
                whole((t, d)), whole((t, d)), whole((t, d)),
                pl.BlockSpec((blocks, r, d), lambda i, c: (0, 0, jnp.minimum(i, 1))),
                pl.BlockSpec((blocks, r, d), lambda i, c: (0, 0, jnp.maximum(i - 2, 0))),
                pspec, pspec,
                whole((4, d)), whole((4, d)),
            ],
            scratch_shapes=[
                pltpu.VMEM((blocks, r, 4 * d), BF),
                pltpu.VMEM((blocks, 4, r, d), BF),
                pltpu.VMEM((d, t), BF),
                pltpu.VMEM((t, d), BF),
                pltpu.VMEM((t, d), F32),
                pltpu.VMEM((t, d), F32),
                pltpu.VMEM((t, d), BF),
                pltpu.VMEM((t, d), BF),
            ],
        ),
        out_shape=[
            jax.ShapeDtypeStruct((t, d), BF), jax.ShapeDtypeStruct((t, d), F32), jax.ShapeDtypeStruct((t, d), BF),
            big, big, big, big,
            jax.ShapeDtypeStruct((4, d), F32), jax.ShapeDtypeStruct((4, d), F32),
        ],
        compiler_params=params(),
        cost_estimate=cost(12 * t * d * 4 * d, 40e6, t * 4 * d),
    )(core, place, lens, mid, low, cot, fb, pb, gain, *[a for a, _ in fcs], *[a for a, _ in projs])

def unmix_kernel(core, lens, gbr_ref, w_ref, *rest):
    parts, (ga_ref, send_ref, keep_ref) = rest[:-3], rest[-3:]
    t, d = gbr_ref.shape
    w = w_ref[...].reshape(d, d)
    seen = lax.broadcasted_iota(jnp.int32, (t, 1), 0) < lens[0]
    ga_ref[...] = jnp.where(seen, mm_nt(gbr_ref[...], w), 0.0).astype(BF)
    dw = jnp.concatenate([mm_tn(p[...], gbr_ref[...]).astype(BF) for p in parts], 0)
    h = d // 2
    for half in range(2):
        @pl.when(core[0] == half)
        def _():
            keep_ref[...] = dw[:, half * h : (half + 1) * h].reshape(keep_ref.shape)
            send_ref[...] = dw[:, (1 - half) * h : (2 - half) * h].reshape(send_ref.shape)

def unmix(core, lens, gbr, parts, w, blocks):
    t, d = gbr.shape
    smem = pl.BlockSpec(memory_space=pltpu.SMEM)
    piece = jax.ShapeDtypeStruct((blocks, d // blocks, d // 2), BF)
    return pl.pallas_call(
        unmix_kernel,
        name="unmix",
        in_specs=[smem, smem] + [pl.BlockSpec(memory_space=pltpu.VMEM)] * (2 + len(parts)),
        out_shape=[jax.ShapeDtypeStruct((t, d), BF), piece, piece],
        compiler_params=params(0),
        cost_estimate=cost(4 * t * d * d, 9e6),
    )(core, lens, gbr, w, *parts)

def unproject_kernel(blocks, core, low_ref, g_ref, send_ref, keep_ref, sums_ref):
    d, w = low_ref.shape[1], g_ref.shape[2]
    r, h = d // blocks, w // 2
    low_t = low_ref[...].T
    q, k, v = [mm(low_t, g_ref[part]).astype(BF).reshape(blocks, r, w) for part in range(3)]
    for half, refs in ((0, (keep_ref, send_ref)), (1, (send_ref, keep_ref))):
        @pl.when(core[0] == half)
        def _():
            refs[0][:, :, :w] = q
            refs[0][:, :, w:] = k[:, :, :h]
            refs[1][:, :, :h] = k[:, :, h:]
            refs[1][:, :, h:] = v
    for part in range(3):
        sums_ref[part : part + 1] = jnp.sum(g_ref[part].astype(F32), axis=0, keepdims=True)

def unproject(core, low, g, blocks):
    t, d = low.shape
    w = g.shape[2]
    piece = jax.ShapeDtypeStruct((blocks, d // blocks, w // 2 * 3), BF)
    return pl.pallas_call(
        functools.partial(unproject_kernel, blocks),
        name="unproject",
        in_specs=[pl.BlockSpec(memory_space=pltpu.SMEM)] + [pl.BlockSpec(memory_space=pltpu.VMEM)] * 2,
        out_shape=[piece, piece, jax.ShapeDtypeStruct((3, w), F32)],
        compiler_params=params(0),
        cost_estimate=cost(6 * t * d * w, 10e6 * w / d),
    )(core, low, g)

def route_kernel(count, steps, table, *refs):
    keeps, gots, (away_ref, stay_ref) = refs[:count], refs[count : 2 * count], refs[2 * count :]
    def write(ref):
        at = 0
        for k, g in zip(keeps, gots):
            w = k.shape[-1]
            total = (k[...].astype(F32) + g[...].astype(F32)).astype(BF)
            ref[..., at : at + w] = total.reshape(ref.shape[:-1] + (w,))
            at += w
    @pl.when(pl.program_id(0) < steps)
    def _():
        write(away_ref)
    @pl.when(pl.program_id(0) >= steps)
    def _():
        write(stay_ref)

def route(table, keeps, gots):
    shape = keeps[0].shape
    z, r = (shape[0], shape[3]) if len(shape) == 5 else (shape[1], shape[2])
    steps = 2 if len(shape) == 5 else 1
    wide = sum(k.shape[-1] for k in keeps)
    def spec(w):
        if len(shape) == 5:
            return pl.BlockSpec((z, 1, 1, r, w), lambda i, t: (0, t[i, 0], t[i, 1], 0, 0))
        return pl.BlockSpec((1, z, r, w), lambda i, t: (t[i, 0], 0, 0, 0))
    out = jax.ShapeDtypeStruct((steps, z, r, wide), BF)
    return pl.pallas_call(
        functools.partial(route_kernel, len(keeps), steps),
        name="route",
        grid_spec=pltpu.PrefetchScalarGridSpec(
            num_scalar_prefetch=1,
            grid=(2 * steps,),
            in_specs=[spec(k.shape[-1]) for k in keeps] * 2,
            out_specs=[
                pl.BlockSpec((1, z, r, wide), lambda i, t: (jnp.minimum(i, steps - 1), 0, 0, 0)),
                pl.BlockSpec((1, z, r, wide), lambda i, t: (jnp.maximum(i - steps, 0), 0, 0, 0)),
            ],
        ),
        out_shape=[out, out],
        compiler_params=params(1, 24 << 20),
        cost_estimate=cost(1e6, steps * 2 * z * r * wide * 6),
    )(table, *keeps, *gots)

def final_kernel(x_ref, w_ref, gmid_ref, gain_ref, *rest):
    parts, (out_ref, vec_ref) = rest[:-2], rest[-2:]
    d = x_ref.shape[1]
    w = w_ref[...].reshape(d, 3 * d)
    gh = jnp.zeros(x_ref.shape, F32)
    at = 0
    for g in parts:
        for i in range(3):
            gh = gh + mm_nt(g[i], w[:, i * d + at : i * d + at + g.shape[2]])
        at += g.shape[2]
    n, scale = normalised(x_ref[...].astype(F32))
    out_ref[...] = (gmid_ref[...] + norm_pull(n, scale, gain_ref[...], gh)).astype(BF)
    @pl.when(pl.program_id(0) == 0)
    def _():
        vec_ref[...] = jnp.zeros_like(vec_ref)
    vec_ref[0:1] += jnp.sum(gh * n, axis=0, keepdims=True)
    vec_ref[1:2] += jnp.sum(gh, axis=0, keepdims=True)

def final(x, parts, w, gmid, gain, rows=256):
    t, d = x.shape
    return pl.pallas_call(
        final_kernel,
        name="final",
        grid=(t // rows,),
        in_specs=[
            pl.BlockSpec((rows, d), lambda i: (i, 0)),
            whole(w.shape),
            pl.BlockSpec((rows, d), lambda i: (i, 0)),
            whole((1, d)),
            *[pl.BlockSpec((3, rows, g.shape[2]), lambda i: (0, i, 0)) for g in parts],
        ],
        out_specs=[pl.BlockSpec((rows, d), lambda i: (i, 0)), whole((2, d))],
        out_shape=[jax.ShapeDtypeStruct((t, d), BF), jax.ShapeDtypeStruct((2, d), F32)],
        compiler_params=params(),
        cost_estimate=cost(6 * t * d * d, 15e6),
    )(x, w, gmid, gain, *parts)
def spread_matrix(size, width):
    row = lax.broadcasted_iota(jnp.int32, (128, width), 0).astype(F32)
    col = lax.broadcasted_iota(jnp.int32, (128, width), 1).astype(F32)
    inside = col - jnp.floor((col + 0.5) / size) * size
    return jnp.where(inside == row, 1.0, 0.0)

def own_columns(count, size, per, width):
    at = lax.broadcasted_iota(jnp.int32, (count, width), 0).astype(F32)
    at = at - jnp.floor((at + 0.5) / per) * per
    col = lax.broadcasted_iota(jnp.int32, (count, width), 1).astype(F32)
    return jnp.logical_and(col >= at * size, col < (at + 1) * size)

SMALL_ROWS = (1, 1, 1, 1, 1, 1, 2, 4)

def unfold_kernel(x_ref, *out_refs):
    count, d = x_ref.shape[1], out_refs[0].shape[1]
    for rows, slots in ((1, range(6)), (2, (6,)), (4, (7,))):
        size, per = d * rows // count, count // rows
        spread = spread_matrix(size, d).astype(BF)
        mine = own_columns(count, size, per, d)
        for s in slots:
            got = jnp.where(mine, mm(x_ref[s], spread), 0.0)
            for r in range(rows):
                to = 2 * r if rows == 2 else r
                out_refs[s][to : to + 1] = jnp.sum(got[r * per : (r + 1) * per], axis=0, keepdims=True)
    out_refs[6][1:2] = jnp.zeros((1, d), F32)

def unfold(x, d):
    return pl.pallas_call(
        unfold_kernel,
        name="unfold",
        in_specs=[pl.BlockSpec(memory_space=pltpu.VMEM)],
        out_shape=[jax.ShapeDtypeStruct((r if r != 2 else 3, d), F32) for r in SMALL_ROWS],
        compiler_params=params(0, 16 << 20),
        cost_estimate=cost(1e8, 1e6),
    )(x)

def fold_kernel(first_ref, sums_ref, qkv_ref, fc_ref, out_ref):
    count, d = out_ref.shape[1], first_ref.shape[1]
    singles = [
        first_ref[0:1], first_ref[1:2], sums_ref[3:4], sums_ref[1:2], sums_ref[2:3], sums_ref[0:1],
    ]
    pairs = [[v] for v in singles] + [[qkv_ref[0:1], qkv_ref[2:3]], [fc_ref[r : r + 1] for r in range(4)]]
    for rows, slots in ((1, range(6)), (2, (6,)), (4, (7,))):
        size, per = d * rows // count, count // rows
        spread = spread_matrix(size, d)
        mine = own_columns(count, size, per, d)
        full = jnp.concatenate(
            [
                jnp.where(mine, jnp.concatenate([jnp.broadcast_to(v, (per, d)) for v in pairs[s]], 0), 0.0)
                for s in slots
            ],
            0,
        )
        got = lax.dot_general(
            full, spread, (((1,), (1,)), ((), ())), precision=lax.Precision.HIGHEST, preferred_element_type=F32
        )
        for i, s in enumerate(slots):
            out_ref[s] = got[i * count : (i + 1) * count]

def fold(first, sums, qkv, fc, count):
    return pl.pallas_call(
        fold_kernel,
        name="fold",
        in_specs=[pl.BlockSpec(memory_space=pltpu.VMEM)] * 4,
        out_shape=jax.ShapeDtypeStruct((8, count, 128), F32),
        compiler_params=params(0, 32 << 20),
        cost_estimate=cost(1e8, 1e6),
    )(first, sums, qkv, fc)


class Grid:
    def __init__(self, mesh, rows):
        wide, narrow = mesh.shape["wide"], mesh.shape["narrow"]
        self.count = wide * narrow
        self.paired = narrow == 4 and wide % 2 == 0 and rows % 8 == 0
        self.blocks = self.count // 2 if self.paired else 1
        self.z = wide // 2

    def index(self, z, x, y, c):
        return ((z * 2 + x) * 2 + y) * 2 + c

    def places(self):
        return [
            (z, x, y, c) for z in range(self.z) for x in range(2) for y in range(2) for c in range(2)
        ]

    def perm(self, target):
        return [(self.index(*at), self.index(*target(*at))) for at in self.places()]

    def here(self):
        w, n = lax.axis_index("wide"), lax.axis_index("narrow")
        return w // 2, w % 2, n // 2, n % 2

    def table(self):
        rows = []
        for z0, x0, y0, c0 in self.places():
            mine = []
            for half in (c0, 1 - c0):
                for ka, kb in ((0, 0), (1, 0), (0, 1), (1, 1)):
                    kx, ky = (ka, kb) if half == 0 else (kb, ka)
                    blocks = [
                        (((z0 - kz) % self.z) * 2 + (x0 ^ kx)) * 2 + (y0 ^ ky) for kz in range(self.z)
                    ]
                    mine.append([half] + blocks)
            rows.append(mine)
        return np.array(rows, np.int32)

    def routes(self):
        near, far = [], []
        for z0, x0, y0, c0 in self.places():
            if c0 == 0:
                near.append([[1 - x0, 0], [1 - x0, 1], [x0, 0], [x0, 1]])
                far.append([[1 - y0], [y0]])
            else:
                near.append([[0, 1 - y0], [1, 1 - y0], [0, y0], [1, y0]])
                far.append([[1 - x0], [x0]])
        return np.array(near, np.int32), np.array(far, np.int32)

    def send(self, value, target):
        return lax.ppermute(value, AXES, self.perm(target))

    def other_core(self, value):
        return self.send(value, lambda z, x, y, c: (z, x, y, 1 - c))

    def along(self, value, turn):
        return self.send(
            value,
            lambda z, x, y, c: (z, 1 - x, y, c) if c == turn else (z, x, 1 - y, c),
        )

    def up(self, value, k):
        return self.send(value, lambda z, x, y, c: ((z + k) % self.z, x, y, c))


def both(first, own, other, axis):
    return jnp.where(
        first, jnp.concatenate([own, other], axis), jnp.concatenate([other, own], axis)
    )


def pair_rows(grid, shard):
    c = grid.here()[3]
    h = shard.shape[1] // 2
    other = grid.other_core(lax.dynamic_slice_in_dim(shard, (1 - c) * h, h, 1))
    return both(c == 0, lax.dynamic_slice_in_dim(shard, c * h, h, 1), other, 0)


def spread_z(grid, pair):
    return jnp.stack([pair] + [grid.up(pair, k) for k in range(1, grid.z)])


def with_other(grid, sources):
    return sources + [grid.other_core(s) for s in sources]


def stage(*values):
    return lax.optimization_barrier(values)


def after(value, *earlier):
    return lax.optimization_barrier((value, *earlier))[0]


def add(a, b):
    return (a.astype(F32) + b.astype(F32)).astype(BF)


def pick(v, at, axis):
    return lax.dynamic_index_in_dim(v, at, axis, keepdims=False)


class Sum:
    def __init__(self, grid, sends, keeps):
        self.grid = grid
        at = lax.axis_index(AXES)
        self.tables = [jnp.asarray(t)[at] for t in grid.routes()]
        self.shape = (grid.z, 2, 2)
        self.keeps = keeps
        self.got = [grid.other_core(s) for s in sends]

    def core(self):
        block = lambda v: v.reshape(*self.shape, *v.shape[1:])
        self.away, self.stay = route(
            self.tables[0], [block(k) for k in self.keeps], [block(g) for g in self.got]
        )
        return self.away

    def near(self):
        self.got = self.grid.along(self.away, 0)

    def middle(self):
        self.away, self.stay = route(self.tables[1], [self.stay], [self.got])
        return self.away

    def far(self):
        self.got = self.grid.along(self.away, 1)

    def last(self):
        self.own = add(self.stay, self.got)[0]
        return self.own

    def up(self):
        grid, z = self.grid, self.grid.here()[0]
        self.got = [
            grid.up(pick(self.own, (z + k) % grid.z, 0), k) for k in range(1, grid.z)
        ]
        self.base = pick(self.own, z, 0)

    def rows(self):
        total = self.base.astype(F32)
        for g in self.got:
            total = total + g.astype(F32)
        return total


def own_rows(grid, total):
    c = grid.here()[3]
    r = total.shape[0] // 2
    other = grid.other_core(lax.dynamic_slice_in_dim(total, (1 - c) * r, r, 0))
    return both(c == 0, lax.dynamic_slice_in_dim(total, c * r, r, 0), other, 1)


def to_chunks(pair):
    r = pair.shape[0] // 4
    return jnp.concatenate([pair[j * r : (j + 1) * r] for j in range(4)], 1)


def from_chunks(total):
    w = total.shape[1] // 4
    return jnp.concatenate([total[:, j * w : (j + 1) * w] for j in range(4)], 0)


def gather_small(count, vectors, first):
    rows = [jnp.pad(v, (0, 128 - v.shape[0])) for v in vectors]
    flat, _ = stage(jnp.stack(rows), first)
    return lax.all_to_all(jnp.broadcast_to(flat[:, None], (8, count, 128)), AXES, 1, 1, tiled=True)


def scatter_small(cut):
    return jnp.sum(lax.all_to_all(cut, AXES, 1, 1, tiled=True), axis=1)


def halves_of(weight):
    h = weight.shape[1] // 2
    return [weight[None, :, :h], weight[None, :, h:]]


def local(
    mesh,
    tokens,
    norm1_gain,
    norm1_bias,
    qkv_weight,
    qkv_bias,
    out_weight,
    out_bias,
    norm2_gain,
    norm2_bias,
    fc_weight,
    fc_bias,
    proj_weight,
    proj_bias,
    seq_lengths,
    out_cotangent,
):
    d = tokens.shape[1]
    grid = Grid(mesh, out_weight.shape[0])
    blocks = grid.blocks
    vectors = [norm1_gain, norm1_bias, out_bias, norm2_gain, norm2_bias, proj_bias, qkv_bias, fc_bias]
    if grid.paired:
        place = jnp.asarray(grid.table())[lax.axis_index(AXES)]
        core = grid.here()[3].reshape(1).astype(jnp.int32)
        pair_qkv = pair_rows(grid, qkv_weight)
        fc_shard, out_shard, proj_shard, pair_qkv = stage(fc_weight, out_weight, proj_weight, pair_qkv)
        stack_qkv = spread_z(grid, pair_qkv)
        first = jnp.concatenate([pair_rows(grid, fc_shard), pair_rows(grid, out_shard)], 1)
        second = to_chunks(pair_rows(grid, proj_shard))
        little_all = gather_small(grid.count, vectors, pair_qkv)
        stack_qkv, first, second = stage(stack_qkv, first, second)
        near_qkv, far_qkv = grid.along(stack_qkv, 0), grid.along(stack_qkv, 1)
        near_qkv, far_qkv, first, little_all = stage(near_qkv, far_qkv, first, little_all)
        last_qkv = grid.along(near_qkv, 1)
        stack_first = spread_z(grid, first)
        qkv_sources = with_other(grid, [stack_qkv, near_qkv, far_qkv, last_qkv])
        *qkv_sources, stack_first, second = stage(*qkv_sources, stack_first, second)
        near_first, far_first = grid.along(stack_first, 0), grid.along(stack_first, 1)
        stack_second = spread_z(grid, second)
    else:
        place = jnp.asarray(np.array([[0, 0], [1, 0]], np.int32))
        core = jnp.zeros((1,), jnp.int32)
        full = lambda v: lax.all_gather(v, AXES, axis=0, tiled=True)
        qkv_sources = halves_of(full(qkv_weight))
        little_all = gather_small(grid.count, vectors, tokens)
    gain_one, shift_one, bias_out, gain_two, shift_two, bias_proj, bias_qkv, bias_fc = unfold(little_all, d)
    qkv, low_one, qkv_full = project(
        place, tokens, gain_one, shift_one, bias_qkv, qkv_sources, blocks
    )
    if grid.paired:
        qkv, stack_second = stage(qkv, stack_second)
        near_second, far_second = grid.along(stack_second, 0), grid.along(stack_second, 1)
        others = [grid.other_core(stack_first)]
    attended = [list(attend(seq_lengths, qkv, 4, 0, 512))]
    if grid.paired:
        attended[0][2], qkv, near_first, far_first, *others = stage(
            attended[0][2], qkv, near_first, far_first, *others
        )
        last_first = grid.along(near_first, 1)
        others += [grid.other_core(near_first), grid.other_core(far_first)]
    else:
        fcs = [(s, 0) for s in halves_of(full(fc_weight))]
        outs, out_at = halves_of(full(out_weight)), 0
        projs = [(to_chunks(s[0])[None], 0) for s in halves_of(full(proj_weight))]
    attended.append(attend(seq_lengths, qkv, 2, 4, 512))
    mixed = [a[1] for a in attended]
    if grid.paired:
        mixed[1], near_second, far_second, last_first, *others = stage(
            mixed[1], near_second, far_second, last_first, *others
        )
        last_second = grid.along(near_second, 1)
        outs = [stack_first, near_first, far_first, last_first, *others, grid.other_core(last_first)]
        seconds = with_other(grid, [stack_second, near_second, far_second, last_second])
        fcs, out_at, projs = [(s, 0) for s in outs], 4, [(s, 0) for s in seconds]
    middle, low_two, out_full = mix(
        place, mixed, tokens, bias_out, gain_two, shift_two, outs, blocks, out_at
    )
    (layer_out, grad_middle, grad_branch, fc_send, fc_keep, proj_send, proj_keep, fc_bias_term, sums) = mlp(
        core, place, seq_lengths, middle, low_two, out_cotangent, bias_fc, bias_proj,
        gain_two, fcs, projs, blocks,
    )
    grad_mixed, out_send, out_keep = unmix(core, seq_lengths, grad_branch, mixed, out_full, blocks)
    if grid.paired:
        fc_sum = Sum(grid, [fc_send], [fc_keep])
        proj_sum = Sum(grid, [proj_send, out_send], [proj_keep, out_keep])
        grad_mixed, fc_sum.away, fc_sum.stay = stage(grad_mixed, fc_sum.core(), fc_sum.stay)
        fc_sum.near()
        grad_mixed, proj_sum.away, proj_sum.stay = stage(grad_mixed, proj_sum.core(), proj_sum.stay)
        proj_sum.near()
    grad_one = attend_grad(qkv, grad_mixed, attended[0][0], attended[0][2], 0)
    qkv_one = list(unproject(core, low_one, grad_one, blocks))
    if grid.paired:
        qkv_one[2], fc_sum.got, proj_sum.got, grad_mixed = stage(
            qkv_one[2], fc_sum.got, proj_sum.got, grad_mixed
        )
        fc_sum.middle()
        fc_sum.far()
        proj_sum.middle()
        grad_mixed, fc_sum.stay, proj_sum.away, proj_sum.stay = stage(
            grad_mixed, fc_sum.stay, proj_sum.away, proj_sum.stay
        )
        proj_sum.far()
    grad_two = attend_grad(qkv, grad_mixed, attended[1][0], attended[1][2], 4)
    if grid.paired:
        fc_sum.got, grad_two = stage(fc_sum.got, grad_two)
        fc_sum.last()
        fc_sum.up()
    grads = [grad_one, grad_two]
    qkv_two = unproject(core, low_one, grad_two, blocks)
    if grid.paired:
        qkv_sum = Sum(grid, [qkv_one[0], qkv_two[0]], [qkv_one[1], qkv_two[1]])
        *qkv_sum.got, proj_sum.got = stage(*qkv_sum.got, proj_sum.got)
        grad_middle, qkv_sum.away, qkv_sum.stay = stage(grad_middle, qkv_sum.core(), qkv_sum.stay)
        qkv_sum.near()
        grad_middle, proj_sum.own = stage(grad_middle, proj_sum.last())
        proj_sum.up()
    input_grad, first_sums = final(tokens, grads, qkv_full, grad_middle, gain_one)
    qkv_sums = jnp.concatenate([qkv_one[2], qkv_two[2]], 1)
    cut = fold(first_sums, sums, qkv_sums, fc_bias_term, grid.count)
    if grid.paired:
        cut, qkv_sum.got, proj_sum.got[0], proj_sum.got[2], *fc_sum.got = stage(
            cut, qkv_sum.got, proj_sum.got[0], proj_sum.got[2], *fc_sum.got
        )
        cut, qkv_sum.away, qkv_sum.stay = stage(cut, qkv_sum.middle(), qkv_sum.stay)
        qkv_sum.far()
    little = scatter_small(cut)
    if grid.paired:
        little, qkv_sum.got = stage(little, qkv_sum.got)
        proj_sum.got[1], proj_sum.base, fc_sum.base, qkv_sum.own = stage(
            proj_sum.got[1], proj_sum.base, fc_sum.base, qkv_sum.last()
        )
        qkv_sum.up()
        fc_weight_grad = own_rows(grid, fc_sum.rows())
        total = proj_sum.rows()
        proj_wide = proj_keep.shape[2]
        proj_weight_grad = own_rows(grid, from_chunks(total[:, :proj_wide]))
        out_weight_grad = own_rows(grid, total[:, proj_wide:])
        total = qkv_sum.rows()
        wide = qkv_one[1].shape[2]
        ends = [own_rows(grid, total[:, :wide]), own_rows(grid, total[:, wide:])]
    else:
        reduce = lambda v: lax.psum_scatter(v.astype(F32), AXES, scatter_dimension=0, tiled=True)
        side = lambda k, s: jnp.concatenate([k[0], s[0]], 1)
        fc_weight_grad = reduce(side(fc_keep, fc_send))
        out_weight_grad = reduce(side(out_keep, out_send))
        ends = [reduce(side(u[1], u[0])) for u in (qkv_one, qkv_two)]
        proj_weight_grad = reduce(
            jnp.concatenate([from_chunks(proj_keep[0]), from_chunks(proj_send[0])], 1)
        )
    third = lambda e, i: e[:, i * e.shape[1] // 3 : (i + 1) * e.shape[1] // 3]
    qkv_weight_grad = jnp.concatenate([third(e, i) for i in range(3) for e in ends], 1)
    shard = lambda s: little[s, : vectors[s].shape[0]]
    return (
        layer_out,
        input_grad,
        shard(0),
        shard(1),
        qkv_weight_grad,
        shard(6),
        out_weight_grad,
        shard(2),
        shard(3),
        shard(4),
        fc_weight_grad,
        shard(7),
        proj_weight_grad,
        shard(5),
    )


def solution(mesh):
    matrix, vector = P(AXES, None), P(AXES)
    ins = (
        matrix, vector, vector, matrix, vector, matrix, vector, vector,
        vector, matrix, vector, matrix, vector, vector, matrix,
    )
    outs = (
        matrix, matrix, vector, vector, matrix, vector, matrix, vector,
        vector, vector, matrix, vector, matrix, vector,
    )
    return jax.shard_map(
        functools.partial(local, mesh), mesh=mesh, in_specs=ins, out_specs=outs, check_vma=False
    )
```

```python
import functools
import math

import jax
import jax.numpy as jnp
import numpy as np
from jax import lax
from jax.experimental import pallas as pl
from jax.experimental.pallas import tpu as pltpu
from jax.sharding import PartitionSpec as P

AXES = ("wide", "narrow")
BF, F32 = jnp.bfloat16, jnp.float32
VMEM_CAP = 58 << 20

def params(n=1, cap=VMEM_CAP):
    return pltpu.CompilerParams(dimension_semantics=("arbitrary",) * n, vmem_limit_bytes=cap)

def cost(flops, bytes_accessed, trans=0):
    return pl.CostEstimate(flops=int(flops), bytes_accessed=int(bytes_accessed), transcendentals=int(trans))

def mm(a, b):
    return jnp.dot(a, b, preferred_element_type=F32)

def diagonal_mask(rows, cols):
    key_at = lax.broadcasted_iota(jnp.int32, (rows, cols), 0)
    query_at = lax.broadcasted_iota(jnp.int32, (rows, cols), 1)
    return key_at <= query_at

def attend_kernel(qb, len_ref, qkv_ref, out_t_ref, out_ref, stat_ref, v_t, q_t):
    slot = qkv_ref.shape[1]
    q_t[...] = (qkv_ref[0] * jnp.asarray(0.125, BF)).T
    v_t[...] = qkv_ref[2].T
    half = lax.broadcasted_iota(jnp.int32, (128, 1), 0) < 64
    causal = diagonal_mask(qb, qb)
    length = len_ref[0]
    for i in range(slot // qb):
        cols = slice(i * qb, (i + 1) * qb)
        parts = []
        for head in range(2):
            mine = half if head == 0 else jnp.logical_not(half)
            qh = jnp.where(mine, q_t[:, cols], jnp.zeros((), BF))
            s_low = mm(qkv_ref[1, : i * qb, :], qh) if i else None
            s_dia = jnp.where(causal, mm(qkv_ref[1, cols, :], qh), -1e30)
            top = jnp.max(s_dia, axis=0, keepdims=True)
            if i:
                top = jnp.maximum(top, jnp.max(s_low, axis=0, keepdims=True))
            e_dia = jnp.exp(s_dia - top)
            total = jnp.sum(e_dia, axis=0, keepdims=True)
            vh = v_t[head * 64 : head * 64 + 64, :]
            acc = mm(vh[:, cols], e_dia.astype(BF))
            if i:
                e_low = jnp.exp(s_low - top)
                total = total + jnp.sum(e_low, axis=0, keepdims=True)
                acc = acc + mm(vh[:, : i * qb], e_low.astype(BF))
            stat_ref[0, head : head + 1, cols] = top + jnp.log(total)
            parts.append(acc / total)
        both = jnp.concatenate(parts, axis=0)
        seen = (i * qb + lax.broadcasted_iota(jnp.int32, (1, qb), 1)) < length
        both = jnp.where(seen, both, 0.0)
        out_t_ref[:, cols] = both
        out_ref[cols, :] = both.T.astype(BF)

def attend(lengths, qkv, pairs, first, qb=256):
    slot, width = qkv.shape[1], qkv.shape[2]
    return pl.pallas_call(
        functools.partial(attend_kernel, qb),
        name="attend",
        grid=(pairs,),
        in_specs=[
            pl.BlockSpec(memory_space=pltpu.SMEM),
            pl.BlockSpec((3, slot, 128), lambda j: (0, 0, j + first)),
        ],
        out_specs=[
            pl.BlockSpec((128, slot), lambda j: (j, 0)),
            pl.BlockSpec((slot, 128), lambda j: (0, j)),
            pl.BlockSpec((1, 2, slot), lambda j: (j, 0, 0)),
        ],
        out_shape=[
            jax.ShapeDtypeStruct((pairs * 128, slot), F32),
            jax.ShapeDtypeStruct((slot, pairs * 128), BF),
            jax.ShapeDtypeStruct((pairs, 2, slot), F32),
        ],
        scratch_shapes=[pltpu.VMEM((128, slot), BF), pltpu.VMEM((128, slot), BF)],
        compiler_params=params(),
        cost_estimate=cost(pairs * 2 * slot * slot * 256, 8e6 * pairs / 6, pairs * slot * slot),
    )(lengths, qkv)

def attend_grad_kernel(qb, qkv_ref, grad_ref, out_t_ref, stat_ref, g_ref, q_t, do_t, k_t, qs, dq_t, dk_s, dv_s):
    slot = qkv_ref.shape[1]
    qs[...] = qkv_ref[0] * jnp.asarray(0.125, BF)
    q_t[...] = qs[...].T
    k_t[...] = qkv_ref[1].T
    do_t[...] = grad_ref[...].T
    half = lax.broadcasted_iota(jnp.int32, (128, 1), 0) < 64
    half_lane = lax.broadcasted_iota(jnp.int32, (1, 128), 1) < 64
    causal = diagonal_mask(qb, qb)
    zero = jnp.zeros((), BF)
    prod = do_t[...].astype(F32) * out_t_ref[...]
    delta = [jnp.sum(prod[h * 64 : h * 64 + 64], axis=0, keepdims=True) for h in range(2)]
    for i in range(slot // qb):
        cols = slice(i * qb, (i + 1) * qb)
        end = (i + 1) * qb
        dv_new = dk_new = None
        for head in range(2):
            mine = half if head == 0 else jnp.logical_not(half)
            mine_lane = half_lane if head == 0 else jnp.logical_not(half_lane)
            qh_t = jnp.where(mine, q_t[:, cols], zero)
            doh_t = jnp.where(mine, do_t[:, cols], zero)
            qh = jnp.where(mine_lane, qs[cols, :], zero)
            doh = jnp.where(mine_lane, grad_ref[cols, :], zero)
            stat = stat_ref[0, head : head + 1, cols]
            dl = delta[head][:, cols]
            s = mm(qkv_ref[1, :end, :], qh_t)
            dp = mm(qkv_ref[2, :end, :], doh_t)
            p = jnp.exp(s - stat)
            p_dia = jnp.where(causal, p[i * qb :], 0.0)
            p = jnp.concatenate([p[: i * qb], p_dia], axis=0) if i else p_dia
            ds = (p * (dp - dl)).astype(BF)
            pb = p.astype(BF)
            dv_h = mm(pb, doh)
            dk_h = mm(ds, qh)
            dv_new = dv_h if head == 0 else dv_new + dv_h
            dk_new = dk_h if head == 0 else dk_new + dk_h
            dq_t[head * 64 : head * 64 + 64, cols] = mm(k_t[head * 64 : head * 64 + 64, :end], ds)
        if i:
            dv_s[: i * qb] += dv_new[: i * qb]
            dk_s[: i * qb] += dk_new[: i * qb]
        dv_s[cols] = dv_new[i * qb :]
        dk_s[cols] = dk_new[i * qb :]
    g_ref[0] = (dq_t[...] * 0.125).T.astype(BF)
    g_ref[1] = dk_s[...].astype(BF)
    g_ref[2] = dv_s[...].astype(BF)

def attend_grad(qkv, grad, out_t, stat, first, qb=256):
    slot = qkv.shape[1]
    pairs = out_t.shape[0] // 128
    width = pairs * 128
    return pl.pallas_call(
        functools.partial(attend_grad_kernel, qb),
        name="attend_grad",
        grid=(pairs,),
        in_specs=[
            pl.BlockSpec((3, slot, 128), lambda j: (0, 0, j + first)),
            pl.BlockSpec((slot, 128), lambda j: (0, j + first)),
            pl.BlockSpec((128, slot), lambda j: (j, 0)),
            pl.BlockSpec((1, 2, slot), lambda j: (j, 0, 0)),
        ],
        out_specs=pl.BlockSpec((3, slot, 128), lambda j: (0, 0, j)),
        out_shape=jax.ShapeDtypeStruct((3, slot, width), BF),
        scratch_shapes=[
            pltpu.VMEM((128, slot), BF),
            pltpu.VMEM((128, slot), BF),
            pltpu.VMEM((128, slot), BF),
            pltpu.VMEM((slot, 128), BF),
            pltpu.VMEM((128, slot), F32),
            pltpu.VMEM((slot, 128), F32),
            pltpu.VMEM((slot, 128), F32),
        ],
        compiler_params=params(),
        cost_estimate=cost(pairs * 5 * slot * slot * 256, 16e6 * pairs / 6, pairs * 2 * slot * slot),
    )(qkv, grad, out_t, stat)
VECTOR_ROWS = 16
GAIN_ONE, SHIFT_ONE, BIAS_OUT, GAIN_TWO, SHIFT_TWO, BIAS_PROJ, BIAS_QKV, BIAS_FC = 0, 1, 2, 3, 4, 5, 6, 9
branch_scale = 1.0 / math.sqrt(48.0)
norm_epsilon = 1e-05
WHOLE = dict(pipeline_mode=pl.Buffered(1))

def mm_nt(a, b):
    return lax.dot_general(a, b, (((1,), (1,)), ((), ())), preferred_element_type=F32)

def mm_tn(a, b):
    return lax.dot_general(a, b, (((0,), (0,)), ((), ())), preferred_element_type=F32)

def normalised(v):
    mean = jnp.mean(v, axis=-1, keepdims=True)
    centred = v - mean
    var = jnp.mean(centred * centred, axis=-1, keepdims=True)
    scale = lax.rsqrt(var + norm_epsilon)
    return centred * scale, scale

def norm_pull(n, scale, gain, u):
    ug = u * gain
    a = jnp.mean(ug, axis=-1, keepdims=True)
    b = jnp.mean(ug * n, axis=-1, keepdims=True)
    return (ug - a - n * b) * scale

def row_of(ref, at):
    return ref[at : at + 1, :]

def whole(shape, index=None):
    zeros = (0,) * len(shape)
    return pl.BlockSpec(shape, (lambda *_: index or zeros), **WHOLE)

def assemble(place, sources, target):
    wide = target.shape[2] // 2
    for s, source in enumerate(sources):
        for half in range(2):
            @pl.when(place[s, 0] == half)
            def _():
                for p in range(source.shape[0]):
                    target[place[s, 1 + p], :, half * wide : (half + 1) * wide] = source[p, :, :wide]

def assemble_chunks(place, sources, target):
    wide = sources[0].shape[2] // 4
    for s, source in enumerate(sources):
        for half in range(2):
            @pl.when(place[s, 0] == half)
            def _():
                for p in range(source.shape[0]):
                    for j in range(4):
                        target[place[s, 1 + p], j, :, half * wide : (half + 1) * wide] = source[p, :, j * wide : (j + 1) * wide]

def project_kernel(n_src, place, x_ref, vec_ref, *rest):
    sources, (qkv_ref, low_ref, w_ref) = rest[:n_src], rest[n_src:]
    @pl.when(pl.program_id(0) == 0)
    def _():
        assemble(place, sources, w_ref)
    n, _ = normalised(x_ref[...].astype(F32))
    low = (n * row_of(vec_ref, GAIN_ONE) + row_of(vec_ref, SHIFT_ONE)).astype(BF)
    low_ref[...] = low
    d = low.shape[1]
    for part in range(3):
        w = w_ref[:, :, part * d : (part + 1) * d].reshape(d, d)
        qkv_ref[part] = (mm(low, w) + row_of(vec_ref, BIAS_QKV + part)).astype(BF)

def project(place, x, vec, sources, blocks, rows=256):
    t, d = x.shape
    r, wide = d // blocks, 3 * d // 2
    return pl.pallas_call(
        functools.partial(project_kernel, len(sources)),
        name="project",
        grid_spec=pltpu.PrefetchScalarGridSpec(
            num_scalar_prefetch=1,
            grid=(t // rows,),
            in_specs=[
                pl.BlockSpec((rows, d), lambda i, p: (i, 0)),
                whole(vec.shape),
                *[whole(s.shape) for s in sources],
            ],
            out_specs=[
                pl.BlockSpec((3, rows, d), lambda i, p: (0, i, 0)),
                pl.BlockSpec((rows, d), lambda i, p: (i, 0)),
                whole((blocks, r, 2 * wide)),
            ],
        ),
        out_shape=[
            jax.ShapeDtypeStruct((3, t, d), BF),
            jax.ShapeDtypeStruct((t, d), BF),
            jax.ShapeDtypeStruct((blocks, r, 2 * wide), BF),
        ],
        compiler_params=params(),
        cost_estimate=cost(2 * t * d * 3 * d, 18e6),
    )(place, x, vec, *sources)

def mix_kernel(n_src, place, x_ref, vec_ref, *rest):
    sources, parts, (mid_ref, low_ref, w_ref) = rest[:n_src], rest[n_src:-3], rest[-3:]
    @pl.when(pl.program_id(0) == 0)
    def _():
        assemble(place, sources, w_ref)
    d = x_ref.shape[1]
    w = w_ref[...].reshape(d, d)
    mid = x_ref[...].astype(F32) + branch_scale * (mm(jnp.concatenate([p[...] for p in parts], 1), w) + row_of(vec_ref, BIAS_OUT))
    mid_ref[...] = mid
    n, _ = normalised(mid)
    low_ref[...] = (n * row_of(vec_ref, GAIN_TWO) + row_of(vec_ref, SHIFT_TWO)).astype(BF)

def mix(place, parts, x, vec, sources, blocks, column, rows=256):
    t, d = x.shape
    r, np_ = d // blocks, sources[0].shape[0]
    return pl.pallas_call(
        functools.partial(mix_kernel, len(sources)),
        name="mix",
        grid_spec=pltpu.PrefetchScalarGridSpec(
            num_scalar_prefetch=1,
            grid=(t // rows,),
            in_specs=[
                pl.BlockSpec((rows, d), lambda i, p: (i, 0)),
                whole(vec.shape),
                *[whole((np_, r, d // 2), (0, 0, column)) for s in sources],
                *[pl.BlockSpec((rows, p.shape[1]), lambda i, p: (i, 0)) for p in parts],
            ],
            out_specs=[
                pl.BlockSpec((rows, d), lambda i, p: (i, 0)),
                pl.BlockSpec((rows, d), lambda i, p: (i, 0)),
                whole((blocks, r, d)),
            ],
        ),
        out_shape=[
            jax.ShapeDtypeStruct((t, d), F32),
            jax.ShapeDtypeStruct((t, d), BF),
            jax.ShapeDtypeStruct((blocks, r, d), BF),
        ],
        compiler_params=params(),
        cost_estimate=cost(2 * t * d * d, 9e6),
    )(place, x, vec, *sources, *parts)

def mlp_kernel(n_src, blocks, rb, core, place, lens, mid_ref, low_ref, cot_ref, bias_ref, *rest):
    fcs, projs, rest = rest[:n_src], rest[n_src : 2 * n_src], rest[2 * n_src :]
    (out_ref, gmid_ref, gbr_ref, fsend_ref, fkeep_ref, psend_ref, pkeep_ref, fbg_ref, vec_ref,
     fc_s, proj_s, low_t, g2_s, second_s, gh_s, act_s, gpre_s) = rest
    t, d = mid_ref.shape
    r = d // blocks
    step = pl.program_id(0)
    mine = core[0]
    chunk = lax.rem(step + 2 * (1 - mine), 4)
    def valid_rows(at):
        return (at * rb + lax.broadcasted_iota(jnp.int32, (rb, 1), 0)) < lens[0]
    @pl.when(step == 0)
    def _():
        assemble(place, fcs, fc_s)
        assemble_chunks(place, projs, proj_s)
        low_t[...] = low_ref[...].T
        def begin(i, total):
            at = pl.ds(pl.multiple_of(i * rb, rb), rb)
            g = jnp.where(valid_rows(i), branch_scale * cot_ref[at, :].astype(F32), 0.0).astype(BF)
            g2_s[at, :] = g
            second_s[at, :] = jnp.zeros((rb, d), F32)
            gh_s[at, :] = jnp.zeros((rb, d), F32)
            return total + jnp.sum(g.astype(F32), axis=0, keepdims=True)
        vec_ref[0:1] = lax.fori_loop(0, t // rb, begin, jnp.zeros((1, d), F32))
    fcol = pl.ds(pl.multiple_of(chunk * d, d), d)
    fc = fc_s.at[:, :, fcol]
    bias = bias_ref[pl.ds(BIAS_FC + chunk, 1), :]
    if blocks % 4 == 0:
        per = blocks // 4
        proj = proj_s.at[pl.ds(chunk * per, per)]
    else:
        proj = proj_s.at[:, pl.ds(chunk, 1)]
    def rows_step(i, total):
        at = pl.ds(pl.multiple_of(i * rb, rb), rb)
        u = mm(low_ref[at, :], fc[...].reshape(d, d)) + bias
        sq = u * u
        th = jnp.tanh(0.7978845608028654 * u * (1.0 + 0.044715 * sq))
        up = 0.5 * (1.0 + th)
        act = (u * up).astype(BF)
        act_s[at, :] = act
        slope = up + u * (0.5 * 0.7978845608028654) * (1.0 - th * th) * (1.0 + 3 * 0.044715 * sq)
        w = proj[...].reshape(d, d)
        second_s[at, :] += mm(act, w)
        gp = mm_nt(g2_s[at, :], w) * slope
        gpb = gp.astype(BF)
        gpre_s[at, :] = gpb
        gh_s[at, :] += mm_nt(gpb, fc[...].reshape(d, d))
        return total + jnp.sum(gpb.astype(F32), axis=0, keepdims=True)
    fbg_ref[pl.ds(chunk, 1), :] = lax.fori_loop(0, t // rb, rows_step, jnp.zeros((1, d), F32))
    dfc = mm(low_t[...], gpre_s[...]).astype(BF).reshape(blocks, r, d)
    @pl.when(step < 2)
    def _():
        fsend_ref[...] = dfc
    @pl.when(step >= 2)
    def _():
        fkeep_ref[...] = dfc
    dproj = mm_tn(act_s[...], g2_s[...]).astype(BF)
    h = d // 2
    for half in range(2):
        @pl.when(mine == half)
        def _():
            for ref, cols in ((pkeep_ref, half), (psend_ref, 1 - half)):
                piece = dproj[:, cols * h : (cols + 1) * h]
                if blocks % 4 == 0:
                    for b in range(blocks // 4):
                        for j in range(4):
                            ref[b, :, j * h : (j + 1) * h] = piece[(b * 4 + j) * r : (b * 4 + j + 1) * r]
                else:
                    ref[0] = piece
    @pl.when(step == 3)
    def _():
        def finish(i, carry):
            at = pl.ds(pl.multiple_of(i * rb, rb), rb)
            mid = mid_ref[at, :]
            out_ref[at, :] = (mid + branch_scale * (second_s[at, :] + row_of(bias_ref, BIAS_PROJ))).astype(BF)
            n, scale = normalised(mid)
            gh = gh_s[at, :]
            cot = jnp.where(valid_rows(i), cot_ref[at, :].astype(F32), 0.0)
            gm = cot + norm_pull(n, scale, row_of(bias_ref, GAIN_TWO), gh)
            gmid_ref[at, :] = gm
            gb = (branch_scale * gm).astype(BF)
            gbr_ref[at, :] = gb
            return (carry[0] + jnp.sum(gh * n, axis=0, keepdims=True),
                    carry[1] + jnp.sum(gh, axis=0, keepdims=True),
                    carry[2] + jnp.sum(gb.astype(F32), axis=0, keepdims=True))
        zero = jnp.zeros((1, d), F32)
        a, b, c = lax.fori_loop(0, t // rb, finish, (zero, zero, zero))
        vec_ref[1:2] = a
        vec_ref[2:3] = b
        vec_ref[3:4] = c

def mlp(core, place, lens, mid, low, cot, vec, fcs, projs, blocks, rb=256):
    t, d = mid.shape
    r, np_ = d // blocks, fcs[0][0].shape[0]
    smem = pl.BlockSpec(memory_space=pltpu.SMEM)
    if blocks % 4 == 0:
        pspec = pl.BlockSpec((blocks // 4, r, 2 * d), lambda i, c: (lax.rem(i + 2 * (1 - c[0]), 4), 0, 0))
    else:
        pspec = pl.BlockSpec((1, r, d // 2), lambda i, c: (0, 0, lax.rem(i + 2 * (1 - c[0]), 4)))
    big = jax.ShapeDtypeStruct((blocks, r, 2 * d), BF)
    return pl.pallas_call(
        functools.partial(mlp_kernel, len(fcs), blocks, rb),
        name="mlp",
        grid_spec=pltpu.PrefetchScalarGridSpec(
            num_scalar_prefetch=1,
            grid=(4,),
            in_specs=[
                smem, smem, whole((t, d)), whole((t, d)), whole((t, d)), whole(vec.shape),
                *[whole((np_, r, 2 * d), (0, 0, at)) for _, at in fcs],
                *[whole((np_, r, 2 * d), (0, 0, at)) for _, at in projs],
            ],
            out_specs=[
                whole((t, d)), whole((t, d)), whole((t, d)),
                pl.BlockSpec((blocks, r, d), lambda i, c: (0, 0, jnp.minimum(i, 1))),
                pl.BlockSpec((blocks, r, d), lambda i, c: (0, 0, jnp.maximum(i - 2, 0))),
                pspec, pspec,
                whole((4, d)), whole((4, d)),
            ],
            scratch_shapes=[
                pltpu.VMEM((blocks, r, 4 * d), BF),
                pltpu.VMEM((blocks, 4, r, d), BF),
                pltpu.VMEM((d, t), BF),
                pltpu.VMEM((t, d), BF),
                pltpu.VMEM((t, d), F32),
                pltpu.VMEM((t, d), F32),
                pltpu.VMEM((t, d), BF),
                pltpu.VMEM((t, d), BF),
            ],
        ),
        out_shape=[
            jax.ShapeDtypeStruct((t, d), BF), jax.ShapeDtypeStruct((t, d), F32), jax.ShapeDtypeStruct((t, d), BF),
            big, big, big, big,
            jax.ShapeDtypeStruct((4, d), F32), jax.ShapeDtypeStruct((4, d), F32),
        ],
        compiler_params=params(),
        cost_estimate=cost(12 * t * d * 4 * d, 40e6, t * 4 * d),
    )(core, place, lens, mid, low, cot, vec, *[a for a, _ in fcs], *[a for a, _ in projs])

def unmix_kernel(core, lens, gbr_ref, w_ref, *rest):
    parts, (ga_ref, send_ref, keep_ref) = rest[:-3], rest[-3:]
    t, d = gbr_ref.shape
    w = w_ref[...].reshape(d, d)
    seen = lax.broadcasted_iota(jnp.int32, (t, 1), 0) < lens[0]
    ga_ref[...] = jnp.where(seen, mm_nt(gbr_ref[...], w), 0.0).astype(BF)
    dw = jnp.concatenate([mm_tn(p[...], gbr_ref[...]).astype(BF) for p in parts], 0)
    h = d // 2
    for half in range(2):
        @pl.when(core[0] == half)
        def _():
            keep_ref[...] = dw[:, half * h : (half + 1) * h].reshape(keep_ref.shape)
            send_ref[...] = dw[:, (1 - half) * h : (2 - half) * h].reshape(send_ref.shape)

def unmix(core, lens, gbr, parts, w, blocks):
    t, d = gbr.shape
    smem = pl.BlockSpec(memory_space=pltpu.SMEM)
    piece = jax.ShapeDtypeStruct((blocks, d // blocks, d // 2), BF)
    return pl.pallas_call(
        unmix_kernel,
        name="unmix",
        in_specs=[smem, smem] + [pl.BlockSpec(memory_space=pltpu.VMEM)] * (2 + len(parts)),
        out_shape=[jax.ShapeDtypeStruct((t, d), BF), piece, piece],
        compiler_params=params(0),
        cost_estimate=cost(4 * t * d * d, 9e6),
    )(core, lens, gbr, w, *parts)

def unproject_kernel(blocks, core, low_ref, g_ref, send_ref, keep_ref, sums_ref):
    d, w = low_ref.shape[1], g_ref.shape[2]
    r, h = d // blocks, w // 2
    low_t = low_ref[...].T
    q, k, v = [mm(low_t, g_ref[part]).astype(BF).reshape(blocks, r, w) for part in range(3)]
    for half, refs in ((0, (keep_ref, send_ref)), (1, (send_ref, keep_ref))):
        @pl.when(core[0] == half)
        def _():
            refs[0][:, :, :w] = q
            refs[0][:, :, w:] = k[:, :, :h]
            refs[1][:, :, :h] = k[:, :, h:]
            refs[1][:, :, h:] = v
    for part in range(3):
        sums_ref[part : part + 1] = jnp.sum(g_ref[part].astype(F32), axis=0, keepdims=True)

def unproject(core, low, g, blocks):
    t, d = low.shape
    w = g.shape[2]
    piece = jax.ShapeDtypeStruct((blocks, d // blocks, w // 2 * 3), BF)
    return pl.pallas_call(
        functools.partial(unproject_kernel, blocks),
        name="unproject",
        in_specs=[pl.BlockSpec(memory_space=pltpu.SMEM)] + [pl.BlockSpec(memory_space=pltpu.VMEM)] * 2,
        out_shape=[piece, piece, jax.ShapeDtypeStruct((3, w), F32)],
        compiler_params=params(0),
        cost_estimate=cost(6 * t * d * w, 10e6 * w / d),
    )(core, low, g)

def route_kernel(count, steps, table, *refs):
    keeps, gots, (away_ref, stay_ref) = refs[:count], refs[count : 2 * count], refs[2 * count :]
    def write(ref):
        at = 0
        for k, g in zip(keeps, gots):
            w = k.shape[-1]
            total = (k[...].astype(F32) + g[...].astype(F32)).astype(BF)
            ref[..., at : at + w] = total.reshape(ref.shape[:-1] + (w,))
            at += w
    @pl.when(pl.program_id(0) < steps)
    def _():
        write(away_ref)
    @pl.when(pl.program_id(0) >= steps)
    def _():
        write(stay_ref)

def route(table, keeps, gots):
    shape = keeps[0].shape
    z, r = (shape[0], shape[3]) if len(shape) == 5 else (shape[1], shape[2])
    steps = 2 if len(shape) == 5 else 1
    wide = sum(k.shape[-1] for k in keeps)
    def spec(w):
        if len(shape) == 5:
            return pl.BlockSpec((z, 1, 1, r, w), lambda i, t: (0, t[i, 0], t[i, 1], 0, 0))
        return pl.BlockSpec((1, z, r, w), lambda i, t: (t[i, 0], 0, 0, 0))
    out = jax.ShapeDtypeStruct((steps, z, r, wide), BF)
    return pl.pallas_call(
        functools.partial(route_kernel, len(keeps), steps),
        name="route",
        grid_spec=pltpu.PrefetchScalarGridSpec(
            num_scalar_prefetch=1,
            grid=(2 * steps,),
            in_specs=[spec(k.shape[-1]) for k in keeps] * 2,
            out_specs=[
                pl.BlockSpec((1, z, r, wide), lambda i, t: (jnp.minimum(i, steps - 1), 0, 0, 0)),
                pl.BlockSpec((1, z, r, wide), lambda i, t: (jnp.maximum(i - steps, 0), 0, 0, 0)),
            ],
        ),
        out_shape=[out, out],
        compiler_params=params(1, 24 << 20),
        cost_estimate=cost(1e6, steps * 2 * z * r * wide * 6),
    )(table, *keeps, *gots)

def final_kernel(x_ref, w_ref, gmid_ref, bias_ref, *rest):
    parts, (out_ref, vec_ref) = rest[:-2], rest[-2:]
    d = x_ref.shape[1]
    w = w_ref[...].reshape(d, 3 * d)
    gh = jnp.zeros(x_ref.shape, F32)
    at = 0
    for g in parts:
        for i in range(3):
            gh = gh + mm_nt(g[i], w[:, i * d + at : i * d + at + g.shape[2]])
        at += g.shape[2]
    n, scale = normalised(x_ref[...].astype(F32))
    out_ref[...] = (gmid_ref[...] + norm_pull(n, scale, row_of(bias_ref, GAIN_ONE), gh)).astype(BF)
    @pl.when(pl.program_id(0) == 0)
    def _():
        vec_ref[...] = jnp.zeros_like(vec_ref)
    vec_ref[0:1] += jnp.sum(gh * n, axis=0, keepdims=True)
    vec_ref[1:2] += jnp.sum(gh, axis=0, keepdims=True)

def final(x, parts, w, gmid, vec, rows=256):
    t, d = x.shape
    return pl.pallas_call(
        final_kernel,
        name="final",
        grid=(t // rows,),
        in_specs=[
            pl.BlockSpec((rows, d), lambda i: (i, 0)),
            whole(w.shape),
            pl.BlockSpec((rows, d), lambda i: (i, 0)),
            whole(vec.shape),
            *[pl.BlockSpec((3, rows, g.shape[2]), lambda i: (0, i, 0)) for g in parts],
        ],
        out_specs=[pl.BlockSpec((rows, d), lambda i: (i, 0)), whole((2, d))],
        out_shape=[jax.ShapeDtypeStruct((t, d), BF), jax.ShapeDtypeStruct((2, d), F32)],
        compiler_params=params(),
        cost_estimate=cost(6 * t * d * d, 15e6),
    )(x, w, gmid, vec, *parts)
def spread_matrix(size, width):
    row = lax.broadcasted_iota(jnp.int32, (128, width), 0).astype(F32)
    col = lax.broadcasted_iota(jnp.int32, (128, width), 1).astype(F32)
    inside = col - jnp.floor((col + 0.5) / size) * size
    return jnp.where(inside == row, 1.0, 0.0)

def own_columns(count, size, per, width):
    at = lax.broadcasted_iota(jnp.int32, (count, width), 0).astype(F32)
    at = at - jnp.floor((at + 0.5) / per) * per
    col = lax.broadcasted_iota(jnp.int32, (count, width), 1).astype(F32)
    return jnp.logical_and(col >= at * size, col < (at + 1) * size)


def unfold_vectors(rows_of, count, out_ref):
    d = out_ref.shape[1]
    out_ref[...] = jnp.zeros_like(out_ref)
    for rows, slots, first in ((1, range(6), 0), (2, (6,), BIAS_QKV), (4, (7,), BIAS_FC)):
        size, per = d * rows // count, count // rows
        spread = spread_matrix(size, d).astype(BF)
        mine = own_columns(count, size, per, d)
        for s in slots:
            got = jnp.where(mine, mm(rows_of(s), spread), 0.0)
            for r in range(rows):
                to = first + (s if rows == 1 else 2 * r if rows == 2 else r)
                out_ref[to : to + 1] = jnp.sum(got[r * per : (r + 1) * per], axis=0, keepdims=True)

def unfold_kernel(x_ref, out_ref):
    unfold_vectors(lambda s: x_ref[s], x_ref.shape[1], out_ref)

def unfold(x, d):
    return pl.pallas_call(
        unfold_kernel,
        name="unfold",
        in_specs=[pl.BlockSpec(memory_space=pltpu.VMEM)],
        out_shape=jax.ShapeDtypeStruct((VECTOR_ROWS, d), F32),
        compiler_params=params(0, 16 << 20),
        cost_estimate=cost(1e8, 1e6),
    )(x)

def unfold_pieces_kernel(n_src, place, *rest):
    sources, out_ref, x_ref = rest[:n_src], rest[n_src], rest[-1]
    r = sources[0].shape[1] // 2
    for s, source in enumerate(sources):
        for p in range(source.shape[0]):
            tile = source[p].astype(F32)
            for c in range(2):
                x_ref[2 * place[s, 1 + p] + c] = tile[c * r : c * r + 8]
    unfold_vectors(lambda s: x_ref[:, s, :].astype(BF), x_ref.shape[0], out_ref)

def unfold_pieces(place, sources, count, d):
    np_, r, wide = sources[0].shape
    return pl.pallas_call(
        functools.partial(unfold_pieces_kernel, len(sources)),
        name="unfold",
        grid_spec=pltpu.PrefetchScalarGridSpec(
            num_scalar_prefetch=1,
            grid=(1,),
            in_specs=[whole((np_, r, 128), (0, 0, wide // 128 - 1)) for _ in sources],
            out_specs=whole((VECTOR_ROWS, d)),
            scratch_shapes=[pltpu.VMEM((count, 8, 128), F32)],
        ),
        out_shape=jax.ShapeDtypeStruct((VECTOR_ROWS, d), F32),
        compiler_params=params(1, 16 << 20),
        cost_estimate=cost(1e8, 1e6),
    )(place, *sources)

def fold_kernel(first_ref, sums_ref, qkv_ref, fc_ref, out_ref):
    count, d = out_ref.shape[1], first_ref.shape[1]
    singles = [
        first_ref[0:1], first_ref[1:2], sums_ref[3:4], sums_ref[1:2], sums_ref[2:3], sums_ref[0:1],
    ]
    pairs = [[v] for v in singles] + [[qkv_ref[0:1], qkv_ref[2:3]], [fc_ref[r : r + 1] for r in range(4)]]
    for rows, slots in ((1, range(6)), (2, (6,)), (4, (7,))):
        size, per = d * rows // count, count // rows
        spread = spread_matrix(size, d)
        mine = own_columns(count, size, per, d)
        full = jnp.concatenate(
            [
                jnp.where(mine, jnp.concatenate([jnp.broadcast_to(v, (per, d)) for v in pairs[s]], 0), 0.0)
                for s in slots
            ],
            0,
        )
        got = lax.dot_general(
            full, spread, (((1,), (1,)), ((), ())), precision=lax.Precision.HIGHEST, preferred_element_type=F32
        )
        for i, s in enumerate(slots):
            out_ref[s] = got[i * count : (i + 1) * count]

def fold(first, sums, qkv, fc, count):
    return pl.pallas_call(
        fold_kernel,
        name="fold",
        in_specs=[pl.BlockSpec(memory_space=pltpu.VMEM)] * 4,
        out_shape=jax.ShapeDtypeStruct((8, count, 128), F32),
        compiler_params=params(0, 32 << 20),
        cost_estimate=cost(1e8, 1e6),
    )(first, sums, qkv, fc)


class Grid:
    order = (0, 2, 1, 3)

    def __init__(self, mesh, rows):
        wide, narrow = mesh.shape["wide"], mesh.shape["narrow"]
        self.count = wide * narrow
        self.paired = narrow == 4 and wide == 8 and rows % 8 == 0
        self.blocks = self.count // 2 if self.paired else 1
        self.z = wide // 2

    def index(self, z, x, y, c):
        return ((z * 2 + x) * 2 + y) * 2 + c

    def places(self):
        return [
            (z, x, y, c) for z in range(self.z) for x in range(2) for y in range(2) for c in range(2)
        ]

    def perm(self, target):
        return [(self.index(*at), self.index(*target(*at))) for at in self.places()]

    def here(self):
        w, n = lax.axis_index("wide"), lax.axis_index("narrow")
        return w // 2, w % 2, n // 2, n % 2

    def table(self):
        rows = []
        for z0, x0, y0, c0 in self.places():
            mine = []
            for half in (c0, 1 - c0):
                for ka, kb in ((0, 0), (1, 0), (0, 1), (1, 1)):
                    kx, ky = (ka, kb) if half == 0 else (kb, ka)
                    blocks = [
                        ((z0 ^ kz) * 2 + (x0 ^ kx)) * 2 + (y0 ^ ky) for kz in self.order
                    ]
                    mine.append([half] + blocks)
            rows.append(mine)
        return np.array(rows, np.int32)

    def routes(self):
        near, far = [], []
        for z0, x0, y0, c0 in self.places():
            if c0 == 0:
                near.append([[1 - x0, 0], [1 - x0, 1], [x0, 0], [x0, 1]])
                far.append([[1 - y0], [y0]])
            else:
                near.append([[0, 1 - y0], [1, 1 - y0], [0, y0], [1, y0]])
                far.append([[1 - x0], [x0]])
        return np.array(near, np.int32), np.array(far, np.int32)

    def send(self, value, target):
        return lax.ppermute(value, AXES, self.perm(target))

    def other_core(self, value):
        return self.send(value, lambda z, x, y, c: (z, x, y, 1 - c))

    def along(self, value, turn):
        return self.send(
            value,
            lambda z, x, y, c: (z, 1 - x, y, c) if c == turn else (z, x, 1 - y, c),
        )

    def up(self, value, k):
        return self.send(value, lambda z, x, y, c: (z ^ k, x, y, c))


def both(first, own, other, axis):
    return jnp.where(
        first, jnp.concatenate([own, other], axis), jnp.concatenate([other, own], axis)
    )


def pair_rows(grid, shard, extra=None):
    c = grid.here()[3]
    h = shard.shape[1] // 2
    mine = lax.dynamic_slice_in_dim(shard, c * h, h, 1)
    away = lax.dynamic_slice_in_dim(shard, (1 - c) * h, h, 1)
    if extra is not None:
        mine, away = jnp.concatenate([mine, extra], 1), jnp.concatenate([away, extra], 1)
    return both(c == 0, mine, grid.other_core(away), 0)


def spread_z(grid, pair):
    return jnp.stack([pair] + [grid.up(pair, k) for k in grid.order[1:]])


def with_other(grid, sources):
    return sources + [grid.other_core(s) for s in sources]


def stage(*values):
    return lax.optimization_barrier(values)


def after(value, *earlier):
    return lax.optimization_barrier((value, *earlier))[0]


def add(a, b):
    return (a.astype(F32) + b.astype(F32)).astype(BF)


def pick(v, at, axis):
    return lax.dynamic_index_in_dim(v, at, axis, keepdims=False)


class Sum:
    def __init__(self, grid, sends, keeps):
        self.grid = grid
        at = lax.axis_index(AXES)
        self.tables = [jnp.asarray(t)[at] for t in grid.routes()]
        self.shape = (grid.z, 2, 2)
        self.keeps = keeps
        self.got = [grid.other_core(s) for s in sends]

    def core(self):
        block = lambda v: v.reshape(*self.shape, *v.shape[1:])
        self.away, self.stay = route(
            self.tables[0], [block(k) for k in self.keeps], [block(g) for g in self.got]
        )
        return self.away

    def near(self):
        self.got = self.grid.along(self.away, 0)

    def middle(self):
        self.away, self.stay = route(self.tables[1], [self.stay], [self.got])
        return self.away

    def far(self):
        self.got = self.grid.along(self.away, 1)

    def last(self):
        self.own = add(self.stay, self.got)[0]
        return self.own

    def up(self):
        z = self.grid.here()[0]
        away = jnp.stack([pick(self.own, z ^ 1, 0), pick(self.own, z ^ 3, 0)])
        self.stay = jnp.stack([pick(self.own, z, 0), pick(self.own, z ^ 2, 0)])
        self.got = self.grid.up(away, 1)

    def across(self):
        self.stay = add(self.stay, self.got)
        self.got = self.grid.up(self.stay[1], 2)

    def rows(self):
        return self.stay[0].astype(F32) + self.got.astype(F32)


def own_rows(grid, total):
    c = grid.here()[3]
    r = total.shape[0] // 2
    other = grid.other_core(lax.dynamic_slice_in_dim(total, (1 - c) * r, r, 0))
    return both(c == 0, lax.dynamic_slice_in_dim(total, c * r, r, 0), other, 1)


def to_chunks(pair):
    r = pair.shape[0] // 4
    return jnp.concatenate([pair[j * r : (j + 1) * r] for j in range(4)], 1)


def from_chunks(total):
    w = total.shape[1] // 4
    return jnp.concatenate([total[:, j * w : (j + 1) * w] for j in range(4)], 0)


def stack_small(vectors):
    total = jnp.zeros((8, 128), BF)
    for i, v in enumerate(vectors):
        total = total + jnp.pad(v.reshape(1, -1), ((i, 7 - i), (0, 128 - v.shape[0])))
    return total


def gather_small(count, vectors):
    flat = stack_small(vectors)
    return lax.all_to_all(jnp.broadcast_to(flat[:, None], (8, count, 128)), AXES, 1, 1, tiled=True)


def scatter_small(cut):
    return jnp.sum(lax.all_to_all(cut, AXES, 1, 1, tiled=True), axis=1)


def halves_of(weight):
    h = weight.shape[1] // 2
    return [weight[None, :, :h], weight[None, :, h:]]


def local(
    mesh,
    tokens,
    norm1_gain,
    norm1_bias,
    qkv_weight,
    qkv_bias,
    out_weight,
    out_bias,
    norm2_gain,
    norm2_bias,
    fc_weight,
    fc_bias,
    proj_weight,
    proj_bias,
    seq_lengths,
    out_cotangent,
):
    d = tokens.shape[1]
    grid = Grid(mesh, out_weight.shape[0])
    blocks = grid.blocks
    vectors = [norm1_gain, norm1_bias, out_bias, norm2_gain, norm2_bias, proj_bias, qkv_bias, fc_bias]
    if grid.paired:
        place = jnp.asarray(grid.table())[lax.axis_index(AXES)]
        core = grid.here()[3].reshape(1).astype(jnp.int32)
        extra = jnp.pad(stack_small(vectors), ((0, qkv_weight.shape[0] - 8), (0, 0)))
        pair_qkv = pair_rows(grid, qkv_weight, extra)
        place, fc_shard, out_shard, proj_shard, pair_qkv = stage(
            place, fc_weight, out_weight, proj_weight, pair_qkv
        )
        stack_qkv = spread_z(grid, pair_qkv)
        first = jnp.concatenate([pair_rows(grid, fc_shard), pair_rows(grid, out_shard)], 1)
        second = to_chunks(pair_rows(grid, proj_shard))
        stack_qkv, first, second = stage(stack_qkv, first, second)
        near_qkv, far_qkv = grid.along(stack_qkv, 0), grid.along(stack_qkv, 1)
        two_first = grid.up(first, 2)
        others = [grid.other_core(stack_qkv)]
        near_qkv, far_qkv, two_first, *others = stage(near_qkv, far_qkv, two_first, *others)
        last_qkv = grid.along(near_qkv, 1)
        two_first = jnp.stack([first, two_first])
        four_first = grid.up(two_first, 1)
        two_second = grid.up(second, 2)
        others += [grid.other_core(v) for v in (near_qkv, far_qkv)]
        last_qkv, two_second, two_first, four_first, *others = stage(
            last_qkv, two_second, two_first, four_first, *others
        )
        qkv_sources = [stack_qkv, near_qkv, far_qkv, last_qkv, *others, grid.other_core(last_qkv)]
        stack_first = jnp.concatenate([two_first, four_first])
        near_first, far_first = grid.along(stack_first, 0), grid.along(stack_first, 1)
        two_second = jnp.stack([second, two_second])
        four_second = grid.up(two_second, 1)
        others = [grid.other_core(stack_first)]
        *qkv_sources, stack_first = stage(*qkv_sources, stack_first)
        vec = unfold_pieces(place, qkv_sources[:4], grid.count, d)
    else:
        place = jnp.asarray(np.array([[0, 0], [1, 0]], np.int32))
        core = jnp.zeros((1,), jnp.int32)
        full = lambda v: lax.all_gather(v, AXES, axis=0, tiled=True)
        qkv_sources = halves_of(full(qkv_weight))
        vec = unfold(gather_small(grid.count, vectors), d)
    qkv, low_one, qkv_full = project(
        place, tokens, vec, qkv_sources, blocks
    )
    if grid.paired:
        qkv, two_second, four_second, near_first, far_first, *others = stage(
            qkv, two_second, four_second, near_first, far_first, *others
        )
        stack_second = jnp.concatenate([two_second, four_second])
        last_first = grid.along(near_first, 1)
        near_second, far_second = grid.along(stack_second, 0), grid.along(stack_second, 1)
        others += [grid.other_core(near_first), grid.other_core(far_first)]
    attended = [list(attend(seq_lengths, qkv, 4, 0, 512))]
    if grid.paired:
        attended[0][2], qkv, *others = stage(attended[0][2], qkv, *others)
        second_others = [grid.other_core(stack_second)]
    else:
        fcs = [(s, 0) for s in halves_of(full(fc_weight))]
        outs, out_at = halves_of(full(out_weight)), 0
        projs = [(to_chunks(s[0])[None], 0) for s in halves_of(full(proj_weight))]
    attended.append(attend(seq_lengths, qkv, 2, 4, 512))
    mixed = [a[1] for a in attended]
    if grid.paired:
        mixed[1], near_second, far_second, last_first, *second_others = stage(
            mixed[1], near_second, far_second, last_first, *second_others
        )
        last_second = grid.along(near_second, 1)
        outs = [stack_first, near_first, far_first, last_first, *others, grid.other_core(last_first)]
        second_others += [grid.other_core(near_second), grid.other_core(far_second)]
        fcs, out_at = [(s, 0) for s in outs], 4
    middle, low_two, out_full = mix(
        place, mixed, tokens, vec, outs, blocks, out_at
    )
    if grid.paired:
        low_two, last_second = stage(low_two, last_second)
        second_others.append(grid.other_core(last_second))
        projs = [(s, 0) for s in (stack_second, near_second, far_second, last_second, *second_others)]
    (layer_out, grad_middle, grad_branch, fc_send, fc_keep, proj_send, proj_keep, fc_bias_term, sums) = mlp(
        core, place, seq_lengths, middle, low_two, out_cotangent, vec,
        fcs, projs, blocks,
    )
    grad_mixed, out_send, out_keep = unmix(core, seq_lengths, grad_branch, mixed, out_full, blocks)
    if grid.paired:
        fc_sum = Sum(grid, [fc_send], [fc_keep])
        proj_sum = Sum(grid, [proj_send, out_send], [proj_keep, out_keep])
        grad_mixed, fc_sum.away, fc_sum.stay = stage(grad_mixed, fc_sum.core(), fc_sum.stay)
        fc_sum.near()
        grad_mixed, proj_sum.away, proj_sum.stay = stage(grad_mixed, proj_sum.core(), proj_sum.stay)
        proj_sum.near()
    grad_one = attend_grad(qkv, grad_mixed, attended[0][0], attended[0][2], 0)
    qkv_one = list(unproject(core, low_one, grad_one, blocks))
    if grid.paired:
        qkv_one[2], fc_sum.got, proj_sum.got, grad_mixed = stage(
            qkv_one[2], fc_sum.got, proj_sum.got, grad_mixed
        )
        fc_sum.middle()
        fc_sum.far()
        proj_sum.middle()
        grad_mixed, fc_sum.stay, proj_sum.away, proj_sum.stay = stage(
            grad_mixed, fc_sum.stay, proj_sum.away, proj_sum.stay
        )
        proj_sum.far()
    grad_two = attend_grad(qkv, grad_mixed, attended[1][0], attended[1][2], 4)
    if grid.paired:
        fc_sum.got, grad_two = stage(fc_sum.got, grad_two)
        fc_sum.last()
        fc_sum.up()
    grads = [grad_one, grad_two]
    qkv_two = unproject(core, low_one, grad_two, blocks)
    if grid.paired:
        qkv_sum = Sum(grid, [qkv_one[0], qkv_two[0]], [qkv_one[1], qkv_two[1]])
        *qkv_sum.got, proj_sum.got = stage(*qkv_sum.got, proj_sum.got)
        grad_middle, qkv_sum.away, qkv_sum.stay = stage(grad_middle, qkv_sum.core(), qkv_sum.stay)
        qkv_sum.near()
        grad_middle, proj_sum.own = stage(grad_middle, proj_sum.last())
        proj_sum.up()
    input_grad, first_sums = final(tokens, grads, qkv_full, grad_middle, vec)
    qkv_sums = jnp.concatenate([qkv_one[2], qkv_two[2]], 1)
    cut = fold(first_sums, sums, qkv_sums, fc_bias_term, grid.count)
    if grid.paired:
        cut, qkv_sum.got, proj_sum.got, fc_sum.got = stage(cut, qkv_sum.got, proj_sum.got, fc_sum.got)
        qkv_sum.middle()
        qkv_sum.far()
        fc_sum.across()
        proj_sum.across()
        cut, qkv_sum.got, fc_sum.stay, proj_sum.stay = stage(cut, qkv_sum.got, fc_sum.stay, proj_sum.stay)
        qkv_sum.last()
        qkv_sum.up()
    little = scatter_small(cut)
    if grid.paired:
        fc_sum.got, proj_sum.got, qkv_sum.got = stage(fc_sum.got, proj_sum.got, qkv_sum.got)
        qkv_sum.across()
        fc_sum.got, proj_sum.got, qkv_sum.stay = stage(fc_sum.got, proj_sum.got, qkv_sum.stay)
        fc_weight_grad = own_rows(grid, fc_sum.rows())
        total = proj_sum.rows()
        proj_wide = proj_keep.shape[2]
        proj_weight_grad = own_rows(grid, from_chunks(total[:, :proj_wide]))
        out_weight_grad = own_rows(grid, total[:, proj_wide:])
        total = qkv_sum.rows()
        wide = qkv_one[1].shape[2]
        ends = [own_rows(grid, total[:, :wide]), own_rows(grid, total[:, wide:])]
    else:
        reduce = lambda v: lax.psum_scatter(v.astype(F32), AXES, scatter_dimension=0, tiled=True)
        side = lambda k, s: jnp.concatenate([k[0], s[0]], 1)
        fc_weight_grad = reduce(side(fc_keep, fc_send))
        out_weight_grad = reduce(side(out_keep, out_send))
        ends = [reduce(side(u[1], u[0])) for u in (qkv_one, qkv_two)]
        proj_weight_grad = reduce(
            jnp.concatenate([from_chunks(proj_keep[0]), from_chunks(proj_send[0])], 1)
        )
    third = lambda e, i: e[:, i * e.shape[1] // 3 : (i + 1) * e.shape[1] // 3]
    qkv_weight_grad = jnp.concatenate([third(e, i) for i in range(3) for e in ends], 1)
    shard = lambda s: little[s, : vectors[s].shape[0]]
    return (
        layer_out,
        input_grad,
        shard(0),
        shard(1),
        qkv_weight_grad,
        shard(6),
        out_weight_grad,
        shard(2),
        shard(3),
        shard(4),
        fc_weight_grad,
        shard(7),
        proj_weight_grad,
        shard(5),
    )


def solution(mesh):
    matrix, vector = P(AXES, None), P(AXES)
    ins = (
        matrix, vector, vector, matrix, vector, matrix, vector, vector,
        vector, matrix, vector, matrix, vector, vector, matrix,
    )
    outs = (
        matrix, matrix, vector, vector, matrix, vector, matrix, vector,
        vector, vector, matrix, vector, matrix, vector,
    )
    return jax.shard_map(
        functools.partial(local, mesh), mesh=mesh, in_specs=ins, out_specs=outs, check_vma=False
    )
```

```python
import functools
import math

import jax
import jax.numpy as jnp
import numpy as np
from jax import lax
from jax.experimental import pallas as pl
from jax.experimental.pallas import tpu as pltpu
from jax.sharding import PartitionSpec as P

AXES = ("wide", "narrow")
BF, F32 = jnp.bfloat16, jnp.float32
VMEM_CAP = 58 << 20

def params(n=1, cap=VMEM_CAP):
    return pltpu.CompilerParams(dimension_semantics=("arbitrary",) * n, vmem_limit_bytes=cap)

def cost(flops, bytes_accessed, trans=0):
    return pl.CostEstimate(flops=int(flops), bytes_accessed=int(bytes_accessed), transcendentals=int(trans))

def mm(a, b):
    return jnp.dot(a, b, preferred_element_type=F32)

def diagonal_mask(rows, cols):
    key_at = lax.broadcasted_iota(jnp.int32, (rows, cols), 0)
    query_at = lax.broadcasted_iota(jnp.int32, (rows, cols), 1)
    return key_at <= query_at

def attend_kernel(qb, len_ref, qkv_ref, out_t_ref, out_ref, stat_ref, v_t, q_t):
    slot = qkv_ref.shape[1]
    q_t[...] = (qkv_ref[0] * jnp.asarray(0.125, BF)).T
    v_t[...] = qkv_ref[2].T
    half = lax.broadcasted_iota(jnp.int32, (128, 1), 0) < 64
    causal = diagonal_mask(qb, qb)
    length = len_ref[0]
    def scores(i, head):
        mine = half if head == 0 else jnp.logical_not(half)
        qh = jnp.where(mine, q_t[:, i * qb : (i + 1) * qb], jnp.zeros((), BF))
        s_dia = jnp.where(causal, mm(qkv_ref[1, i * qb : (i + 1) * qb, :], qh), -1e30)
        return s_dia, mm(qkv_ref[1, : i * qb, :], qh) if i else None
    tasks = [(i, head) for i in range(slot // qb) for head in range(2)]
    ahead = scores(*tasks[0])
    parts = []
    for at, (i, head) in enumerate(tasks):
        cols = slice(i * qb, (i + 1) * qb)
        s_dia, s_low = ahead
        if at + 1 < len(tasks):
            ahead = scores(*tasks[at + 1])
        top = jnp.max(s_dia, axis=0, keepdims=True)
        if i:
            top = jnp.maximum(top, jnp.max(s_low, axis=0, keepdims=True))
        e_dia = jnp.exp(s_dia - top)
        total = jnp.sum(e_dia, axis=0, keepdims=True)
        vh = v_t[head * 64 : head * 64 + 64, :]
        acc = mm(vh[:, cols], e_dia.astype(BF))
        if i:
            e_low = jnp.exp(s_low - top)
            total = total + jnp.sum(e_low, axis=0, keepdims=True)
            acc = acc + mm(vh[:, : i * qb], e_low.astype(BF))
        stat_ref[0, head : head + 1, cols] = top + jnp.log(total)
        parts.append(acc / total)
        if head == 1:
            both = jnp.concatenate(parts, axis=0)
            parts = []
            seen = (i * qb + lax.broadcasted_iota(jnp.int32, (1, qb), 1)) < length
            both = jnp.where(seen, both, 0.0)
            out_t_ref[:, cols] = both
            out_ref[cols, :] = both.T.astype(BF)

def attend(lengths, qkv, pairs, first, qb=256):
    slot, width = qkv.shape[1], qkv.shape[2]
    return pl.pallas_call(
        functools.partial(attend_kernel, qb),
        name="attend",
        grid=(pairs,),
        in_specs=[
            pl.BlockSpec(memory_space=pltpu.SMEM),
            pl.BlockSpec((3, slot, 128), lambda j: (0, 0, j + first)),
        ],
        out_specs=[
            pl.BlockSpec((128, slot), lambda j: (j, 0)),
            pl.BlockSpec((slot, 128), lambda j: (0, j)),
            pl.BlockSpec((1, 2, slot), lambda j: (j, 0, 0)),
        ],
        out_shape=[
            jax.ShapeDtypeStruct((pairs * 128, slot), F32),
            jax.ShapeDtypeStruct((slot, pairs * 128), BF),
            jax.ShapeDtypeStruct((pairs, 2, slot), F32),
        ],
        scratch_shapes=[pltpu.VMEM((128, slot), BF), pltpu.VMEM((128, slot), BF)],
        compiler_params=params(1, 28 << 20),
        cost_estimate=cost(pairs * 2 * slot * slot * 256, 8e6 * pairs / 6, pairs * slot * slot),
    )(lengths, qkv)

def attend_grad_kernel(qb, qkv_ref, grad_ref, out_t_ref, stat_ref, g_ref, q_t, do_t, k_t, qs, dq_t, dk_s, dv_s):
    slot = qkv_ref.shape[1]
    qs[...] = qkv_ref[0] * jnp.asarray(0.125, BF)
    q_t[...] = qs[...].T
    k_t[...] = qkv_ref[1].T
    do_t[...] = grad_ref[...].T
    half = lax.broadcasted_iota(jnp.int32, (128, 1), 0) < 64
    half_lane = lax.broadcasted_iota(jnp.int32, (1, 128), 1) < 64
    causal = diagonal_mask(qb, qb)
    zero = jnp.zeros((), BF)
    prod = do_t[...].astype(F32) * out_t_ref[...]
    delta = [jnp.sum(prod[h * 64 : h * 64 + 64], axis=0, keepdims=True) for h in range(2)]
    def scores(i, head):
        cols, end = slice(i * qb, (i + 1) * qb), (i + 1) * qb
        mine = half if head == 0 else jnp.logical_not(half)
        qh_t = jnp.where(mine, q_t[:, cols], zero)
        doh_t = jnp.where(mine, do_t[:, cols], zero)
        return mm(qkv_ref[1, :end, :], qh_t), mm(qkv_ref[2, :end, :], doh_t)
    tasks = [(i, head) for i in range(slot // qb) for head in range(2)]
    ahead = scores(*tasks[0])
    for at, (i, head) in enumerate(tasks):
        cols, end = slice(i * qb, (i + 1) * qb), (i + 1) * qb
        s, dp = ahead
        if at + 1 < len(tasks):
            ahead = scores(*tasks[at + 1])
        mine_lane = half_lane if head == 0 else jnp.logical_not(half_lane)
        qh = jnp.where(mine_lane, qs[cols, :], zero)
        doh = jnp.where(mine_lane, grad_ref[cols, :], zero)
        stat = stat_ref[0, head : head + 1, cols]
        dl = delta[head][:, cols]
        p = jnp.exp(s - stat)
        p_dia = jnp.where(causal, p[i * qb :], 0.0)
        p = jnp.concatenate([p[: i * qb], p_dia], axis=0) if i else p_dia
        ds = (p * (dp - dl)).astype(BF)
        pb = p.astype(BF)
        dv_h = mm(pb, doh)
        dk_h = mm(ds, qh)
        dq_t[head * 64 : head * 64 + 64, cols] = mm(k_t[head * 64 : head * 64 + 64, :end], ds)
        if head == 0:
            dv_new, dk_new = dv_h, dk_h
            continue
        dv_new, dk_new = dv_new + dv_h, dk_new + dk_h
        if i:
            dv_s[: i * qb] += dv_new[: i * qb]
            dk_s[: i * qb] += dk_new[: i * qb]
        dv_s[cols] = dv_new[i * qb :]
        dk_s[cols] = dk_new[i * qb :]
    g_ref[0] = (dq_t[...] * 0.125).T.astype(BF)
    g_ref[1] = dk_s[...].astype(BF)
    g_ref[2] = dv_s[...].astype(BF)

def attend_grad(qkv, grad, out_t, stat, first, qb=256):
    slot = qkv.shape[1]
    pairs = out_t.shape[0] // 128
    width = pairs * 128
    return pl.pallas_call(
        functools.partial(attend_grad_kernel, qb),
        name="attend_grad",
        grid=(pairs,),
        in_specs=[
            pl.BlockSpec((3, slot, 128), lambda j: (0, 0, j + first)),
            pl.BlockSpec((slot, 128), lambda j: (0, j + first)),
            pl.BlockSpec((128, slot), lambda j: (j, 0)),
            pl.BlockSpec((1, 2, slot), lambda j: (j, 0, 0)),
        ],
        out_specs=pl.BlockSpec((3, slot, 128), lambda j: (0, 0, j)),
        out_shape=jax.ShapeDtypeStruct((3, slot, width), BF),
        scratch_shapes=[
            pltpu.VMEM((128, slot), BF),
            pltpu.VMEM((128, slot), BF),
            pltpu.VMEM((128, slot), BF),
            pltpu.VMEM((slot, 128), BF),
            pltpu.VMEM((128, slot), F32),
            pltpu.VMEM((slot, 128), F32),
            pltpu.VMEM((slot, 128), F32),
        ],
        compiler_params=params(1, 32 << 20),
        cost_estimate=cost(pairs * 5 * slot * slot * 256, 16e6 * pairs / 6, pairs * 2 * slot * slot),
    )(qkv, grad, out_t, stat)
VECTOR_ROWS = 16
GAIN_ONE, SHIFT_ONE, BIAS_OUT, GAIN_TWO, SHIFT_TWO, BIAS_PROJ, BIAS_QKV, BIAS_FC = 0, 1, 2, 3, 4, 5, 6, 9
branch_scale = 1.0 / math.sqrt(48.0)
norm_epsilon = 1e-05
WHOLE = dict(pipeline_mode=pl.Buffered(1))

def mm_nt(a, b):
    return lax.dot_general(a, b, (((1,), (1,)), ((), ())), preferred_element_type=F32)

def mm_tn(a, b):
    return lax.dot_general(a, b, (((0,), (0,)), ((), ())), preferred_element_type=F32)

def normalised(v):
    mean = jnp.mean(v, axis=-1, keepdims=True)
    centred = v - mean
    var = jnp.mean(centred * centred, axis=-1, keepdims=True)
    scale = lax.rsqrt(var + norm_epsilon)
    return centred * scale, scale

def norm_pull(n, scale, gain, u):
    ug = u * gain
    a = jnp.mean(ug, axis=-1, keepdims=True)
    b = jnp.mean(ug * n, axis=-1, keepdims=True)
    return (ug - a - n * b) * scale

def row_of(ref, at):
    return ref[at : at + 1, :]

def whole(shape, index=None):
    zeros = (0,) * len(shape)
    return pl.BlockSpec(shape, (lambda *_: index or zeros), **WHOLE)

def assemble(place, sources, target):
    wide = target.shape[2] // 2
    for s, source in enumerate(sources):
        for half in range(2):
            @pl.when(place[s, 0] == half)
            def _():
                for p in range(source.shape[0]):
                    target[place[s, 1 + p], :, half * wide : (half + 1) * wide] = source[p, :, :wide]

def fetch(place, sources, target, sem):
    wide = target.shape[2] // 2
    for s, source in enumerate(sources):
        lanes = pl.ds(pl.multiple_of(place[s, 0] * wide, 128), wide)
        for p in range(source.shape[0]):
            pltpu.make_async_copy(
                source.at[p, :, pl.ds(0, wide)], target.at[place[s, 1 + p], :, lanes], sem
            ).start()

def arrived(target, sem):
    pltpu.make_async_copy(target, target, sem).wait()

def project_kernel(n_src, place, x_ref, vec_ref, *rest):
    sources, (qkv_ref, low_ref, w_ref) = rest[:n_src], rest[n_src:]
    @pl.when(pl.program_id(0) == 0)
    def _():
        assemble(place, sources, w_ref)
    n, _ = normalised(x_ref[...].astype(F32))
    low = (n * row_of(vec_ref, GAIN_ONE) + row_of(vec_ref, SHIFT_ONE)).astype(BF)
    low_ref[...] = low
    d = low.shape[1]
    for part in range(3):
        w = w_ref[:, :, part * d : (part + 1) * d].reshape(d, d)
        qkv_ref[part] = (mm(low, w) + row_of(vec_ref, BIAS_QKV + part)).astype(BF)

def project(place, x, vec, sources, blocks, rows=256):
    t, d = x.shape
    r, wide = d // blocks, 3 * d // 2
    return pl.pallas_call(
        functools.partial(project_kernel, len(sources)),
        name="project",
        grid_spec=pltpu.PrefetchScalarGridSpec(
            num_scalar_prefetch=1,
            grid=(t // rows,),
            in_specs=[
                pl.BlockSpec((rows, d), lambda i, p: (i, 0)),
                whole(vec.shape),
                *[whole(s.shape) for s in sources],
            ],
            out_specs=[
                pl.BlockSpec((3, rows, d), lambda i, p: (0, i, 0)),
                pl.BlockSpec((rows, d), lambda i, p: (i, 0)),
                whole((blocks, r, 2 * wide)),
            ],
        ),
        out_shape=[
            jax.ShapeDtypeStruct((3, t, d), BF),
            jax.ShapeDtypeStruct((t, d), BF),
            jax.ShapeDtypeStruct((blocks, r, 2 * wide), BF),
        ],
        compiler_params=params(1, 32 << 20),
        cost_estimate=cost(2 * t * d * 3 * d, 18e6),
    )(place, x, vec, *sources)

def mix_kernel(n_src, place, x_ref, vec_ref, *rest):
    sources, parts, (mid_ref, low_ref, w_ref) = rest[:n_src], rest[n_src:-3], rest[-3:]
    @pl.when(pl.program_id(0) == 0)
    def _():
        assemble(place, sources, w_ref)
    d = x_ref.shape[1]
    w = w_ref[...].reshape(d, d)
    mid = x_ref[...].astype(F32) + branch_scale * (mm(jnp.concatenate([p[...] for p in parts], 1), w) + row_of(vec_ref, BIAS_OUT))
    mid_ref[...] = mid
    n, _ = normalised(mid)
    low_ref[...] = (n * row_of(vec_ref, GAIN_TWO) + row_of(vec_ref, SHIFT_TWO)).astype(BF)

def mix(place, parts, x, vec, sources, blocks, column, rows=256):
    t, d = x.shape
    r, np_ = d // blocks, sources[0].shape[0]
    return pl.pallas_call(
        functools.partial(mix_kernel, len(sources)),
        name="mix",
        grid_spec=pltpu.PrefetchScalarGridSpec(
            num_scalar_prefetch=1,
            grid=(t // rows,),
            in_specs=[
                pl.BlockSpec((rows, d), lambda i, p: (i, 0)),
                whole(vec.shape),
                *[whole((np_, r, d // 2), (0, 0, column)) for s in sources],
                *[pl.BlockSpec((rows, p.shape[1]), lambda i, p: (i, 0)) for p in parts],
            ],
            out_specs=[
                pl.BlockSpec((rows, d), lambda i, p: (i, 0)),
                pl.BlockSpec((rows, d), lambda i, p: (i, 0)),
                whole((blocks, r, d)),
            ],
        ),
        out_shape=[
            jax.ShapeDtypeStruct((t, d), F32),
            jax.ShapeDtypeStruct((t, d), BF),
            jax.ShapeDtypeStruct((blocks, r, d), BF),
        ],
        compiler_params=params(1, 24 << 20),
        cost_estimate=cost(2 * t * d * d, 9e6),
    )(place, x, vec, *sources, *parts)

def mlp_kernel(n_src, rb, core, place, lens, low_ref, cot_ref, bias_ref, mid_hbm, *rest):
    fcs, projs, rest = rest[:n_src], rest[n_src : 2 * n_src], rest[2 * n_src :]
    (out_hbm, gmid_hbm, gbr_hbm, fsend_hbm, fkeep_hbm, psend_ref, pkeep_ref, fbg_ref, vec_ref,
     fc_s, proj_s, low_t, g2_s, second_s, act_s, gpre_s, mid_s, out_s, gmid_s, gbr_s, f_s, sems) = rest
    t, d = mid_s.shape
    w, h = 2 * d, d // 2
    step = pl.program_id(0)
    mine = core[0]
    chunk = lax.rem(step + 1 - mine, 2)
    mid_copy = pltpu.make_async_copy(mid_hbm, mid_s, sems.at[2])
    outs = [
        pltpu.make_async_copy(a, b, sems.at[3 + k])
        for k, (a, b) in enumerate(
            ((out_s, out_hbm), (gmid_s, gmid_hbm), (gbr_s, gbr_hbm), (f_s.at[0], fsend_hbm), (f_s.at[1], fkeep_hbm))
        )
    ]
    def valid_rows(at):
        return (at * rb + lax.broadcasted_iota(jnp.int32, (rb, 1), 0)) < lens[0]
    @pl.when(step == 0)
    def _():
        fetch(place, projs, proj_s, sems.at[0])
        fetch(place, fcs, fc_s, sems.at[1])
        mid_copy.start()
        low_t[...] = low_ref[...].T
        def begin(i, total):
            at = pl.ds(pl.multiple_of(i * rb, rb), rb)
            g = jnp.where(valid_rows(i), branch_scale * cot_ref[at, :].astype(F32), 0.0).astype(BF)
            g2_s[at, :] = g
            return total + jnp.sum(g.astype(F32), axis=0, keepdims=True)
        vec_ref[0:1] = lax.fori_loop(0, t // rb, begin, jnp.zeros((1, d), F32))
        arrived(proj_s, sems.at[0])
        arrived(fc_s, sems.at[1])
        mid_copy.wait()
    fc = fc_s.at[:, :, pl.ds(pl.multiple_of(chunk * w, w), w)]
    bias = jnp.concatenate([bias_ref[pl.ds(BIAS_FC + 2 * chunk + i, 1), :] for i in range(2)], 1)
    blocks, pr = proj_s.shape[0], proj_s.shape[1]
    if blocks > 1:
        proj = proj_s.at[pl.ds(chunk * (blocks // 2), blocks // 2)]
    else:
        proj = proj_s.at[:, pl.ds(pl.multiple_of(chunk * w, w), w)]
    def rows_step(i, total):
        at = pl.ds(pl.multiple_of(i * rb, rb), rb)
        wf = fc[...].reshape(d, w)
        wp = proj[...].reshape(w, d)
        ga = mm_nt(g2_s[at, :], wp)
        u = mm(low_ref[at, :], wf) + bias
        sq = u * u
        th = jnp.tanh(u * (0.7978845608028654 + (0.7978845608028654 * 0.044715) * sq))
        up = 0.5 + 0.5 * th
        act = (u * up).astype(BF)
        act_s[at, :] = act
        slope = up * (1.0 + (1.0 - up) * (u * (2 * 0.7978845608028654 + (6 * 0.7978845608028654 * 0.044715) * sq)))
        gpb = (ga * slope).astype(BF)
        gpre_s[at, :] = gpb
        more, back = mm(act, wp), mm_nt(gpb, wf)
        @pl.when(step == 0)
        def _():
            second_s[at, :] = more
            gmid_s[at, :] = back
        @pl.when(step == 1)
        def _():
            second_s[at, :] += more
            gmid_s[at, :] += back
        return total + jnp.sum(gpb.astype(F32), axis=0, keepdims=True)
    sums = lax.fori_loop(0, t // rb, rows_step, jnp.zeros((1, w), F32))
    for i in range(2):
        fbg_ref[pl.ds(2 * chunk + i, 1), :] = sums[:, i * d : (i + 1) * d]
    @pl.when(step == 1)
    def _():
        def finish(i, carry):
            at = pl.ds(pl.multiple_of(i * rb, rb), rb)
            mid = mid_s[at, :]
            out_s[at, :] = (mid + branch_scale * (second_s[at, :] + row_of(bias_ref, BIAS_PROJ))).astype(BF)
            n, scale = normalised(mid)
            gh = gmid_s[at, :]
            cot = jnp.where(valid_rows(i), cot_ref[at, :].astype(F32), 0.0)
            gm = cot + norm_pull(n, scale, row_of(bias_ref, GAIN_TWO), gh)
            gmid_s[at, :] = gm
            gb = (branch_scale * gm).astype(BF)
            gbr_s[at, :] = gb
            return (carry[0] + jnp.sum(gh * n, axis=0, keepdims=True),
                    carry[1] + jnp.sum(gh, axis=0, keepdims=True),
                    carry[2] + jnp.sum(gb.astype(F32), axis=0, keepdims=True))
        zero = jnp.zeros((1, d), F32)
        a, b, c = lax.fori_loop(0, t // rb, finish, (zero, zero, zero))
        vec_ref[1:2] = a
        vec_ref[2:3] = b
        vec_ref[3:4] = c
        for copy in outs[:3]:
            copy.start()
    f_s[step] = mm(low_t[...], gpre_s[...]).astype(BF).reshape(f_s.shape[1:])
    @pl.when(step == 0)
    def _():
        outs[3].start()
    @pl.when(step == 1)
    def _():
        outs[4].start()
    dproj = mm_tn(act_s[...], g2_s[...]).astype(BF)
    for half in range(2):
        @pl.when(mine == half)
        def _():
            pkeep_ref[...] = dproj[:, half * h : (half + 1) * h].reshape(pkeep_ref.shape)
            psend_ref[...] = dproj[:, (1 - half) * h : (2 - half) * h].reshape(psend_ref.shape)
    @pl.when(step == 1)
    def _():
        for copy in outs:
            copy.wait()

def mlp(core, place, lens, mid, low, cot, vec, fcs, projs, blocks, rb=256):
    t, d = mid.shape
    r, pr = d // blocks, 4 * d // blocks
    smem, hbm = pl.BlockSpec(memory_space=pltpu.SMEM), pl.BlockSpec(memory_space=pl.ANY)
    turn = lambda i, c: lax.rem(i + 1 - c[0], 2)
    if blocks > 1:
        pspec = pl.BlockSpec((blocks // 2, pr, d // 2), lambda i, c: (turn(i, c), 0, 0))
    else:
        pspec = pl.BlockSpec((1, pr // 2, d // 2), lambda i, c: (0, turn(i, c), 0))
    of = jax.ShapeDtypeStruct
    return pl.pallas_call(
        functools.partial(mlp_kernel, len(fcs), rb),
        name="mlp",
        grid_spec=pltpu.PrefetchScalarGridSpec(
            num_scalar_prefetch=1,
            grid=(2,),
            in_specs=[smem, smem, whole((t, d)), whole((t, d)), whole(vec.shape), hbm] + [hbm] * len(fcs + projs),
            out_specs=[hbm] * 5 + [pspec, pspec, whole((4, d)), whole((4, d))],
            scratch_shapes=[
                pltpu.VMEM((blocks, r, 4 * d), BF),
                pltpu.VMEM((blocks, pr, d), BF),
                pltpu.VMEM((d, t), BF),
                pltpu.VMEM((t, d), BF),
                pltpu.VMEM((t, d), F32),
                pltpu.VMEM((t, 2 * d), BF),
                pltpu.VMEM((t, 2 * d), BF),
                pltpu.VMEM((t, d), F32),
                pltpu.VMEM((t, d), BF),
                pltpu.VMEM((t, d), F32),
                pltpu.VMEM((t, d), BF),
                pltpu.VMEM((2, blocks, r, 2 * d), BF),
                pltpu.SemaphoreType.DMA((8,)),
            ],
        ),
        out_shape=[
            of((t, d), BF), of((t, d), F32), of((t, d), BF),
            of((blocks, r, 2 * d), BF), of((blocks, r, 2 * d), BF),
            of((blocks, pr, d // 2), BF), of((blocks, pr, d // 2), BF),
            of((4, d), F32), of((4, d), F32),
        ],
        compiler_params=params(),
        cost_estimate=cost(12 * t * d * 4 * d, 40e6, t * 4 * d),
    )(core, place, lens, low, cot, vec, mid, *fcs, *projs)

def unmix_kernel(core, lens, gbr_ref, w_ref, *rest):
    parts, (ga_ref, send_ref, keep_ref) = rest[:-3], rest[-3:]
    t, d = gbr_ref.shape
    w = w_ref[...].reshape(d, d)
    seen = lax.broadcasted_iota(jnp.int32, (t, 1), 0) < lens[0]
    ga_ref[...] = jnp.where(seen, mm_nt(gbr_ref[...], w), 0.0).astype(BF)
    dw = jnp.concatenate([mm_tn(p[...], gbr_ref[...]).astype(BF) for p in parts], 0)
    h = d // 2
    for half in range(2):
        @pl.when(core[0] == half)
        def _():
            keep_ref[...] = dw[:, half * h : (half + 1) * h].reshape(keep_ref.shape)
            send_ref[...] = dw[:, (1 - half) * h : (2 - half) * h].reshape(send_ref.shape)

def unmix(core, lens, gbr, parts, w, blocks):
    t, d = gbr.shape
    smem = pl.BlockSpec(memory_space=pltpu.SMEM)
    piece = jax.ShapeDtypeStruct((blocks, d // blocks, d // 2), BF)
    return pl.pallas_call(
        unmix_kernel,
        name="unmix",
        in_specs=[smem, smem] + [pl.BlockSpec(memory_space=pltpu.VMEM)] * (2 + len(parts)),
        out_shape=[jax.ShapeDtypeStruct((t, d), BF), piece, piece],
        compiler_params=params(0, 24 << 20),
        cost_estimate=cost(4 * t * d * d, 9e6),
    )(core, lens, gbr, w, *parts)

def unproject_kernel(blocks, core, low_ref, g_ref, send_ref, keep_ref, sums_ref):
    d, w = low_ref.shape[1], g_ref.shape[2]
    r, h = d // blocks, w // 2
    low_t = low_ref[...].T
    q, k, v = [mm(low_t, g_ref[part]).astype(BF).reshape(blocks, r, w) for part in range(3)]
    for half, refs in ((0, (keep_ref, send_ref)), (1, (send_ref, keep_ref))):
        @pl.when(core[0] == half)
        def _():
            refs[0][:, :, :w] = q
            refs[0][:, :, w:] = k[:, :, :h]
            refs[1][:, :, :h] = k[:, :, h:]
            refs[1][:, :, h:] = v
    for part in range(3):
        sums_ref[part : part + 1] = jnp.sum(g_ref[part].astype(F32), axis=0, keepdims=True)

def unproject(core, low, g, blocks):
    t, d = low.shape
    w = g.shape[2]
    piece = jax.ShapeDtypeStruct((blocks, d // blocks, w // 2 * 3), BF)
    return pl.pallas_call(
        functools.partial(unproject_kernel, blocks),
        name="unproject",
        in_specs=[pl.BlockSpec(memory_space=pltpu.SMEM)] + [pl.BlockSpec(memory_space=pltpu.VMEM)] * 2,
        out_shape=[piece, piece, jax.ShapeDtypeStruct((3, w), F32)],
        compiler_params=params(0, 24 << 20),
        cost_estimate=cost(6 * t * d * w, 10e6 * w / d),
    )(core, low, g)

def route_kernel(count, steps, rows, near, table, *refs):
    inputs, outs = refs[: 2 * count + near], refs[2 * count + near :]
    def write(ref):
        at = 0
        for k, g in zip(inputs[:count], inputs[count : 2 * count]):
            r, w = k.shape[-2:]
            place = (slice(at, at + r), slice(0, w)) if rows else (slice(0, r), slice(at, at + w))
            at += r if rows else w
            total = (k[...].astype(F32) + g[...].astype(F32)).reshape(1, ref.shape[1], r, w)
            came = [v[:, :, place[0], place[1]] for v in inputs[2 * count :]]
            if near == 2:
                came = [jnp.where(table[pl.program_id(0), 2] == 0, *came)]
            if near:
                total = total + came[0].astype(F32)
            ref[:, :, place[0], place[1]] = total.astype(BF)
    for s, ref in enumerate(outs):
        @pl.when(pl.program_id(0) // steps == s)
        def _():
            write(ref)

def route(table, keeps, gots, near=(), rows=False, split=False):
    z = keeps[0].shape[0]
    sizes = [k.shape[-2:] for k in keeps]
    tall = sum(r for r, _ in sizes) if rows else sizes[0][0]
    wide = sizes[0][1] if rows else sum(w for _, w in sizes)
    block = (1, z, tall, wide)
    specs = [pl.BlockSpec((z, 1, 1, *s), lambda i, t: (0, t[i, 0], t[i, 1], 0, 0)) for s in sizes] * 2
    fixed = pl.BlockSpec(block, lambda i, t: (0, 0, 0, 0))
    if near or split:
        steps, outs = 1, [fixed] * 2
        specs += [pl.BlockSpec(block, lambda i, t: (t[i, 2], 0, 0, 0))] if len(near) == 1 else [fixed] * len(near)
    else:
        steps, outs = 2, [pl.BlockSpec(block, lambda i, t: (i, 0, 0, 0))]
    return pl.pallas_call(
        functools.partial(route_kernel, len(keeps), steps, rows, len(near)),
        name="route",
        grid_spec=pltpu.PrefetchScalarGridSpec(
            num_scalar_prefetch=1, grid=(2,), in_specs=specs, out_specs=outs
        ),
        out_shape=[jax.ShapeDtypeStruct((steps, z, tall, wide), BF)] * len(outs),
        compiler_params=params(1, 24 << 20),
        cost_estimate=cost(1e6, 2 * z * tall * wide * 6),
    )(table, *keeps, *gots, *near)

def final_kernel(x_ref, w_ref, gmid_ref, bias_ref, *rest):
    parts, (out_ref, vec_ref) = rest[:-2], rest[-2:]
    d = x_ref.shape[1]
    w = w_ref[...].reshape(d, 3 * d)
    gh = jnp.zeros(x_ref.shape, F32)
    at = 0
    for g in parts:
        for i in range(3):
            gh = gh + mm_nt(g[i], w[:, i * d + at : i * d + at + g.shape[2]])
        at += g.shape[2]
    n, scale = normalised(x_ref[...].astype(F32))
    out_ref[...] = (gmid_ref[...] + norm_pull(n, scale, row_of(bias_ref, GAIN_ONE), gh)).astype(BF)
    @pl.when(pl.program_id(0) == 0)
    def _():
        vec_ref[...] = jnp.zeros_like(vec_ref)
    vec_ref[0:1] += jnp.sum(gh * n, axis=0, keepdims=True)
    vec_ref[1:2] += jnp.sum(gh, axis=0, keepdims=True)

def final(x, parts, w, gmid, vec, rows=256):
    t, d = x.shape
    return pl.pallas_call(
        final_kernel,
        name="final",
        grid=(t // rows,),
        in_specs=[
            pl.BlockSpec((rows, d), lambda i: (i, 0)),
            whole(w.shape),
            pl.BlockSpec((rows, d), lambda i: (i, 0)),
            whole(vec.shape),
            *[pl.BlockSpec((3, rows, g.shape[2]), lambda i: (0, i, 0)) for g in parts],
        ],
        out_specs=[pl.BlockSpec((rows, d), lambda i: (i, 0)), whole((2, d))],
        out_shape=[jax.ShapeDtypeStruct((t, d), BF), jax.ShapeDtypeStruct((2, d), F32)],
        compiler_params=params(1, 32 << 20),
        cost_estimate=cost(6 * t * d * d, 15e6),
    )(x, w, gmid, vec, *parts)
def spread_matrix(size, width):
    row = lax.broadcasted_iota(jnp.int32, (128, width), 0).astype(F32)
    col = lax.broadcasted_iota(jnp.int32, (128, width), 1).astype(F32)
    inside = col - jnp.floor((col + 0.5) / size) * size
    return jnp.where(inside == row, 1.0, 0.0)

def own_columns(count, size, per, width):
    at = lax.broadcasted_iota(jnp.int32, (count, width), 0).astype(F32)
    at = at - jnp.floor((at + 0.5) / per) * per
    col = lax.broadcasted_iota(jnp.int32, (count, width), 1).astype(F32)
    return jnp.logical_and(col >= at * size, col < (at + 1) * size)


def unfold_vectors(rows_of, count, out_ref):
    d = out_ref.shape[1]
    out_ref[...] = jnp.zeros_like(out_ref)
    for rows, slots, first in ((1, range(6), 0), (2, (6,), BIAS_QKV), (4, (7,), BIAS_FC)):
        size, per = d * rows // count, count // rows
        spread = spread_matrix(size, d).astype(BF)
        mine = own_columns(count, size, per, d)
        for s in slots:
            got = jnp.where(mine, mm(rows_of(s), spread), 0.0)
            for r in range(rows):
                to = first + (s if rows == 1 else 2 * r if rows == 2 else r)
                out_ref[to : to + 1] = jnp.sum(got[r * per : (r + 1) * per], axis=0, keepdims=True)

def unfold_kernel(x_ref, out_ref):
    unfold_vectors(lambda s: x_ref[s], x_ref.shape[1], out_ref)

def unfold(x, d):
    return pl.pallas_call(
        unfold_kernel,
        name="unfold",
        in_specs=[pl.BlockSpec(memory_space=pltpu.VMEM)],
        out_shape=jax.ShapeDtypeStruct((VECTOR_ROWS, d), F32),
        compiler_params=params(0, 16 << 20),
        cost_estimate=cost(1e8, 1e6),
    )(x)

def unfold_pieces_kernel(n_src, place, *rest):
    sources, out_ref, x_ref = rest[:n_src], rest[n_src], rest[-1]
    r = sources[0].shape[1] // 2
    for s, source in enumerate(sources):
        for p in range(source.shape[0]):
            tile = source[p].astype(F32)
            for c in range(2):
                x_ref[2 * place[s, 1 + p] + c] = tile[c * r : c * r + 8]
    unfold_vectors(lambda s: x_ref[:, s, :].astype(BF), x_ref.shape[0], out_ref)

def unfold_pieces(place, sources, count, d):
    np_, r, wide = sources[0].shape
    return pl.pallas_call(
        functools.partial(unfold_pieces_kernel, len(sources)),
        name="unfold",
        grid_spec=pltpu.PrefetchScalarGridSpec(
            num_scalar_prefetch=1,
            grid=(1,),
            in_specs=[whole((np_, r, 128), (0, 0, wide // 128 - 1)) for _ in sources],
            out_specs=whole((VECTOR_ROWS, d)),
            scratch_shapes=[pltpu.VMEM((count, 8, 128), F32)],
        ),
        out_shape=jax.ShapeDtypeStruct((VECTOR_ROWS, d), F32),
        compiler_params=params(1, 16 << 20),
        cost_estimate=cost(1e8, 1e6),
    )(place, *sources)

def fold_kernel(first_ref, sums_ref, qkv_ref, fc_ref, out_ref):
    count, d = out_ref.shape[1], first_ref.shape[1]
    singles = [
        first_ref[0:1], first_ref[1:2], sums_ref[3:4], sums_ref[1:2], sums_ref[2:3], sums_ref[0:1],
    ]
    pairs = [[v] for v in singles] + [[qkv_ref[0:1], qkv_ref[2:3]], [fc_ref[r : r + 1] for r in range(4)]]
    for rows, slots in ((1, range(6)), (2, (6,)), (4, (7,))):
        size, per = d * rows // count, count // rows
        spread = spread_matrix(size, d)
        mine = own_columns(count, size, per, d)
        full = jnp.concatenate(
            [
                jnp.where(mine, jnp.concatenate([jnp.broadcast_to(v, (per, d)) for v in pairs[s]], 0), 0.0)
                for s in slots
            ],
            0,
        )
        got = lax.dot_general(
            full, spread, (((1,), (1,)), ((), ())), precision=lax.Precision.HIGHEST, preferred_element_type=F32
        )
        for i, s in enumerate(slots):
            out_ref[s] = got[i * count : (i + 1) * count]

def fold(first, sums, qkv, fc, count):
    return pl.pallas_call(
        fold_kernel,
        name="fold",
        in_specs=[pl.BlockSpec(memory_space=pltpu.VMEM)] * 4,
        out_shape=jax.ShapeDtypeStruct((8, count, 128), F32),
        compiler_params=params(0, 32 << 20),
        cost_estimate=cost(1e8, 1e6),
    )(first, sums, qkv, fc)


class Grid:
    order = (0, 2, 1, 3)

    def __init__(self, mesh, rows):
        wide, narrow = mesh.shape["wide"], mesh.shape["narrow"]
        self.count = wide * narrow
        self.paired = narrow == 4 and wide == 8 and rows % 8 == 0
        self.blocks = self.count // 2 if self.paired else 1
        self.z = wide // 2

    def index(self, z, x, y, c):
        return ((z * 2 + x) * 2 + y) * 2 + c

    def places(self):
        return [
            (z, x, y, c) for z in range(self.z) for x in range(2) for y in range(2) for c in range(2)
        ]

    def perm(self, target):
        return [(self.index(*at), self.index(*target(*at))) for at in self.places()]

    def here(self):
        w, n = lax.axis_index("wide"), lax.axis_index("narrow")
        return w // 2, w % 2, n // 2, n % 2

    def table(self):
        rows = []
        for z0, x0, y0, c0 in self.places():
            mine = []
            for half in (c0, 1 - c0):
                for ka, kb in ((0, 0), (1, 0), (0, 1), (1, 1)):
                    kx, ky = (ka, kb) if half == 0 else (kb, ka)
                    blocks = [
                        ((z0 ^ kz) * 2 + (x0 ^ kx)) * 2 + (y0 ^ ky) for kz in self.order
                    ]
                    mine.append([half] + blocks)
            rows.append(mine)
        return np.array(rows, np.int32)

    def routes(self):
        near, far = [], []
        for z0, x0, y0, c0 in self.places():
            if c0 == 0:
                near.append([[1 - x0, 0], [1 - x0, 1]])
                far.append([[x0, 1 - y0, 1 - y0], [x0, y0, y0]])
            else:
                near.append([[0, 1 - y0], [1, 1 - y0]])
                far.append([[1 - x0, y0, 1 - x0], [x0, y0, x0]])
        return np.array(near, np.int32), np.array(far, np.int32)

    def send(self, value, target):
        return lax.ppermute(value, AXES, self.perm(target))

    def other_core(self, value):
        return self.send(value, lambda z, x, y, c: (z, x, y, 1 - c))

    def along(self, value, turn):
        return self.send(
            value,
            lambda z, x, y, c: (z, 1 - x, y, c) if c == turn else (z, x, 1 - y, c),
        )

    def up(self, value, k):
        return self.send(value, lambda z, x, y, c: (z ^ k, x, y, c))


def both(first, own, other, axis):
    return jnp.where(
        first, jnp.concatenate([own, other], axis), jnp.concatenate([other, own], axis)
    )


def pair_rows(grid, shard, extra=None):
    c = grid.here()[3]
    h = shard.shape[1] // 2
    mine = lax.dynamic_slice_in_dim(shard, c * h, h, 1)
    away = lax.dynamic_slice_in_dim(shard, (1 - c) * h, h, 1)
    if extra is not None:
        mine, away = jnp.concatenate([mine, extra], 1), jnp.concatenate([away, extra], 1)
    return both(c == 0, mine, grid.other_core(away), 0)


def spread_z(grid, pair):
    return jnp.stack([pair] + [grid.up(pair, k) for k in grid.order[1:]])


def with_other(grid, sources):
    return sources + [grid.other_core(s) for s in sources]


def stage(*values):
    return lax.optimization_barrier(values)


def after(value, *earlier):
    return lax.optimization_barrier((value, *earlier))[0]


def add(a, b):
    return (a.astype(F32) + b.astype(F32)).astype(BF)


def pick(v, at, axis):
    return lax.dynamic_index_in_dim(v, at, axis, keepdims=False)


class Sum:
    def __init__(self, grid, sends, keeps, rows=False, split=False):
        self.grid, self.rows_under, self.split = grid, rows, split
        at = lax.axis_index(AXES)
        self.tables = [jnp.asarray(t)[at] for t in grid.routes()]
        self.shape = (grid.z, 2, 2)
        self.keeps = keeps
        self.got = [grid.other_core(s) for s in sends]

    def core(self):
        block = lambda v: v.reshape(*self.shape, *v.shape[1:])
        self.keeps, self.got = [block(k) for k in self.keeps], [block(g) for g in self.got]
        self.away = route(self.tables[0], self.keeps, self.got, (), self.rows_under, self.split)
        return self.away

    def near(self):
        self.came = [self.grid.along(v, 0) for v in self.away]

    def middle(self):
        self.away, self.stay = route(self.tables[1], self.keeps, self.got, self.came, self.rows_under)
        return self.away

    def far(self):
        self.got = self.grid.along(self.away, 1)

    def last(self):
        self.own = add(self.stay, self.got)[0]
        return self.own

    def up(self):
        z = self.grid.here()[0]
        away = jnp.stack([pick(self.own, z ^ 1, 0), pick(self.own, z ^ 3, 0)])
        self.stay = jnp.stack([pick(self.own, z, 0), pick(self.own, z ^ 2, 0)])
        self.got = self.grid.up(away, 1)

    def across(self):
        self.stay = add(self.stay, self.got)
        self.got = self.grid.up(self.stay[1], 2)

    def rows(self):
        return self.stay[0].astype(F32) + self.got.astype(F32)


def own_rows(grid, total):
    c = grid.here()[3]
    r = total.shape[0] // 2
    other = grid.other_core(lax.dynamic_slice_in_dim(total, (1 - c) * r, r, 0))
    return both(c == 0, lax.dynamic_slice_in_dim(total, c * r, r, 0), other, 1)


def stack_small(vectors):
    total = jnp.zeros((8, 128), BF)
    for i, v in enumerate(vectors):
        total = total + jnp.pad(v.reshape(1, -1), ((i, 7 - i), (0, 128 - v.shape[0])))
    return total


def gather_small(count, vectors):
    flat = stack_small(vectors)
    return lax.all_to_all(jnp.broadcast_to(flat[:, None], (8, count, 128)), AXES, 1, 1, tiled=True)


def scatter_small(cut):
    return jnp.sum(lax.all_to_all(cut, AXES, 1, 1, tiled=True), axis=1)


def halves_of(weight):
    h = weight.shape[1] // 2
    return [weight[None, :, :h], weight[None, :, h:]]


def local(
    mesh,
    tokens,
    norm1_gain,
    norm1_bias,
    qkv_weight,
    qkv_bias,
    out_weight,
    out_bias,
    norm2_gain,
    norm2_bias,
    fc_weight,
    fc_bias,
    proj_weight,
    proj_bias,
    seq_lengths,
    out_cotangent,
):
    d = tokens.shape[1]
    grid = Grid(mesh, out_weight.shape[0])
    blocks = grid.blocks
    vectors = [norm1_gain, norm1_bias, out_bias, norm2_gain, norm2_bias, proj_bias, qkv_bias, fc_bias]
    if grid.paired:
        place = jnp.asarray(grid.table())[lax.axis_index(AXES)]
        core = grid.here()[3].reshape(1).astype(jnp.int32)
        extra = jnp.pad(stack_small(vectors), ((0, qkv_weight.shape[0] - 8), (0, 0)))
        pair_qkv = pair_rows(grid, qkv_weight, extra)
        place, fc_shard, out_shard, proj_shard, pair_qkv = stage(
            place, fc_weight, out_weight, proj_weight, pair_qkv
        )
        stack_qkv = spread_z(grid, pair_qkv)
        first = jnp.concatenate([pair_rows(grid, fc_shard), pair_rows(grid, out_shard)], 1)
        second = pair_rows(grid, proj_shard)
        stack_qkv, first, second = stage(stack_qkv, first, second)
        near_qkv, far_qkv = grid.along(stack_qkv, 0), grid.along(stack_qkv, 1)
        two_first = grid.up(first, 2)
        others = [grid.other_core(stack_qkv)]
        near_qkv, far_qkv, two_first, *others = stage(near_qkv, far_qkv, two_first, *others)
        last_qkv = grid.along(near_qkv, 1)
        two_first = jnp.stack([first, two_first])
        four_first = grid.up(two_first, 1)
        two_second = grid.up(second, 2)
        others += [grid.other_core(v) for v in (near_qkv, far_qkv)]
        last_qkv, two_second, two_first, four_first, *others = stage(
            last_qkv, two_second, two_first, four_first, *others
        )
        qkv_sources = [stack_qkv, near_qkv, far_qkv, last_qkv, *others, grid.other_core(last_qkv)]
        stack_first = jnp.concatenate([two_first, four_first])
        near_first, far_first = grid.along(stack_first, 0), grid.along(stack_first, 1)
        two_second = jnp.stack([second, two_second])
        four_second = grid.up(two_second, 1)
        others = [grid.other_core(stack_first)]
        *qkv_sources, stack_first = stage(*qkv_sources, stack_first)
        vec = unfold_pieces(place, qkv_sources[:4], grid.count, d)
    else:
        place = jnp.asarray(np.array([[0, 0], [1, 0]], np.int32))
        core = jnp.zeros((1,), jnp.int32)
        full = lambda v: lax.all_gather(v, AXES, axis=0, tiled=True)
        qkv_sources = halves_of(full(qkv_weight))
        vec = unfold(gather_small(grid.count, vectors), d)
    qkv, low_one, qkv_full = project(
        place, tokens, vec, qkv_sources, blocks
    )
    if grid.paired:
        qkv, two_second, four_second, near_first, far_first, *others = stage(
            qkv, two_second, four_second, near_first, far_first, *others
        )
        stack_second = jnp.concatenate([two_second, four_second])
        last_first = grid.along(near_first, 1)
        near_second, far_second = grid.along(stack_second, 0), grid.along(stack_second, 1)
        others += [grid.other_core(near_first), grid.other_core(far_first)]
    attended = [list(attend(seq_lengths, qkv, 4, 0, 512))]
    if grid.paired:
        attended[0][2], qkv, *others = stage(attended[0][2], qkv, *others)
        second_others = [grid.other_core(stack_second)]
    else:
        fcs = halves_of(full(fc_weight))
        outs, out_at = halves_of(full(out_weight)), 0
        projs = halves_of(full(proj_weight))
    attended.append(attend(seq_lengths, qkv, 2, 4, 512))
    mixed = [a[1] for a in attended]
    if grid.paired:
        mixed[1], near_second, far_second, last_first, *second_others = stage(
            mixed[1], near_second, far_second, last_first, *second_others
        )
        last_second = grid.along(near_second, 1)
        outs = [stack_first, near_first, far_first, last_first, *others, grid.other_core(last_first)]
        second_others += [grid.other_core(near_second), grid.other_core(far_second)]
        fcs, out_at = outs, 4
    middle, low_two, out_full = mix(
        place, mixed, tokens, vec, outs, blocks, out_at
    )
    if grid.paired:
        low_two, last_second = stage(low_two, last_second)
        second_others.append(grid.other_core(last_second))
        projs = [stack_second, near_second, far_second, last_second, *second_others]
    (layer_out, grad_middle, grad_branch, fc_send, fc_keep, proj_send, proj_keep, fc_bias_term, sums) = mlp(
        core, place, seq_lengths, middle, low_two, out_cotangent, vec,
        fcs, projs, blocks,
    )
    grad_mixed, out_send, out_keep = unmix(core, seq_lengths, grad_branch, mixed, out_full, blocks)
    if grid.paired:
        fc_sum = Sum(grid, [fc_send], [fc_keep])
        proj_sum = Sum(grid, [proj_send, out_send], [proj_keep, out_keep], True)
        grad_mixed, *fc_sum.away = stage(grad_mixed, *fc_sum.core())
        fc_sum.near()
        grad_mixed, *proj_sum.away = stage(grad_mixed, *proj_sum.core())
        proj_sum.near()
    grad_one = attend_grad(qkv, grad_mixed, attended[0][0], attended[0][2], 0)
    qkv_one = list(unproject(core, low_one, grad_one, blocks))
    if grid.paired:
        qkv_one[2], grad_mixed, fc_sum.came[0], proj_sum.came[0] = stage(
            qkv_one[2], grad_mixed, fc_sum.came[0], proj_sum.came[0]
        )
        fc_sum.middle()
        fc_sum.far()
        proj_sum.middle()
        grad_mixed, fc_sum.stay, proj_sum.away, proj_sum.stay = stage(
            grad_mixed, fc_sum.stay, proj_sum.away, proj_sum.stay
        )
        proj_sum.far()
    grad_two = attend_grad(qkv, grad_mixed, attended[1][0], attended[1][2], 4)
    if grid.paired:
        fc_sum.got, grad_two = stage(fc_sum.got, grad_two)
        fc_sum.last()
        fc_sum.up()
    grads = [grad_one, grad_two]
    qkv_two = unproject(core, low_one, grad_two, blocks)
    if grid.paired:
        qkv_sum = Sum(grid, [qkv_one[0], qkv_two[0]], [qkv_one[1], qkv_two[1]])
        *qkv_sum.got, proj_sum.got = stage(*qkv_sum.got, proj_sum.got)
        grad_middle, *qkv_sum.away = stage(grad_middle, *qkv_sum.core())
        qkv_sum.near()
        grad_middle, proj_sum.own = stage(grad_middle, proj_sum.last())
        proj_sum.up()
    input_grad, first_sums = final(tokens, grads, qkv_full, grad_middle, vec)
    qkv_sums = jnp.concatenate([qkv_one[2], qkv_two[2]], 1)
    cut = fold(first_sums, sums, qkv_sums, fc_bias_term, grid.count)
    if grid.paired:
        cut, qkv_sum.came[0], proj_sum.got, fc_sum.got = stage(cut, qkv_sum.came[0], proj_sum.got, fc_sum.got)
        qkv_sum.middle()
        qkv_sum.far()
        fc_sum.across()
        proj_sum.across()
        cut, qkv_sum.got, fc_sum.stay, proj_sum.stay = stage(cut, qkv_sum.got, fc_sum.stay, proj_sum.stay)
        qkv_sum.last()
        qkv_sum.up()
    little = scatter_small(cut)
    if grid.paired:
        fc_sum.got, proj_sum.got, qkv_sum.got = stage(fc_sum.got, proj_sum.got, qkv_sum.got)
        qkv_sum.across()
        fc_sum.got, proj_sum.got, qkv_sum.stay = stage(fc_sum.got, proj_sum.got, qkv_sum.stay)
        fc_weight_grad = own_rows(grid, fc_sum.rows())
        total = proj_sum.rows()
        proj_rows = proj_keep.shape[1]
        proj_weight_grad = own_rows(grid, total[:proj_rows])
        out_weight_grad = own_rows(grid, total[proj_rows:])
        total = qkv_sum.rows()
        wide = qkv_one[1].shape[2]
        ends = [own_rows(grid, total[:, :wide]), own_rows(grid, total[:, wide:])]
    else:
        reduce = lambda v: lax.psum_scatter(v.astype(F32), AXES, scatter_dimension=0, tiled=True)
        side = lambda k, s: jnp.concatenate([k[0], s[0]], 1)
        fc_weight_grad = reduce(side(fc_keep, fc_send))
        out_weight_grad = reduce(side(out_keep, out_send))
        ends = [reduce(side(u[1], u[0])) for u in (qkv_one, qkv_two)]
        proj_weight_grad = reduce(side(proj_keep, proj_send))
    third = lambda e, i: e[:, i * e.shape[1] // 3 : (i + 1) * e.shape[1] // 3]
    qkv_weight_grad = jnp.concatenate([third(e, i) for i in range(3) for e in ends], 1)
    shard = lambda s: little[s, : vectors[s].shape[0]]
    return (
        layer_out,
        input_grad,
        shard(0),
        shard(1),
        qkv_weight_grad,
        shard(6),
        out_weight_grad,
        shard(2),
        shard(3),
        shard(4),
        fc_weight_grad,
        shard(7),
        proj_weight_grad,
        shard(5),
    )


def solution(mesh):
    matrix, vector = P(AXES, None), P(AXES)
    ins = (
        matrix, vector, vector, matrix, vector, matrix, vector, vector,
        vector, matrix, vector, matrix, vector, vector, matrix,
    )
    outs = (
        matrix, matrix, vector, vector, matrix, vector, matrix, vector,
        vector, vector, matrix, vector, matrix, vector,
    )
    return jax.shard_map(
        functools.partial(local, mesh), mesh=mesh, in_specs=ins, out_specs=outs, check_vma=False
    )
```

```python
import functools
import math

import jax
import jax.numpy as jnp
import numpy as np
from jax import lax
from jax.experimental import pallas as pl
from jax.experimental.pallas import tpu as pltpu
from jax.sharding import PartitionSpec as P

AXES = ("wide", "narrow")
BF, F32 = jnp.bfloat16, jnp.float32
VMEM_CAP = 58 << 20

def params(n=1, cap=VMEM_CAP):
    return pltpu.CompilerParams(dimension_semantics=("arbitrary",) * n, vmem_limit_bytes=cap)

def cost(flops, bytes_accessed, trans=0):
    return pl.CostEstimate(flops=int(flops), bytes_accessed=int(bytes_accessed), transcendentals=int(trans))

def mm(a, b):
    return jnp.dot(a, b, preferred_element_type=F32)

def diagonal_mask(rows, cols):
    key_at = lax.broadcasted_iota(jnp.int32, (rows, cols), 0)
    query_at = lax.broadcasted_iota(jnp.int32, (rows, cols), 1)
    return key_at <= query_at

def attend_kernel(qb, len_ref, qkv_ref, out_t_ref, out_ref, stat_ref, v_t, q_t):
    slot = qkv_ref.shape[1]
    q_t[...] = (qkv_ref[0] * jnp.asarray(0.125, BF)).T
    v_t[...] = qkv_ref[2].T
    half = lax.broadcasted_iota(jnp.int32, (128, 1), 0) < 64
    causal = diagonal_mask(qb, qb)
    length = len_ref[0]
    def scores(i, head):
        mine = half if head == 0 else jnp.logical_not(half)
        qh = jnp.where(mine, q_t[:, i * qb : (i + 1) * qb], jnp.zeros((), BF))
        s_dia = jnp.where(causal, mm(qkv_ref[1, i * qb : (i + 1) * qb, :], qh), -1e30)
        return s_dia, mm(qkv_ref[1, : i * qb, :], qh) if i else None
    tasks = [(i, head) for i in range(slot // qb) for head in range(2)]
    ahead = scores(*tasks[0])
    parts = []
    for at, (i, head) in enumerate(tasks):
        cols = slice(i * qb, (i + 1) * qb)
        s_dia, s_low = ahead
        if at + 1 < len(tasks):
            ahead = scores(*tasks[at + 1])
        top = jnp.max(s_dia, axis=0, keepdims=True)
        if i:
            top = jnp.maximum(top, jnp.max(s_low, axis=0, keepdims=True))
        e_dia = jnp.exp(s_dia - top)
        total = jnp.sum(e_dia, axis=0, keepdims=True)
        vh = v_t[head * 64 : head * 64 + 64, :]
        acc = mm(vh[:, cols], e_dia.astype(BF))
        if i:
            e_low = jnp.exp(s_low - top)
            total = total + jnp.sum(e_low, axis=0, keepdims=True)
            acc = acc + mm(vh[:, : i * qb], e_low.astype(BF))
        stat_ref[0, head : head + 1, cols] = top + jnp.log(total)
        parts.append(acc / total)
        if head == 1:
            both = jnp.concatenate(parts, axis=0)
            parts = []
            seen = (i * qb + lax.broadcasted_iota(jnp.int32, (1, qb), 1)) < length
            both = jnp.where(seen, both, 0.0)
            out_t_ref[:, cols] = both
            out_ref[cols, :] = both.T.astype(BF)

def attend(lengths, qkv, pairs, first, qb=256):
    slot, width = qkv.shape[1], qkv.shape[2]
    return pl.pallas_call(
        functools.partial(attend_kernel, qb),
        name="attend",
        grid=(pairs,),
        in_specs=[
            pl.BlockSpec(memory_space=pltpu.SMEM),
            pl.BlockSpec((3, slot, 128), lambda j: (0, 0, j + first)),
        ],
        out_specs=[
            pl.BlockSpec((128, slot), lambda j: (j, 0)),
            pl.BlockSpec((slot, 128), lambda j: (0, j)),
            pl.BlockSpec((1, 2, slot), lambda j: (j, 0, 0)),
        ],
        out_shape=[
            jax.ShapeDtypeStruct((pairs * 128, slot), F32),
            jax.ShapeDtypeStruct((slot, pairs * 128), BF),
            jax.ShapeDtypeStruct((pairs, 2, slot), F32),
        ],
        scratch_shapes=[pltpu.VMEM((128, slot), BF), pltpu.VMEM((128, slot), BF)],
        compiler_params=params(1, 28 << 20),
        cost_estimate=cost(pairs * 2 * slot * slot * 256, 8e6 * pairs / 6, pairs * slot * slot),
    )(lengths, qkv)

def attend_grad_kernel(qb, qkv_ref, grad_ref, out_t_ref, stat_ref, g_ref, q_t, do_t, k_t, qs, dq_t, dk_s, dv_s):
    slot = qkv_ref.shape[1]
    qs[...] = qkv_ref[0] * jnp.asarray(0.125, BF)
    q_t[...] = qs[...].T
    k_t[...] = qkv_ref[1].T
    do_t[...] = grad_ref[...].T
    half = lax.broadcasted_iota(jnp.int32, (128, 1), 0) < 64
    half_lane = lax.broadcasted_iota(jnp.int32, (1, 128), 1) < 64
    causal = diagonal_mask(qb, qb)
    zero = jnp.zeros((), BF)
    prod = do_t[...].astype(F32) * out_t_ref[...]
    delta = [jnp.sum(prod[h * 64 : h * 64 + 64], axis=0, keepdims=True) for h in range(2)]
    def scores(i, head):
        cols, end = slice(i * qb, (i + 1) * qb), (i + 1) * qb
        mine = half if head == 0 else jnp.logical_not(half)
        qh_t = jnp.where(mine, q_t[:, cols], zero)
        doh_t = jnp.where(mine, do_t[:, cols], zero)
        return mm(qkv_ref[1, :end, :], qh_t), mm(qkv_ref[2, :end, :], doh_t)
    tasks = [(i, head) for i in range(slot // qb) for head in range(2)]
    ahead = scores(*tasks[0])
    for at, (i, head) in enumerate(tasks):
        cols, end = slice(i * qb, (i + 1) * qb), (i + 1) * qb
        s, dp = ahead
        if at + 1 < len(tasks):
            ahead = scores(*tasks[at + 1])
        mine_lane = half_lane if head == 0 else jnp.logical_not(half_lane)
        qh = jnp.where(mine_lane, qs[cols, :], zero)
        doh = jnp.where(mine_lane, grad_ref[cols, :], zero)
        stat = stat_ref[0, head : head + 1, cols]
        dl = delta[head][:, cols]
        p = jnp.exp(s - stat)
        p_dia = jnp.where(causal, p[i * qb :], 0.0)
        p = jnp.concatenate([p[: i * qb], p_dia], axis=0) if i else p_dia
        ds = (p * (dp - dl)).astype(BF)
        pb = p.astype(BF)
        dv_h = mm(pb, doh)
        dk_h = mm(ds, qh)
        dq_t[head * 64 : head * 64 + 64, cols] = mm(k_t[head * 64 : head * 64 + 64, :end], ds)
        if head == 0:
            dv_new, dk_new = dv_h, dk_h
            continue
        dv_new, dk_new = dv_new + dv_h, dk_new + dk_h
        if i:
            dv_s[: i * qb] += dv_new[: i * qb]
            dk_s[: i * qb] += dk_new[: i * qb]
        dv_s[cols] = dv_new[i * qb :]
        dk_s[cols] = dk_new[i * qb :]
    g_ref[0] = (dq_t[...] * 0.125).T.astype(BF)
    g_ref[1] = dk_s[...].astype(BF)
    g_ref[2] = dv_s[...].astype(BF)

def attend_grad(qkv, grad, out_t, stat, first, qb=256):
    slot = qkv.shape[1]
    pairs = out_t.shape[0] // 128
    width = pairs * 128
    return pl.pallas_call(
        functools.partial(attend_grad_kernel, qb),
        name="attend_grad",
        grid=(pairs,),
        in_specs=[
            pl.BlockSpec((3, slot, 128), lambda j: (0, 0, j + first)),
            pl.BlockSpec((slot, 128), lambda j: (0, j + first)),
            pl.BlockSpec((128, slot), lambda j: (j, 0)),
            pl.BlockSpec((1, 2, slot), lambda j: (j, 0, 0)),
        ],
        out_specs=pl.BlockSpec((3, slot, 128), lambda j: (0, 0, j)),
        out_shape=jax.ShapeDtypeStruct((3, slot, width), BF),
        scratch_shapes=[
            pltpu.VMEM((128, slot), BF),
            pltpu.VMEM((128, slot), BF),
            pltpu.VMEM((128, slot), BF),
            pltpu.VMEM((slot, 128), BF),
            pltpu.VMEM((128, slot), F32),
            pltpu.VMEM((slot, 128), F32),
            pltpu.VMEM((slot, 128), F32),
        ],
        compiler_params=params(1, 32 << 20),
        cost_estimate=cost(pairs * 5 * slot * slot * 256, 16e6 * pairs / 6, pairs * 2 * slot * slot),
    )(qkv, grad, out_t, stat)
VECTOR_ROWS = 16
GAIN_ONE, SHIFT_ONE, BIAS_OUT, GAIN_TWO, SHIFT_TWO, BIAS_PROJ, BIAS_QKV, BIAS_FC = 0, 1, 2, 3, 4, 5, 6, 9
branch_scale = 1.0 / math.sqrt(48.0)
norm_epsilon = 1e-05
WHOLE = dict(pipeline_mode=pl.Buffered(1))

def mm_nt(a, b):
    return lax.dot_general(a, b, (((1,), (1,)), ((), ())), preferred_element_type=F32)

def mm_tn(a, b):
    return lax.dot_general(a, b, (((0,), (0,)), ((), ())), preferred_element_type=F32)

def normalised(v):
    mean = jnp.mean(v, axis=-1, keepdims=True)
    centred = v - mean
    var = jnp.mean(centred * centred, axis=-1, keepdims=True)
    scale = lax.rsqrt(var + norm_epsilon)
    return centred * scale, scale

def norm_pull(n, scale, gain, u):
    ug = u * gain
    a = jnp.mean(ug, axis=-1, keepdims=True)
    b = jnp.mean(ug * n, axis=-1, keepdims=True)
    return (ug - a - n * b) * scale

def row_of(ref, at):
    return ref[at : at + 1, :]

def whole(shape, index=None):
    zeros = (0,) * len(shape)
    return pl.BlockSpec(shape, (lambda *_: index or zeros), **WHOLE)

def assemble(place, sources, target):
    wide = target.shape[2] // 2
    for s, source in enumerate(sources):
        for half in range(2):
            @pl.when(place[s, 0] == half)
            def _():
                for p in range(source.shape[0]):
                    target[place[s, 1 + p], :, half * wide : (half + 1) * wide] = source[p, :, :wide]

def fetch(place, sources, target, sem):
    wide = target.shape[2] // 2
    for s, source in enumerate(sources):
        lanes = pl.ds(pl.multiple_of(place[s, 0] * wide, 128), wide)
        for p in range(source.shape[0]):
            pltpu.make_async_copy(
                source.at[p, :, pl.ds(0, wide)], target.at[place[s, 1 + p], :, lanes], sem
            ).start()

def arrived(target, sem):
    pltpu.make_async_copy(target, target, sem).wait()

def project_kernel(n_src, place, x_ref, vec_ref, *rest):
    sources, (qkv_ref, low_ref, w_ref) = rest[:n_src], rest[n_src:]
    @pl.when(pl.program_id(0) == 0)
    def _():
        assemble(place, sources, w_ref)
    n, _ = normalised(x_ref[...].astype(F32))
    low = (n * row_of(vec_ref, GAIN_ONE) + row_of(vec_ref, SHIFT_ONE)).astype(BF)
    low_ref[...] = low
    d = low.shape[1]
    for part in range(3):
        w = w_ref[:, :, part * d : (part + 1) * d].reshape(d, d)
        qkv_ref[part] = (mm(low, w) + row_of(vec_ref, BIAS_QKV + part)).astype(BF)

def project(place, x, vec, sources, blocks, rows=256):
    t, d = x.shape
    r, wide = d // blocks, 3 * d // 2
    return pl.pallas_call(
        functools.partial(project_kernel, len(sources)),
        name="project",
        grid_spec=pltpu.PrefetchScalarGridSpec(
            num_scalar_prefetch=1,
            grid=(t // rows,),
            in_specs=[
                pl.BlockSpec((rows, d), lambda i, p: (i, 0)),
                whole(vec.shape),
                *[whole(s.shape) for s in sources],
            ],
            out_specs=[
                pl.BlockSpec((3, rows, d), lambda i, p: (0, i, 0)),
                pl.BlockSpec((rows, d), lambda i, p: (i, 0)),
                whole((blocks, r, 2 * wide)),
            ],
        ),
        out_shape=[
            jax.ShapeDtypeStruct((3, t, d), BF),
            jax.ShapeDtypeStruct((t, d), BF),
            jax.ShapeDtypeStruct((blocks, r, 2 * wide), BF),
        ],
        compiler_params=params(1, 32 << 20),
        cost_estimate=cost(2 * t * d * 3 * d, 18e6),
    )(place, x, vec, *sources)

def mix_kernel(n_src, place, x_ref, vec_ref, *rest):
    sources, parts, (mid_ref, low_ref, w_ref) = rest[:n_src], rest[n_src:-3], rest[-3:]
    @pl.when(pl.program_id(0) == 0)
    def _():
        assemble(place, sources, w_ref)
    d = x_ref.shape[1]
    w = w_ref[...].reshape(d, d)
    mid = x_ref[...].astype(F32) + branch_scale * (mm(jnp.concatenate([p[...] for p in parts], 1), w) + row_of(vec_ref, BIAS_OUT))
    mid_ref[...] = mid
    n, _ = normalised(mid)
    low_ref[...] = (n * row_of(vec_ref, GAIN_TWO) + row_of(vec_ref, SHIFT_TWO)).astype(BF)

def mix(place, parts, x, vec, sources, blocks, column, rows=256):
    t, d = x.shape
    r, np_ = d // blocks, sources[0].shape[0]
    return pl.pallas_call(
        functools.partial(mix_kernel, len(sources)),
        name="mix",
        grid_spec=pltpu.PrefetchScalarGridSpec(
            num_scalar_prefetch=1,
            grid=(t // rows,),
            in_specs=[
                pl.BlockSpec((rows, d), lambda i, p: (i, 0)),
                whole(vec.shape),
                *[whole((np_, r, d // 2), (0, 0, column)) for s in sources],
                *[pl.BlockSpec((rows, p.shape[1]), lambda i, p: (i, 0)) for p in parts],
            ],
            out_specs=[
                pl.BlockSpec((rows, d), lambda i, p: (i, 0)),
                pl.BlockSpec((rows, d), lambda i, p: (i, 0)),
                whole((blocks, r, d)),
            ],
        ),
        out_shape=[
            jax.ShapeDtypeStruct((t, d), F32),
            jax.ShapeDtypeStruct((t, d), BF),
            jax.ShapeDtypeStruct((blocks, r, d), BF),
        ],
        compiler_params=params(1, 24 << 20),
        cost_estimate=cost(2 * t * d * d, 9e6),
    )(place, x, vec, *sources, *parts)

def mlp_kernel(n_src, rb, core, place, wide_place, lens, low_ref, cot_ref, bias_ref, mid_hbm, *rest):
    fcs, projs, rest = rest[: n_src[0]], rest[n_src[0] : sum(n_src)], rest[sum(n_src) :]
    (out_hbm, gmid_hbm, gbr_hbm, fsend_hbm, fkeep_hbm, psend_ref, pkeep_ref, fbg_ref, vec_ref,
     fc_s, proj_s, low_t, g2_s, second_s, act_s, gpre_s, mid_s, out_s, gmid_s, gbr_s, f_s, sems) = rest
    t, d = mid_s.shape
    w, h = 2 * d, d // 2
    step = pl.program_id(0)
    mine = core[0]
    chunk = lax.rem(step + 1 - mine, 2)
    mid_copy = pltpu.make_async_copy(mid_hbm, mid_s, sems.at[2])
    outs = [
        pltpu.make_async_copy(a, b, sems.at[3 + k])
        for k, (a, b) in enumerate(
            ((out_s, out_hbm), (gmid_s, gmid_hbm), (gbr_s, gbr_hbm), (f_s.at[0], fsend_hbm), (f_s.at[1], fkeep_hbm))
        )
    ]
    def valid_rows(at):
        return (at * rb + lax.broadcasted_iota(jnp.int32, (rb, 1), 0)) < lens[0]
    @pl.when(step == 0)
    def _():
        fetch(wide_place, projs, proj_s, sems.at[0])
        fetch(place, fcs, fc_s, sems.at[1])
        mid_copy.start()
        low_t[...] = low_ref[...].T
        def begin(i, total):
            at = pl.ds(pl.multiple_of(i * rb, rb), rb)
            g = jnp.where(valid_rows(i), branch_scale * cot_ref[at, :].astype(F32), 0.0).astype(BF)
            g2_s[at, :] = g
            return total + jnp.sum(g.astype(F32), axis=0, keepdims=True)
        vec_ref[0:1] = lax.fori_loop(0, t // rb, begin, jnp.zeros((1, d), F32))
        arrived(proj_s, sems.at[0])
        arrived(fc_s, sems.at[1])
        mid_copy.wait()
    fc = fc_s.at[:, :, pl.ds(pl.multiple_of(chunk * w, w), w)]
    bias = jnp.concatenate([bias_ref[pl.ds(BIAS_FC + 2 * chunk + i, 1), :] for i in range(2)], 1)
    blocks, pr = proj_s.shape[0], proj_s.shape[1]
    if blocks > 1:
        proj = proj_s.at[pl.ds(chunk * (blocks // 2), blocks // 2)]
    else:
        proj = proj_s.at[:, pl.ds(pl.multiple_of(chunk * w, w), w)]
    def rows_step(i, total):
        at = pl.ds(pl.multiple_of(i * rb, rb), rb)
        wf = fc[...].reshape(d, w)
        wp = proj[...].reshape(w, d)
        ga = mm_nt(g2_s[at, :], wp)
        u = mm(low_ref[at, :], wf) + bias
        sq = u * u
        th = jnp.tanh(u * (0.7978845608028654 + (0.7978845608028654 * 0.044715) * sq))
        up = 0.5 + 0.5 * th
        act = (u * up).astype(BF)
        act_s[at, :] = act
        slope = up * (1.0 + (1.0 - up) * (u * (2 * 0.7978845608028654 + (6 * 0.7978845608028654 * 0.044715) * sq)))
        gpb = (ga * slope).astype(BF)
        gpre_s[at, :] = gpb
        more, back = mm(act, wp), mm_nt(gpb, wf)
        @pl.when(step == 0)
        def _():
            second_s[at, :] = more
            gmid_s[at, :] = back
        @pl.when(step == 1)
        def _():
            second_s[at, :] += more
            gmid_s[at, :] += back
        return total + jnp.sum(gpb.astype(F32), axis=0, keepdims=True)
    sums = lax.fori_loop(0, t // rb, rows_step, jnp.zeros((1, w), F32))
    for i in range(2):
        fbg_ref[pl.ds(2 * chunk + i, 1), :] = sums[:, i * d : (i + 1) * d]
    @pl.when(step == 1)
    def _():
        def finish(i, carry):
            at = pl.ds(pl.multiple_of(i * rb, rb), rb)
            mid = mid_s[at, :]
            out_s[at, :] = (mid + branch_scale * (second_s[at, :] + row_of(bias_ref, BIAS_PROJ))).astype(BF)
            n, scale = normalised(mid)
            gh = gmid_s[at, :]
            cot = jnp.where(valid_rows(i), cot_ref[at, :].astype(F32), 0.0)
            gm = cot + norm_pull(n, scale, row_of(bias_ref, GAIN_TWO), gh)
            gmid_s[at, :] = gm
            gb = (branch_scale * gm).astype(BF)
            gbr_s[at, :] = gb
            return (carry[0] + jnp.sum(gh * n, axis=0, keepdims=True),
                    carry[1] + jnp.sum(gh, axis=0, keepdims=True),
                    carry[2] + jnp.sum(gb.astype(F32), axis=0, keepdims=True))
        zero = jnp.zeros((1, d), F32)
        a, b, c = lax.fori_loop(0, t // rb, finish, (zero, zero, zero))
        vec_ref[1:2] = a
        vec_ref[2:3] = b
        vec_ref[3:4] = c
        for copy in outs[:3]:
            copy.start()
    f_s[step] = mm(low_t[...], gpre_s[...]).astype(BF).reshape(f_s.shape[1:])
    @pl.when(step == 0)
    def _():
        outs[3].start()
    @pl.when(step == 1)
    def _():
        outs[4].start()
    dproj = mm_tn(act_s[...], g2_s[...]).astype(BF)
    for half in range(2):
        @pl.when(mine == half)
        def _():
            pkeep_ref[...] = dproj[:, half * h : (half + 1) * h].reshape(pkeep_ref.shape)
            psend_ref[...] = dproj[:, (1 - half) * h : (2 - half) * h].reshape(psend_ref.shape)
    @pl.when(step == 1)
    def _():
        for copy in outs:
            copy.wait()

def mlp(core, place, wide_place, lens, mid, low, cot, vec, fcs, projs, blocks, rb=256):
    t, d = mid.shape
    r, pr = d // blocks, 4 * d // blocks
    smem, hbm = pl.BlockSpec(memory_space=pltpu.SMEM), pl.BlockSpec(memory_space=pl.ANY)
    turn = lambda i, c: lax.rem(i + 1 - c[0], 2)
    if blocks > 1:
        pspec = pl.BlockSpec((blocks // 2, pr, d // 2), lambda i, c: (turn(i, c), 0, 0))
    else:
        pspec = pl.BlockSpec((1, pr // 2, d // 2), lambda i, c: (0, turn(i, c), 0))
    of = jax.ShapeDtypeStruct
    return pl.pallas_call(
        functools.partial(mlp_kernel, (len(fcs), len(projs)), rb),
        name="mlp",
        grid_spec=pltpu.PrefetchScalarGridSpec(
            num_scalar_prefetch=1,
            grid=(2,),
            in_specs=[smem, smem, smem, whole((t, d)), whole((t, d)), whole(vec.shape), hbm] + [hbm] * len(fcs + projs),
            out_specs=[hbm] * 5 + [pspec, pspec, whole((4, d)), whole((4, d))],
            scratch_shapes=[
                pltpu.VMEM((blocks, r, 4 * d), BF),
                pltpu.VMEM((blocks, pr, d), BF),
                pltpu.VMEM((d, t), BF),
                pltpu.VMEM((t, d), BF),
                pltpu.VMEM((t, d), F32),
                pltpu.VMEM((t, 2 * d), BF),
                pltpu.VMEM((t, 2 * d), BF),
                pltpu.VMEM((t, d), F32),
                pltpu.VMEM((t, d), BF),
                pltpu.VMEM((t, d), F32),
                pltpu.VMEM((t, d), BF),
                pltpu.VMEM((2, blocks, r, 2 * d), BF),
                pltpu.SemaphoreType.DMA((8,)),
            ],
        ),
        out_shape=[
            of((t, d), BF), of((t, d), F32), of((t, d), BF),
            of((blocks, r, 2 * d), BF), of((blocks, r, 2 * d), BF),
            of((blocks, pr, d // 2), BF), of((blocks, pr, d // 2), BF),
            of((4, d), F32), of((4, d), F32),
        ],
        compiler_params=params(),
        cost_estimate=cost(12 * t * d * 4 * d, 40e6, t * 4 * d),
    )(core, place, wide_place, lens, low, cot, vec, mid, *fcs, *projs)

def unmix_kernel(core, lens, gbr_ref, w_ref, *rest):
    parts, (ga_ref, send_ref, keep_ref) = rest[:-3], rest[-3:]
    t, d = gbr_ref.shape
    w = w_ref[...].reshape(d, d)
    seen = lax.broadcasted_iota(jnp.int32, (t, 1), 0) < lens[0]
    ga_ref[...] = jnp.where(seen, mm_nt(gbr_ref[...], w), 0.0).astype(BF)
    dw = jnp.concatenate([mm_tn(p[...], gbr_ref[...]).astype(BF) for p in parts], 0)
    h = d // 2
    for half in range(2):
        @pl.when(core[0] == half)
        def _():
            keep_ref[...] = dw[:, half * h : (half + 1) * h].reshape(keep_ref.shape)
            send_ref[...] = dw[:, (1 - half) * h : (2 - half) * h].reshape(send_ref.shape)

def unmix(core, lens, gbr, parts, w, blocks):
    t, d = gbr.shape
    smem = pl.BlockSpec(memory_space=pltpu.SMEM)
    piece = jax.ShapeDtypeStruct((blocks, d // blocks, d // 2), BF)
    return pl.pallas_call(
        unmix_kernel,
        name="unmix",
        in_specs=[smem, smem] + [pl.BlockSpec(memory_space=pltpu.VMEM)] * (2 + len(parts)),
        out_shape=[jax.ShapeDtypeStruct((t, d), BF), piece, piece],
        compiler_params=params(0, 24 << 20),
        cost_estimate=cost(4 * t * d * d, 9e6),
    )(core, lens, gbr, w, *parts)

def unproject_kernel(blocks, core, low_ref, g_ref, send_ref, keep_ref, sums_ref):
    d, w = low_ref.shape[1], g_ref.shape[2]
    r, h = d // blocks, w // 2
    low_t = low_ref[...].T
    q, k, v = [mm(low_t, g_ref[part]).astype(BF).reshape(blocks, r, w) for part in range(3)]
    for half, refs in ((0, (keep_ref, send_ref)), (1, (send_ref, keep_ref))):
        @pl.when(core[0] == half)
        def _():
            refs[0][:, :, :w] = q
            refs[0][:, :, w:] = k[:, :, :h]
            refs[1][:, :, :h] = k[:, :, h:]
            refs[1][:, :, h:] = v
    for part in range(3):
        sums_ref[part : part + 1] = jnp.sum(g_ref[part].astype(F32), axis=0, keepdims=True)

def unproject(core, low, g, blocks):
    t, d = low.shape
    w = g.shape[2]
    piece = jax.ShapeDtypeStruct((blocks, d // blocks, w // 2 * 3), BF)
    return pl.pallas_call(
        functools.partial(unproject_kernel, blocks),
        name="unproject",
        in_specs=[pl.BlockSpec(memory_space=pltpu.SMEM)] + [pl.BlockSpec(memory_space=pltpu.VMEM)] * 2,
        out_shape=[piece, piece, jax.ShapeDtypeStruct((3, w), F32)],
        compiler_params=params(0, 24 << 20),
        cost_estimate=cost(6 * t * d * w, 10e6 * w / d),
    )(core, low, g)

def route_kernel(count, steps, rows, near, table, *refs):
    inputs, outs = refs[: 2 * count + near], refs[2 * count + near :]
    def write(ref):
        at = 0
        for k, g in zip(inputs[:count], inputs[count : 2 * count]):
            r, w = k.shape[-2:]
            place = (slice(at, at + r), slice(0, w)) if rows else (slice(0, r), slice(at, at + w))
            at += r if rows else w
            total = (k[...].astype(F32) + g[...].astype(F32)).reshape(1, ref.shape[1], r, w)
            came = [v[:, :, place[0], place[1]] for v in inputs[2 * count :]]
            if near == 2:
                came = [jnp.where(table[pl.program_id(0), 2] == 0, *came)]
            if near:
                total = total + came[0].astype(F32)
            ref[:, :, place[0], place[1]] = total.astype(BF)
    for s, ref in enumerate(outs):
        @pl.when(pl.program_id(0) // steps == s)
        def _():
            write(ref)

def route(table, keeps, gots, near=(), rows=False, split=False):
    z = keeps[0].shape[0]
    sizes = [k.shape[-2:] for k in keeps]
    tall = sum(r for r, _ in sizes) if rows else sizes[0][0]
    wide = sizes[0][1] if rows else sum(w for _, w in sizes)
    block = (1, z, tall, wide)
    specs = [pl.BlockSpec((z, 1, 1, *s), lambda i, t: (0, t[i, 0], t[i, 1], 0, 0)) for s in sizes] * 2
    fixed = pl.BlockSpec(block, lambda i, t: (0, 0, 0, 0))
    if near or split:
        steps, outs = 1, [fixed] * 2
        specs += [pl.BlockSpec(block, lambda i, t: (t[i, 2], 0, 0, 0))] if len(near) == 1 else [fixed] * len(near)
    else:
        steps, outs = 2, [pl.BlockSpec(block, lambda i, t: (i, 0, 0, 0))]
    return pl.pallas_call(
        functools.partial(route_kernel, len(keeps), steps, rows, len(near)),
        name="route",
        grid_spec=pltpu.PrefetchScalarGridSpec(
            num_scalar_prefetch=1, grid=(2,), in_specs=specs, out_specs=outs
        ),
        out_shape=[jax.ShapeDtypeStruct((steps, z, tall, wide), BF)] * len(outs),
        compiler_params=params(1, 24 << 20),
        cost_estimate=cost(1e6, 2 * z * tall * wide * 6),
    )(table, *keeps, *gots, *near)

def final_kernel(x_ref, w_ref, gmid_ref, bias_ref, *rest):
    parts, (out_ref, vec_ref) = rest[:-2], rest[-2:]
    d = x_ref.shape[1]
    w = w_ref[...].reshape(d, 3 * d)
    gh = jnp.zeros(x_ref.shape, F32)
    at = 0
    for g in parts:
        for i in range(3):
            gh = gh + mm_nt(g[i], w[:, i * d + at : i * d + at + g.shape[2]])
        at += g.shape[2]
    n, scale = normalised(x_ref[...].astype(F32))
    out_ref[...] = (gmid_ref[...] + norm_pull(n, scale, row_of(bias_ref, GAIN_ONE), gh)).astype(BF)
    @pl.when(pl.program_id(0) == 0)
    def _():
        vec_ref[...] = jnp.zeros_like(vec_ref)
    vec_ref[0:1] += jnp.sum(gh * n, axis=0, keepdims=True)
    vec_ref[1:2] += jnp.sum(gh, axis=0, keepdims=True)

def final(x, parts, w, gmid, vec, rows=256):
    t, d = x.shape
    return pl.pallas_call(
        final_kernel,
        name="final",
        grid=(t // rows,),
        in_specs=[
            pl.BlockSpec((rows, d), lambda i: (i, 0)),
            whole(w.shape),
            pl.BlockSpec((rows, d), lambda i: (i, 0)),
            whole(vec.shape),
            *[pl.BlockSpec((3, rows, g.shape[2]), lambda i: (0, i, 0)) for g in parts],
        ],
        out_specs=[pl.BlockSpec((rows, d), lambda i: (i, 0)), whole((2, d))],
        out_shape=[jax.ShapeDtypeStruct((t, d), BF), jax.ShapeDtypeStruct((2, d), F32)],
        compiler_params=params(1, 32 << 20),
        cost_estimate=cost(6 * t * d * d, 15e6),
    )(x, w, gmid, vec, *parts)
def spread_matrix(size, width):
    row = lax.broadcasted_iota(jnp.int32, (128, width), 0).astype(F32)
    col = lax.broadcasted_iota(jnp.int32, (128, width), 1).astype(F32)
    inside = col - jnp.floor((col + 0.5) / size) * size
    return jnp.where(inside == row, 1.0, 0.0)

def own_columns(count, size, per, width):
    at = lax.broadcasted_iota(jnp.int32, (count, width), 0).astype(F32)
    at = at - jnp.floor((at + 0.5) / per) * per
    col = lax.broadcasted_iota(jnp.int32, (count, width), 1).astype(F32)
    return jnp.logical_and(col >= at * size, col < (at + 1) * size)


def unfold_vectors(rows_of, count, out_ref):
    d = out_ref.shape[1]
    out_ref[...] = jnp.zeros_like(out_ref)
    for rows, slots, first in ((1, range(6), 0), (2, (6,), BIAS_QKV), (4, (7,), BIAS_FC)):
        size, per = d * rows // count, count // rows
        spread = spread_matrix(size, d).astype(BF)
        mine = own_columns(count, size, per, d)
        for s in slots:
            got = jnp.where(mine, mm(rows_of(s), spread), 0.0)
            for r in range(rows):
                to = first + (s if rows == 1 else 2 * r if rows == 2 else r)
                out_ref[to : to + 1] = jnp.sum(got[r * per : (r + 1) * per], axis=0, keepdims=True)

def unfold_kernel(x_ref, out_ref):
    unfold_vectors(lambda s: x_ref[s], x_ref.shape[1], out_ref)

def unfold(x, d):
    return pl.pallas_call(
        unfold_kernel,
        name="unfold",
        in_specs=[pl.BlockSpec(memory_space=pltpu.VMEM)],
        out_shape=jax.ShapeDtypeStruct((VECTOR_ROWS, d), F32),
        compiler_params=params(0, 16 << 20),
        cost_estimate=cost(1e8, 1e6),
    )(x)

def unfold_pieces_kernel(n_src, place, *rest):
    sources, out_ref, x_ref = rest[:n_src], rest[n_src], rest[-1]
    r = sources[0].shape[1] // 2
    for s, source in enumerate(sources):
        for p in range(source.shape[0]):
            tile = source[p].astype(F32)
            for c in range(2):
                x_ref[2 * place[s, 1 + p] + c] = tile[c * r : c * r + 8]
    unfold_vectors(lambda s: x_ref[:, s, :].astype(BF), x_ref.shape[0], out_ref)

def unfold_pieces(place, sources, count, d):
    np_, r, wide = sources[0].shape
    return pl.pallas_call(
        functools.partial(unfold_pieces_kernel, len(sources)),
        name="unfold",
        grid_spec=pltpu.PrefetchScalarGridSpec(
            num_scalar_prefetch=1,
            grid=(1,),
            in_specs=[whole((np_, r, 128), (0, 0, wide // 128 - 1)) for _ in sources],
            out_specs=whole((VECTOR_ROWS, d)),
            scratch_shapes=[pltpu.VMEM((count, 8, 128), F32)],
        ),
        out_shape=jax.ShapeDtypeStruct((VECTOR_ROWS, d), F32),
        compiler_params=params(1, 16 << 20),
        cost_estimate=cost(1e8, 1e6),
    )(place, *sources)

def fold_kernel(first_ref, sums_ref, qkv_ref, fc_ref, out_ref):
    count, d = out_ref.shape[1], first_ref.shape[1]
    singles = [
        first_ref[0:1], first_ref[1:2], sums_ref[3:4], sums_ref[1:2], sums_ref[2:3], sums_ref[0:1],
    ]
    pairs = [[v] for v in singles] + [[qkv_ref[0:1], qkv_ref[2:3]], [fc_ref[r : r + 1] for r in range(4)]]
    for rows, slots in ((1, range(6)), (2, (6,)), (4, (7,))):
        size, per = d * rows // count, count // rows
        spread = spread_matrix(size, d)
        mine = own_columns(count, size, per, d)
        full = jnp.concatenate(
            [
                jnp.where(mine, jnp.concatenate([jnp.broadcast_to(v, (per, d)) for v in pairs[s]], 0), 0.0)
                for s in slots
            ],
            0,
        )
        got = lax.dot_general(
            full, spread, (((1,), (1,)), ((), ())), precision=lax.Precision.HIGHEST, preferred_element_type=F32
        )
        for i, s in enumerate(slots):
            out_ref[s] = got[i * count : (i + 1) * count]

def fold(first, sums, qkv, fc, count):
    return pl.pallas_call(
        fold_kernel,
        name="fold",
        in_specs=[pl.BlockSpec(memory_space=pltpu.VMEM)] * 4,
        out_shape=jax.ShapeDtypeStruct((8, count, 128), F32),
        compiler_params=params(0, 32 << 20),
        cost_estimate=cost(1e8, 1e6),
    )(first, sums, qkv, fc)


class Grid:
    order = (0, 2, 1, 3)

    def __init__(self, mesh, rows):
        wide, narrow = mesh.shape["wide"], mesh.shape["narrow"]
        self.count = wide * narrow
        self.paired = narrow == 4 and wide == 8 and rows % 8 == 0
        self.blocks = self.count // 2 if self.paired else 1
        self.z = wide // 2

    def index(self, z, x, y, c):
        return ((z * 2 + x) * 2 + y) * 2 + c

    def places(self):
        return [
            (z, x, y, c) for z in range(self.z) for x in range(2) for y in range(2) for c in range(2)
        ]

    def perm(self, target):
        return [(self.index(*at), self.index(*target(*at))) for at in self.places()]

    def here(self):
        w, n = lax.axis_index("wide"), lax.axis_index("narrow")
        return w // 2, w % 2, n // 2, n % 2

    def table(self):
        rows = []
        for z0, x0, y0, c0 in self.places():
            mine = []
            for half in (c0, 1 - c0):
                for ka, kb in ((0, 0), (1, 0), (0, 1), (1, 1)):
                    kx, ky = (ka, kb) if half == 0 else (kb, ka)
                    blocks = [
                        ((z0 ^ kz) * 2 + (x0 ^ kx)) * 2 + (y0 ^ ky) for kz in self.order
                    ]
                    mine.append([half] + blocks)
            rows.append(mine)
        return np.array(rows, np.int32)

    def wide_table(self):
        rows = []
        for z0, x0, y0, c0 in self.places():
            mine = []
            for half in (c0, 1 - c0):
                for kb in (0, 1):
                    line = [half]
                    for kz in self.order:
                        for ka in (0, 1):
                            kx, ky = (ka, kb) if half == 0 else (kb, ka)
                            line.append(((z0 ^ kz) * 2 + (x0 ^ kx)) * 2 + (y0 ^ ky))
                    mine.append(line)
            rows.append(mine)
        return np.array(rows, np.int32)

    def routes(self):
        near, far = [], []
        for z0, x0, y0, c0 in self.places():
            if c0 == 0:
                near.append([[1 - x0, 0], [1 - x0, 1]])
                far.append([[x0, 1 - y0, 1 - y0], [x0, y0, y0]])
            else:
                near.append([[0, 1 - y0], [1, 1 - y0]])
                far.append([[1 - x0, y0, 1 - x0], [x0, y0, x0]])
        return np.array(near, np.int32), np.array(far, np.int32)

    def send(self, value, target):
        return lax.ppermute(value, AXES, self.perm(target))

    def other_core(self, value):
        return self.send(value, lambda z, x, y, c: (z, x, y, 1 - c))

    def along(self, value, turn):
        return self.send(
            value,
            lambda z, x, y, c: (z, 1 - x, y, c) if c == turn else (z, x, 1 - y, c),
        )

    def up(self, value, k):
        return self.send(value, lambda z, x, y, c: (z ^ k, x, y, c))


def both(first, own, other, axis):
    return jnp.where(
        first, jnp.concatenate([own, other], axis), jnp.concatenate([other, own], axis)
    )


def pair_rows(grid, shard, extra=None):
    c = grid.here()[3]
    h = shard.shape[1] // 2
    mine = lax.dynamic_slice_in_dim(shard, c * h, h, 1)
    away = lax.dynamic_slice_in_dim(shard, (1 - c) * h, h, 1)
    if extra is not None:
        mine, away = jnp.concatenate([mine, extra], 1), jnp.concatenate([away, extra], 1)
    return both(c == 0, mine, grid.other_core(away), 0)


def spread_z(grid, pair):
    return jnp.stack([pair] + [grid.up(pair, k) for k in grid.order[1:]])


def with_other(grid, sources):
    return sources + [grid.other_core(s) for s in sources]


def stage(*values):
    return lax.optimization_barrier(values)


def after(value, *earlier):
    return lax.optimization_barrier((value, *earlier))[0]


def add(a, b):
    return (a.astype(F32) + b.astype(F32)).astype(BF)


def pick(v, at, axis):
    return lax.dynamic_index_in_dim(v, at, axis, keepdims=False)


class Sum:
    def __init__(self, grid, tables, sends, keeps, rows=False, split=False):
        self.grid, self.tables, self.rows_under, self.split = grid, tables, rows, split
        self.shape = (grid.z, 2, 2)
        self.keeps = keeps
        self.got = [grid.other_core(s) for s in sends]

    def core(self):
        block = lambda v: v.reshape(*self.shape, *v.shape[1:])
        self.keeps, self.got = [block(k) for k in self.keeps], [block(g) for g in self.got]
        self.away = route(self.tables[0], self.keeps, self.got, (), self.rows_under, self.split)
        return self.away

    def near(self):
        self.came = [self.grid.along(v, 0) for v in self.away]

    def middle(self):
        self.away, self.stay = route(self.tables[1], self.keeps, self.got, self.came, self.rows_under)
        return self.away

    def far(self):
        self.got = self.grid.along(self.away, 1)

    def last(self):
        self.own = add(self.stay, self.got)[0]
        return self.own

    def up(self):
        z = self.grid.here()[0]
        away = jnp.stack([pick(self.own, z ^ 1, 0), pick(self.own, z ^ 3, 0)])
        self.stay = jnp.stack([pick(self.own, z, 0), pick(self.own, z ^ 2, 0)])
        self.got = self.grid.up(away, 1)

    def across(self):
        self.stay = add(self.stay, self.got)
        self.got = self.grid.up(self.stay[1], 2)

    def rows(self):
        return self.stay[0].astype(F32) + self.got.astype(F32)


def own_rows(grid, total):
    c = grid.here()[3]
    r = total.shape[0] // 2
    other = grid.other_core(lax.dynamic_slice_in_dim(total, (1 - c) * r, r, 0))
    return both(c == 0, lax.dynamic_slice_in_dim(total, c * r, r, 0), other, 1)


def stack_small(vectors):
    total = jnp.zeros((8, 128), BF)
    for i, v in enumerate(vectors):
        total = total + jnp.pad(v.reshape(1, -1), ((i, 7 - i), (0, 128 - v.shape[0])))
    return total


def gather_small(count, vectors):
    flat = stack_small(vectors)
    return lax.all_to_all(jnp.broadcast_to(flat[:, None], (8, count, 128)), AXES, 1, 1, tiled=True)


def scatter_small(cut):
    return jnp.sum(lax.all_to_all(cut, AXES, 1, 1, tiled=True), axis=1)


def halves_of(weight):
    h = weight.shape[1] // 2
    return [weight[None, :, :h], weight[None, :, h:]]


def local(
    mesh,
    tokens,
    norm1_gain,
    norm1_bias,
    qkv_weight,
    qkv_bias,
    out_weight,
    out_bias,
    norm2_gain,
    norm2_bias,
    fc_weight,
    fc_bias,
    proj_weight,
    proj_bias,
    seq_lengths,
    out_cotangent,
):
    d = tokens.shape[1]
    grid = Grid(mesh, out_weight.shape[0])
    blocks = grid.blocks
    vectors = [norm1_gain, norm1_bias, out_bias, norm2_gain, norm2_bias, proj_bias, qkv_bias, fc_bias]
    if grid.paired:
        place = jnp.asarray(grid.table())[lax.axis_index(AXES)]
        wide_place = jnp.asarray(grid.wide_table())[lax.axis_index(AXES)]
        tables = [jnp.asarray(v)[lax.axis_index(AXES)] for v in grid.routes()]
        core = grid.here()[3].reshape(1).astype(jnp.int32)
        extra = jnp.pad(stack_small(vectors), ((0, qkv_weight.shape[0] - 8), (0, 0)))
        pair_qkv = pair_rows(grid, qkv_weight, extra)
        place, fc_shard, out_shard, proj_shard, pair_qkv = stage(
            place, fc_weight, out_weight, proj_weight, pair_qkv
        )
        stack_qkv = spread_z(grid, pair_qkv)
        first = jnp.concatenate([pair_rows(grid, fc_shard), pair_rows(grid, out_shard)], 1)
        second = pair_rows(grid, proj_shard)
        near_second = grid.along(second, 0)
        stack_qkv, first, second, near_second = stage(stack_qkv, first, second, near_second)
        two_second = jnp.stack([second, near_second])
        near_qkv, far_qkv = grid.along(stack_qkv, 0), grid.along(stack_qkv, 1)
        two_first = grid.up(first, 2)
        others = [grid.other_core(stack_qkv)]
        near_qkv, far_qkv, two_first, *others = stage(near_qkv, far_qkv, two_first, *others)
        last_qkv = grid.along(near_qkv, 1)
        two_first = jnp.stack([first, two_first])
        four_first = grid.up(two_first, 1)
        across_second = grid.up(two_second, 2)
        others += [grid.other_core(v) for v in (near_qkv, far_qkv)]
        last_qkv, across_second, two_first, four_first, *others = stage(
            last_qkv, across_second, two_first, four_first, *others
        )
        qkv_sources = [stack_qkv, near_qkv, far_qkv, last_qkv, *others, grid.other_core(last_qkv)]
        stack_first = jnp.concatenate([two_first, four_first])
        near_first, far_first = grid.along(stack_first, 0), grid.along(stack_first, 1)
        four_second = jnp.concatenate([two_second, across_second])
        beyond_second = grid.up(four_second, 1)
        others = [grid.other_core(stack_first)]
        *qkv_sources, stack_first = stage(*qkv_sources, stack_first)
        vec = unfold_pieces(place, qkv_sources[:4], grid.count, d)
    else:
        place = wide_place = jnp.asarray(np.array([[0, 0], [1, 0]], np.int32))
        core = jnp.zeros((1,), jnp.int32)
        full = lambda v: lax.all_gather(v, AXES, axis=0, tiled=True)
        qkv_sources = halves_of(full(qkv_weight))
        vec = unfold(gather_small(grid.count, vectors), d)
    qkv, low_one, qkv_full = project(
        place, tokens, vec, qkv_sources, blocks
    )
    if grid.paired:
        qkv, four_second, beyond_second, near_first, far_first, *others = stage(
            qkv, four_second, beyond_second, near_first, far_first, *others
        )
        stack_second = jnp.concatenate([four_second, beyond_second])
        last_first = grid.along(near_first, 1)
        far_second = grid.along(stack_second, 1)
        others += [grid.other_core(near_first), grid.other_core(far_first)]
    attended = [list(attend(seq_lengths, qkv, 4, 0, 512))]
    if grid.paired:
        attended[0][2], qkv, *others = stage(attended[0][2], qkv, *others)
        second_others = [grid.other_core(stack_second)]
    else:
        fcs = halves_of(full(fc_weight))
        outs, out_at = halves_of(full(out_weight)), 0
        projs = halves_of(full(proj_weight))
    attended.append(attend(seq_lengths, qkv, 2, 4, 512))
    mixed = [a[1] for a in attended]
    if grid.paired:
        mixed[1], last_first, *second_others = stage(mixed[1], last_first, *second_others)
        outs = [stack_first, near_first, far_first, last_first, *others, grid.other_core(last_first)]
        fcs, out_at = outs, 4
    middle, low_two, out_full = mix(
        place, mixed, tokens, vec, outs, blocks, out_at
    )
    if grid.paired:
        low_two, far_second = stage(low_two, far_second)
        projs = [stack_second, far_second, *second_others, grid.other_core(far_second)]
    (layer_out, grad_middle, grad_branch, fc_send, fc_keep, proj_send, proj_keep, fc_bias_term, sums) = mlp(
        core, place, wide_place, seq_lengths, middle, low_two, out_cotangent, vec,
        fcs, projs, blocks,
    )
    grad_mixed, out_send, out_keep = unmix(core, seq_lengths, grad_branch, mixed, out_full, blocks)
    if grid.paired:
        fc_sum = Sum(grid, tables, [fc_send], [fc_keep])
        proj_sum = Sum(grid, tables, [proj_send, out_send], [proj_keep, out_keep], True)
        grad_mixed, *fc_sum.away = stage(grad_mixed, *fc_sum.core())
        fc_sum.near()
        grad_mixed, *proj_sum.away = stage(grad_mixed, *proj_sum.core())
        proj_sum.near()
    grad_one = attend_grad(qkv, grad_mixed, attended[0][0], attended[0][2], 0)
    qkv_one = list(unproject(core, low_one, grad_one, blocks))
    if grid.paired:
        qkv_one[2], grad_mixed, fc_sum.came[0], proj_sum.came[0] = stage(
            qkv_one[2], grad_mixed, fc_sum.came[0], proj_sum.came[0]
        )
        fc_sum.middle()
        fc_sum.far()
        proj_sum.middle()
        grad_mixed, fc_sum.stay, proj_sum.away, proj_sum.stay = stage(
            grad_mixed, fc_sum.stay, proj_sum.away, proj_sum.stay
        )
        proj_sum.far()
    grad_two = attend_grad(qkv, grad_mixed, attended[1][0], attended[1][2], 4)
    if grid.paired:
        fc_sum.got, grad_two = stage(fc_sum.got, grad_two)
        fc_sum.last()
        fc_sum.up()
    grads = [grad_one, grad_two]
    qkv_two = unproject(core, low_one, grad_two, blocks)
    if grid.paired:
        qkv_sum = Sum(grid, tables, [qkv_one[0], qkv_two[0]], [qkv_one[1], qkv_two[1]])
        *qkv_sum.got, proj_sum.got = stage(*qkv_sum.got, proj_sum.got)
        grad_middle, *qkv_sum.away = stage(grad_middle, *qkv_sum.core())
        qkv_sum.near()
        grad_middle, proj_sum.own = stage(grad_middle, proj_sum.last())
        proj_sum.up()
    input_grad, first_sums = final(tokens, grads, qkv_full, grad_middle, vec)
    qkv_sums = jnp.concatenate([qkv_one[2], qkv_two[2]], 1)
    cut = fold(first_sums, sums, qkv_sums, fc_bias_term, grid.count)
    if grid.paired:
        cut, qkv_sum.came[0], proj_sum.got, fc_sum.got = stage(cut, qkv_sum.came[0], proj_sum.got, fc_sum.got)
        qkv_sum.middle()
        qkv_sum.far()
        fc_sum.across()
        proj_sum.stay = add(proj_sum.stay, proj_sum.got)
        cut, qkv_sum.got, fc_sum.got, proj_sum.stay = stage(cut, qkv_sum.got, fc_sum.got, proj_sum.stay)
        proj_sum.got = grid.up(proj_sum.stay[1], 2)
        qkv_sum.last()
        qkv_sum.up()
    little = scatter_small(cut)
    if grid.paired:
        qkv_sum.across()
        fc_sum.got, proj_sum.got, qkv_sum.stay = stage(fc_sum.got, proj_sum.got, qkv_sum.stay)
        fc_weight_grad = own_rows(grid, fc_sum.rows())
        total = proj_sum.rows()
        proj_rows = proj_keep.shape[1]
        proj_weight_grad = own_rows(grid, total[:proj_rows])
        out_weight_grad = own_rows(grid, total[proj_rows:])
        shards = [little[s, : vectors[s].shape[0]] for s in range(8)]
        fc_weight_grad, proj_weight_grad, out_weight_grad, qkv_sum.got, *shards = stage(
            fc_weight_grad, proj_weight_grad, out_weight_grad, qkv_sum.got, *shards
        )
        total = qkv_sum.rows()
        wide = qkv_one[1].shape[2]
        ends = [own_rows(grid, total[:, :wide]), own_rows(grid, total[:, wide:])]
    else:
        reduce = lambda v: lax.psum_scatter(v.astype(F32), AXES, scatter_dimension=0, tiled=True)
        side = lambda k, s: jnp.concatenate([k[0], s[0]], 1)
        fc_weight_grad = reduce(side(fc_keep, fc_send))
        out_weight_grad = reduce(side(out_keep, out_send))
        ends = [reduce(side(u[1], u[0])) for u in (qkv_one, qkv_two)]
        proj_weight_grad = reduce(side(proj_keep, proj_send))
        shards = [little[s, : vectors[s].shape[0]] for s in range(8)]
    third = lambda e, i: e[:, i * e.shape[1] // 3 : (i + 1) * e.shape[1] // 3]
    qkv_weight_grad = jnp.concatenate([third(e, i) for i in range(3) for e in ends], 1)
    shard = lambda s: shards[s]
    return (
        layer_out,
        input_grad,
        shard(0),
        shard(1),
        qkv_weight_grad,
        shard(6),
        out_weight_grad,
        shard(2),
        shard(3),
        shard(4),
        fc_weight_grad,
        shard(7),
        proj_weight_grad,
        shard(5),
    )


def solution(mesh):
    matrix, vector = P(AXES, None), P(AXES)
    ins = (
        matrix, vector, vector, matrix, vector, matrix, vector, vector,
        vector, matrix, vector, matrix, vector, vector, matrix,
    )
    outs = (
        matrix, matrix, vector, vector, matrix, vector, matrix, vector,
        vector, vector, matrix, vector, matrix, vector,
    )
    return jax.shard_map(
        functools.partial(local, mesh), mesh=mesh, in_specs=ins, out_specs=outs, check_vma=False
    )
```

```python
import functools
import math

import jax
import jax.numpy as jnp
import numpy as np
from jax import lax
from jax.experimental import pallas as pl
from jax.experimental.pallas import tpu as pltpu
from jax.sharding import PartitionSpec as P

AXES = ("wide", "narrow")
BF, F32 = jnp.bfloat16, jnp.float32
VMEM_CAP = 58 << 20

def params(n=1, cap=VMEM_CAP):
    return pltpu.CompilerParams(dimension_semantics=("arbitrary",) * n, vmem_limit_bytes=cap)

def cost(flops, bytes_accessed, trans=0):
    return pl.CostEstimate(flops=int(flops), bytes_accessed=int(bytes_accessed), transcendentals=int(trans))

def mm(a, b):
    return jnp.dot(a, b, preferred_element_type=F32)

def diagonal_mask(rows, cols):
    key_at = lax.broadcasted_iota(jnp.int32, (rows, cols), 0)
    query_at = lax.broadcasted_iota(jnp.int32, (rows, cols), 1)
    return key_at <= query_at

def attend_kernel(qb, len_ref, qkv_ref, out_t_ref, out_ref, stat_ref, v_t, q_t):
    slot = qkv_ref.shape[1]
    q_t[...] = (qkv_ref[0] * jnp.asarray(0.125, BF)).T
    v_t[...] = qkv_ref[2].T
    half = lax.broadcasted_iota(jnp.int32, (128, 1), 0) < 64
    causal = diagonal_mask(qb, qb)
    length = len_ref[0]
    def scores(i, head):
        mine = half if head == 0 else jnp.logical_not(half)
        qh = jnp.where(mine, q_t[:, i * qb : (i + 1) * qb], jnp.zeros((), BF))
        s_dia = jnp.where(causal, mm(qkv_ref[1, i * qb : (i + 1) * qb, :], qh), -1e30)
        return s_dia, mm(qkv_ref[1, : i * qb, :], qh) if i else None
    tasks = [(i, head) for i in range(slot // qb) for head in range(2)]
    ahead = scores(*tasks[0])
    parts = []
    for at, (i, head) in enumerate(tasks):
        cols = slice(i * qb, (i + 1) * qb)
        s_dia, s_low = ahead
        if at + 1 < len(tasks):
            ahead = scores(*tasks[at + 1])
        top = jnp.max(s_dia, axis=0, keepdims=True)
        if i:
            top = jnp.maximum(top, jnp.max(s_low, axis=0, keepdims=True))
        e_dia = jnp.exp(s_dia - top)
        total = jnp.sum(e_dia, axis=0, keepdims=True)
        vh = v_t[head * 64 : head * 64 + 64, :]
        acc = mm(vh[:, cols], e_dia.astype(BF))
        if i:
            e_low = jnp.exp(s_low - top)
            total = total + jnp.sum(e_low, axis=0, keepdims=True)
            acc = acc + mm(vh[:, : i * qb], e_low.astype(BF))
        stat_ref[0, head : head + 1, cols] = top + jnp.log(total)
        parts.append(acc / total)
        if head == 1:
            both = jnp.concatenate(parts, axis=0)
            parts = []
            seen = (i * qb + lax.broadcasted_iota(jnp.int32, (1, qb), 1)) < length
            both = jnp.where(seen, both, 0.0)
            out_t_ref[:, cols] = both
            out_ref[cols, :] = both.T.astype(BF)

def attend(lengths, qkv, pairs, first, qb=256):
    slot, width = qkv.shape[1], qkv.shape[2]
    return pl.pallas_call(
        functools.partial(attend_kernel, qb),
        name="attend",
        grid=(pairs,),
        in_specs=[
            pl.BlockSpec(memory_space=pltpu.SMEM),
            pl.BlockSpec((3, slot, 128), lambda j: (0, 0, j + first)),
        ],
        out_specs=[
            pl.BlockSpec((128, slot), lambda j: (j, 0)),
            pl.BlockSpec((slot, 128), lambda j: (0, j)),
            pl.BlockSpec((1, 2, slot), lambda j: (j, 0, 0)),
        ],
        out_shape=[
            jax.ShapeDtypeStruct((pairs * 128, slot), F32),
            jax.ShapeDtypeStruct((slot, pairs * 128), BF),
            jax.ShapeDtypeStruct((pairs, 2, slot), F32),
        ],
        scratch_shapes=[pltpu.VMEM((128, slot), BF), pltpu.VMEM((128, slot), BF)],
        compiler_params=params(1, 28 << 20),
        cost_estimate=cost(pairs * 2 * slot * slot * 256, 8e6 * pairs / 6, pairs * slot * slot),
    )(lengths, qkv)

def attend_grad_kernel(qb, qkv_ref, grad_ref, out_t_ref, stat_ref, g_ref, q_t, do_t, k_t, qs, dq_t, dk_s, dv_s):
    slot = qkv_ref.shape[1]
    qs[...] = qkv_ref[0] * jnp.asarray(0.125, BF)
    q_t[...] = qs[...].T
    k_t[...] = qkv_ref[1].T
    do_t[...] = grad_ref[...].T
    half = lax.broadcasted_iota(jnp.int32, (128, 1), 0) < 64
    half_lane = lax.broadcasted_iota(jnp.int32, (1, 128), 1) < 64
    causal = diagonal_mask(qb, qb)
    zero = jnp.zeros((), BF)
    prod = do_t[...].astype(F32) * out_t_ref[...]
    delta = [jnp.sum(prod[h * 64 : h * 64 + 64], axis=0, keepdims=True) for h in range(2)]
    def scores(i, head):
        cols, end = slice(i * qb, (i + 1) * qb), (i + 1) * qb
        mine = half if head == 0 else jnp.logical_not(half)
        qh_t = jnp.where(mine, q_t[:, cols], zero)
        doh_t = jnp.where(mine, do_t[:, cols], zero)
        return mm(qkv_ref[1, :end, :], qh_t), mm(qkv_ref[2, :end, :], doh_t)
    tasks = [(i, head) for i in range(slot // qb) for head in range(2)]
    ahead = scores(*tasks[0])
    for at, (i, head) in enumerate(tasks):
        cols, end = slice(i * qb, (i + 1) * qb), (i + 1) * qb
        s, dp = ahead
        if at + 1 < len(tasks):
            ahead = scores(*tasks[at + 1])
        mine_lane = half_lane if head == 0 else jnp.logical_not(half_lane)
        qh = jnp.where(mine_lane, qs[cols, :], zero)
        doh = jnp.where(mine_lane, grad_ref[cols, :], zero)
        stat = stat_ref[0, head : head + 1, cols]
        dl = delta[head][:, cols]
        p = jnp.exp(s - stat)
        p_dia = jnp.where(causal, p[i * qb :], 0.0)
        p = jnp.concatenate([p[: i * qb], p_dia], axis=0) if i else p_dia
        ds = (p * (dp - dl)).astype(BF)
        pb = p.astype(BF)
        dv_h = mm(pb, doh)
        dk_h = mm(ds, qh)
        dq_t[head * 64 : head * 64 + 64, cols] = mm(k_t[head * 64 : head * 64 + 64, :end], ds)
        if head == 0:
            dv_new, dk_new = dv_h, dk_h
            continue
        dv_new, dk_new = dv_new + dv_h, dk_new + dk_h
        if i:
            dv_s[: i * qb] += dv_new[: i * qb]
            dk_s[: i * qb] += dk_new[: i * qb]
        dv_s[cols] = dv_new[i * qb :]
        dk_s[cols] = dk_new[i * qb :]
    g_ref[0] = (dq_t[...] * 0.125).T.astype(BF)
    g_ref[1] = dk_s[...].astype(BF)
    g_ref[2] = dv_s[...].astype(BF)

def attend_grad(qkv, grad, out_t, stat, first, qb=256):
    slot = qkv.shape[1]
    pairs = out_t.shape[0] // 128
    width = pairs * 128
    return pl.pallas_call(
        functools.partial(attend_grad_kernel, qb),
        name="attend_grad",
        grid=(pairs,),
        in_specs=[
            pl.BlockSpec((3, slot, 128), lambda j: (0, 0, j + first)),
            pl.BlockSpec((slot, 128), lambda j: (0, j + first)),
            pl.BlockSpec((128, slot), lambda j: (j, 0)),
            pl.BlockSpec((1, 2, slot), lambda j: (j, 0, 0)),
        ],
        out_specs=pl.BlockSpec((3, slot, 128), lambda j: (0, 0, j)),
        out_shape=jax.ShapeDtypeStruct((3, slot, width), BF),
        scratch_shapes=[
            pltpu.VMEM((128, slot), BF),
            pltpu.VMEM((128, slot), BF),
            pltpu.VMEM((128, slot), BF),
            pltpu.VMEM((slot, 128), BF),
            pltpu.VMEM((128, slot), F32),
            pltpu.VMEM((slot, 128), F32),
            pltpu.VMEM((slot, 128), F32),
        ],
        compiler_params=params(1, 32 << 20),
        cost_estimate=cost(pairs * 5 * slot * slot * 256, 16e6 * pairs / 6, pairs * 2 * slot * slot),
    )(qkv, grad, out_t, stat)
VECTOR_ROWS = 16
GAIN_ONE, SHIFT_ONE, BIAS_OUT, GAIN_TWO, SHIFT_TWO, BIAS_PROJ, BIAS_QKV, BIAS_FC = 0, 1, 2, 3, 4, 5, 6, 9
branch_scale = 1.0 / math.sqrt(48.0)
norm_epsilon = 1e-05
WHOLE = dict(pipeline_mode=pl.Buffered(1))

def mm_nt(a, b):
    return lax.dot_general(a, b, (((1,), (1,)), ((), ())), preferred_element_type=F32)

def mm_tn(a, b):
    return lax.dot_general(a, b, (((0,), (0,)), ((), ())), preferred_element_type=F32)

def normalised(v):
    mean = jnp.mean(v, axis=-1, keepdims=True)
    centred = v - mean
    var = jnp.mean(centred * centred, axis=-1, keepdims=True)
    scale = lax.rsqrt(var + norm_epsilon)
    return centred * scale, scale

def norm_pull(n, scale, gain, u):
    ug = u * gain
    a = jnp.mean(ug, axis=-1, keepdims=True)
    b = jnp.mean(ug * n, axis=-1, keepdims=True)
    return (ug - a - n * b) * scale

def row_of(ref, at):
    return ref[at : at + 1, :]

def whole(shape, index=None):
    zeros = (0,) * len(shape)
    return pl.BlockSpec(shape, (lambda *_: index or zeros), **WHOLE)

def assemble(place, sources, target):
    wide = target.shape[2] // 2
    for s, source in enumerate(sources):
        for half in range(2):
            @pl.when(place[s, 0] == half)
            def _():
                for p in range(source.shape[0]):
                    target[place[s, 1 + p], :, half * wide : (half + 1) * wide] = source[p, :, :wide]

def fetch(place, sources, target, sem):
    wide = target.shape[2] // 2
    for s, source in enumerate(sources):
        lanes = pl.ds(pl.multiple_of(place[s, 0] * wide, 128), wide)
        for p in range(source.shape[0]):
            pltpu.make_async_copy(
                source.at[p, :, pl.ds(0, wide)], target.at[place[s, 1 + p], :, lanes], sem
            ).start()

def arrived(target, sem):
    pltpu.make_async_copy(target, target, sem).wait()

def project_kernel(n_src, place, x_ref, vec_ref, *rest):
    sources, (qkv_ref, low_ref, w_ref) = rest[:n_src], rest[n_src:]
    @pl.when(pl.program_id(0) == 0)
    def _():
        assemble(place, sources, w_ref)
    n, _ = normalised(x_ref[...].astype(F32))
    low = (n * row_of(vec_ref, GAIN_ONE) + row_of(vec_ref, SHIFT_ONE)).astype(BF)
    low_ref[...] = low
    d = low.shape[1]
    for part in range(3):
        w = w_ref[:, :, part * d : (part + 1) * d].reshape(d, d)
        qkv_ref[part] = (mm(low, w) + row_of(vec_ref, BIAS_QKV + part)).astype(BF)

def project(place, x, vec, sources, blocks, rows=256):
    t, d = x.shape
    r, wide = d // blocks, 3 * d // 2
    return pl.pallas_call(
        functools.partial(project_kernel, len(sources)),
        name="project",
        grid_spec=pltpu.PrefetchScalarGridSpec(
            num_scalar_prefetch=1,
            grid=(t // rows,),
            in_specs=[
                pl.BlockSpec((rows, d), lambda i, p: (i, 0)),
                whole(vec.shape),
                *[whole(s.shape) for s in sources],
            ],
            out_specs=[
                pl.BlockSpec((3, rows, d), lambda i, p: (0, i, 0)),
                pl.BlockSpec((rows, d), lambda i, p: (i, 0)),
                whole((blocks, r, 2 * wide)),
            ],
        ),
        out_shape=[
            jax.ShapeDtypeStruct((3, t, d), BF),
            jax.ShapeDtypeStruct((t, d), BF),
            jax.ShapeDtypeStruct((blocks, r, 2 * wide), BF),
        ],
        compiler_params=params(1, 32 << 20),
        cost_estimate=cost(2 * t * d * 3 * d, 18e6),
    )(place, x, vec, *sources)

def mix_kernel(n_src, place, x_ref, vec_ref, *rest):
    sources, parts, (mid_ref, low_ref, w_ref) = rest[:n_src], rest[n_src:-3], rest[-3:]
    @pl.when(pl.program_id(0) == 0)
    def _():
        assemble(place, sources, w_ref)
    d = x_ref.shape[1]
    w = w_ref[...].reshape(d, d)
    mid = x_ref[...].astype(F32) + branch_scale * (mm(jnp.concatenate([p[...] for p in parts], 1), w) + row_of(vec_ref, BIAS_OUT))
    mid_ref[...] = mid
    n, _ = normalised(mid)
    low_ref[...] = (n * row_of(vec_ref, GAIN_TWO) + row_of(vec_ref, SHIFT_TWO)).astype(BF)

def mix(place, parts, x, vec, sources, blocks, column, rows=256):
    t, d = x.shape
    r, np_ = d // blocks, sources[0].shape[0]
    return pl.pallas_call(
        functools.partial(mix_kernel, len(sources)),
        name="mix",
        grid_spec=pltpu.PrefetchScalarGridSpec(
            num_scalar_prefetch=1,
            grid=(t // rows,),
            in_specs=[
                pl.BlockSpec((rows, d), lambda i, p: (i, 0)),
                whole(vec.shape),
                *[whole((np_, r, d // 2), (0, 0, column)) for s in sources],
                *[pl.BlockSpec((rows, p.shape[1]), lambda i, p: (i, 0)) for p in parts],
            ],
            out_specs=[
                pl.BlockSpec((rows, d), lambda i, p: (i, 0)),
                pl.BlockSpec((rows, d), lambda i, p: (i, 0)),
                whole((blocks, r, d)),
            ],
        ),
        out_shape=[
            jax.ShapeDtypeStruct((t, d), F32),
            jax.ShapeDtypeStruct((t, d), BF),
            jax.ShapeDtypeStruct((blocks, r, d), BF),
        ],
        compiler_params=params(1, 24 << 20),
        cost_estimate=cost(2 * t * d * d, 9e6),
    )(place, x, vec, *sources, *parts)

def mlp_kernel(n_src, rb, core, place, wide_place, lens, low_ref, cot_ref, bias_ref, mid_hbm, *rest):
    fcs, projs, rest = rest[: n_src[0]], rest[n_src[0] : sum(n_src)], rest[sum(n_src) :]
    (out_hbm, gmid_hbm, gbr_hbm, fsend_hbm, fkeep_hbm, psend_ref, pkeep_ref, fbg_ref, vec_ref,
     fc_s, proj_s, g2_s, second_s, act_s, gpre_s, mid_s, out_s, gmid_s, gbr_s, f_s, sems) = rest
    t, d = mid_s.shape
    w, h = 2 * d, d // 2
    step = pl.program_id(0)
    mine = core[0]
    chunk = lax.rem(step + 1 - mine, 2)
    mid_copy = pltpu.make_async_copy(mid_hbm, mid_s, sems.at[2])
    outs = [
        pltpu.make_async_copy(a, b, sems.at[3 + k])
        for k, (a, b) in enumerate(
            ((out_s, out_hbm), (gmid_s, gmid_hbm), (gbr_s, gbr_hbm), (f_s, fsend_hbm), (f_s, fkeep_hbm))
        )
    ]
    def valid_rows(at):
        return (at * rb + lax.broadcasted_iota(jnp.int32, (rb, 1), 0)) < lens[0]
    @pl.when(step == 0)
    def _():
        fetch(wide_place, projs, proj_s, sems.at[0])
        fetch(place, fcs, fc_s, sems.at[1])
        mid_copy.start()
        def begin(i, total):
            at = pl.ds(pl.multiple_of(i * rb, rb), rb)
            g = jnp.where(valid_rows(i), branch_scale * cot_ref[at, :].astype(F32), 0.0).astype(BF)
            g2_s[at, :] = g
            return total + jnp.sum(g.astype(F32), axis=0, keepdims=True)
        vec_ref[0:1] = lax.fori_loop(0, t // rb, begin, jnp.zeros((1, d), F32))
        arrived(proj_s, sems.at[0])
        arrived(fc_s, sems.at[1])
        mid_copy.wait()
    fc = fc_s.at[:, :, pl.ds(pl.multiple_of(chunk * w, w), w)]
    bias = jnp.concatenate([bias_ref[pl.ds(BIAS_FC + 2 * chunk + i, 1), :] for i in range(2)], 1)
    blocks, pr = proj_s.shape[0], proj_s.shape[1]
    if blocks > 1:
        proj = proj_s.at[pl.ds(chunk * (blocks // 2), blocks // 2)]
    else:
        proj = proj_s.at[:, pl.ds(pl.multiple_of(chunk * w, w), w)]
    def rows_step(i, total):
        at = pl.ds(pl.multiple_of(i * rb, rb), rb)
        wf = fc[...].reshape(d, w)
        wp = proj[...].reshape(w, d)
        ga = mm_nt(g2_s[at, :], wp)
        u = mm(low_ref[at, :], wf) + bias
        sq = u * u
        th = jnp.tanh(u * (0.7978845608028654 + (0.7978845608028654 * 0.044715) * sq))
        up = 0.5 + 0.5 * th
        act = (u * up).astype(BF)
        act_s[at, :] = act
        slope = up * (1.0 + (1.0 - up) * (u * (2 * 0.7978845608028654 + (6 * 0.7978845608028654 * 0.044715) * sq)))
        gpb = (ga * slope).astype(BF)
        gpre_s[at, :] = gpb
        more, back = mm(act, wp), mm_nt(gpb, wf)
        @pl.when(step == 0)
        def _():
            second_s[at, :] = more
            gmid_s[at, :] = back
        @pl.when(step == 1)
        def _():
            second_s[at, :] += more
            gmid_s[at, :] += back
        return total + jnp.sum(gpb.astype(F32), axis=0, keepdims=True)
    sums = lax.fori_loop(0, t // rb, rows_step, jnp.zeros((1, w), F32))
    for i in range(2):
        fbg_ref[pl.ds(2 * chunk + i, 1), :] = sums[:, i * d : (i + 1) * d]
    @pl.when(step == 1)
    def _():
        def finish(i, carry):
            at = pl.ds(pl.multiple_of(i * rb, rb), rb)
            mid = mid_s[at, :]
            out_s[at, :] = (mid + branch_scale * (second_s[at, :] + row_of(bias_ref, BIAS_PROJ))).astype(BF)
            n, scale = normalised(mid)
            gh = gmid_s[at, :]
            cot = jnp.where(valid_rows(i), cot_ref[at, :].astype(F32), 0.0)
            gm = cot + norm_pull(n, scale, row_of(bias_ref, GAIN_TWO), gh)
            gmid_s[at, :] = gm
            gb = (branch_scale * gm).astype(BF)
            gbr_s[at, :] = gb
            return (carry[0] + jnp.sum(gh * n, axis=0, keepdims=True),
                    carry[1] + jnp.sum(gh, axis=0, keepdims=True),
                    carry[2] + jnp.sum(gb.astype(F32), axis=0, keepdims=True))
        zero = jnp.zeros((1, d), F32)
        a, b, c = lax.fori_loop(0, t // rb, finish, (zero, zero, zero))
        vec_ref[1:2] = a
        vec_ref[2:3] = b
        vec_ref[3:4] = c
        for copy in outs[:3]:
            copy.start()
    @pl.when(step == 1)
    def _():
        outs[3].wait()
    f_s[...] = mm_tn(low_ref[...], gpre_s[...]).astype(BF).reshape(f_s.shape)
    @pl.when(step == 0)
    def _():
        outs[3].start()
    @pl.when(step == 1)
    def _():
        outs[4].start()
    dproj = mm_tn(act_s[...], g2_s[...]).astype(BF)
    for half in range(2):
        @pl.when(mine == half)
        def _():
            pkeep_ref[...] = dproj[:, half * h : (half + 1) * h].reshape(pkeep_ref.shape)
            psend_ref[...] = dproj[:, (1 - half) * h : (2 - half) * h].reshape(psend_ref.shape)
    @pl.when(step == 1)
    def _():
        for copy in outs[:3] + outs[4:]:
            copy.wait()

def mlp(core, place, wide_place, lens, mid, low, cot, vec, fcs, projs, blocks, rb=512):
    t, d = mid.shape
    r, pr = d // blocks, 4 * d // blocks
    smem, hbm = pl.BlockSpec(memory_space=pltpu.SMEM), pl.BlockSpec(memory_space=pl.ANY)
    turn = lambda i, c: lax.rem(i + 1 - c[0], 2)
    if blocks > 1:
        pspec = pl.BlockSpec((blocks // 2, pr, d // 2), lambda i, c: (turn(i, c), 0, 0))
    else:
        pspec = pl.BlockSpec((1, pr // 2, d // 2), lambda i, c: (0, turn(i, c), 0))
    of = jax.ShapeDtypeStruct
    return pl.pallas_call(
        functools.partial(mlp_kernel, (len(fcs), len(projs)), rb),
        name="mlp",
        grid_spec=pltpu.PrefetchScalarGridSpec(
            num_scalar_prefetch=1,
            grid=(2,),
            in_specs=[smem, smem, smem, whole((t, d)), whole((t, d)), whole(vec.shape), hbm] + [hbm] * len(fcs + projs),
            out_specs=[hbm] * 5 + [pspec, pspec, whole((4, d)), whole((4, d))],
            scratch_shapes=[
                pltpu.VMEM((blocks, r, 4 * d), BF),
                pltpu.VMEM((blocks, pr, d), BF),
                pltpu.VMEM((t, d), BF),
                pltpu.VMEM((t, d), F32),
                pltpu.VMEM((t, 2 * d), BF),
                pltpu.VMEM((t, 2 * d), BF),
                pltpu.VMEM((t, d), F32),
                pltpu.VMEM((t, d), BF),
                pltpu.VMEM((t, d), F32),
                pltpu.VMEM((t, d), BF),
                pltpu.VMEM((blocks, r, 2 * d), BF),
                pltpu.SemaphoreType.DMA((8,)),
            ],
        ),
        out_shape=[
            of((t, d), BF), of((t, d), F32), of((t, d), BF),
            of((blocks, r, 2 * d), BF), of((blocks, r, 2 * d), BF),
            of((blocks, pr, d // 2), BF), of((blocks, pr, d // 2), BF),
            of((4, d), F32), of((4, d), F32),
        ],
        compiler_params=params(),
        cost_estimate=cost(12 * t * d * 4 * d, 40e6, t * 4 * d),
    )(core, place, wide_place, lens, low, cot, vec, mid, *fcs, *projs)

def unmix_kernel(core, lens, gbr_ref, w_ref, *rest):
    parts, (ga_ref, send_ref, keep_ref) = rest[:-3], rest[-3:]
    t, d = gbr_ref.shape
    w = w_ref[...].reshape(d, d)
    seen = lax.broadcasted_iota(jnp.int32, (t, 1), 0) < lens[0]
    ga_ref[...] = jnp.where(seen, mm_nt(gbr_ref[...], w), 0.0).astype(BF)
    dw = jnp.concatenate([mm_tn(p[...], gbr_ref[...]).astype(BF) for p in parts], 0)
    h = d // 2
    for half in range(2):
        @pl.when(core[0] == half)
        def _():
            keep_ref[...] = dw[:, half * h : (half + 1) * h].reshape(keep_ref.shape)
            send_ref[...] = dw[:, (1 - half) * h : (2 - half) * h].reshape(send_ref.shape)

def unmix(core, lens, gbr, parts, w, blocks):
    t, d = gbr.shape
    smem = pl.BlockSpec(memory_space=pltpu.SMEM)
    piece = jax.ShapeDtypeStruct((blocks, d // blocks, d // 2), BF)
    return pl.pallas_call(
        unmix_kernel,
        name="unmix",
        in_specs=[smem, smem] + [pl.BlockSpec(memory_space=pltpu.VMEM)] * (2 + len(parts)),
        out_shape=[jax.ShapeDtypeStruct((t, d), BF), piece, piece],
        compiler_params=params(0, 24 << 20),
        cost_estimate=cost(4 * t * d * d, 9e6),
    )(core, lens, gbr, w, *parts)

def unproject_kernel(blocks, core, low_ref, g_ref, send_ref, keep_ref, sums_ref):
    d, w = low_ref.shape[1], g_ref.shape[2]
    r, h = d // blocks, w // 2
    low_t = low_ref[...].T
    q, k, v = [mm(low_t, g_ref[part]).astype(BF).reshape(blocks, r, w) for part in range(3)]
    for half, refs in ((0, (keep_ref, send_ref)), (1, (send_ref, keep_ref))):
        @pl.when(core[0] == half)
        def _():
            refs[0][:, :, :w] = q
            refs[0][:, :, w:] = k[:, :, :h]
            refs[1][:, :, :h] = k[:, :, h:]
            refs[1][:, :, h:] = v
    for part in range(3):
        sums_ref[part : part + 1] = jnp.sum(g_ref[part].astype(F32), axis=0, keepdims=True)

def unproject(core, low, g, blocks):
    t, d = low.shape
    w = g.shape[2]
    piece = jax.ShapeDtypeStruct((blocks, d // blocks, w // 2 * 3), BF)
    return pl.pallas_call(
        functools.partial(unproject_kernel, blocks),
        name="unproject",
        in_specs=[pl.BlockSpec(memory_space=pltpu.SMEM)] + [pl.BlockSpec(memory_space=pltpu.VMEM)] * 2,
        out_shape=[piece, piece, jax.ShapeDtypeStruct((3, w), F32)],
        compiler_params=params(0, 24 << 20),
        cost_estimate=cost(6 * t * d * w, 10e6 * w / d),
    )(core, low, g)

def route_kernel(count, steps, rows, near, table, *refs):
    inputs, outs = refs[: 2 * count + near], refs[2 * count + near :]
    def write(ref):
        at = 0
        for k, g in zip(inputs[:count], inputs[count : 2 * count]):
            r, w = k.shape[-2:]
            place = (slice(at, at + r), slice(0, w)) if rows else (slice(0, r), slice(at, at + w))
            at += r if rows else w
            total = (k[...].astype(F32) + g[...].astype(F32)).reshape(1, ref.shape[1], r, w)
            came = [v[:, :, place[0], place[1]] for v in inputs[2 * count :]]
            if near == 2:
                came = [jnp.where(table[pl.program_id(0), 2] == 0, *came)]
            if near:
                total = total + came[0].astype(F32)
            ref[:, :, place[0], place[1]] = total.astype(BF)
    for s, ref in enumerate(outs):
        @pl.when(pl.program_id(0) // steps == s)
        def _():
            write(ref)

def route(table, keeps, gots, near=(), rows=False, split=False):
    z = keeps[0].shape[0]
    sizes = [k.shape[-2:] for k in keeps]
    tall = sum(r for r, _ in sizes) if rows else sizes[0][0]
    wide = sizes[0][1] if rows else sum(w for _, w in sizes)
    block = (1, z, tall, wide)
    specs = [pl.BlockSpec((z, 1, 1, *s), lambda i, t: (0, t[i, 0], t[i, 1], 0, 0)) for s in sizes] * 2
    fixed = pl.BlockSpec(block, lambda i, t: (0, 0, 0, 0))
    if near or split:
        steps, outs = 1, [fixed] * 2
        specs += [pl.BlockSpec(block, lambda i, t: (t[i, 2], 0, 0, 0))] if len(near) == 1 else [fixed] * len(near)
    else:
        steps, outs = 2, [pl.BlockSpec(block, lambda i, t: (i, 0, 0, 0))]
    return pl.pallas_call(
        functools.partial(route_kernel, len(keeps), steps, rows, len(near)),
        name="route",
        grid_spec=pltpu.PrefetchScalarGridSpec(
            num_scalar_prefetch=1, grid=(2,), in_specs=specs, out_specs=outs
        ),
        out_shape=[jax.ShapeDtypeStruct((steps, z, tall, wide), BF)] * len(outs),
        compiler_params=params(1, 24 << 20),
        cost_estimate=cost(1e6, 2 * z * tall * wide * 6),
    )(table, *keeps, *gots, *near)

def final_kernel(x_ref, w_ref, gmid_ref, bias_ref, *rest):
    parts, (out_ref, vec_ref) = rest[:-2], rest[-2:]
    d = x_ref.shape[1]
    w = w_ref[...].reshape(d, 3 * d)
    gh = jnp.zeros(x_ref.shape, F32)
    at = 0
    for g in parts:
        for i in range(3):
            gh = gh + mm_nt(g[i], w[:, i * d + at : i * d + at + g.shape[2]])
        at += g.shape[2]
    n, scale = normalised(x_ref[...].astype(F32))
    out_ref[...] = (gmid_ref[...] + norm_pull(n, scale, row_of(bias_ref, GAIN_ONE), gh)).astype(BF)
    @pl.when(pl.program_id(0) == 0)
    def _():
        vec_ref[...] = jnp.zeros_like(vec_ref)
    vec_ref[0:1] += jnp.sum(gh * n, axis=0, keepdims=True)
    vec_ref[1:2] += jnp.sum(gh, axis=0, keepdims=True)

def final(x, parts, w, gmid, vec, rows=256):
    t, d = x.shape
    return pl.pallas_call(
        final_kernel,
        name="final",
        grid=(t // rows,),
        in_specs=[
            pl.BlockSpec((rows, d), lambda i: (i, 0)),
            whole(w.shape),
            pl.BlockSpec((rows, d), lambda i: (i, 0)),
            whole(vec.shape),
            *[pl.BlockSpec((3, rows, g.shape[2]), lambda i: (0, i, 0)) for g in parts],
        ],
        out_specs=[pl.BlockSpec((rows, d), lambda i: (i, 0)), whole((2, d))],
        out_shape=[jax.ShapeDtypeStruct((t, d), BF), jax.ShapeDtypeStruct((2, d), F32)],
        compiler_params=params(1, 32 << 20),
        cost_estimate=cost(6 * t * d * d, 15e6),
    )(x, w, gmid, vec, *parts)
def spread_matrix(size, width):
    row = lax.broadcasted_iota(jnp.int32, (128, width), 0).astype(F32)
    col = lax.broadcasted_iota(jnp.int32, (128, width), 1).astype(F32)
    inside = col - jnp.floor((col + 0.5) / size) * size
    return jnp.where(inside == row, 1.0, 0.0)

def own_columns(count, size, per, width):
    at = lax.broadcasted_iota(jnp.int32, (count, width), 0).astype(F32)
    at = at - jnp.floor((at + 0.5) / per) * per
    col = lax.broadcasted_iota(jnp.int32, (count, width), 1).astype(F32)
    return jnp.logical_and(col >= at * size, col < (at + 1) * size)


def unfold_vectors(rows_of, count, out_ref):
    d = out_ref.shape[1]
    out_ref[...] = jnp.zeros_like(out_ref)
    for rows, slots, first in ((1, range(6), 0), (2, (6,), BIAS_QKV), (4, (7,), BIAS_FC)):
        size, per = d * rows // count, count // rows
        spread = spread_matrix(size, d).astype(BF)
        mine = own_columns(count, size, per, d)
        for s in slots:
            got = jnp.where(mine, mm(rows_of(s), spread), 0.0)
            for r in range(rows):
                to = first + (s if rows == 1 else 2 * r if rows == 2 else r)
                out_ref[to : to + 1] = jnp.sum(got[r * per : (r + 1) * per], axis=0, keepdims=True)

def unfold_kernel(x_ref, out_ref):
    unfold_vectors(lambda s: x_ref[s], x_ref.shape[1], out_ref)

def unfold(x, d):
    return pl.pallas_call(
        unfold_kernel,
        name="unfold",
        in_specs=[pl.BlockSpec(memory_space=pltpu.VMEM)],
        out_shape=jax.ShapeDtypeStruct((VECTOR_ROWS, d), F32),
        compiler_params=params(0, 16 << 20),
        cost_estimate=cost(1e8, 1e6),
    )(x)

def unfold_pieces_kernel(n_src, place, *rest):
    sources, out_ref, x_ref = rest[:n_src], rest[n_src], rest[-1]
    r = sources[0].shape[1] // 2
    for s, source in enumerate(sources):
        for p in range(source.shape[0]):
            tile = source[p].astype(F32)
            for c in range(2):
                x_ref[2 * place[s, 1 + p] + c] = tile[c * r : c * r + 8]
    unfold_vectors(lambda s: x_ref[:, s, :].astype(BF), x_ref.shape[0], out_ref)

def unfold_pieces(place, sources, count, d):
    np_, r, wide = sources[0].shape
    return pl.pallas_call(
        functools.partial(unfold_pieces_kernel, len(sources)),
        name="unfold",
        grid_spec=pltpu.PrefetchScalarGridSpec(
            num_scalar_prefetch=1,
            grid=(1,),
            in_specs=[whole((np_, r, 128), (0, 0, wide // 128 - 1)) for _ in sources],
            out_specs=whole((VECTOR_ROWS, d)),
            scratch_shapes=[pltpu.VMEM((count, 8, 128), F32)],
        ),
        out_shape=jax.ShapeDtypeStruct((VECTOR_ROWS, d), F32),
        compiler_params=params(1, 16 << 20),
        cost_estimate=cost(1e8, 1e6),
    )(place, *sources)

def fold_kernel(first_ref, sums_ref, qkv_ref, fc_ref, out_ref):
    count, d = out_ref.shape[1], first_ref.shape[1]
    singles = [
        first_ref[0:1], first_ref[1:2], sums_ref[3:4], sums_ref[1:2], sums_ref[2:3], sums_ref[0:1],
    ]
    pairs = [[v] for v in singles] + [[qkv_ref[0:1], qkv_ref[2:3]], [fc_ref[r : r + 1] for r in range(4)]]
    for rows, slots in ((1, range(6)), (2, (6,)), (4, (7,))):
        size, per = d * rows // count, count // rows
        spread = spread_matrix(size, d)
        mine = own_columns(count, size, per, d)
        full = jnp.concatenate(
            [
                jnp.where(mine, jnp.concatenate([jnp.broadcast_to(v, (per, d)) for v in pairs[s]], 0), 0.0)
                for s in slots
            ],
            0,
        )
        got = lax.dot_general(
            full, spread, (((1,), (1,)), ((), ())), precision=lax.Precision.HIGHEST, preferred_element_type=F32
        )
        for i, s in enumerate(slots):
            out_ref[s] = got[i * count : (i + 1) * count]

def fold(first, sums, qkv, fc, count):
    return pl.pallas_call(
        fold_kernel,
        name="fold",
        in_specs=[pl.BlockSpec(memory_space=pltpu.VMEM)] * 4,
        out_shape=jax.ShapeDtypeStruct((8, count, 128), F32),
        compiler_params=params(0, 32 << 20),
        cost_estimate=cost(1e8, 1e6),
    )(first, sums, qkv, fc)


class Grid:
    order = (0, 2, 1, 3)

    def __init__(self, mesh, rows):
        wide, narrow = mesh.shape["wide"], mesh.shape["narrow"]
        self.count = wide * narrow
        self.paired = narrow == 4 and wide == 8 and rows % 8 == 0
        self.blocks = self.count // 2 if self.paired else 1
        self.z = wide // 2

    def index(self, z, x, y, c):
        return ((z * 2 + x) * 2 + y) * 2 + c

    def places(self):
        return [
            (z, x, y, c) for z in range(self.z) for x in range(2) for y in range(2) for c in range(2)
        ]

    def perm(self, target):
        return [(self.index(*at), self.index(*target(*at))) for at in self.places()]

    def here(self):
        w, n = lax.axis_index("wide"), lax.axis_index("narrow")
        return w // 2, w % 2, n // 2, n % 2

    def table(self):
        rows = []
        for z0, x0, y0, c0 in self.places():
            mine = []
            for half in (c0, 1 - c0):
                for ka, kb in ((0, 0), (1, 0), (0, 1), (1, 1)):
                    kx, ky = (ka, kb) if half == 0 else (kb, ka)
                    blocks = [
                        ((z0 ^ kz) * 2 + (x0 ^ kx)) * 2 + (y0 ^ ky) for kz in self.order
                    ]
                    mine.append([half] + blocks)
            rows.append(mine)
        return np.array(rows, np.int32)

    def wide_table(self):
        rows = []
        for z0, x0, y0, c0 in self.places():
            mine = []
            for half in (c0, 1 - c0):
                for kb in (0, 1):
                    line = [half]
                    for kz in self.order:
                        for ka in (0, 1):
                            kx, ky = (ka, kb) if half == 0 else (kb, ka)
                            line.append(((z0 ^ kz) * 2 + (x0 ^ kx)) * 2 + (y0 ^ ky))
                    mine.append(line)
            rows.append(mine)
        return np.array(rows, np.int32)

    def routes(self):
        near, far = [], []
        for z0, x0, y0, c0 in self.places():
            if c0 == 0:
                near.append([[1 - x0, 0], [1 - x0, 1]])
                far.append([[x0, 1 - y0, 1 - y0], [x0, y0, y0]])
            else:
                near.append([[0, 1 - y0], [1, 1 - y0]])
                far.append([[1 - x0, y0, 1 - x0], [x0, y0, x0]])
        return np.array(near, np.int32), np.array(far, np.int32)

    def send(self, value, target):
        return lax.ppermute(value, AXES, self.perm(target))

    def other_core(self, value):
        return self.send(value, lambda z, x, y, c: (z, x, y, 1 - c))

    def along(self, value, turn):
        return self.send(
            value,
            lambda z, x, y, c: (z, 1 - x, y, c) if c == turn else (z, x, 1 - y, c),
        )

    def up(self, value, k):
        return self.send(value, lambda z, x, y, c: (z ^ k, x, y, c))


def both(first, own, other, axis):
    return jnp.where(
        first, jnp.concatenate([own, other], axis), jnp.concatenate([other, own], axis)
    )


def pair_rows(grid, shard, extra=None):
    c = grid.here()[3]
    h = shard.shape[1] // 2
    mine = lax.dynamic_slice_in_dim(shard, c * h, h, 1)
    away = lax.dynamic_slice_in_dim(shard, (1 - c) * h, h, 1)
    if extra is not None:
        mine, away = jnp.concatenate([mine, extra], 1), jnp.concatenate([away, extra], 1)
    return both(c == 0, mine, grid.other_core(away), 0)


def spread_z(grid, pair):
    return jnp.stack([pair] + [grid.up(pair, k) for k in grid.order[1:]])


def with_other(grid, sources):
    return sources + [grid.other_core(s) for s in sources]


def stage(*values):
    return lax.optimization_barrier(values)


def after(value, *earlier):
    return lax.optimization_barrier((value, *earlier))[0]


def add(a, b):
    return (a.astype(F32) + b.astype(F32)).astype(BF)


def pick(v, at, axis):
    return lax.dynamic_index_in_dim(v, at, axis, keepdims=False)


class Sum:
    def __init__(self, grid, tables, sends, keeps, rows=False, split=False):
        self.grid, self.tables, self.rows_under, self.split = grid, tables, rows, split
        self.shape = (grid.z, 2, 2)
        self.keeps = keeps
        self.got = [grid.other_core(s) for s in sends]

    def core(self):
        block = lambda v: v.reshape(*self.shape, *v.shape[1:])
        self.keeps, self.got = [block(k) for k in self.keeps], [block(g) for g in self.got]
        self.away = route(self.tables[0], self.keeps, self.got, (), self.rows_under, self.split)
        return self.away

    def near(self):
        self.came = [self.grid.along(v, 0) for v in self.away]

    def middle(self):
        self.away, self.stay = route(self.tables[1], self.keeps, self.got, self.came, self.rows_under)
        return self.away

    def far(self):
        self.got = self.grid.along(self.away, 1)

    def last(self):
        self.own = add(self.stay, self.got)[0]
        return self.own

    def up(self):
        z = self.grid.here()[0]
        away = jnp.stack([pick(self.own, z ^ 1, 0), pick(self.own, z ^ 3, 0)])
        self.stay = jnp.stack([pick(self.own, z, 0), pick(self.own, z ^ 2, 0)])
        self.got = self.grid.up(away, 1)

    def across(self):
        self.stay = add(self.stay, self.got)
        self.got = self.grid.up(self.stay[1], 2)

    def rows(self):
        return self.stay[0].astype(F32) + self.got.astype(F32)


def own_rows(grid, total):
    c = grid.here()[3]
    r = total.shape[0] // 2
    other = grid.other_core(lax.dynamic_slice_in_dim(total, (1 - c) * r, r, 0))
    return both(c == 0, lax.dynamic_slice_in_dim(total, c * r, r, 0), other, 1)


def stack_small(vectors):
    total = jnp.zeros((8, 128), BF)
    for i, v in enumerate(vectors):
        total = total + jnp.pad(v.reshape(1, -1), ((i, 7 - i), (0, 128 - v.shape[0])))
    return total


def gather_small(count, vectors):
    flat = stack_small(vectors)
    return lax.all_to_all(jnp.broadcast_to(flat[:, None], (8, count, 128)), AXES, 1, 1, tiled=True)


def scatter_small(cut):
    return jnp.sum(lax.all_to_all(cut, AXES, 1, 1, tiled=True), axis=1)


def halves_of(weight):
    h = weight.shape[1] // 2
    return [weight[None, :, :h], weight[None, :, h:]]


def local(
    mesh,
    tokens,
    norm1_gain,
    norm1_bias,
    qkv_weight,
    qkv_bias,
    out_weight,
    out_bias,
    norm2_gain,
    norm2_bias,
    fc_weight,
    fc_bias,
    proj_weight,
    proj_bias,
    seq_lengths,
    out_cotangent,
):
    d = tokens.shape[1]
    grid = Grid(mesh, out_weight.shape[0])
    blocks = grid.blocks
    vectors = [norm1_gain, norm1_bias, out_bias, norm2_gain, norm2_bias, proj_bias, qkv_bias, fc_bias]
    if grid.paired:
        place = jnp.asarray(grid.table())[lax.axis_index(AXES)]
        wide_place = jnp.asarray(grid.wide_table())[lax.axis_index(AXES)]
        tables = [jnp.asarray(v)[lax.axis_index(AXES)] for v in grid.routes()]
        core = grid.here()[3].reshape(1).astype(jnp.int32)
        extra = jnp.pad(stack_small(vectors), ((0, qkv_weight.shape[0] - 8), (0, 0)))
        pair_qkv = pair_rows(grid, qkv_weight, extra)
        place, fc_shard, out_shard, proj_shard, pair_qkv = stage(
            place, fc_weight, out_weight, proj_weight, pair_qkv
        )
        stack_qkv = spread_z(grid, pair_qkv)
        first = jnp.concatenate([pair_rows(grid, fc_shard), pair_rows(grid, out_shard)], 1)
        second = pair_rows(grid, proj_shard)
        near_second = grid.along(second, 0)
        stack_qkv, first, second, near_second = stage(stack_qkv, first, second, near_second)
        two_second = jnp.stack([second, near_second])
        near_qkv, far_qkv = grid.along(stack_qkv, 0), grid.along(stack_qkv, 1)
        two_first = grid.up(first, 2)
        others = [grid.other_core(stack_qkv)]
        near_qkv, far_qkv, two_first, *others = stage(near_qkv, far_qkv, two_first, *others)
        last_qkv = grid.along(near_qkv, 1)
        two_first = jnp.stack([first, two_first])
        four_first = grid.up(two_first, 1)
        across_second = grid.up(two_second, 2)
        others += [grid.other_core(v) for v in (near_qkv, far_qkv)]
        last_qkv, across_second, two_first, four_first, *others = stage(
            last_qkv, across_second, two_first, four_first, *others
        )
        qkv_sources = [stack_qkv, near_qkv, far_qkv, last_qkv, *others, grid.other_core(last_qkv)]
        stack_first = jnp.concatenate([two_first, four_first])
        near_first, far_first = grid.along(stack_first, 0), grid.along(stack_first, 1)
        four_second = jnp.concatenate([two_second, across_second])
        beyond_second = grid.up(four_second, 1)
        others = [grid.other_core(stack_first)]
        *qkv_sources, stack_first = stage(*qkv_sources, stack_first)
        vec = unfold_pieces(place, qkv_sources[:4], grid.count, d)
    else:
        place = wide_place = jnp.asarray(np.array([[0, 0], [1, 0]], np.int32))
        core = jnp.zeros((1,), jnp.int32)
        full = lambda v: lax.all_gather(v, AXES, axis=0, tiled=True)
        qkv_sources = halves_of(full(qkv_weight))
        vec = unfold(gather_small(grid.count, vectors), d)
    qkv, low_one, qkv_full = project(
        place, tokens, vec, qkv_sources, blocks
    )
    if grid.paired:
        qkv, four_second, beyond_second, near_first, far_first, *others = stage(
            qkv, four_second, beyond_second, near_first, far_first, *others
        )
        stack_second = jnp.concatenate([four_second, beyond_second])
        last_first = grid.along(near_first, 1)
        far_second = grid.along(stack_second, 1)
        others += [grid.other_core(near_first), grid.other_core(far_first)]
    attended = [list(attend(seq_lengths, qkv, 4, 0, 512))]
    if grid.paired:
        attended[0][2], qkv, *others = stage(attended[0][2], qkv, *others)
        second_others = [grid.other_core(stack_second)]
    else:
        fcs = halves_of(full(fc_weight))
        outs, out_at = halves_of(full(out_weight)), 0
        projs = halves_of(full(proj_weight))
    attended.append(attend(seq_lengths, qkv, 2, 4, 512))
    mixed = [a[1] for a in attended]
    if grid.paired:
        mixed[1], last_first, *second_others = stage(mixed[1], last_first, *second_others)
        outs = [stack_first, near_first, far_first, last_first, *others, grid.other_core(last_first)]
        fcs, out_at = outs, 4
    middle, low_two, out_full = mix(
        place, mixed, tokens, vec, outs, blocks, out_at
    )
    if grid.paired:
        low_two, far_second = stage(low_two, far_second)
        projs = [stack_second, far_second, *second_others, grid.other_core(far_second)]
    (layer_out, grad_middle, grad_branch, fc_send, fc_keep, proj_send, proj_keep, fc_bias_term, sums) = mlp(
        core, place, wide_place, seq_lengths, middle, low_two, out_cotangent, vec,
        fcs, projs, blocks,
    )
    grad_mixed, out_send, out_keep = unmix(core, seq_lengths, grad_branch, mixed, out_full, blocks)
    if grid.paired:
        fc_sum = Sum(grid, tables, [fc_send], [fc_keep])
        proj_sum = Sum(grid, tables, [proj_send, out_send], [proj_keep, out_keep], True)
        grad_mixed, *fc_sum.away = stage(grad_mixed, *fc_sum.core())
        fc_sum.near()
        grad_mixed, *proj_sum.away = stage(grad_mixed, *proj_sum.core())
        proj_sum.near()
    grad_one = attend_grad(qkv, grad_mixed, attended[0][0], attended[0][2], 0)
    qkv_one = list(unproject(core, low_one, grad_one, blocks))
    if grid.paired:
        qkv_one[2], grad_mixed, fc_sum.came[0], proj_sum.came[0] = stage(
            qkv_one[2], grad_mixed, fc_sum.came[0], proj_sum.came[0]
        )
        fc_sum.middle()
        fc_sum.far()
        proj_sum.middle()
        grad_mixed, fc_sum.stay, proj_sum.away, proj_sum.stay = stage(
            grad_mixed, fc_sum.stay, proj_sum.away, proj_sum.stay
        )
        proj_sum.far()
    grad_two = attend_grad(qkv, grad_mixed, attended[1][0], attended[1][2], 4)
    if grid.paired:
        fc_sum.got, grad_two = stage(fc_sum.got, grad_two)
        fc_sum.last()
        fc_sum.up()
    grads = [grad_one, grad_two]
    qkv_two = unproject(core, low_one, grad_two, blocks)
    if grid.paired:
        qkv_sum = Sum(grid, tables, [qkv_one[0], qkv_two[0]], [qkv_one[1], qkv_two[1]])
        *qkv_sum.got, proj_sum.got = stage(*qkv_sum.got, proj_sum.got)
        grad_middle, *qkv_sum.away = stage(grad_middle, *qkv_sum.core())
        qkv_sum.near()
        grad_middle, proj_sum.own = stage(grad_middle, proj_sum.last())
        proj_sum.up()
    input_grad, first_sums = final(tokens, grads, qkv_full, grad_middle, vec)
    qkv_sums = jnp.concatenate([qkv_one[2], qkv_two[2]], 1)
    cut = fold(first_sums, sums, qkv_sums, fc_bias_term, grid.count)
    if grid.paired:
        cut, qkv_sum.came[0], proj_sum.got, fc_sum.got = stage(cut, qkv_sum.came[0], proj_sum.got, fc_sum.got)
        qkv_sum.middle()
        qkv_sum.far()
        fc_sum.across()
        proj_sum.stay = add(proj_sum.stay, proj_sum.got)
        cut, qkv_sum.got, fc_sum.got, proj_sum.stay = stage(cut, qkv_sum.got, fc_sum.got, proj_sum.stay)
        proj_sum.got = grid.up(proj_sum.stay[1], 2)
        qkv_sum.last()
        qkv_sum.up()
    little = scatter_small(cut)
    if grid.paired:
        qkv_sum.across()
        fc_sum.got, proj_sum.got, qkv_sum.stay = stage(fc_sum.got, proj_sum.got, qkv_sum.stay)
        fc_weight_grad = own_rows(grid, fc_sum.rows())
        total = proj_sum.rows()
        proj_rows = proj_keep.shape[1]
        proj_weight_grad = own_rows(grid, total[:proj_rows])
        out_weight_grad = own_rows(grid, total[proj_rows:])
        shards = [little[s, : vectors[s].shape[0]] for s in range(8)]
        fc_weight_grad, proj_weight_grad, out_weight_grad, qkv_sum.got, *shards = stage(
            fc_weight_grad, proj_weight_grad, out_weight_grad, qkv_sum.got, *shards
        )
        total = qkv_sum.rows()
        wide = qkv_one[1].shape[2]
        ends = [own_rows(grid, total[:, :wide]), own_rows(grid, total[:, wide:])]
    else:
        reduce = lambda v: lax.psum_scatter(v.astype(F32), AXES, scatter_dimension=0, tiled=True)
        side = lambda k, s: jnp.concatenate([k[0], s[0]], 1)
        fc_weight_grad = reduce(side(fc_keep, fc_send))
        out_weight_grad = reduce(side(out_keep, out_send))
        ends = [reduce(side(u[1], u[0])) for u in (qkv_one, qkv_two)]
        proj_weight_grad = reduce(side(proj_keep, proj_send))
        shards = [little[s, : vectors[s].shape[0]] for s in range(8)]
    third = lambda e, i: e[:, i * e.shape[1] // 3 : (i + 1) * e.shape[1] // 3]
    qkv_weight_grad = jnp.concatenate([third(e, i) for i in range(3) for e in ends], 1)
    shard = lambda s: shards[s]
    return (
        layer_out,
        input_grad,
        shard(0),
        shard(1),
        qkv_weight_grad,
        shard(6),
        out_weight_grad,
        shard(2),
        shard(3),
        shard(4),
        fc_weight_grad,
        shard(7),
        proj_weight_grad,
        shard(5),
    )


def solution(mesh):
    matrix, vector = P(AXES, None), P(AXES)
    ins = (
        matrix, vector, vector, matrix, vector, matrix, vector, vector,
        vector, matrix, vector, matrix, vector, vector, matrix,
    )
    outs = (
        matrix, matrix, vector, vector, matrix, vector, matrix, vector,
        vector, vector, matrix, vector, matrix, vector,
    )
    return jax.shard_map(
        functools.partial(local, mesh), mesh=mesh, in_specs=ins, out_specs=outs, check_vma=False
    )
```

```python
import functools
import math

import jax
import jax.numpy as jnp
import numpy as np
from jax import lax
from jax.experimental import pallas as pl
from jax.experimental.pallas import tpu as pltpu
from jax.sharding import PartitionSpec as P

AXES = ("wide", "narrow")
BF, F32 = jnp.bfloat16, jnp.float32
VMEM_CAP = 58 << 20

def params(n=1, cap=VMEM_CAP):
    return pltpu.CompilerParams(dimension_semantics=("arbitrary",) * n, vmem_limit_bytes=cap)

def cost(flops, bytes_accessed, trans=0):
    return pl.CostEstimate(flops=int(3 * flops), bytes_accessed=int(3 * bytes_accessed), transcendentals=int(trans))

def mm(a, b):
    return jnp.dot(a, b, preferred_element_type=F32)

def diagonal_mask(rows, cols):
    key_at = lax.broadcasted_iota(jnp.int32, (rows, cols), 0)
    query_at = lax.broadcasted_iota(jnp.int32, (rows, cols), 1)
    return key_at <= query_at

def attend_kernel(qb, len_ref, qkv_ref, out_t_ref, out_ref, stat_ref, v_t, q_t):
    slot = qkv_ref.shape[1]
    q_t[...] = (qkv_ref[0] * jnp.asarray(0.125, BF)).T
    v_t[...] = qkv_ref[2].T
    half = lax.broadcasted_iota(jnp.int32, (128, 1), 0) < 64
    causal = diagonal_mask(qb, qb)
    length = len_ref[0]
    def scores(i, head):
        mine = half if head == 0 else jnp.logical_not(half)
        qh = jnp.where(mine, q_t[:, i * qb : (i + 1) * qb], jnp.zeros((), BF))
        s_dia = jnp.where(causal, mm(qkv_ref[1, i * qb : (i + 1) * qb, :], qh), -1e30)
        return s_dia, mm(qkv_ref[1, : i * qb, :], qh) if i else None
    tasks = [(i, head) for i in range(slot // qb) for head in range(2)]
    ahead = scores(*tasks[0])
    parts = []
    for at, (i, head) in enumerate(tasks):
        cols = slice(i * qb, (i + 1) * qb)
        s_dia, s_low = ahead
        if at + 1 < len(tasks):
            ahead = scores(*tasks[at + 1])
        top = jnp.max(s_dia, axis=0, keepdims=True)
        if i:
            top = jnp.maximum(top, jnp.max(s_low, axis=0, keepdims=True))
        e_dia = jnp.exp(s_dia - top)
        total = jnp.sum(e_dia, axis=0, keepdims=True)
        vh = v_t[head * 64 : head * 64 + 64, :]
        acc = mm(vh[:, cols], e_dia.astype(BF))
        if i:
            e_low = jnp.exp(s_low - top)
            total = total + jnp.sum(e_low, axis=0, keepdims=True)
            acc = acc + mm(vh[:, : i * qb], e_low.astype(BF))
        stat_ref[0, head : head + 1, cols] = top + jnp.log(total)
        parts.append(acc / total)
        if head == 1:
            both = jnp.concatenate(parts, axis=0)
            parts = []
            seen = (i * qb + lax.broadcasted_iota(jnp.int32, (1, qb), 1)) < length
            both = jnp.where(seen, both, 0.0)
            out_t_ref[:, cols] = both
            out_ref[cols, :] = both.T.astype(BF)

def attend(lengths, qkv, pairs, first, qb=256):
    slot, width = qkv.shape[1], qkv.shape[2]
    return pl.pallas_call(
        functools.partial(attend_kernel, qb),
        name="attend",
        grid=(pairs,),
        in_specs=[
            pl.BlockSpec(memory_space=pltpu.SMEM),
            pl.BlockSpec((3, slot, 128), lambda j: (0, 0, j + first)),
        ],
        out_specs=[
            pl.BlockSpec((128, slot), lambda j: (j, 0)),
            pl.BlockSpec((slot, 128), lambda j: (0, j)),
            pl.BlockSpec((1, 2, slot), lambda j: (j, 0, 0)),
        ],
        out_shape=[
            jax.ShapeDtypeStruct((pairs * 128, slot), F32),
            jax.ShapeDtypeStruct((slot, pairs * 128), BF),
            jax.ShapeDtypeStruct((pairs, 2, slot), F32),
        ],
        scratch_shapes=[pltpu.VMEM((128, slot), BF), pltpu.VMEM((128, slot), BF)],
        compiler_params=params(1, 28 << 20),
        cost_estimate=cost(pairs * 2 * slot * slot * 256, 8e6 * pairs / 6, pairs * slot * slot),
    )(lengths, qkv)

def attend_grad_kernel(qb, qkv_ref, grad_ref, out_t_ref, stat_ref, g_ref, q_t, do_t, k_t, qs, dq_t, dk_s, dv_s):
    slot = qkv_ref.shape[1]
    qs[...] = qkv_ref[0] * jnp.asarray(0.125, BF)
    q_t[...] = qs[...].T
    k_t[...] = qkv_ref[1].T
    do_t[...] = grad_ref[...].T
    half = lax.broadcasted_iota(jnp.int32, (128, 1), 0) < 64
    half_lane = lax.broadcasted_iota(jnp.int32, (1, 128), 1) < 64
    causal = diagonal_mask(qb, qb)
    zero = jnp.zeros((), BF)
    prod = do_t[...].astype(F32) * out_t_ref[...]
    delta = [jnp.sum(prod[h * 64 : h * 64 + 64], axis=0, keepdims=True) for h in range(2)]
    def scores(i, head):
        cols, end = slice(i * qb, (i + 1) * qb), (i + 1) * qb
        mine = half if head == 0 else jnp.logical_not(half)
        qh_t = jnp.where(mine, q_t[:, cols], zero)
        doh_t = jnp.where(mine, do_t[:, cols], zero)
        return mm(qkv_ref[1, :end, :], qh_t), mm(qkv_ref[2, :end, :], doh_t)
    tasks = [(i, head) for i in range(slot // qb) for head in range(2)]
    ahead = scores(*tasks[0])
    for at, (i, head) in enumerate(tasks):
        cols, end = slice(i * qb, (i + 1) * qb), (i + 1) * qb
        s, dp = ahead
        if at + 1 < len(tasks):
            ahead = scores(*tasks[at + 1])
        mine_lane = half_lane if head == 0 else jnp.logical_not(half_lane)
        qh = jnp.where(mine_lane, qs[cols, :], zero)
        doh = jnp.where(mine_lane, grad_ref[cols, :], zero)
        stat = stat_ref[0, head : head + 1, cols]
        dl = delta[head][:, cols]
        p = jnp.exp(s - stat)
        p_dia = jnp.where(causal, p[i * qb :], 0.0)
        p = jnp.concatenate([p[: i * qb], p_dia], axis=0) if i else p_dia
        ds = (p * (dp - dl)).astype(BF)
        pb = p.astype(BF)
        dv_h = mm(pb, doh)
        dk_h = mm(ds, qh)
        dq_t[head * 64 : head * 64 + 64, cols] = mm(k_t[head * 64 : head * 64 + 64, :end], ds)
        if head == 0:
            dv_new, dk_new = dv_h, dk_h
            continue
        dv_new, dk_new = dv_new + dv_h, dk_new + dk_h
        if i:
            dv_s[: i * qb] += dv_new[: i * qb]
            dk_s[: i * qb] += dk_new[: i * qb]
        dv_s[cols] = dv_new[i * qb :]
        dk_s[cols] = dk_new[i * qb :]
    g_ref[0] = (dq_t[...] * 0.125).T.astype(BF)
    g_ref[1] = dk_s[...].astype(BF)
    g_ref[2] = dv_s[...].astype(BF)

def attend_grad(qkv, grad, out_t, stat, first, qb=256):
    slot = qkv.shape[1]
    pairs = out_t.shape[0] // 128
    width = pairs * 128
    return pl.pallas_call(
        functools.partial(attend_grad_kernel, qb),
        name="attend_grad",
        grid=(pairs,),
        in_specs=[
            pl.BlockSpec((3, slot, 128), lambda j: (0, 0, j + first)),
            pl.BlockSpec((slot, 128), lambda j: (0, j + first)),
            pl.BlockSpec((128, slot), lambda j: (j, 0)),
            pl.BlockSpec((1, 2, slot), lambda j: (j, 0, 0)),
        ],
        out_specs=pl.BlockSpec((3, slot, 128), lambda j: (0, 0, j)),
        out_shape=jax.ShapeDtypeStruct((3, slot, width), BF),
        scratch_shapes=[
            pltpu.VMEM((128, slot), BF),
            pltpu.VMEM((128, slot), BF),
            pltpu.VMEM((128, slot), BF),
            pltpu.VMEM((slot, 128), BF),
            pltpu.VMEM((128, slot), F32),
            pltpu.VMEM((slot, 128), F32),
            pltpu.VMEM((slot, 128), F32),
        ],
        compiler_params=params(1, 32 << 20),
        cost_estimate=cost(pairs * 5 * slot * slot * 256, 16e6 * pairs / 6, pairs * 2 * slot * slot),
    )(qkv, grad, out_t, stat)
VECTOR_ROWS = 16
GAIN_ONE, SHIFT_ONE, BIAS_OUT, GAIN_TWO, SHIFT_TWO, BIAS_PROJ, BIAS_QKV, BIAS_FC = 0, 1, 2, 3, 4, 5, 6, 9
branch_scale = 1.0 / math.sqrt(48.0)
norm_epsilon = 1e-05
WHOLE = dict(pipeline_mode=pl.Buffered(1))

def mm_nt(a, b):
    return lax.dot_general(a, b, (((1,), (1,)), ((), ())), preferred_element_type=F32)

def mm_tn(a, b):
    return lax.dot_general(a, b, (((0,), (0,)), ((), ())), preferred_element_type=F32)

def normalised(v):
    mean = jnp.mean(v, axis=-1, keepdims=True)
    centred = v - mean
    var = jnp.mean(centred * centred, axis=-1, keepdims=True)
    scale = lax.rsqrt(var + norm_epsilon)
    return centred * scale, scale

def norm_pull(n, scale, gain, u):
    ug = u * gain
    a = jnp.mean(ug, axis=-1, keepdims=True)
    b = jnp.mean(ug * n, axis=-1, keepdims=True)
    return (ug - a - n * b) * scale

def row_of(ref, at):
    return ref[at : at + 1, :]

def whole(shape, index=None):
    zeros = (0,) * len(shape)
    return pl.BlockSpec(shape, (lambda *_: index or zeros), **WHOLE)

def assemble(place, sources, target):
    wide = target.shape[2] // 2
    for s, source in enumerate(sources):
        for half in range(2):
            @pl.when(place[s, 0] == half)
            def _():
                for p in range(source.shape[0]):
                    target[place[s, 1 + p], :, half * wide : (half + 1) * wide] = source[p, :, :wide]

def fetch(place, sources, target, sem):
    wide = target.shape[2] // 2
    for s, source in enumerate(sources):
        lanes = pl.ds(pl.multiple_of(place[s, 0] * wide, 128), wide)
        for p in range(source.shape[0]):
            pltpu.make_async_copy(
                source.at[p, :, pl.ds(0, wide)], target.at[place[s, 1 + p], :, lanes], sem
            ).start()

def arrived(target, sem):
    pltpu.make_async_copy(target, target, sem).wait()

def project_kernel(n_src, place, x_ref, vec_ref, *rest):
    sources, (qkv_ref, low_ref, w_ref) = rest[:n_src], rest[n_src:]
    @pl.when(pl.program_id(0) == 0)
    def _():
        assemble(place, sources, w_ref)
    n, _ = normalised(x_ref[...].astype(F32))
    low = (n * row_of(vec_ref, GAIN_ONE) + row_of(vec_ref, SHIFT_ONE)).astype(BF)
    low_ref[...] = low
    d = low.shape[1]
    for part in range(3):
        w = w_ref[:, :, part * d : (part + 1) * d].reshape(d, d)
        qkv_ref[part] = (mm(low, w) + row_of(vec_ref, BIAS_QKV + part)).astype(BF)

def project(place, x, vec, sources, blocks, rows=256):
    t, d = x.shape
    r, wide = d // blocks, 3 * d // 2
    return pl.pallas_call(
        functools.partial(project_kernel, len(sources)),
        name="project",
        grid_spec=pltpu.PrefetchScalarGridSpec(
            num_scalar_prefetch=1,
            grid=(t // rows,),
            in_specs=[
                pl.BlockSpec((rows, d), lambda i, p: (i, 0)),
                whole(vec.shape),
                *[whole(s.shape) for s in sources],
            ],
            out_specs=[
                pl.BlockSpec((3, rows, d), lambda i, p: (0, i, 0)),
                pl.BlockSpec((rows, d), lambda i, p: (i, 0)),
                whole((blocks, r, 2 * wide)),
            ],
        ),
        out_shape=[
            jax.ShapeDtypeStruct((3, t, d), BF),
            jax.ShapeDtypeStruct((t, d), BF),
            jax.ShapeDtypeStruct((blocks, r, 2 * wide), BF),
        ],
        compiler_params=params(1, 32 << 20),
        cost_estimate=cost(2 * t * d * 3 * d, 18e6),
    )(place, x, vec, *sources)

def mix_kernel(n_src, place, x_ref, vec_ref, *rest):
    sources, parts, (mid_ref, low_ref, w_ref) = rest[:n_src], rest[n_src:-3], rest[-3:]
    @pl.when(pl.program_id(0) == 0)
    def _():
        assemble(place, sources, w_ref)
    d = x_ref.shape[1]
    w = w_ref[...].reshape(d, d)
    mid = x_ref[...].astype(F32) + branch_scale * (mm(jnp.concatenate([p[...] for p in parts], 1), w) + row_of(vec_ref, BIAS_OUT))
    mid_ref[...] = mid
    n, _ = normalised(mid)
    low_ref[...] = (n * row_of(vec_ref, GAIN_TWO) + row_of(vec_ref, SHIFT_TWO)).astype(BF)

def mix(place, parts, x, vec, sources, blocks, column, rows=256):
    t, d = x.shape
    r, np_ = d // blocks, sources[0].shape[0]
    return pl.pallas_call(
        functools.partial(mix_kernel, len(sources)),
        name="mix",
        grid_spec=pltpu.PrefetchScalarGridSpec(
            num_scalar_prefetch=1,
            grid=(t // rows,),
            in_specs=[
                pl.BlockSpec((rows, d), lambda i, p: (i, 0)),
                whole(vec.shape),
                *[whole((np_, r, d // 2), (0, 0, column)) for s in sources],
                *[pl.BlockSpec((rows, p.shape[1]), lambda i, p: (i, 0)) for p in parts],
            ],
            out_specs=[
                pl.BlockSpec((rows, d), lambda i, p: (i, 0)),
                pl.BlockSpec((rows, d), lambda i, p: (i, 0)),
                whole((blocks, r, d)),
            ],
        ),
        out_shape=[
            jax.ShapeDtypeStruct((t, d), F32),
            jax.ShapeDtypeStruct((t, d), BF),
            jax.ShapeDtypeStruct((blocks, r, d), BF),
        ],
        compiler_params=params(1, 24 << 20),
        cost_estimate=cost(2 * t * d * d, 9e6),
    )(place, x, vec, *sources, *parts)

def mlp_kernel(n_src, rb, core, place, wide_place, lens, low_ref, cot_ref, bias_ref, mid_hbm, *rest):
    fcs, projs, rest = rest[: n_src[0]], rest[n_src[0] : sum(n_src)], rest[sum(n_src) :]
    (out_hbm, gmid_hbm, gbr_hbm, fsend_hbm, fkeep_hbm, psend_ref, pkeep_ref, fbg_ref, vec_ref,
     fc_s, proj_s, g2_s, second_s, act_s, gpre_s, mid_s, out_s, gmid_s, gbr_s, f_s, sems) = rest
    t, d = mid_s.shape
    w, h = 2 * d, d // 2
    step = pl.program_id(0)
    mine = core[0]
    chunk = lax.rem(step + 1 - mine, 2)
    mid_copy = pltpu.make_async_copy(mid_hbm, mid_s, sems.at[2])
    outs = [
        pltpu.make_async_copy(a, b, sems.at[3 + k])
        for k, (a, b) in enumerate(
            ((out_s, out_hbm), (gmid_s, gmid_hbm), (gbr_s, gbr_hbm), (f_s, fsend_hbm), (f_s, fkeep_hbm))
        )
    ]
    def valid_rows(at):
        return (at * rb + lax.broadcasted_iota(jnp.int32, (rb, 1), 0)) < lens[0]
    @pl.when(step == 0)
    def _():
        fetch(wide_place, projs, proj_s, sems.at[0])
        fetch(place, fcs, fc_s, sems.at[1])
        mid_copy.start()
        def begin(i, total):
            at = pl.ds(pl.multiple_of(i * rb, rb), rb)
            g = jnp.where(valid_rows(i), branch_scale * cot_ref[at, :].astype(F32), 0.0).astype(BF)
            g2_s[at, :] = g
            return total + jnp.sum(g.astype(F32), axis=0, keepdims=True)
        vec_ref[0:1] = lax.fori_loop(0, t // rb, begin, jnp.zeros((1, d), F32))
        arrived(proj_s, sems.at[0])
        arrived(fc_s, sems.at[1])
        mid_copy.wait()
    fc = fc_s.at[:, :, pl.ds(pl.multiple_of(chunk * w, w), w)]
    bias = jnp.concatenate([bias_ref[pl.ds(BIAS_FC + 2 * chunk + i, 1), :] for i in range(2)], 1)
    blocks, pr = proj_s.shape[0], proj_s.shape[1]
    if blocks > 1:
        proj = proj_s.at[pl.ds(chunk * (blocks // 2), blocks // 2)]
    else:
        proj = proj_s.at[:, pl.ds(pl.multiple_of(chunk * w, w), w)]
    def rows_step(i, total):
        at = pl.ds(pl.multiple_of(i * rb, rb), rb)
        wf = fc[...].reshape(d, w)
        wp = proj[...].reshape(w, d)
        ga = mm_nt(g2_s[at, :], wp)
        u = mm(low_ref[at, :], wf) + bias
        sq = u * u
        th = jnp.tanh(u * (0.7978845608028654 + (0.7978845608028654 * 0.044715) * sq))
        up = 0.5 + 0.5 * th
        act = (u * up).astype(BF)
        act_s[at, :] = act
        slope = up * (1.0 + (1.0 - up) * (u * (2 * 0.7978845608028654 + (6 * 0.7978845608028654 * 0.044715) * sq)))
        gpb = (ga * slope).astype(BF)
        gpre_s[at, :] = gpb
        more, back = mm(act, wp), mm_nt(gpb, wf)
        @pl.when(step == 0)
        def _():
            second_s[at, :] = more
            gmid_s[at, :] = back
        @pl.when(step == 1)
        def _():
            second_s[at, :] += more
            gmid_s[at, :] += back
        return total + jnp.sum(gpb.astype(F32), axis=0, keepdims=True)
    sums = lax.fori_loop(0, t // rb, rows_step, jnp.zeros((1, w), F32))
    for i in range(2):
        fbg_ref[pl.ds(2 * chunk + i, 1), :] = sums[:, i * d : (i + 1) * d]
    @pl.when(step == 1)
    def _():
        def finish(i, carry):
            at = pl.ds(pl.multiple_of(i * rb, rb), rb)
            mid = mid_s[at, :]
            out_s[at, :] = (mid + branch_scale * (second_s[at, :] + row_of(bias_ref, BIAS_PROJ))).astype(BF)
            n, scale = normalised(mid)
            gh = gmid_s[at, :]
            cot = jnp.where(valid_rows(i), cot_ref[at, :].astype(F32), 0.0)
            gm = cot + norm_pull(n, scale, row_of(bias_ref, GAIN_TWO), gh)
            gmid_s[at, :] = gm
            gb = (branch_scale * gm).astype(BF)
            gbr_s[at, :] = gb
            return (carry[0] + jnp.sum(gh * n, axis=0, keepdims=True),
                    carry[1] + jnp.sum(gh, axis=0, keepdims=True),
                    carry[2] + jnp.sum(gb.astype(F32), axis=0, keepdims=True))
        zero = jnp.zeros((1, d), F32)
        a, b, c = lax.fori_loop(0, t // rb, finish, (zero, zero, zero))
        vec_ref[1:2] = a
        vec_ref[2:3] = b
        vec_ref[3:4] = c
        for copy in outs[:3]:
            copy.start()
    @pl.when(step == 1)
    def _():
        outs[3].wait()
    f_s[...] = mm_tn(low_ref[...], gpre_s[...]).astype(BF).reshape(f_s.shape)
    @pl.when(step == 0)
    def _():
        outs[3].start()
    @pl.when(step == 1)
    def _():
        outs[4].start()
    dproj = mm_tn(act_s[...], g2_s[...]).astype(BF)
    for half in range(2):
        @pl.when(mine == half)
        def _():
            pkeep_ref[...] = dproj[:, half * h : (half + 1) * h].reshape(pkeep_ref.shape)
            psend_ref[...] = dproj[:, (1 - half) * h : (2 - half) * h].reshape(psend_ref.shape)
    @pl.when(step == 1)
    def _():
        for copy in outs[:3] + outs[4:]:
            copy.wait()

def mlp(core, place, wide_place, lens, mid, low, cot, vec, fcs, projs, blocks, rb=512):
    t, d = mid.shape
    r, pr = d // blocks, 4 * d // blocks
    smem, hbm = pl.BlockSpec(memory_space=pltpu.SMEM), pl.BlockSpec(memory_space=pl.ANY)
    turn = lambda i, c: lax.rem(i + 1 - c[0], 2)
    if blocks > 1:
        pspec = pl.BlockSpec((blocks // 2, pr, d // 2), lambda i, c: (turn(i, c), 0, 0))
    else:
        pspec = pl.BlockSpec((1, pr // 2, d // 2), lambda i, c: (0, turn(i, c), 0))
    of = jax.ShapeDtypeStruct
    return pl.pallas_call(
        functools.partial(mlp_kernel, (len(fcs), len(projs)), rb),
        name="mlp",
        grid_spec=pltpu.PrefetchScalarGridSpec(
            num_scalar_prefetch=1,
            grid=(2,),
            in_specs=[smem, smem, smem, whole((t, d)), whole((t, d)), whole(vec.shape), hbm] + [hbm] * len(fcs + projs),
            out_specs=[hbm] * 5 + [pspec, pspec, whole((4, d)), whole((4, d))],
            scratch_shapes=[
                pltpu.VMEM((blocks, r, 4 * d), BF),
                pltpu.VMEM((blocks, pr, d), BF),
                pltpu.VMEM((t, d), BF),
                pltpu.VMEM((t, d), F32),
                pltpu.VMEM((t, 2 * d), BF),
                pltpu.VMEM((t, 2 * d), BF),
                pltpu.VMEM((t, d), F32),
                pltpu.VMEM((t, d), BF),
                pltpu.VMEM((t, d), F32),
                pltpu.VMEM((t, d), BF),
                pltpu.VMEM((blocks, r, 2 * d), BF),
                pltpu.SemaphoreType.DMA((8,)),
            ],
        ),
        out_shape=[
            of((t, d), BF), of((t, d), F32), of((t, d), BF),
            of((blocks, r, 2 * d), BF), of((blocks, r, 2 * d), BF),
            of((blocks, pr, d // 2), BF), of((blocks, pr, d // 2), BF),
            of((4, d), F32), of((4, d), F32),
        ],
        compiler_params=params(),
        cost_estimate=cost(12 * t * d * 4 * d, 40e6, t * 4 * d),
    )(core, place, wide_place, lens, low, cot, vec, mid, *fcs, *projs)

def unmix_kernel(core, lens, gbr_ref, w_ref, *rest):
    parts, (ga_ref, send_ref, keep_ref) = rest[:-3], rest[-3:]
    t, d = gbr_ref.shape
    w = w_ref[...].reshape(d, d)
    seen = lax.broadcasted_iota(jnp.int32, (t, 1), 0) < lens[0]
    ga_ref[...] = jnp.where(seen, mm_nt(gbr_ref[...], w), 0.0).astype(BF)
    dw = jnp.concatenate([mm_tn(p[...], gbr_ref[...]).astype(BF) for p in parts], 0)
    h = d // 2
    for half in range(2):
        @pl.when(core[0] == half)
        def _():
            keep_ref[...] = dw[:, half * h : (half + 1) * h].reshape(keep_ref.shape)
            send_ref[...] = dw[:, (1 - half) * h : (2 - half) * h].reshape(send_ref.shape)

def unmix(core, lens, gbr, parts, w, blocks):
    t, d = gbr.shape
    smem = pl.BlockSpec(memory_space=pltpu.SMEM)
    piece = jax.ShapeDtypeStruct((blocks, d // blocks, d // 2), BF)
    return pl.pallas_call(
        unmix_kernel,
        name="unmix",
        in_specs=[smem, smem] + [pl.BlockSpec(memory_space=pltpu.VMEM)] * (2 + len(parts)),
        out_shape=[jax.ShapeDtypeStruct((t, d), BF), piece, piece],
        compiler_params=params(0, 24 << 20),
        cost_estimate=cost(4 * t * d * d, 9e6),
    )(core, lens, gbr, w, *parts)

def unproject_kernel(blocks, core, low_ref, g_ref, send_ref, keep_ref, sums_ref):
    d, w = low_ref.shape[1], g_ref.shape[2]
    r, h = d // blocks, w // 2
    low_t = low_ref[...].T
    q, k, v = [mm(low_t, g_ref[part]).astype(BF).reshape(blocks, r, w) for part in range(3)]
    for half, refs in ((0, (keep_ref, send_ref)), (1, (send_ref, keep_ref))):
        @pl.when(core[0] == half)
        def _():
            refs[0][:, :, :w] = q
            refs[0][:, :, w:] = k[:, :, :h]
            refs[1][:, :, :h] = k[:, :, h:]
            refs[1][:, :, h:] = v
    for part in range(3):
        sums_ref[part : part + 1] = jnp.sum(g_ref[part].astype(F32), axis=0, keepdims=True)

def unproject(core, low, g, blocks):
    t, d = low.shape
    w = g.shape[2]
    piece = jax.ShapeDtypeStruct((blocks, d // blocks, w // 2 * 3), BF)
    return pl.pallas_call(
        functools.partial(unproject_kernel, blocks),
        name="unproject",
        in_specs=[pl.BlockSpec(memory_space=pltpu.SMEM)] + [pl.BlockSpec(memory_space=pltpu.VMEM)] * 2,
        out_shape=[piece, piece, jax.ShapeDtypeStruct((3, w), F32)],
        compiler_params=params(0, 24 << 20),
        cost_estimate=cost(6 * t * d * w, 10e6 * w / d),
    )(core, low, g)

def route_kernel(count, steps, rows, near, table, *refs):
    inputs, outs = refs[: 2 * count + near], refs[2 * count + near :]
    def write(ref):
        at = 0
        for k, g in zip(inputs[:count], inputs[count : 2 * count]):
            r, w = k.shape[-2:]
            place = (slice(at, at + r), slice(0, w)) if rows else (slice(0, r), slice(at, at + w))
            at += r if rows else w
            total = (k[...].astype(F32) + g[...].astype(F32)).reshape(1, ref.shape[1], r, w)
            came = [v[:, :, place[0], place[1]] for v in inputs[2 * count :]]
            if near == 2:
                came = [jnp.where(table[pl.program_id(0), 2] == 0, *came)]
            if near:
                total = total + came[0].astype(F32)
            ref[:, :, place[0], place[1]] = total.astype(BF)
    for s, ref in enumerate(outs):
        @pl.when(pl.program_id(0) // steps == s)
        def _():
            write(ref)

def route(table, keeps, gots, near=(), rows=False, split=False):
    z = keeps[0].shape[0]
    sizes = [k.shape[-2:] for k in keeps]
    tall = sum(r for r, _ in sizes) if rows else sizes[0][0]
    wide = sizes[0][1] if rows else sum(w for _, w in sizes)
    block = (1, z, tall, wide)
    specs = [pl.BlockSpec((z, 1, 1, *s), lambda i, t: (0, t[i, 0], t[i, 1], 0, 0)) for s in sizes] * 2
    fixed = pl.BlockSpec(block, lambda i, t: (0, 0, 0, 0))
    if near or split:
        steps, outs = 1, [fixed] * 2
        specs += [pl.BlockSpec(block, lambda i, t: (t[i, 2], 0, 0, 0))] if len(near) == 1 else [fixed] * len(near)
    else:
        steps, outs = 2, [pl.BlockSpec(block, lambda i, t: (i, 0, 0, 0))]
    return pl.pallas_call(
        functools.partial(route_kernel, len(keeps), steps, rows, len(near)),
        name="route",
        grid_spec=pltpu.PrefetchScalarGridSpec(
            num_scalar_prefetch=1, grid=(2,), in_specs=specs, out_specs=outs
        ),
        out_shape=[jax.ShapeDtypeStruct((steps, z, tall, wide), BF)] * len(outs),
        compiler_params=params(1, 24 << 20),
        cost_estimate=cost(1e6, 2 * z * tall * wide * 6),
    )(table, *keeps, *gots, *near)

def final_kernel(x_ref, w_ref, gmid_ref, bias_ref, *rest):
    parts, (out_ref, vec_ref) = rest[:-2], rest[-2:]
    d = x_ref.shape[1]
    w = w_ref[...].reshape(d, 3 * d)
    gh = jnp.zeros(x_ref.shape, F32)
    at = 0
    for g in parts:
        for i in range(3):
            gh = gh + mm_nt(g[i], w[:, i * d + at : i * d + at + g.shape[2]])
        at += g.shape[2]
    n, scale = normalised(x_ref[...].astype(F32))
    out_ref[...] = (gmid_ref[...] + norm_pull(n, scale, row_of(bias_ref, GAIN_ONE), gh)).astype(BF)
    @pl.when(pl.program_id(0) == 0)
    def _():
        vec_ref[...] = jnp.zeros_like(vec_ref)
    vec_ref[0:1] += jnp.sum(gh * n, axis=0, keepdims=True)
    vec_ref[1:2] += jnp.sum(gh, axis=0, keepdims=True)

def final(x, parts, w, gmid, vec, rows=256):
    t, d = x.shape
    return pl.pallas_call(
        final_kernel,
        name="final",
        grid=(t // rows,),
        in_specs=[
            pl.BlockSpec((rows, d), lambda i: (i, 0)),
            whole(w.shape),
            pl.BlockSpec((rows, d), lambda i: (i, 0)),
            whole(vec.shape),
            *[pl.BlockSpec((3, rows, g.shape[2]), lambda i: (0, i, 0)) for g in parts],
        ],
        out_specs=[pl.BlockSpec((rows, d), lambda i: (i, 0)), whole((2, d))],
        out_shape=[jax.ShapeDtypeStruct((t, d), BF), jax.ShapeDtypeStruct((2, d), F32)],
        compiler_params=params(1, 32 << 20),
        cost_estimate=cost(6 * t * d * d, 15e6),
    )(x, w, gmid, vec, *parts)
def spread_matrix(size, width):
    row = lax.broadcasted_iota(jnp.int32, (128, width), 0).astype(F32)
    col = lax.broadcasted_iota(jnp.int32, (128, width), 1).astype(F32)
    inside = col - jnp.floor((col + 0.5) / size) * size
    return jnp.where(inside == row, 1.0, 0.0)

def own_columns(count, size, per, width):
    at = lax.broadcasted_iota(jnp.int32, (count, width), 0).astype(F32)
    at = at - jnp.floor((at + 0.5) / per) * per
    col = lax.broadcasted_iota(jnp.int32, (count, width), 1).astype(F32)
    return jnp.logical_and(col >= at * size, col < (at + 1) * size)


def unfold_vectors(rows_of, count, out_ref):
    d = out_ref.shape[1]
    out_ref[...] = jnp.zeros_like(out_ref)
    for rows, slots, first in ((1, range(6), 0), (2, (6,), BIAS_QKV), (4, (7,), BIAS_FC)):
        size, per = d * rows // count, count // rows
        spread = spread_matrix(size, d).astype(BF)
        mine = own_columns(count, size, per, d)
        for s in slots:
            got = jnp.where(mine, mm(rows_of(s), spread), 0.0)
            for r in range(rows):
                to = first + (s if rows == 1 else 2 * r if rows == 2 else r)
                out_ref[to : to + 1] = jnp.sum(got[r * per : (r + 1) * per], axis=0, keepdims=True)

def unfold_kernel(x_ref, out_ref):
    unfold_vectors(lambda s: x_ref[s], x_ref.shape[1], out_ref)

def unfold(x, d):
    return pl.pallas_call(
        unfold_kernel,
        name="unfold",
        in_specs=[pl.BlockSpec(memory_space=pltpu.VMEM)],
        out_shape=jax.ShapeDtypeStruct((VECTOR_ROWS, d), F32),
        compiler_params=params(0, 16 << 20),
        cost_estimate=cost(1e8, 1e6),
    )(x)

def unfold_pieces_kernel(n_src, place, *rest):
    sources, out_ref, x_ref = rest[:n_src], rest[n_src], rest[-1]
    r = sources[0].shape[1] // 2
    for s, source in enumerate(sources):
        for p in range(source.shape[0]):
            tile = source[p].astype(F32)
            for c in range(2):
                x_ref[2 * place[s, 1 + p] + c] = tile[c * r : c * r + 8]
    unfold_vectors(lambda s: x_ref[:, s, :].astype(BF), x_ref.shape[0], out_ref)

def unfold_pieces(place, sources, count, d):
    np_, r, wide = sources[0].shape
    return pl.pallas_call(
        functools.partial(unfold_pieces_kernel, len(sources)),
        name="unfold",
        grid_spec=pltpu.PrefetchScalarGridSpec(
            num_scalar_prefetch=1,
            grid=(1,),
            in_specs=[whole((np_, r, 128), (0, 0, wide // 128 - 1)) for _ in sources],
            out_specs=whole((VECTOR_ROWS, d)),
            scratch_shapes=[pltpu.VMEM((count, 8, 128), F32)],
        ),
        out_shape=jax.ShapeDtypeStruct((VECTOR_ROWS, d), F32),
        compiler_params=params(1, 16 << 20),
        cost_estimate=cost(1e8, 1e6),
    )(place, *sources)

def fold_kernel(first_ref, sums_ref, qkv_ref, fc_ref, out_ref):
    count, d = out_ref.shape[1], first_ref.shape[1]
    singles = [
        first_ref[0:1], first_ref[1:2], sums_ref[3:4], sums_ref[1:2], sums_ref[2:3], sums_ref[0:1],
    ]
    pairs = [[v] for v in singles] + [[qkv_ref[0:1], qkv_ref[2:3]], [fc_ref[r : r + 1] for r in range(4)]]
    for rows, slots in ((1, range(6)), (2, (6,)), (4, (7,))):
        size, per = d * rows // count, count // rows
        spread = spread_matrix(size, d)
        mine = own_columns(count, size, per, d)
        full = jnp.concatenate(
            [
                jnp.where(mine, jnp.concatenate([jnp.broadcast_to(v, (per, d)) for v in pairs[s]], 0), 0.0)
                for s in slots
            ],
            0,
        )
        got = lax.dot_general(
            full, spread, (((1,), (1,)), ((), ())), precision=lax.Precision.HIGHEST, preferred_element_type=F32
        )
        for i, s in enumerate(slots):
            out_ref[s] = got[i * count : (i + 1) * count]

def fold(first, sums, qkv, fc, count):
    return pl.pallas_call(
        fold_kernel,
        name="fold",
        in_specs=[pl.BlockSpec(memory_space=pltpu.VMEM)] * 4,
        out_shape=jax.ShapeDtypeStruct((8, count, 128), F32),
        compiler_params=params(0, 32 << 20),
        cost_estimate=cost(1e8, 1e6),
    )(first, sums, qkv, fc)


class Grid:
    order = (0, 2, 1, 3)

    def __init__(self, mesh, rows):
        wide, narrow = mesh.shape["wide"], mesh.shape["narrow"]
        self.count = wide * narrow
        self.paired = narrow == 4 and wide == 8 and rows % 8 == 0
        self.blocks = self.count // 2 if self.paired else 1
        self.z = wide // 2

    def index(self, z, x, y, c):
        return ((z * 2 + x) * 2 + y) * 2 + c

    def places(self):
        return [
            (z, x, y, c) for z in range(self.z) for x in range(2) for y in range(2) for c in range(2)
        ]

    def perm(self, target):
        return [(self.index(*at), self.index(*target(*at))) for at in self.places()]

    def here(self):
        w, n = lax.axis_index("wide"), lax.axis_index("narrow")
        return w // 2, w % 2, n // 2, n % 2

    def table(self):
        rows = []
        for z0, x0, y0, c0 in self.places():
            mine = []
            for half in (c0, 1 - c0):
                for ka, kb in ((0, 0), (1, 0), (0, 1), (1, 1)):
                    kx, ky = (ka, kb) if half == 0 else (kb, ka)
                    blocks = [
                        ((z0 ^ kz) * 2 + (x0 ^ kx)) * 2 + (y0 ^ ky) for kz in self.order
                    ]
                    mine.append([half] + blocks)
            rows.append(mine)
        return np.array(rows, np.int32)

    def wide_table(self):
        rows = []
        for z0, x0, y0, c0 in self.places():
            mine = []
            for half in (c0, 1 - c0):
                for kb in (0, 1):
                    line = [half]
                    for kz in self.order:
                        for ka in (0, 1):
                            kx, ky = (ka, kb) if half == 0 else (kb, ka)
                            line.append(((z0 ^ kz) * 2 + (x0 ^ kx)) * 2 + (y0 ^ ky))
                    mine.append(line)
            rows.append(mine)
        return np.array(rows, np.int32)

    def routes(self):
        near, far = [], []
        for z0, x0, y0, c0 in self.places():
            if c0 == 0:
                near.append([[1 - x0, 0], [1 - x0, 1]])
                far.append([[x0, 1 - y0, 1 - y0], [x0, y0, y0]])
            else:
                near.append([[0, 1 - y0], [1, 1 - y0]])
                far.append([[1 - x0, y0, 1 - x0], [x0, y0, x0]])
        return np.array(near, np.int32), np.array(far, np.int32)

    def send(self, value, target):
        return lax.ppermute(value, AXES, self.perm(target))

    def other_core(self, value):
        return self.send(value, lambda z, x, y, c: (z, x, y, 1 - c))

    def along(self, value, turn):
        return self.send(
            value,
            lambda z, x, y, c: (z, 1 - x, y, c) if c == turn else (z, x, 1 - y, c),
        )

    def up(self, value, k):
        return self.send(value, lambda z, x, y, c: (z ^ k, x, y, c))


def both(first, own, other, axis):
    return jnp.where(
        first, jnp.concatenate([own, other], axis), jnp.concatenate([other, own], axis)
    )


def pair_rows(grid, shard, extra=None):
    c = grid.here()[3]
    h = shard.shape[1] // 2
    mine = lax.dynamic_slice_in_dim(shard, c * h, h, 1)
    away = lax.dynamic_slice_in_dim(shard, (1 - c) * h, h, 1)
    if extra is not None:
        mine, away = jnp.concatenate([mine, extra], 1), jnp.concatenate([away, extra], 1)
    return both(c == 0, mine, grid.other_core(away), 0)


def spread_z(grid, pair):
    return jnp.stack([pair] + [grid.up(pair, k) for k in grid.order[1:]])


def with_other(grid, sources):
    return sources + [grid.other_core(s) for s in sources]


def stage(*values):
    return lax.optimization_barrier(values)


def after(value, *earlier):
    return lax.optimization_barrier((value, *earlier))[0]


def add(a, b):
    return (a.astype(F32) + b.astype(F32)).astype(BF)


def pick(v, at, axis):
    return lax.dynamic_index_in_dim(v, at, axis, keepdims=False)


class Sum:
    def __init__(self, grid, tables, sends, keeps, rows=False, split=False):
        self.grid, self.tables, self.rows_under, self.split = grid, tables, rows, split
        self.shape = (grid.z, 2, 2)
        self.keeps = keeps
        self.got = [grid.other_core(s) for s in sends]

    def core(self):
        block = lambda v: v.reshape(*self.shape, *v.shape[1:])
        self.keeps, self.got = [block(k) for k in self.keeps], [block(g) for g in self.got]
        self.away = route(self.tables[0], self.keeps, self.got, (), self.rows_under, self.split)
        return self.away

    def near(self):
        self.came = [self.grid.along(v, 0) for v in self.away]

    def middle(self):
        self.away, self.stay = route(self.tables[1], self.keeps, self.got, self.came, self.rows_under)
        return self.away

    def far(self):
        self.got = self.grid.along(self.away, 1)

    def last(self):
        self.own = add(self.stay, self.got)[0]
        return self.own

    def up(self):
        z = self.grid.here()[0]
        away = jnp.stack([pick(self.own, z ^ 1, 0), pick(self.own, z ^ 3, 0)])
        self.stay = jnp.stack([pick(self.own, z, 0), pick(self.own, z ^ 2, 0)])
        self.got = self.grid.up(away, 1)

    def across(self):
        self.stay = add(self.stay, self.got)
        self.got = self.grid.up(self.stay[1], 2)

    def rows(self):
        return self.stay[0].astype(F32) + self.got.astype(F32)


def own_rows(grid, total):
    c = grid.here()[3]
    r = total.shape[0] // 2
    other = grid.other_core(lax.dynamic_slice_in_dim(total, (1 - c) * r, r, 0))
    return both(c == 0, lax.dynamic_slice_in_dim(total, c * r, r, 0), other, 1)


def stack_small(vectors):
    total = jnp.zeros((8, 128), BF)
    for i, v in enumerate(vectors):
        total = total + jnp.pad(v.reshape(1, -1), ((i, 7 - i), (0, 128 - v.shape[0])))
    return total


def gather_small(count, vectors):
    flat = stack_small(vectors)
    return lax.all_to_all(jnp.broadcast_to(flat[:, None], (8, count, 128)), AXES, 1, 1, tiled=True)


def scatter_small(cut):
    return jnp.sum(lax.all_to_all(cut, AXES, 1, 1, tiled=True), axis=1)


def halves_of(weight):
    h = weight.shape[1] // 2
    return [weight[None, :, :h], weight[None, :, h:]]


def local(
    mesh,
    tokens,
    norm1_gain,
    norm1_bias,
    qkv_weight,
    qkv_bias,
    out_weight,
    out_bias,
    norm2_gain,
    norm2_bias,
    fc_weight,
    fc_bias,
    proj_weight,
    proj_bias,
    seq_lengths,
    out_cotangent,
):
    d = tokens.shape[1]
    grid = Grid(mesh, out_weight.shape[0])
    blocks = grid.blocks
    vectors = [norm1_gain, norm1_bias, out_bias, norm2_gain, norm2_bias, proj_bias, qkv_bias, fc_bias]
    if grid.paired:
        place = jnp.asarray(grid.table())[lax.axis_index(AXES)]
        wide_place = jnp.asarray(grid.wide_table())[lax.axis_index(AXES)]
        tables = [jnp.asarray(v)[lax.axis_index(AXES)] for v in grid.routes()]
        core = grid.here()[3].reshape(1).astype(jnp.int32)
        extra = jnp.pad(stack_small(vectors), ((0, qkv_weight.shape[0] - 8), (0, 0)))
        pair_qkv = pair_rows(grid, qkv_weight, extra)
        place, fc_shard, out_shard, proj_shard, pair_qkv = stage(
            place, fc_weight, out_weight, proj_weight, pair_qkv
        )
        stack_qkv = spread_z(grid, pair_qkv)
        first = jnp.concatenate([pair_rows(grid, fc_shard), pair_rows(grid, out_shard)], 1)
        second = pair_rows(grid, proj_shard)
        near_second = grid.along(second, 0)
        stack_qkv, first, second, near_second = stage(stack_qkv, first, second, near_second)
        two_second = jnp.stack([second, near_second])
        near_qkv, far_qkv = grid.along(stack_qkv, 0), grid.along(stack_qkv, 1)
        two_first = grid.up(first, 2)
        others = [grid.other_core(stack_qkv)]
        near_qkv, far_qkv, two_first, *others = stage(near_qkv, far_qkv, two_first, *others)
        last_qkv = grid.along(near_qkv, 1)
        two_first = jnp.stack([first, two_first])
        four_first = grid.up(two_first, 1)
        across_second = grid.up(two_second, 2)
        others += [grid.other_core(v) for v in (near_qkv, far_qkv)]
        last_qkv, across_second, two_first, four_first, *others = stage(
            last_qkv, across_second, two_first, four_first, *others
        )
        qkv_sources = [stack_qkv, near_qkv, far_qkv, last_qkv, *others, grid.other_core(last_qkv)]
        stack_first = jnp.concatenate([two_first, four_first])
        near_first, far_first = grid.along(stack_first, 0), grid.along(stack_first, 1)
        four_second = jnp.concatenate([two_second, across_second])
        beyond_second = grid.up(four_second, 1)
        others = [grid.other_core(stack_first)]
        *qkv_sources, stack_first = stage(*qkv_sources, stack_first)
        vec = unfold_pieces(place, qkv_sources[:4], grid.count, d)
    else:
        place = wide_place = jnp.asarray(np.array([[0, 0], [1, 0]], np.int32))
        core = jnp.zeros((1,), jnp.int32)
        full = lambda v: lax.all_gather(v, AXES, axis=0, tiled=True)
        qkv_sources = halves_of(full(qkv_weight))
        vec = unfold(gather_small(grid.count, vectors), d)
    qkv, low_one, qkv_full = project(
        place, tokens, vec, qkv_sources, blocks
    )
    if grid.paired:
        qkv, four_second, beyond_second, near_first, far_first, *others = stage(
            qkv, four_second, beyond_second, near_first, far_first, *others
        )
        stack_second = jnp.concatenate([four_second, beyond_second])
        last_first = grid.along(near_first, 1)
        far_second = grid.along(stack_second, 1)
        others += [grid.other_core(near_first), grid.other_core(far_first)]
    attended = [list(attend(seq_lengths, qkv, 4, 0, 512))]
    if grid.paired:
        attended[0][2], qkv, *others = stage(attended[0][2], qkv, *others)
        second_others = [grid.other_core(stack_second)]
    else:
        fcs = halves_of(full(fc_weight))
        outs, out_at = halves_of(full(out_weight)), 0
        projs = halves_of(full(proj_weight))
    attended.append(attend(seq_lengths, qkv, 2, 4, 512))
    mixed = [a[1] for a in attended]
    if grid.paired:
        mixed[1], last_first, *second_others = stage(mixed[1], last_first, *second_others)
        outs = [stack_first, near_first, far_first, last_first, *others, grid.other_core(last_first)]
        fcs, out_at = outs, 4
    middle, low_two, out_full = mix(
        place, mixed, tokens, vec, outs, blocks, out_at
    )
    if grid.paired:
        low_two, far_second = stage(low_two, far_second)
        projs = [stack_second, far_second, *second_others, grid.other_core(far_second)]
    (layer_out, grad_middle, grad_branch, fc_send, fc_keep, proj_send, proj_keep, fc_bias_term, sums) = mlp(
        core, place, wide_place, seq_lengths, middle, low_two, out_cotangent, vec,
        fcs, projs, blocks,
    )
    grad_mixed, out_send, out_keep = unmix(core, seq_lengths, grad_branch, mixed, out_full, blocks)
    if grid.paired:
        fc_sum = Sum(grid, tables, [fc_send], [fc_keep])
        proj_sum = Sum(grid, tables, [proj_send, out_send], [proj_keep, out_keep], True)
        grad_mixed, *fc_sum.away = stage(grad_mixed, *fc_sum.core())
        fc_sum.near()
        grad_mixed, *proj_sum.away = stage(grad_mixed, *proj_sum.core())
        proj_sum.near()
    grad_one = attend_grad(qkv, grad_mixed, attended[0][0], attended[0][2], 0)
    qkv_one = list(unproject(core, low_one, grad_one, blocks))
    if grid.paired:
        qkv_one[2], grad_mixed, fc_sum.came[0], proj_sum.came[0] = stage(
            qkv_one[2], grad_mixed, fc_sum.came[0], proj_sum.came[0]
        )
        fc_sum.middle()
        fc_sum.far()
        proj_sum.middle()
        grad_mixed, fc_sum.stay, proj_sum.away, proj_sum.stay = stage(
            grad_mixed, fc_sum.stay, proj_sum.away, proj_sum.stay
        )
        proj_sum.far()
    grad_two = attend_grad(qkv, grad_mixed, attended[1][0], attended[1][2], 4)
    if grid.paired:
        fc_sum.got, grad_two = stage(fc_sum.got, grad_two)
        fc_sum.last()
        fc_sum.up()
    grads = [grad_one, grad_two]
    qkv_two = unproject(core, low_one, grad_two, blocks)
    if grid.paired:
        qkv_sum = Sum(grid, tables, [qkv_one[0], qkv_two[0]], [qkv_one[1], qkv_two[1]])
        *qkv_sum.got, proj_sum.got = stage(*qkv_sum.got, proj_sum.got)
        grad_middle, *qkv_sum.away = stage(grad_middle, *qkv_sum.core())
        qkv_sum.near()
        grad_middle, proj_sum.own = stage(grad_middle, proj_sum.last())
        proj_sum.up()
    input_grad, first_sums = final(tokens, grads, qkv_full, grad_middle, vec)
    qkv_sums = jnp.concatenate([qkv_one[2], qkv_two[2]], 1)
    cut = fold(first_sums, sums, qkv_sums, fc_bias_term, grid.count)
    if grid.paired:
        cut, qkv_sum.came[0], proj_sum.got, fc_sum.got = stage(cut, qkv_sum.came[0], proj_sum.got, fc_sum.got)
        qkv_sum.middle()
        qkv_sum.far()
        fc_sum.across()
        proj_sum.stay = add(proj_sum.stay, proj_sum.got)
        cut, qkv_sum.got, fc_sum.got, proj_sum.stay = stage(cut, qkv_sum.got, fc_sum.got, proj_sum.stay)
        proj_sum.got = grid.up(proj_sum.stay[1], 2)
        qkv_sum.last()
        qkv_sum.up()
    little = scatter_small(cut)
    if grid.paired:
        qkv_sum.across()
        fc_sum.got, proj_sum.got, qkv_sum.stay = stage(fc_sum.got, proj_sum.got, qkv_sum.stay)
        fc_weight_grad = own_rows(grid, fc_sum.rows())
        total = proj_sum.rows()
        proj_rows = proj_keep.shape[1]
        proj_weight_grad = own_rows(grid, total[:proj_rows])
        out_weight_grad = own_rows(grid, total[proj_rows:])
        shards = [little[s, : vectors[s].shape[0]] for s in range(8)]
        fc_weight_grad, proj_weight_grad, out_weight_grad, qkv_sum.got, *shards = stage(
            fc_weight_grad, proj_weight_grad, out_weight_grad, qkv_sum.got, *shards
        )
        total = qkv_sum.rows()
        wide = qkv_one[1].shape[2]
        ends = [own_rows(grid, total[:, :wide]), own_rows(grid, total[:, wide:])]
    else:
        reduce = lambda v: lax.psum_scatter(v.astype(F32), AXES, scatter_dimension=0, tiled=True)
        side = lambda k, s: jnp.concatenate([k[0], s[0]], 1)
        fc_weight_grad = reduce(side(fc_keep, fc_send))
        out_weight_grad = reduce(side(out_keep, out_send))
        ends = [reduce(side(u[1], u[0])) for u in (qkv_one, qkv_two)]
        proj_weight_grad = reduce(side(proj_keep, proj_send))
        shards = [little[s, : vectors[s].shape[0]] for s in range(8)]
    third = lambda e, i: e[:, i * e.shape[1] // 3 : (i + 1) * e.shape[1] // 3]
    qkv_weight_grad = jnp.concatenate([third(e, i) for i in range(3) for e in ends], 1)
    shard = lambda s: shards[s]
    return (
        layer_out,
        input_grad,
        shard(0),
        shard(1),
        qkv_weight_grad,
        shard(6),
        out_weight_grad,
        shard(2),
        shard(3),
        shard(4),
        fc_weight_grad,
        shard(7),
        proj_weight_grad,
        shard(5),
    )


def solution(mesh):
    matrix, vector = P(AXES, None), P(AXES)
    ins = (
        matrix, vector, vector, matrix, vector, matrix, vector, vector,
        vector, matrix, vector, matrix, vector, vector, matrix,
    )
    outs = (
        matrix, matrix, vector, vector, matrix, vector, matrix, vector,
        vector, vector, matrix, vector, matrix, vector,
    )
    return jax.shard_map(
        functools.partial(local, mesh), mesh=mesh, in_specs=ins, out_specs=outs, check_vma=False
    )
```

```python
import functools
import math

import jax
import jax.numpy as jnp
import numpy as np
from jax import lax
from jax.experimental import pallas as pl
from jax.experimental.pallas import tpu as pltpu
from jax.sharding import PartitionSpec as P

AXES = ("wide", "narrow")
BF, F32 = jnp.bfloat16, jnp.float32
VMEM_CAP = 58 << 20

def params(n=1, cap=VMEM_CAP):
    return pltpu.CompilerParams(dimension_semantics=("arbitrary",) * n, vmem_limit_bytes=cap)

def cost(flops, bytes_accessed, trans=0):
    return pl.CostEstimate(flops=int(2.5 * flops), bytes_accessed=int(2.5 * bytes_accessed), transcendentals=int(trans))

def mm(a, b):
    return jnp.dot(a, b, preferred_element_type=F32)

def diagonal_mask(rows, cols):
    key_at = lax.broadcasted_iota(jnp.int32, (rows, cols), 0)
    query_at = lax.broadcasted_iota(jnp.int32, (rows, cols), 1)
    return key_at <= query_at

def attend_kernel(qb, len_ref, qkv_ref, out_t_ref, out_ref, stat_ref, v_t, q_t):
    slot = qkv_ref.shape[1]
    q_t[...] = (qkv_ref[0] * jnp.asarray(0.125, BF)).T
    v_t[...] = qkv_ref[2].T
    half = lax.broadcasted_iota(jnp.int32, (128, 1), 0) < 64
    causal = diagonal_mask(qb, qb)
    length = len_ref[0]
    def scores(i, head):
        mine = half if head == 0 else jnp.logical_not(half)
        qh = jnp.where(mine, q_t[:, i * qb : (i + 1) * qb], jnp.zeros((), BF))
        s_dia = jnp.where(causal, mm(qkv_ref[1, i * qb : (i + 1) * qb, :], qh), -1e30)
        return s_dia, mm(qkv_ref[1, : i * qb, :], qh) if i else None
    tasks = [(i, head) for i in range(slot // qb) for head in range(2)]
    ahead = scores(*tasks[0])
    parts = []
    for at, (i, head) in enumerate(tasks):
        cols = slice(i * qb, (i + 1) * qb)
        s_dia, s_low = ahead
        if at + 1 < len(tasks):
            ahead = scores(*tasks[at + 1])
        top = jnp.max(s_dia, axis=0, keepdims=True)
        if i:
            top = jnp.maximum(top, jnp.max(s_low, axis=0, keepdims=True))
        e_dia = jnp.exp(s_dia - top)
        total = jnp.sum(e_dia, axis=0, keepdims=True)
        vh = v_t[head * 64 : head * 64 + 64, :]
        acc = mm(vh[:, cols], e_dia.astype(BF))
        if i:
            e_low = jnp.exp(s_low - top)
            total = total + jnp.sum(e_low, axis=0, keepdims=True)
            acc = acc + mm(vh[:, : i * qb], e_low.astype(BF))
        stat_ref[0, head : head + 1, cols] = top + jnp.log(total)
        parts.append(acc / total)
        if head == 1:
            both = jnp.concatenate(parts, axis=0)
            parts = []
            seen = (i * qb + lax.broadcasted_iota(jnp.int32, (1, qb), 1)) < length
            both = jnp.where(seen, both, 0.0)
            out_t_ref[:, cols] = both
            out_ref[cols, :] = both.T.astype(BF)

def attend(lengths, qkv, pairs, first, qb=256):
    slot, width = qkv.shape[1], qkv.shape[2]
    return pl.pallas_call(
        functools.partial(attend_kernel, qb),
        name="attend",
        grid=(pairs,),
        in_specs=[
            pl.BlockSpec(memory_space=pltpu.SMEM),
            pl.BlockSpec((3, slot, 128), lambda j: (0, 0, j + first)),
        ],
        out_specs=[
            pl.BlockSpec((128, slot), lambda j: (j, 0)),
            pl.BlockSpec((slot, 128), lambda j: (0, j)),
            pl.BlockSpec((1, 2, slot), lambda j: (j, 0, 0)),
        ],
        out_shape=[
            jax.ShapeDtypeStruct((pairs * 128, slot), F32),
            jax.ShapeDtypeStruct((slot, pairs * 128), BF),
            jax.ShapeDtypeStruct((pairs, 2, slot), F32),
        ],
        scratch_shapes=[pltpu.VMEM((128, slot), BF), pltpu.VMEM((128, slot), BF)],
        compiler_params=params(1, 28 << 20),
        cost_estimate=cost(pairs * 2 * slot * slot * 256, 8e6 * pairs / 6, pairs * slot * slot),
    )(lengths, qkv)

def attend_grad_kernel(qb, qkv_ref, grad_ref, out_t_ref, stat_ref, g_ref, q_t, do_t, k_t, qs, dq_t, dk_s, dv_s):
    slot = qkv_ref.shape[1]
    qs[...] = qkv_ref[0] * jnp.asarray(0.125, BF)
    q_t[...] = qs[...].T
    k_t[...] = qkv_ref[1].T
    do_t[...] = grad_ref[...].T
    half = lax.broadcasted_iota(jnp.int32, (128, 1), 0) < 64
    half_lane = lax.broadcasted_iota(jnp.int32, (1, 128), 1) < 64
    causal = diagonal_mask(qb, qb)
    zero = jnp.zeros((), BF)
    prod = do_t[...].astype(F32) * out_t_ref[...]
    delta = [jnp.sum(prod[h * 64 : h * 64 + 64], axis=0, keepdims=True) for h in range(2)]
    def scores(i, head):
        cols, end = slice(i * qb, (i + 1) * qb), (i + 1) * qb
        mine = half if head == 0 else jnp.logical_not(half)
        qh_t = jnp.where(mine, q_t[:, cols], zero)
        doh_t = jnp.where(mine, do_t[:, cols], zero)
        return mm(qkv_ref[1, :end, :], qh_t), mm(qkv_ref[2, :end, :], doh_t)
    tasks = [(i, head) for i in range(slot // qb) for head in range(2)]
    ahead = scores(*tasks[0])
    for at, (i, head) in enumerate(tasks):
        cols, end = slice(i * qb, (i + 1) * qb), (i + 1) * qb
        s, dp = ahead
        if at + 1 < len(tasks):
            ahead = scores(*tasks[at + 1])
        mine_lane = half_lane if head == 0 else jnp.logical_not(half_lane)
        qh = jnp.where(mine_lane, qs[cols, :], zero)
        doh = jnp.where(mine_lane, grad_ref[cols, :], zero)
        stat = stat_ref[0, head : head + 1, cols]
        dl = delta[head][:, cols]
        p = jnp.exp(s - stat)
        p_dia = jnp.where(causal, p[i * qb :], 0.0)
        p = jnp.concatenate([p[: i * qb], p_dia], axis=0) if i else p_dia
        ds = (p * (dp - dl)).astype(BF)
        pb = p.astype(BF)
        dv_h = mm(pb, doh)
        dk_h = mm(ds, qh)
        dq_t[head * 64 : head * 64 + 64, cols] = mm(k_t[head * 64 : head * 64 + 64, :end], ds)
        if head == 0:
            dv_new, dk_new = dv_h, dk_h
            continue
        dv_new, dk_new = dv_new + dv_h, dk_new + dk_h
        if i:
            dv_s[: i * qb] += dv_new[: i * qb]
            dk_s[: i * qb] += dk_new[: i * qb]
        dv_s[cols] = dv_new[i * qb :]
        dk_s[cols] = dk_new[i * qb :]
    g_ref[0] = (dq_t[...] * 0.125).T.astype(BF)
    g_ref[1] = dk_s[...].astype(BF)
    g_ref[2] = dv_s[...].astype(BF)

def attend_grad(qkv, grad, out_t, stat, first, qb=256):
    slot = qkv.shape[1]
    pairs = out_t.shape[0] // 128
    width = pairs * 128
    return pl.pallas_call(
        functools.partial(attend_grad_kernel, qb),
        name="attend_grad",
        grid=(pairs,),
        in_specs=[
            pl.BlockSpec((3, slot, 128), lambda j: (0, 0, j + first)),
            pl.BlockSpec((slot, 128), lambda j: (0, j + first)),
            pl.BlockSpec((128, slot), lambda j: (j, 0)),
            pl.BlockSpec((1, 2, slot), lambda j: (j, 0, 0)),
        ],
        out_specs=pl.BlockSpec((3, slot, 128), lambda j: (0, 0, j)),
        out_shape=jax.ShapeDtypeStruct((3, slot, width), BF),
        scratch_shapes=[
            pltpu.VMEM((128, slot), BF),
            pltpu.VMEM((128, slot), BF),
            pltpu.VMEM((128, slot), BF),
            pltpu.VMEM((slot, 128), BF),
            pltpu.VMEM((128, slot), F32),
            pltpu.VMEM((slot, 128), F32),
            pltpu.VMEM((slot, 128), F32),
        ],
        compiler_params=params(1, 32 << 20),
        cost_estimate=cost(pairs * 5 * slot * slot * 256, 16e6 * pairs / 6, pairs * 2 * slot * slot),
    )(qkv, grad, out_t, stat)
VECTOR_ROWS = 16
GAIN_ONE, SHIFT_ONE, BIAS_OUT, GAIN_TWO, SHIFT_TWO, BIAS_PROJ, BIAS_QKV, BIAS_FC = 0, 1, 2, 3, 4, 5, 6, 9
branch_scale = 1.0 / math.sqrt(48.0)
norm_epsilon = 1e-05
WHOLE = dict(pipeline_mode=pl.Buffered(1))

def mm_nt(a, b):
    return lax.dot_general(a, b, (((1,), (1,)), ((), ())), preferred_element_type=F32)

def mm_tn(a, b):
    return lax.dot_general(a, b, (((0,), (0,)), ((), ())), preferred_element_type=F32)

def normalised(v):
    mean = jnp.mean(v, axis=-1, keepdims=True)
    centred = v - mean
    var = jnp.mean(centred * centred, axis=-1, keepdims=True)
    scale = lax.rsqrt(var + norm_epsilon)
    return centred * scale, scale

def norm_pull(n, scale, gain, u):
    ug = u * gain
    a = jnp.mean(ug, axis=-1, keepdims=True)
    b = jnp.mean(ug * n, axis=-1, keepdims=True)
    return (ug - a - n * b) * scale

def row_of(ref, at):
    return ref[at : at + 1, :]

def whole(shape, index=None):
    zeros = (0,) * len(shape)
    return pl.BlockSpec(shape, (lambda *_: index or zeros), **WHOLE)

def assemble(place, sources, target):
    wide = target.shape[2] // 2
    for s, source in enumerate(sources):
        for half in range(2):
            @pl.when(place[s, 0] == half)
            def _():
                for p in range(source.shape[0]):
                    target[place[s, 1 + p], :, half * wide : (half + 1) * wide] = source[p, :, :wide]

def fetch(place, sources, target, sem):
    wide = target.shape[2] // 2
    for s, source in enumerate(sources):
        lanes = pl.ds(pl.multiple_of(place[s, 0] * wide, 128), wide)
        for p in range(source.shape[0]):
            pltpu.make_async_copy(
                source.at[p, :, pl.ds(0, wide)], target.at[place[s, 1 + p], :, lanes], sem
            ).start()

def arrived(target, sem):
    pltpu.make_async_copy(target, target, sem).wait()

def project_kernel(n_src, place, x_ref, vec_ref, *rest):
    sources, (qkv_ref, low_ref, w_ref) = rest[:n_src], rest[n_src:]
    @pl.when(pl.program_id(0) == 0)
    def _():
        assemble(place, sources, w_ref)
    n, _ = normalised(x_ref[...].astype(F32))
    low = (n * row_of(vec_ref, GAIN_ONE) + row_of(vec_ref, SHIFT_ONE)).astype(BF)
    low_ref[...] = low
    d = low.shape[1]
    for part in range(3):
        w = w_ref[:, :, part * d : (part + 1) * d].reshape(d, d)
        qkv_ref[part] = (mm(low, w) + row_of(vec_ref, BIAS_QKV + part)).astype(BF)

def project(place, x, vec, sources, blocks, rows=256):
    t, d = x.shape
    r, wide = d // blocks, 3 * d // 2
    return pl.pallas_call(
        functools.partial(project_kernel, len(sources)),
        name="project",
        grid_spec=pltpu.PrefetchScalarGridSpec(
            num_scalar_prefetch=1,
            grid=(t // rows,),
            in_specs=[
                pl.BlockSpec((rows, d), lambda i, p: (i, 0)),
                whole(vec.shape),
                *[whole(s.shape) for s in sources],
            ],
            out_specs=[
                pl.BlockSpec((3, rows, d), lambda i, p: (0, i, 0)),
                pl.BlockSpec((rows, d), lambda i, p: (i, 0)),
                whole((blocks, r, 2 * wide)),
            ],
        ),
        out_shape=[
            jax.ShapeDtypeStruct((3, t, d), BF),
            jax.ShapeDtypeStruct((t, d), BF),
            jax.ShapeDtypeStruct((blocks, r, 2 * wide), BF),
        ],
        compiler_params=params(1, 32 << 20),
        cost_estimate=cost(2 * t * d * 3 * d, 18e6),
    )(place, x, vec, *sources)

def mix_kernel(n_src, place, x_ref, vec_ref, *rest):
    sources, parts, (mid_ref, low_ref, w_ref) = rest[:n_src], rest[n_src:-3], rest[-3:]
    @pl.when(pl.program_id(0) == 0)
    def _():
        assemble(place, sources, w_ref)
    d = x_ref.shape[1]
    w = w_ref[...].reshape(d, d)
    mid = x_ref[...].astype(F32) + branch_scale * (mm(jnp.concatenate([p[...] for p in parts], 1), w) + row_of(vec_ref, BIAS_OUT))
    mid_ref[...] = mid
    n, _ = normalised(mid)
    low_ref[...] = (n * row_of(vec_ref, GAIN_TWO) + row_of(vec_ref, SHIFT_TWO)).astype(BF)

def mix(place, parts, x, vec, sources, blocks, column, rows=256):
    t, d = x.shape
    r, np_ = d // blocks, sources[0].shape[0]
    return pl.pallas_call(
        functools.partial(mix_kernel, len(sources)),
        name="mix",
        grid_spec=pltpu.PrefetchScalarGridSpec(
            num_scalar_prefetch=1,
            grid=(t // rows,),
            in_specs=[
                pl.BlockSpec((rows, d), lambda i, p: (i, 0)),
                whole(vec.shape),
                *[whole((np_, r, d // 2), (0, 0, column)) for s in sources],
                *[pl.BlockSpec((rows, p.shape[1]), lambda i, p: (i, 0)) for p in parts],
            ],
            out_specs=[
                pl.BlockSpec((rows, d), lambda i, p: (i, 0)),
                pl.BlockSpec((rows, d), lambda i, p: (i, 0)),
                whole((blocks, r, d)),
            ],
        ),
        out_shape=[
            jax.ShapeDtypeStruct((t, d), F32),
            jax.ShapeDtypeStruct((t, d), BF),
            jax.ShapeDtypeStruct((blocks, r, d), BF),
        ],
        compiler_params=params(1, 24 << 20),
        cost_estimate=cost(2 * t * d * d, 9e6),
    )(place, x, vec, *sources, *parts)

def mlp_kernel(n_src, rb, core, place, wide_place, lens, low_ref, cot_ref, bias_ref, mid_hbm, *rest):
    fcs, projs, rest = rest[: n_src[0]], rest[n_src[0] : sum(n_src)], rest[sum(n_src) :]
    (out_hbm, gmid_hbm, gbr_hbm, fsend_hbm, fkeep_hbm, psend_ref, pkeep_ref, fbg_ref, vec_ref,
     fc_s, proj_s, g2_s, second_s, act_s, gpre_s, mid_s, out_s, gmid_s, gbr_s, f_s, sems) = rest
    t, d = mid_s.shape
    w, h = 2 * d, d // 2
    step = pl.program_id(0)
    mine = core[0]
    chunk = lax.rem(step + 1 - mine, 2)
    mid_copy = pltpu.make_async_copy(mid_hbm, mid_s, sems.at[2])
    outs = [
        pltpu.make_async_copy(a, b, sems.at[3 + k])
        for k, (a, b) in enumerate(
            ((out_s, out_hbm), (gmid_s, gmid_hbm), (gbr_s, gbr_hbm), (f_s, fsend_hbm), (f_s, fkeep_hbm))
        )
    ]
    def valid_rows(at):
        return (at * rb + lax.broadcasted_iota(jnp.int32, (rb, 1), 0)) < lens[0]
    @pl.when(step == 0)
    def _():
        fetch(wide_place, projs, proj_s, sems.at[0])
        fetch(place, fcs, fc_s, sems.at[1])
        mid_copy.start()
        def begin(i, total):
            at = pl.ds(pl.multiple_of(i * rb, rb), rb)
            g = jnp.where(valid_rows(i), branch_scale * cot_ref[at, :].astype(F32), 0.0).astype(BF)
            g2_s[at, :] = g
            return total + jnp.sum(g.astype(F32), axis=0, keepdims=True)
        vec_ref[0:1] = lax.fori_loop(0, t // rb, begin, jnp.zeros((1, d), F32))
        arrived(proj_s, sems.at[0])
        arrived(fc_s, sems.at[1])
        mid_copy.wait()
    fc = fc_s.at[:, :, pl.ds(pl.multiple_of(chunk * w, w), w)]
    bias = jnp.concatenate([bias_ref[pl.ds(BIAS_FC + 2 * chunk + i, 1), :] for i in range(2)], 1)
    blocks, pr = proj_s.shape[0], proj_s.shape[1]
    if blocks > 1:
        proj = proj_s.at[pl.ds(chunk * (blocks // 2), blocks // 2)]
    else:
        proj = proj_s.at[:, pl.ds(pl.multiple_of(chunk * w, w), w)]
    def rows_step(i, total):
        at = pl.ds(pl.multiple_of(i * rb, rb), rb)
        wf = fc[...].reshape(d, w)
        wp = proj[...].reshape(w, d)
        ga = mm_nt(g2_s[at, :], wp)
        u = mm(low_ref[at, :], wf) + bias
        sq = u * u
        th = jnp.tanh(u * (0.7978845608028654 + (0.7978845608028654 * 0.044715) * sq))
        up = 0.5 + 0.5 * th
        act = (u * up).astype(BF)
        act_s[at, :] = act
        slope = up * (1.0 + (1.0 - up) * (u * (2 * 0.7978845608028654 + (6 * 0.7978845608028654 * 0.044715) * sq)))
        gpb = (ga * slope).astype(BF)
        gpre_s[at, :] = gpb
        more, back = mm(act, wp), mm_nt(gpb, wf)
        @pl.when(step == 0)
        def _():
            second_s[at, :] = more
            gmid_s[at, :] = back
        @pl.when(step == 1)
        def _():
            second_s[at, :] += more
            gmid_s[at, :] += back
        return total + jnp.sum(gpb.astype(F32), axis=0, keepdims=True)
    sums = lax.fori_loop(0, t // rb, rows_step, jnp.zeros((1, w), F32))
    for i in range(2):
        fbg_ref[pl.ds(2 * chunk + i, 1), :] = sums[:, i * d : (i + 1) * d]
    @pl.when(step == 1)
    def _():
        def finish(i, carry):
            at = pl.ds(pl.multiple_of(i * rb, rb), rb)
            mid = mid_s[at, :]
            out_s[at, :] = (mid + branch_scale * (second_s[at, :] + row_of(bias_ref, BIAS_PROJ))).astype(BF)
            n, scale = normalised(mid)
            gh = gmid_s[at, :]
            cot = jnp.where(valid_rows(i), cot_ref[at, :].astype(F32), 0.0)
            gm = cot + norm_pull(n, scale, row_of(bias_ref, GAIN_TWO), gh)
            gmid_s[at, :] = gm
            gb = (branch_scale * gm).astype(BF)
            gbr_s[at, :] = gb
            return (carry[0] + jnp.sum(gh * n, axis=0, keepdims=True),
                    carry[1] + jnp.sum(gh, axis=0, keepdims=True),
                    carry[2] + jnp.sum(gb.astype(F32), axis=0, keepdims=True))
        zero = jnp.zeros((1, d), F32)
        a, b, c = lax.fori_loop(0, t // rb, finish, (zero, zero, zero))
        vec_ref[1:2] = a
        vec_ref[2:3] = b
        vec_ref[3:4] = c
        for copy in outs[:3]:
            copy.start()
    @pl.when(step == 1)
    def _():
        outs[3].wait()
    f_s[...] = mm_tn(low_ref[...], gpre_s[...]).astype(BF).reshape(f_s.shape)
    @pl.when(step == 0)
    def _():
        outs[3].start()
    @pl.when(step == 1)
    def _():
        outs[4].start()
    dproj = mm_tn(act_s[...], g2_s[...]).astype(BF)
    for half in range(2):
        @pl.when(mine == half)
        def _():
            pkeep_ref[...] = dproj[:, half * h : (half + 1) * h].reshape(pkeep_ref.shape)
            psend_ref[...] = dproj[:, (1 - half) * h : (2 - half) * h].reshape(psend_ref.shape)
    @pl.when(step == 1)
    def _():
        for copy in outs[:3] + outs[4:]:
            copy.wait()

def mlp(core, place, wide_place, lens, mid, low, cot, vec, fcs, projs, blocks, rb=512):
    t, d = mid.shape
    r, pr = d // blocks, 4 * d // blocks
    smem, hbm = pl.BlockSpec(memory_space=pltpu.SMEM), pl.BlockSpec(memory_space=pl.ANY)
    turn = lambda i, c: lax.rem(i + 1 - c[0], 2)
    if blocks > 1:
        pspec = pl.BlockSpec((blocks // 2, pr, d // 2), lambda i, c: (turn(i, c), 0, 0))
    else:
        pspec = pl.BlockSpec((1, pr // 2, d // 2), lambda i, c: (0, turn(i, c), 0))
    of = jax.ShapeDtypeStruct
    return pl.pallas_call(
        functools.partial(mlp_kernel, (len(fcs), len(projs)), rb),
        name="mlp",
        grid_spec=pltpu.PrefetchScalarGridSpec(
            num_scalar_prefetch=1,
            grid=(2,),
            in_specs=[smem, smem, smem, whole((t, d)), whole((t, d)), whole(vec.shape), hbm] + [hbm] * len(fcs + projs),
            out_specs=[hbm] * 5 + [pspec, pspec, whole((4, d)), whole((4, d))],
            scratch_shapes=[
                pltpu.VMEM((blocks, r, 4 * d), BF),
                pltpu.VMEM((blocks, pr, d), BF),
                pltpu.VMEM((t, d), BF),
                pltpu.VMEM((t, d), F32),
                pltpu.VMEM((t, 2 * d), BF),
                pltpu.VMEM((t, 2 * d), BF),
                pltpu.VMEM((t, d), F32),
                pltpu.VMEM((t, d), BF),
                pltpu.VMEM((t, d), F32),
                pltpu.VMEM((t, d), BF),
                pltpu.VMEM((blocks, r, 2 * d), BF),
                pltpu.SemaphoreType.DMA((8,)),
            ],
        ),
        out_shape=[
            of((t, d), BF), of((t, d), F32), of((t, d), BF),
            of((blocks, r, 2 * d), BF), of((blocks, r, 2 * d), BF),
            of((blocks, pr, d // 2), BF), of((blocks, pr, d // 2), BF),
            of((4, d), F32), of((4, d), F32),
        ],
        compiler_params=params(),
        cost_estimate=cost(12 * t * d * 4 * d, 40e6, t * 4 * d),
    )(core, place, wide_place, lens, low, cot, vec, mid, *fcs, *projs)

def unmix_kernel(core, lens, gbr_ref, w_ref, *rest):
    parts, (ga_ref, send_ref, keep_ref) = rest[:-3], rest[-3:]
    t, d = gbr_ref.shape
    w = w_ref[...].reshape(d, d)
    seen = lax.broadcasted_iota(jnp.int32, (t, 1), 0) < lens[0]
    ga_ref[...] = jnp.where(seen, mm_nt(gbr_ref[...], w), 0.0).astype(BF)
    dw = jnp.concatenate([mm_tn(p[...], gbr_ref[...]).astype(BF) for p in parts], 0)
    h = d // 2
    for half in range(2):
        @pl.when(core[0] == half)
        def _():
            keep_ref[...] = dw[:, half * h : (half + 1) * h].reshape(keep_ref.shape)
            send_ref[...] = dw[:, (1 - half) * h : (2 - half) * h].reshape(send_ref.shape)

def unmix(core, lens, gbr, parts, w, blocks):
    t, d = gbr.shape
    smem = pl.BlockSpec(memory_space=pltpu.SMEM)
    piece = jax.ShapeDtypeStruct((blocks, d // blocks, d // 2), BF)
    return pl.pallas_call(
        unmix_kernel,
        name="unmix",
        in_specs=[smem, smem] + [pl.BlockSpec(memory_space=pltpu.VMEM)] * (2 + len(parts)),
        out_shape=[jax.ShapeDtypeStruct((t, d), BF), piece, piece],
        compiler_params=params(0, 24 << 20),
        cost_estimate=cost(4 * t * d * d, 9e6),
    )(core, lens, gbr, w, *parts)

def unproject_kernel(blocks, core, low_ref, g_ref, send_ref, keep_ref, sums_ref):
    d, w = low_ref.shape[1], g_ref.shape[2]
    r, h = d // blocks, w // 2
    low_t = low_ref[...].T
    q, k, v = [mm(low_t, g_ref[part]).astype(BF).reshape(blocks, r, w) for part in range(3)]
    for half, refs in ((0, (keep_ref, send_ref)), (1, (send_ref, keep_ref))):
        @pl.when(core[0] == half)
        def _():
            refs[0][:, :, :w] = q
            refs[0][:, :, w:] = k[:, :, :h]
            refs[1][:, :, :h] = k[:, :, h:]
            refs[1][:, :, h:] = v
    for part in range(3):
        sums_ref[part : part + 1] = jnp.sum(g_ref[part].astype(F32), axis=0, keepdims=True)

def unproject(core, low, g, blocks):
    t, d = low.shape
    w = g.shape[2]
    piece = jax.ShapeDtypeStruct((blocks, d // blocks, w // 2 * 3), BF)
    return pl.pallas_call(
        functools.partial(unproject_kernel, blocks),
        name="unproject",
        in_specs=[pl.BlockSpec(memory_space=pltpu.SMEM)] + [pl.BlockSpec(memory_space=pltpu.VMEM)] * 2,
        out_shape=[piece, piece, jax.ShapeDtypeStruct((3, w), F32)],
        compiler_params=params(0, 24 << 20),
        cost_estimate=cost(6 * t * d * w, 10e6 * w / d),
    )(core, low, g)

def route_kernel(count, steps, rows, near, table, *refs):
    inputs, outs = refs[: 2 * count + near], refs[2 * count + near :]
    def write(ref):
        at = 0
        for k, g in zip(inputs[:count], inputs[count : 2 * count]):
            r, w = k.shape[-2:]
            place = (slice(at, at + r), slice(0, w)) if rows else (slice(0, r), slice(at, at + w))
            at += r if rows else w
            total = (k[...].astype(F32) + g[...].astype(F32)).reshape(1, ref.shape[1], r, w)
            came = [v[:, :, place[0], place[1]] for v in inputs[2 * count :]]
            if near == 2:
                came = [jnp.where(table[pl.program_id(0), 2] == 0, *came)]
            if near:
                total = total + came[0].astype(F32)
            ref[:, :, place[0], place[1]] = total.astype(BF)
    for s, ref in enumerate(outs):
        @pl.when(pl.program_id(0) // steps == s)
        def _():
            write(ref)

def route(table, keeps, gots, near=(), rows=False, split=False):
    z = keeps[0].shape[0]
    sizes = [k.shape[-2:] for k in keeps]
    tall = sum(r for r, _ in sizes) if rows else sizes[0][0]
    wide = sizes[0][1] if rows else sum(w for _, w in sizes)
    block = (1, z, tall, wide)
    specs = [pl.BlockSpec((z, 1, 1, *s), lambda i, t: (0, t[i, 0], t[i, 1], 0, 0)) for s in sizes] * 2
    fixed = pl.BlockSpec(block, lambda i, t: (0, 0, 0, 0))
    if near or split:
        steps, outs = 1, [fixed] * 2
        specs += [pl.BlockSpec(block, lambda i, t: (t[i, 2], 0, 0, 0))] if len(near) == 1 else [fixed] * len(near)
    else:
        steps, outs = 2, [pl.BlockSpec(block, lambda i, t: (i, 0, 0, 0))]
    return pl.pallas_call(
        functools.partial(route_kernel, len(keeps), steps, rows, len(near)),
        name="route",
        grid_spec=pltpu.PrefetchScalarGridSpec(
            num_scalar_prefetch=1, grid=(2,), in_specs=specs, out_specs=outs
        ),
        out_shape=[jax.ShapeDtypeStruct((steps, z, tall, wide), BF)] * len(outs),
        compiler_params=params(1, 24 << 20),
        cost_estimate=cost(1e6, 2 * z * tall * wide * 6),
    )(table, *keeps, *gots, *near)

def final_kernel(x_ref, w_ref, gmid_ref, bias_ref, *rest):
    parts, (out_ref, vec_ref) = rest[:-2], rest[-2:]
    d = x_ref.shape[1]
    w = w_ref[...].reshape(d, 3 * d)
    gh = jnp.zeros(x_ref.shape, F32)
    at = 0
    for g in parts:
        for i in range(3):
            gh = gh + mm_nt(g[i], w[:, i * d + at : i * d + at + g.shape[2]])
        at += g.shape[2]
    n, scale = normalised(x_ref[...].astype(F32))
    out_ref[...] = (gmid_ref[...] + norm_pull(n, scale, row_of(bias_ref, GAIN_ONE), gh)).astype(BF)
    @pl.when(pl.program_id(0) == 0)
    def _():
        vec_ref[...] = jnp.zeros_like(vec_ref)
    vec_ref[0:1] += jnp.sum(gh * n, axis=0, keepdims=True)
    vec_ref[1:2] += jnp.sum(gh, axis=0, keepdims=True)

def final(x, parts, w, gmid, vec, rows=256):
    t, d = x.shape
    return pl.pallas_call(
        final_kernel,
        name="final",
        grid=(t // rows,),
        in_specs=[
            pl.BlockSpec((rows, d), lambda i: (i, 0)),
            whole(w.shape),
            pl.BlockSpec((rows, d), lambda i: (i, 0)),
            whole(vec.shape),
            *[pl.BlockSpec((3, rows, g.shape[2]), lambda i: (0, i, 0)) for g in parts],
        ],
        out_specs=[pl.BlockSpec((rows, d), lambda i: (i, 0)), whole((2, d))],
        out_shape=[jax.ShapeDtypeStruct((t, d), BF), jax.ShapeDtypeStruct((2, d), F32)],
        compiler_params=params(1, 32 << 20),
        cost_estimate=cost(6 * t * d * d, 15e6),
    )(x, w, gmid, vec, *parts)
def spread_matrix(size, width):
    row = lax.broadcasted_iota(jnp.int32, (128, width), 0).astype(F32)
    col = lax.broadcasted_iota(jnp.int32, (128, width), 1).astype(F32)
    inside = col - jnp.floor((col + 0.5) / size) * size
    return jnp.where(inside == row, 1.0, 0.0)

def own_columns(count, size, per, width):
    at = lax.broadcasted_iota(jnp.int32, (count, width), 0).astype(F32)
    at = at - jnp.floor((at + 0.5) / per) * per
    col = lax.broadcasted_iota(jnp.int32, (count, width), 1).astype(F32)
    return jnp.logical_and(col >= at * size, col < (at + 1) * size)


def unfold_vectors(rows_of, count, out_ref):
    d = out_ref.shape[1]
    out_ref[...] = jnp.zeros_like(out_ref)
    for rows, slots, first in ((1, range(6), 0), (2, (6,), BIAS_QKV), (4, (7,), BIAS_FC)):
        size, per = d * rows // count, count // rows
        spread = spread_matrix(size, d).astype(BF)
        mine = own_columns(count, size, per, d)
        for s in slots:
            got = jnp.where(mine, mm(rows_of(s), spread), 0.0)
            for r in range(rows):
                to = first + (s if rows == 1 else 2 * r if rows == 2 else r)
                out_ref[to : to + 1] = jnp.sum(got[r * per : (r + 1) * per], axis=0, keepdims=True)

def unfold_kernel(x_ref, out_ref):
    unfold_vectors(lambda s: x_ref[s], x_ref.shape[1], out_ref)

def unfold(x, d):
    return pl.pallas_call(
        unfold_kernel,
        name="unfold",
        in_specs=[pl.BlockSpec(memory_space=pltpu.VMEM)],
        out_shape=jax.ShapeDtypeStruct((VECTOR_ROWS, d), F32),
        compiler_params=params(0, 16 << 20),
        cost_estimate=cost(1e8, 1e6),
    )(x)

def unfold_pieces_kernel(n_src, place, *rest):
    sources, out_ref, x_ref = rest[:n_src], rest[n_src], rest[-1]
    r = sources[0].shape[1] // 2
    for s, source in enumerate(sources):
        for p in range(source.shape[0]):
            tile = source[p].astype(F32)
            for c in range(2):
                x_ref[2 * place[s, 1 + p] + c] = tile[c * r : c * r + 8]
    unfold_vectors(lambda s: x_ref[:, s, :].astype(BF), x_ref.shape[0], out_ref)

def unfold_pieces(place, sources, count, d):
    np_, r, wide = sources[0].shape
    return pl.pallas_call(
        functools.partial(unfold_pieces_kernel, len(sources)),
        name="unfold",
        grid_spec=pltpu.PrefetchScalarGridSpec(
            num_scalar_prefetch=1,
            grid=(1,),
            in_specs=[whole((np_, r, 128), (0, 0, wide // 128 - 1)) for _ in sources],
            out_specs=whole((VECTOR_ROWS, d)),
            scratch_shapes=[pltpu.VMEM((count, 8, 128), F32)],
        ),
        out_shape=jax.ShapeDtypeStruct((VECTOR_ROWS, d), F32),
        compiler_params=params(1, 16 << 20),
        cost_estimate=cost(1e8, 1e6),
    )(place, *sources)

def fold_kernel(first_ref, sums_ref, qkv_ref, fc_ref, out_ref):
    count, d = out_ref.shape[1], first_ref.shape[1]
    singles = [
        first_ref[0:1], first_ref[1:2], sums_ref[3:4], sums_ref[1:2], sums_ref[2:3], sums_ref[0:1],
    ]
    pairs = [[v] for v in singles] + [[qkv_ref[0:1], qkv_ref[2:3]], [fc_ref[r : r + 1] for r in range(4)]]
    for rows, slots in ((1, range(6)), (2, (6,)), (4, (7,))):
        size, per = d * rows // count, count // rows
        spread = spread_matrix(size, d)
        mine = own_columns(count, size, per, d)
        full = jnp.concatenate(
            [
                jnp.where(mine, jnp.concatenate([jnp.broadcast_to(v, (per, d)) for v in pairs[s]], 0), 0.0)
                for s in slots
            ],
            0,
        )
        got = lax.dot_general(
            full, spread, (((1,), (1,)), ((), ())), precision=lax.Precision.HIGHEST, preferred_element_type=F32
        )
        for i, s in enumerate(slots):
            out_ref[s] = got[i * count : (i + 1) * count]

def fold(first, sums, qkv, fc, count):
    return pl.pallas_call(
        fold_kernel,
        name="fold",
        in_specs=[pl.BlockSpec(memory_space=pltpu.VMEM)] * 4,
        out_shape=jax.ShapeDtypeStruct((8, count, 128), F32),
        compiler_params=params(0, 32 << 20),
        cost_estimate=cost(1e8, 1e6),
    )(first, sums, qkv, fc)


class Grid:
    order = (0, 2, 1, 3)

    def __init__(self, mesh, rows):
        wide, narrow = mesh.shape["wide"], mesh.shape["narrow"]
        self.count = wide * narrow
        self.paired = narrow == 4 and wide == 8 and rows % 8 == 0
        self.blocks = self.count // 2 if self.paired else 1
        self.z = wide // 2

    def index(self, z, x, y, c):
        return ((z * 2 + x) * 2 + y) * 2 + c

    def places(self):
        return [
            (z, x, y, c) for z in range(self.z) for x in range(2) for y in range(2) for c in range(2)
        ]

    def perm(self, target):
        return [(self.index(*at), self.index(*target(*at))) for at in self.places()]

    def here(self):
        w, n = lax.axis_index("wide"), lax.axis_index("narrow")
        return w // 2, w % 2, n // 2, n % 2

    def table(self):
        rows = []
        for z0, x0, y0, c0 in self.places():
            mine = []
            for half in (c0, 1 - c0):
                for ka, kb in ((0, 0), (1, 0), (0, 1), (1, 1)):
                    kx, ky = (ka, kb) if half == 0 else (kb, ka)
                    blocks = [
                        ((z0 ^ kz) * 2 + (x0 ^ kx)) * 2 + (y0 ^ ky) for kz in self.order
                    ]
                    mine.append([half] + blocks)
            rows.append(mine)
        return np.array(rows, np.int32)

    def wide_table(self):
        rows = []
        for z0, x0, y0, c0 in self.places():
            mine = []
            for half in (c0, 1 - c0):
                for kb in (0, 1):
                    line = [half]
                    for kz in self.order:
                        for ka in (0, 1):
                            kx, ky = (ka, kb) if half == 0 else (kb, ka)
                            line.append(((z0 ^ kz) * 2 + (x0 ^ kx)) * 2 + (y0 ^ ky))
                    mine.append(line)
            rows.append(mine)
        return np.array(rows, np.int32)

    def routes(self):
        near, far = [], []
        for z0, x0, y0, c0 in self.places():
            if c0 == 0:
                near.append([[1 - x0, 0], [1 - x0, 1]])
                far.append([[x0, 1 - y0, 1 - y0], [x0, y0, y0]])
            else:
                near.append([[0, 1 - y0], [1, 1 - y0]])
                far.append([[1 - x0, y0, 1 - x0], [x0, y0, x0]])
        return np.array(near, np.int32), np.array(far, np.int32)

    def send(self, value, target):
        return lax.ppermute(value, AXES, self.perm(target))

    def other_core(self, value):
        return self.send(value, lambda z, x, y, c: (z, x, y, 1 - c))

    def along(self, value, turn):
        return self.send(
            value,
            lambda z, x, y, c: (z, 1 - x, y, c) if c == turn else (z, x, 1 - y, c),
        )

    def up(self, value, k):
        return self.send(value, lambda z, x, y, c: (z ^ k, x, y, c))


def both(first, own, other, axis):
    return jnp.where(
        first, jnp.concatenate([own, other], axis), jnp.concatenate([other, own], axis)
    )


def pair_rows(grid, shard, extra=None):
    c = grid.here()[3]
    h = shard.shape[1] // 2
    mine = lax.dynamic_slice_in_dim(shard, c * h, h, 1)
    away = lax.dynamic_slice_in_dim(shard, (1 - c) * h, h, 1)
    if extra is not None:
        mine, away = jnp.concatenate([mine, extra], 1), jnp.concatenate([away, extra], 1)
    return both(c == 0, mine, grid.other_core(away), 0)


def spread_z(grid, pair):
    return jnp.stack([pair] + [grid.up(pair, k) for k in grid.order[1:]])


def with_other(grid, sources):
    return sources + [grid.other_core(s) for s in sources]


def stage(*values):
    return lax.optimization_barrier(values)


def after(value, *earlier):
    return lax.optimization_barrier((value, *earlier))[0]


def add(a, b):
    return (a.astype(F32) + b.astype(F32)).astype(BF)


def pick(v, at, axis):
    return lax.dynamic_index_in_dim(v, at, axis, keepdims=False)


class Sum:
    def __init__(self, grid, tables, sends, keeps, rows=False, split=False):
        self.grid, self.tables, self.rows_under, self.split = grid, tables, rows, split
        self.shape = (grid.z, 2, 2)
        self.keeps = keeps
        self.got = [grid.other_core(s) for s in sends]

    def core(self):
        block = lambda v: v.reshape(*self.shape, *v.shape[1:])
        self.keeps, self.got = [block(k) for k in self.keeps], [block(g) for g in self.got]
        self.away = route(self.tables[0], self.keeps, self.got, (), self.rows_under, self.split)
        return self.away

    def near(self):
        self.came = [self.grid.along(v, 0) for v in self.away]

    def middle(self):
        self.away, self.stay = route(self.tables[1], self.keeps, self.got, self.came, self.rows_under)
        return self.away

    def far(self):
        self.got = self.grid.along(self.away, 1)

    def last(self):
        self.own = add(self.stay, self.got)[0]
        return self.own

    def up(self):
        z = self.grid.here()[0]
        away = jnp.stack([pick(self.own, z ^ 1, 0), pick(self.own, z ^ 3, 0)])
        self.stay = jnp.stack([pick(self.own, z, 0), pick(self.own, z ^ 2, 0)])
        self.got = self.grid.up(away, 1)

    def across(self):
        self.stay = add(self.stay, self.got)
        self.got = self.grid.up(self.stay[1], 2)

    def rows(self):
        return self.stay[0].astype(F32) + self.got.astype(F32)


def own_rows(grid, total):
    c = grid.here()[3]
    r = total.shape[0] // 2
    other = grid.other_core(lax.dynamic_slice_in_dim(total, (1 - c) * r, r, 0))
    return both(c == 0, lax.dynamic_slice_in_dim(total, c * r, r, 0), other, 1)


def stack_small(vectors):
    total = jnp.zeros((8, 128), BF)
    for i, v in enumerate(vectors):
        total = total + jnp.pad(v.reshape(1, -1), ((i, 7 - i), (0, 128 - v.shape[0])))
    return total


def gather_small(count, vectors):
    flat = stack_small(vectors)
    return lax.all_to_all(jnp.broadcast_to(flat[:, None], (8, count, 128)), AXES, 1, 1, tiled=True)


def scatter_small(cut):
    return jnp.sum(lax.all_to_all(cut, AXES, 1, 1, tiled=True), axis=1)


def halves_of(weight):
    h = weight.shape[1] // 2
    return [weight[None, :, :h], weight[None, :, h:]]


def local(
    mesh,
    tokens,
    norm1_gain,
    norm1_bias,
    qkv_weight,
    qkv_bias,
    out_weight,
    out_bias,
    norm2_gain,
    norm2_bias,
    fc_weight,
    fc_bias,
    proj_weight,
    proj_bias,
    seq_lengths,
    out_cotangent,
):
    d = tokens.shape[1]
    grid = Grid(mesh, out_weight.shape[0])
    blocks = grid.blocks
    vectors = [norm1_gain, norm1_bias, out_bias, norm2_gain, norm2_bias, proj_bias, qkv_bias, fc_bias]
    if grid.paired:
        place = jnp.asarray(grid.table())[lax.axis_index(AXES)]
        wide_place = jnp.asarray(grid.wide_table())[lax.axis_index(AXES)]
        tables = [jnp.asarray(v)[lax.axis_index(AXES)] for v in grid.routes()]
        core = grid.here()[3].reshape(1).astype(jnp.int32)
        extra = jnp.pad(stack_small(vectors), ((0, qkv_weight.shape[0] - 8), (0, 0)))
        pair_qkv = pair_rows(grid, qkv_weight, extra)
        place, fc_shard, out_shard, proj_shard, pair_qkv = stage(
            place, fc_weight, out_weight, proj_weight, pair_qkv
        )
        stack_qkv = spread_z(grid, pair_qkv)
        first = jnp.concatenate([pair_rows(grid, fc_shard), pair_rows(grid, out_shard)], 1)
        second = pair_rows(grid, proj_shard)
        near_second = grid.along(second, 0)
        stack_qkv, first, second, near_second = stage(stack_qkv, first, second, near_second)
        two_second = jnp.stack([second, near_second])
        near_qkv, far_qkv = grid.along(stack_qkv, 0), grid.along(stack_qkv, 1)
        two_first = grid.up(first, 2)
        others = [grid.other_core(stack_qkv)]
        near_qkv, far_qkv, two_first, *others = stage(near_qkv, far_qkv, two_first, *others)
        last_qkv = grid.along(near_qkv, 1)
        two_first = jnp.stack([first, two_first])
        four_first = grid.up(two_first, 1)
        across_second = grid.up(two_second, 2)
        others += [grid.other_core(v) for v in (near_qkv, far_qkv)]
        last_qkv, across_second, two_first, four_first, *others = stage(
            last_qkv, across_second, two_first, four_first, *others
        )
        qkv_sources = [stack_qkv, near_qkv, far_qkv, last_qkv, *others, grid.other_core(last_qkv)]
        stack_first = jnp.concatenate([two_first, four_first])
        near_first, far_first = grid.along(stack_first, 0), grid.along(stack_first, 1)
        four_second = jnp.concatenate([two_second, across_second])
        beyond_second = grid.up(four_second, 1)
        others = [grid.other_core(stack_first)]
        *qkv_sources, stack_first = stage(*qkv_sources, stack_first)
        vec = unfold_pieces(place, qkv_sources[:4], grid.count, d)
    else:
        place = wide_place = jnp.asarray(np.array([[0, 0], [1, 0]], np.int32))
        core = jnp.zeros((1,), jnp.int32)
        full = lambda v: lax.all_gather(v, AXES, axis=0, tiled=True)
        qkv_sources = halves_of(full(qkv_weight))
        vec = unfold(gather_small(grid.count, vectors), d)
    qkv, low_one, qkv_full = project(
        place, tokens, vec, qkv_sources, blocks
    )
    if grid.paired:
        qkv, four_second, beyond_second, near_first, far_first, *others = stage(
            qkv, four_second, beyond_second, near_first, far_first, *others
        )
        stack_second = jnp.concatenate([four_second, beyond_second])
        last_first = grid.along(near_first, 1)
        far_second = grid.along(stack_second, 1)
        others += [grid.other_core(near_first), grid.other_core(far_first)]
    attended = [list(attend(seq_lengths, qkv, 4, 0, 512))]
    if grid.paired:
        attended[0][2], qkv, *others = stage(attended[0][2], qkv, *others)
        second_others = [grid.other_core(stack_second)]
    else:
        fcs = halves_of(full(fc_weight))
        outs, out_at = halves_of(full(out_weight)), 0
        projs = halves_of(full(proj_weight))
    attended.append(attend(seq_lengths, qkv, 2, 4, 512))
    mixed = [a[1] for a in attended]
    if grid.paired:
        mixed[1], last_first, *second_others = stage(mixed[1], last_first, *second_others)
        outs = [stack_first, near_first, far_first, last_first, *others, grid.other_core(last_first)]
        fcs, out_at = outs, 4
    middle, low_two, out_full = mix(
        place, mixed, tokens, vec, outs, blocks, out_at
    )
    if grid.paired:
        low_two, far_second = stage(low_two, far_second)
        projs = [stack_second, far_second, *second_others, grid.other_core(far_second)]
    (layer_out, grad_middle, grad_branch, fc_send, fc_keep, proj_send, proj_keep, fc_bias_term, sums) = mlp(
        core, place, wide_place, seq_lengths, middle, low_two, out_cotangent, vec,
        fcs, projs, blocks,
    )
    grad_mixed, out_send, out_keep = unmix(core, seq_lengths, grad_branch, mixed, out_full, blocks)
    if grid.paired:
        fc_sum = Sum(grid, tables, [fc_send], [fc_keep])
        proj_sum = Sum(grid, tables, [proj_send, out_send], [proj_keep, out_keep], True)
        grad_mixed, *fc_sum.away = stage(grad_mixed, *fc_sum.core())
        fc_sum.near()
        grad_mixed, *proj_sum.away = stage(grad_mixed, *proj_sum.core())
        proj_sum.near()
    grad_one = attend_grad(qkv, grad_mixed, attended[0][0], attended[0][2], 0)
    qkv_one = list(unproject(core, low_one, grad_one, blocks))
    if grid.paired:
        qkv_one[2], grad_mixed, fc_sum.came[0], proj_sum.came[0] = stage(
            qkv_one[2], grad_mixed, fc_sum.came[0], proj_sum.came[0]
        )
        fc_sum.middle()
        fc_sum.far()
        proj_sum.middle()
        grad_mixed, fc_sum.stay, proj_sum.away, proj_sum.stay = stage(
            grad_mixed, fc_sum.stay, proj_sum.away, proj_sum.stay
        )
        proj_sum.far()
    grad_two = attend_grad(qkv, grad_mixed, attended[1][0], attended[1][2], 4)
    if grid.paired:
        fc_sum.got, grad_two = stage(fc_sum.got, grad_two)
        fc_sum.last()
        fc_sum.up()
    grads = [grad_one, grad_two]
    qkv_two = unproject(core, low_one, grad_two, blocks)
    if grid.paired:
        qkv_sum = Sum(grid, tables, [qkv_one[0], qkv_two[0]], [qkv_one[1], qkv_two[1]])
        *qkv_sum.got, proj_sum.got = stage(*qkv_sum.got, proj_sum.got)
        grad_middle, *qkv_sum.away = stage(grad_middle, *qkv_sum.core())
        qkv_sum.near()
        grad_middle, proj_sum.own = stage(grad_middle, proj_sum.last())
        proj_sum.up()
    input_grad, first_sums = final(tokens, grads, qkv_full, grad_middle, vec)
    qkv_sums = jnp.concatenate([qkv_one[2], qkv_two[2]], 1)
    cut = fold(first_sums, sums, qkv_sums, fc_bias_term, grid.count)
    if grid.paired:
        cut, qkv_sum.came[0], proj_sum.got, fc_sum.got = stage(cut, qkv_sum.came[0], proj_sum.got, fc_sum.got)
        qkv_sum.middle()
        qkv_sum.far()
        fc_sum.across()
        proj_sum.stay = add(proj_sum.stay, proj_sum.got)
        cut, qkv_sum.got, fc_sum.got, proj_sum.stay = stage(cut, qkv_sum.got, fc_sum.got, proj_sum.stay)
        proj_sum.got = grid.up(proj_sum.stay[1], 2)
        qkv_sum.last()
        qkv_sum.up()
    little = scatter_small(cut)
    if grid.paired:
        qkv_sum.across()
        fc_sum.got, proj_sum.got, qkv_sum.stay = stage(fc_sum.got, proj_sum.got, qkv_sum.stay)
        fc_weight_grad = own_rows(grid, fc_sum.rows())
        total = proj_sum.rows()
        proj_rows = proj_keep.shape[1]
        proj_weight_grad = own_rows(grid, total[:proj_rows])
        out_weight_grad = own_rows(grid, total[proj_rows:])
        shards = [little[s, : vectors[s].shape[0]] for s in range(8)]
        fc_weight_grad, proj_weight_grad, out_weight_grad, qkv_sum.got, *shards = stage(
            fc_weight_grad, proj_weight_grad, out_weight_grad, qkv_sum.got, *shards
        )
        total = qkv_sum.rows()
        wide = qkv_one[1].shape[2]
        ends = [own_rows(grid, total[:, :wide]), own_rows(grid, total[:, wide:])]
    else:
        reduce = lambda v: lax.psum_scatter(v.astype(F32), AXES, scatter_dimension=0, tiled=True)
        side = lambda k, s: jnp.concatenate([k[0], s[0]], 1)
        fc_weight_grad = reduce(side(fc_keep, fc_send))
        out_weight_grad = reduce(side(out_keep, out_send))
        ends = [reduce(side(u[1], u[0])) for u in (qkv_one, qkv_two)]
        proj_weight_grad = reduce(side(proj_keep, proj_send))
        shards = [little[s, : vectors[s].shape[0]] for s in range(8)]
    third = lambda e, i: e[:, i * e.shape[1] // 3 : (i + 1) * e.shape[1] // 3]
    qkv_weight_grad = jnp.concatenate([third(e, i) for i in range(3) for e in ends], 1)
    shard = lambda s: shards[s]
    return (
        layer_out,
        input_grad,
        shard(0),
        shard(1),
        qkv_weight_grad,
        shard(6),
        out_weight_grad,
        shard(2),
        shard(3),
        shard(4),
        fc_weight_grad,
        shard(7),
        proj_weight_grad,
        shard(5),
    )


def solution(mesh):
    matrix, vector = P(AXES, None), P(AXES)
    ins = (
        matrix, vector, vector, matrix, vector, matrix, vector, vector,
        vector, matrix, vector, matrix, vector, vector, matrix,
    )
    outs = (
        matrix, matrix, vector, vector, matrix, vector, matrix, vector,
        vector, vector, matrix, vector, matrix, vector,
    )
    return jax.shard_map(
        functools.partial(local, mesh), mesh=mesh, in_specs=ins, out_specs=outs, check_vma=False
    )
```

```python
import functools
import math

import jax
import jax.numpy as jnp
import numpy as np
from jax import lax
from jax.experimental import pallas as pl
from jax.experimental.pallas import tpu as pltpu
from jax.sharding import PartitionSpec as P

AXES = ("wide", "narrow")
BF, F32 = jnp.bfloat16, jnp.float32
VMEM_CAP = 58 << 20

def params(n=1, cap=VMEM_CAP):
    return pltpu.CompilerParams(dimension_semantics=("arbitrary",) * n, vmem_limit_bytes=cap)

def cost(flops, bytes_accessed, trans=0):
    return pl.CostEstimate(flops=int(2.3 * flops), bytes_accessed=int(2.3 * bytes_accessed), transcendentals=int(trans))

def mm(a, b):
    return jnp.dot(a, b, preferred_element_type=F32)

def diagonal_mask(rows, cols):
    key_at = lax.broadcasted_iota(jnp.int32, (rows, cols), 0)
    query_at = lax.broadcasted_iota(jnp.int32, (rows, cols), 1)
    return key_at <= query_at

def attend_kernel(qb, len_ref, qkv_ref, out_t_ref, out_ref, stat_ref, v_t, q_t):
    slot = qkv_ref.shape[1]
    q_t[...] = (qkv_ref[0] * jnp.asarray(0.125, BF)).T
    v_t[...] = qkv_ref[2].T
    half = lax.broadcasted_iota(jnp.int32, (128, 1), 0) < 64
    causal = diagonal_mask(qb, qb)
    length = len_ref[0]
    def scores(i, head):
        mine = half if head == 0 else jnp.logical_not(half)
        qh = jnp.where(mine, q_t[:, i * qb : (i + 1) * qb], jnp.zeros((), BF))
        s_dia = jnp.where(causal, mm(qkv_ref[1, i * qb : (i + 1) * qb, :], qh), -1e30)
        return s_dia, mm(qkv_ref[1, : i * qb, :], qh) if i else None
    tasks = [(i, head) for i in range(slot // qb) for head in range(2)]
    ahead = scores(*tasks[0])
    parts = []
    for at, (i, head) in enumerate(tasks):
        cols = slice(i * qb, (i + 1) * qb)
        s_dia, s_low = ahead
        if at + 1 < len(tasks):
            ahead = scores(*tasks[at + 1])
        top = jnp.max(s_dia, axis=0, keepdims=True)
        if i:
            top = jnp.maximum(top, jnp.max(s_low, axis=0, keepdims=True))
        e_dia = jnp.exp(s_dia - top)
        total = jnp.sum(e_dia, axis=0, keepdims=True)
        vh = v_t[head * 64 : head * 64 + 64, :]
        acc = mm(vh[:, cols], e_dia.astype(BF))
        if i:
            e_low = jnp.exp(s_low - top)
            total = total + jnp.sum(e_low, axis=0, keepdims=True)
            acc = acc + mm(vh[:, : i * qb], e_low.astype(BF))
        stat_ref[0, head : head + 1, cols] = top + jnp.log(total)
        parts.append(acc / total)
        if head == 1:
            both = jnp.concatenate(parts, axis=0)
            parts = []
            seen = (i * qb + lax.broadcasted_iota(jnp.int32, (1, qb), 1)) < length
            both = jnp.where(seen, both, 0.0)
            out_t_ref[:, cols] = both
            out_ref[cols, :] = both.T.astype(BF)

def attend(lengths, qkv, pairs, first, qb=256):
    slot, width = qkv.shape[1], qkv.shape[2]
    return pl.pallas_call(
        functools.partial(attend_kernel, qb),
        name="attend",
        grid=(pairs,),
        in_specs=[
            pl.BlockSpec(memory_space=pltpu.SMEM),
            pl.BlockSpec((3, slot, 128), lambda j: (0, 0, j + first)),
        ],
        out_specs=[
            pl.BlockSpec((128, slot), lambda j: (j, 0)),
            pl.BlockSpec((slot, 128), lambda j: (0, j)),
            pl.BlockSpec((1, 2, slot), lambda j: (j, 0, 0)),
        ],
        out_shape=[
            jax.ShapeDtypeStruct((pairs * 128, slot), F32),
            jax.ShapeDtypeStruct((slot, pairs * 128), BF),
            jax.ShapeDtypeStruct((pairs, 2, slot), F32),
        ],
        scratch_shapes=[pltpu.VMEM((128, slot), BF), pltpu.VMEM((128, slot), BF)],
        compiler_params=params(1, 28 << 20),
        cost_estimate=cost(pairs * 2 * slot * slot * 256, 8e6 * pairs / 6, pairs * slot * slot),
    )(lengths, qkv)

def attend_grad_kernel(qb, qkv_ref, grad_ref, out_t_ref, stat_ref, g_ref, q_t, do_t, k_t, qs, dq_t, dk_s, dv_s):
    slot = qkv_ref.shape[1]
    qs[...] = qkv_ref[0] * jnp.asarray(0.125, BF)
    q_t[...] = qs[...].T
    k_t[...] = qkv_ref[1].T
    do_t[...] = grad_ref[...].T
    half = lax.broadcasted_iota(jnp.int32, (128, 1), 0) < 64
    half_lane = lax.broadcasted_iota(jnp.int32, (1, 128), 1) < 64
    causal = diagonal_mask(qb, qb)
    zero = jnp.zeros((), BF)
    prod = do_t[...].astype(F32) * out_t_ref[...]
    delta = [jnp.sum(prod[h * 64 : h * 64 + 64], axis=0, keepdims=True) for h in range(2)]
    def scores(i, head):
        cols, end = slice(i * qb, (i + 1) * qb), (i + 1) * qb
        mine = half if head == 0 else jnp.logical_not(half)
        qh_t = jnp.where(mine, q_t[:, cols], zero)
        doh_t = jnp.where(mine, do_t[:, cols], zero)
        return mm(qkv_ref[1, :end, :], qh_t), mm(qkv_ref[2, :end, :], doh_t)
    tasks = [(i, head) for i in range(slot // qb) for head in range(2)]
    ahead = scores(*tasks[0])
    for at, (i, head) in enumerate(tasks):
        cols, end = slice(i * qb, (i + 1) * qb), (i + 1) * qb
        s, dp = ahead
        if at + 1 < len(tasks):
            ahead = scores(*tasks[at + 1])
        mine_lane = half_lane if head == 0 else jnp.logical_not(half_lane)
        qh = jnp.where(mine_lane, qs[cols, :], zero)
        doh = jnp.where(mine_lane, grad_ref[cols, :], zero)
        stat = stat_ref[0, head : head + 1, cols]
        dl = delta[head][:, cols]
        p = jnp.exp(s - stat)
        p_dia = jnp.where(causal, p[i * qb :], 0.0)
        p = jnp.concatenate([p[: i * qb], p_dia], axis=0) if i else p_dia
        ds = (p * (dp - dl)).astype(BF)
        pb = p.astype(BF)
        dv_h = mm(pb, doh)
        dk_h = mm(ds, qh)
        dq_t[head * 64 : head * 64 + 64, cols] = mm(k_t[head * 64 : head * 64 + 64, :end], ds)
        if head == 0:
            dv_new, dk_new = dv_h, dk_h
            continue
        dv_new, dk_new = dv_new + dv_h, dk_new + dk_h
        if i:
            dv_s[: i * qb] += dv_new[: i * qb]
            dk_s[: i * qb] += dk_new[: i * qb]
        dv_s[cols] = dv_new[i * qb :]
        dk_s[cols] = dk_new[i * qb :]
    g_ref[0] = (dq_t[...] * 0.125).T.astype(BF)
    g_ref[1] = dk_s[...].astype(BF)
    g_ref[2] = dv_s[...].astype(BF)

def attend_grad(qkv, grad, out_t, stat, first, qb=256):
    slot = qkv.shape[1]
    pairs = out_t.shape[0] // 128
    width = pairs * 128
    return pl.pallas_call(
        functools.partial(attend_grad_kernel, qb),
        name="attend_grad",
        grid=(pairs,),
        in_specs=[
            pl.BlockSpec((3, slot, 128), lambda j: (0, 0, j + first)),
            pl.BlockSpec((slot, 128), lambda j: (0, j + first)),
            pl.BlockSpec((128, slot), lambda j: (j, 0)),
            pl.BlockSpec((1, 2, slot), lambda j: (j, 0, 0)),
        ],
        out_specs=pl.BlockSpec((3, slot, 128), lambda j: (0, 0, j)),
        out_shape=jax.ShapeDtypeStruct((3, slot, width), BF),
        scratch_shapes=[
            pltpu.VMEM((128, slot), BF),
            pltpu.VMEM((128, slot), BF),
            pltpu.VMEM((128, slot), BF),
            pltpu.VMEM((slot, 128), BF),
            pltpu.VMEM((128, slot), F32),
            pltpu.VMEM((slot, 128), F32),
            pltpu.VMEM((slot, 128), F32),
        ],
        compiler_params=params(1, 32 << 20),
        cost_estimate=cost(pairs * 5 * slot * slot * 256, 16e6 * pairs / 6, pairs * 2 * slot * slot),
    )(qkv, grad, out_t, stat)
VECTOR_ROWS = 16
GAIN_ONE, SHIFT_ONE, BIAS_OUT, GAIN_TWO, SHIFT_TWO, BIAS_PROJ, BIAS_QKV, BIAS_FC = 0, 1, 2, 3, 4, 5, 6, 9
branch_scale = 1.0 / math.sqrt(48.0)
norm_epsilon = 1e-05
WHOLE = dict(pipeline_mode=pl.Buffered(1))

def mm_nt(a, b):
    return lax.dot_general(a, b, (((1,), (1,)), ((), ())), preferred_element_type=F32)

def mm_tn(a, b):
    return lax.dot_general(a, b, (((0,), (0,)), ((), ())), preferred_element_type=F32)

def normalised(v):
    mean = jnp.mean(v, axis=-1, keepdims=True)
    centred = v - mean
    var = jnp.mean(centred * centred, axis=-1, keepdims=True)
    scale = lax.rsqrt(var + norm_epsilon)
    return centred * scale, scale

def norm_pull(n, scale, gain, u):
    ug = u * gain
    a = jnp.mean(ug, axis=-1, keepdims=True)
    b = jnp.mean(ug * n, axis=-1, keepdims=True)
    return (ug - a - n * b) * scale

def row_of(ref, at):
    return ref[at : at + 1, :]

def whole(shape, index=None):
    zeros = (0,) * len(shape)
    return pl.BlockSpec(shape, (lambda *_: index or zeros), **WHOLE)

def assemble(place, sources, target):
    wide = target.shape[2] // 2
    for s, source in enumerate(sources):
        for half in range(2):
            @pl.when(place[s, 0] == half)
            def _():
                for p in range(source.shape[0]):
                    target[place[s, 1 + p], :, half * wide : (half + 1) * wide] = source[p, :, :wide]

def fetch(place, sources, target, sem):
    wide = target.shape[2] // 2
    for s, source in enumerate(sources):
        lanes = pl.ds(pl.multiple_of(place[s, 0] * wide, 128), wide)
        for p in range(source.shape[0]):
            pltpu.make_async_copy(
                source.at[p, :, pl.ds(0, wide)], target.at[place[s, 1 + p], :, lanes], sem
            ).start()

def arrived(target, sem):
    pltpu.make_async_copy(target, target, sem).wait()

def project_kernel(n_src, place, x_ref, vec_ref, *rest):
    sources, (qkv_ref, low_ref, w_ref) = rest[:n_src], rest[n_src:]
    @pl.when(pl.program_id(0) == 0)
    def _():
        assemble(place, sources, w_ref)
    n, _ = normalised(x_ref[...].astype(F32))
    low = (n * row_of(vec_ref, GAIN_ONE) + row_of(vec_ref, SHIFT_ONE)).astype(BF)
    low_ref[...] = low
    d = low.shape[1]
    for part in range(3):
        w = w_ref[:, :, part * d : (part + 1) * d].reshape(d, d)
        qkv_ref[part] = (mm(low, w) + row_of(vec_ref, BIAS_QKV + part)).astype(BF)

def project(place, x, vec, sources, blocks, rows=256):
    t, d = x.shape
    r, wide = d // blocks, 3 * d // 2
    return pl.pallas_call(
        functools.partial(project_kernel, len(sources)),
        name="project",
        grid_spec=pltpu.PrefetchScalarGridSpec(
            num_scalar_prefetch=1,
            grid=(t // rows,),
            in_specs=[
                pl.BlockSpec((rows, d), lambda i, p: (i, 0)),
                whole(vec.shape),
                *[whole(s.shape) for s in sources],
            ],
            out_specs=[
                pl.BlockSpec((3, rows, d), lambda i, p: (0, i, 0)),
                pl.BlockSpec((rows, d), lambda i, p: (i, 0)),
                whole((blocks, r, 2 * wide)),
            ],
        ),
        out_shape=[
            jax.ShapeDtypeStruct((3, t, d), BF),
            jax.ShapeDtypeStruct((t, d), BF),
            jax.ShapeDtypeStruct((blocks, r, 2 * wide), BF),
        ],
        compiler_params=params(1, 32 << 20),
        cost_estimate=cost(2 * t * d * 3 * d, 18e6),
    )(place, x, vec, *sources)

def mix_kernel(n_src, place, x_ref, vec_ref, *rest):
    sources, parts, (mid_ref, low_ref, w_ref) = rest[:n_src], rest[n_src:-3], rest[-3:]
    @pl.when(pl.program_id(0) == 0)
    def _():
        assemble(place, sources, w_ref)
    d = x_ref.shape[1]
    w = w_ref[...].reshape(d, d)
    mid = x_ref[...].astype(F32) + branch_scale * (mm(jnp.concatenate([p[...] for p in parts], 1), w) + row_of(vec_ref, BIAS_OUT))
    mid_ref[...] = mid
    n, _ = normalised(mid)
    low_ref[...] = (n * row_of(vec_ref, GAIN_TWO) + row_of(vec_ref, SHIFT_TWO)).astype(BF)

def mix(place, parts, x, vec, sources, blocks, column, rows=256):
    t, d = x.shape
    r, np_ = d // blocks, sources[0].shape[0]
    return pl.pallas_call(
        functools.partial(mix_kernel, len(sources)),
        name="mix",
        grid_spec=pltpu.PrefetchScalarGridSpec(
            num_scalar_prefetch=1,
            grid=(t // rows,),
            in_specs=[
                pl.BlockSpec((rows, d), lambda i, p: (i, 0)),
                whole(vec.shape),
                *[whole((np_, r, d // 2), (0, 0, column)) for s in sources],
                *[pl.BlockSpec((rows, p.shape[1]), lambda i, p: (i, 0)) for p in parts],
            ],
            out_specs=[
                pl.BlockSpec((rows, d), lambda i, p: (i, 0)),
                pl.BlockSpec((rows, d), lambda i, p: (i, 0)),
                whole((blocks, r, d)),
            ],
        ),
        out_shape=[
            jax.ShapeDtypeStruct((t, d), F32),
            jax.ShapeDtypeStruct((t, d), BF),
            jax.ShapeDtypeStruct((blocks, r, d), BF),
        ],
        compiler_params=params(1, 24 << 20),
        cost_estimate=cost(2 * t * d * d, 9e6),
    )(place, x, vec, *sources, *parts)

def mlp_kernel(n_src, rb, core, place, wide_place, lens, low_ref, cot_ref, bias_ref, mid_hbm, *rest):
    fcs, projs, rest = rest[: n_src[0]], rest[n_src[0] : sum(n_src)], rest[sum(n_src) :]
    (out_hbm, gmid_hbm, gbr_hbm, fsend_hbm, fkeep_hbm, psend_ref, pkeep_ref, fbg_ref, vec_ref,
     fc_s, proj_s, g2_s, second_s, act_s, gpre_s, mid_s, out_s, gmid_s, gbr_s, f_s, sems) = rest
    t, d = mid_s.shape
    w, h = 2 * d, d // 2
    step = pl.program_id(0)
    mine = core[0]
    chunk = lax.rem(step + 1 - mine, 2)
    mid_copy = pltpu.make_async_copy(mid_hbm, mid_s, sems.at[2])
    outs = [
        pltpu.make_async_copy(a, b, sems.at[3 + k])
        for k, (a, b) in enumerate(
            ((out_s, out_hbm), (gmid_s, gmid_hbm), (gbr_s, gbr_hbm), (f_s, fsend_hbm), (f_s, fkeep_hbm))
        )
    ]
    def valid_rows(at):
        return (at * rb + lax.broadcasted_iota(jnp.int32, (rb, 1), 0)) < lens[0]
    @pl.when(step == 0)
    def _():
        fetch(wide_place, projs, proj_s, sems.at[0])
        fetch(place, fcs, fc_s, sems.at[1])
        mid_copy.start()
        def begin(i, total):
            at = pl.ds(pl.multiple_of(i * rb, rb), rb)
            g = jnp.where(valid_rows(i), branch_scale * cot_ref[at, :].astype(F32), 0.0).astype(BF)
            g2_s[at, :] = g
            return total + jnp.sum(g.astype(F32), axis=0, keepdims=True)
        vec_ref[0:1] = lax.fori_loop(0, t // rb, begin, jnp.zeros((1, d), F32))
        arrived(proj_s, sems.at[0])
        arrived(fc_s, sems.at[1])
        mid_copy.wait()
    fc = fc_s.at[:, :, pl.ds(pl.multiple_of(chunk * w, w), w)]
    bias = jnp.concatenate([bias_ref[pl.ds(BIAS_FC + 2 * chunk + i, 1), :] for i in range(2)], 1)
    blocks, pr = proj_s.shape[0], proj_s.shape[1]
    if blocks > 1:
        proj = proj_s.at[pl.ds(chunk * (blocks // 2), blocks // 2)]
    else:
        proj = proj_s.at[:, pl.ds(pl.multiple_of(chunk * w, w), w)]
    def rows_step(i, total):
        at = pl.ds(pl.multiple_of(i * rb, rb), rb)
        wf = fc[...].reshape(d, w)
        wp = proj[...].reshape(w, d)
        ga = mm_nt(g2_s[at, :], wp)
        u = mm(low_ref[at, :], wf) + bias
        sq = u * u
        th = jnp.tanh(u * (0.7978845608028654 + (0.7978845608028654 * 0.044715) * sq))
        up = 0.5 + 0.5 * th
        act = (u * up).astype(BF)
        act_s[at, :] = act
        slope = up * (1.0 + (1.0 - up) * (u * (2 * 0.7978845608028654 + (6 * 0.7978845608028654 * 0.044715) * sq)))
        gpb = (ga * slope).astype(BF)
        gpre_s[at, :] = gpb
        more, back = mm(act, wp), mm_nt(gpb, wf)
        @pl.when(step == 0)
        def _():
            second_s[at, :] = more
            gmid_s[at, :] = back
        @pl.when(step == 1)
        def _():
            second_s[at, :] += more
            gmid_s[at, :] += back
        return total + jnp.sum(gpb.astype(F32), axis=0, keepdims=True)
    sums = lax.fori_loop(0, t // rb, rows_step, jnp.zeros((1, w), F32))
    for i in range(2):
        fbg_ref[pl.ds(2 * chunk + i, 1), :] = sums[:, i * d : (i + 1) * d]
    @pl.when(step == 1)
    def _():
        def finish(i, carry):
            at = pl.ds(pl.multiple_of(i * rb, rb), rb)
            mid = mid_s[at, :]
            out_s[at, :] = (mid + branch_scale * (second_s[at, :] + row_of(bias_ref, BIAS_PROJ))).astype(BF)
            n, scale = normalised(mid)
            gh = gmid_s[at, :]
            cot = jnp.where(valid_rows(i), cot_ref[at, :].astype(F32), 0.0)
            gm = cot + norm_pull(n, scale, row_of(bias_ref, GAIN_TWO), gh)
            gmid_s[at, :] = gm
            gb = (branch_scale * gm).astype(BF)
            gbr_s[at, :] = gb
            return (carry[0] + jnp.sum(gh * n, axis=0, keepdims=True),
                    carry[1] + jnp.sum(gh, axis=0, keepdims=True),
                    carry[2] + jnp.sum(gb.astype(F32), axis=0, keepdims=True))
        zero = jnp.zeros((1, d), F32)
        a, b, c = lax.fori_loop(0, t // rb, finish, (zero, zero, zero))
        vec_ref[1:2] = a
        vec_ref[2:3] = b
        vec_ref[3:4] = c
        for copy in outs[:3]:
            copy.start()
    @pl.when(step == 1)
    def _():
        outs[3].wait()
    f_s[...] = mm_tn(low_ref[...], gpre_s[...]).astype(BF).reshape(f_s.shape)
    @pl.when(step == 0)
    def _():
        outs[3].start()
    @pl.when(step == 1)
    def _():
        outs[4].start()
    dproj = mm_tn(act_s[...], g2_s[...]).astype(BF)
    for half in range(2):
        @pl.when(mine == half)
        def _():
            pkeep_ref[...] = dproj[:, half * h : (half + 1) * h].reshape(pkeep_ref.shape)
            psend_ref[...] = dproj[:, (1 - half) * h : (2 - half) * h].reshape(psend_ref.shape)
    @pl.when(step == 1)
    def _():
        for copy in outs[:3] + outs[4:]:
            copy.wait()

def mlp(core, place, wide_place, lens, mid, low, cot, vec, fcs, projs, blocks, rb=512):
    t, d = mid.shape
    r, pr = d // blocks, 4 * d // blocks
    smem, hbm = pl.BlockSpec(memory_space=pltpu.SMEM), pl.BlockSpec(memory_space=pl.ANY)
    turn = lambda i, c: lax.rem(i + 1 - c[0], 2)
    if blocks > 1:
        pspec = pl.BlockSpec((blocks // 2, pr, d // 2), lambda i, c: (turn(i, c), 0, 0))
    else:
        pspec = pl.BlockSpec((1, pr // 2, d // 2), lambda i, c: (0, turn(i, c), 0))
    of = jax.ShapeDtypeStruct
    return pl.pallas_call(
        functools.partial(mlp_kernel, (len(fcs), len(projs)), rb),
        name="mlp",
        grid_spec=pltpu.PrefetchScalarGridSpec(
            num_scalar_prefetch=1,
            grid=(2,),
            in_specs=[smem, smem, smem, whole((t, d)), whole((t, d)), whole(vec.shape), hbm] + [hbm] * len(fcs + projs),
            out_specs=[hbm] * 5 + [pspec, pspec, whole((4, d)), whole((4, d))],
            scratch_shapes=[
                pltpu.VMEM((blocks, r, 4 * d), BF),
                pltpu.VMEM((blocks, pr, d), BF),
                pltpu.VMEM((t, d), BF),
                pltpu.VMEM((t, d), F32),
                pltpu.VMEM((t, 2 * d), BF),
                pltpu.VMEM((t, 2 * d), BF),
                pltpu.VMEM((t, d), F32),
                pltpu.VMEM((t, d), BF),
                pltpu.VMEM((t, d), F32),
                pltpu.VMEM((t, d), BF),
                pltpu.VMEM((blocks, r, 2 * d), BF),
                pltpu.SemaphoreType.DMA((8,)),
            ],
        ),
        out_shape=[
            of((t, d), BF), of((t, d), F32), of((t, d), BF),
            of((blocks, r, 2 * d), BF), of((blocks, r, 2 * d), BF),
            of((blocks, pr, d // 2), BF), of((blocks, pr, d // 2), BF),
            of((4, d), F32), of((4, d), F32),
        ],
        compiler_params=params(),
        cost_estimate=cost(12 * t * d * 4 * d, 40e6, t * 4 * d),
    )(core, place, wide_place, lens, low, cot, vec, mid, *fcs, *projs)

def unmix_kernel(core, lens, gbr_ref, w_ref, *rest):
    parts, (ga_ref, send_ref, keep_ref) = rest[:-3], rest[-3:]
    t, d = gbr_ref.shape
    w = w_ref[...].reshape(d, d)
    seen = lax.broadcasted_iota(jnp.int32, (t, 1), 0) < lens[0]
    ga_ref[...] = jnp.where(seen, mm_nt(gbr_ref[...], w), 0.0).astype(BF)
    dw = jnp.concatenate([mm_tn(p[...], gbr_ref[...]).astype(BF) for p in parts], 0)
    h = d // 2
    for half in range(2):
        @pl.when(core[0] == half)
        def _():
            keep_ref[...] = dw[:, half * h : (half + 1) * h].reshape(keep_ref.shape)
            send_ref[...] = dw[:, (1 - half) * h : (2 - half) * h].reshape(send_ref.shape)

def unmix(core, lens, gbr, parts, w, blocks):
    t, d = gbr.shape
    smem = pl.BlockSpec(memory_space=pltpu.SMEM)
    piece = jax.ShapeDtypeStruct((blocks, d // blocks, d // 2), BF)
    return pl.pallas_call(
        unmix_kernel,
        name="unmix",
        in_specs=[smem, smem] + [pl.BlockSpec(memory_space=pltpu.VMEM)] * (2 + len(parts)),
        out_shape=[jax.ShapeDtypeStruct((t, d), BF), piece, piece],
        compiler_params=params(0, 24 << 20),
        cost_estimate=cost(4 * t * d * d, 9e6),
    )(core, lens, gbr, w, *parts)

def unproject_kernel(blocks, core, low_ref, g_ref, send_ref, keep_ref, sums_ref):
    d, w = low_ref.shape[1], g_ref.shape[2]
    r, h = d // blocks, w // 2
    low_t = low_ref[...].T
    q, k, v = [mm(low_t, g_ref[part]).astype(BF).reshape(blocks, r, w) for part in range(3)]
    for half, refs in ((0, (keep_ref, send_ref)), (1, (send_ref, keep_ref))):
        @pl.when(core[0] == half)
        def _():
            refs[0][:, :, :w] = q
            refs[0][:, :, w:] = k[:, :, :h]
            refs[1][:, :, :h] = k[:, :, h:]
            refs[1][:, :, h:] = v
    for part in range(3):
        sums_ref[part : part + 1] = jnp.sum(g_ref[part].astype(F32), axis=0, keepdims=True)

def unproject(core, low, g, blocks):
    t, d = low.shape
    w = g.shape[2]
    piece = jax.ShapeDtypeStruct((blocks, d // blocks, w // 2 * 3), BF)
    return pl.pallas_call(
        functools.partial(unproject_kernel, blocks),
        name="unproject",
        in_specs=[pl.BlockSpec(memory_space=pltpu.SMEM)] + [pl.BlockSpec(memory_space=pltpu.VMEM)] * 2,
        out_shape=[piece, piece, jax.ShapeDtypeStruct((3, w), F32)],
        compiler_params=params(0, 24 << 20),
        cost_estimate=cost(6 * t * d * w, 10e6 * w / d),
    )(core, low, g)

def route_kernel(count, steps, rows, near, table, *refs):
    inputs, outs = refs[: 2 * count + near], refs[2 * count + near :]
    def write(ref):
        at = 0
        for k, g in zip(inputs[:count], inputs[count : 2 * count]):
            r, w = k.shape[-2:]
            place = (slice(at, at + r), slice(0, w)) if rows else (slice(0, r), slice(at, at + w))
            at += r if rows else w
            total = (k[...].astype(F32) + g[...].astype(F32)).reshape(1, ref.shape[1], r, w)
            came = [v[:, :, place[0], place[1]] for v in inputs[2 * count :]]
            if near == 2:
                came = [jnp.where(table[pl.program_id(0), 2] == 0, *came)]
            if near:
                total = total + came[0].astype(F32)
            ref[:, :, place[0], place[1]] = total.astype(BF)
    for s, ref in enumerate(outs):
        @pl.when(pl.program_id(0) // steps == s)
        def _():
            write(ref)

def route(table, keeps, gots, near=(), rows=False, split=False):
    z = keeps[0].shape[0]
    sizes = [k.shape[-2:] for k in keeps]
    tall = sum(r for r, _ in sizes) if rows else sizes[0][0]
    wide = sizes[0][1] if rows else sum(w for _, w in sizes)
    block = (1, z, tall, wide)
    specs = [pl.BlockSpec((z, 1, 1, *s), lambda i, t: (0, t[i, 0], t[i, 1], 0, 0)) for s in sizes] * 2
    fixed = pl.BlockSpec(block, lambda i, t: (0, 0, 0, 0))
    if near or split:
        steps, outs = 1, [fixed] * 2
        specs += [pl.BlockSpec(block, lambda i, t: (t[i, 2], 0, 0, 0))] if len(near) == 1 else [fixed] * len(near)
    else:
        steps, outs = 2, [pl.BlockSpec(block, lambda i, t: (i, 0, 0, 0))]
    return pl.pallas_call(
        functools.partial(route_kernel, len(keeps), steps, rows, len(near)),
        name="route",
        grid_spec=pltpu.PrefetchScalarGridSpec(
            num_scalar_prefetch=1, grid=(2,), in_specs=specs, out_specs=outs
        ),
        out_shape=[jax.ShapeDtypeStruct((steps, z, tall, wide), BF)] * len(outs),
        compiler_params=params(1, 24 << 20),
        cost_estimate=cost(1e6, 2 * z * tall * wide * 6),
    )(table, *keeps, *gots, *near)

def final_kernel(x_ref, w_ref, gmid_ref, bias_ref, *rest):
    parts, (out_ref, vec_ref) = rest[:-2], rest[-2:]
    d = x_ref.shape[1]
    w = w_ref[...].reshape(d, 3 * d)
    gh = jnp.zeros(x_ref.shape, F32)
    at = 0
    for g in parts:
        for i in range(3):
            gh = gh + mm_nt(g[i], w[:, i * d + at : i * d + at + g.shape[2]])
        at += g.shape[2]
    n, scale = normalised(x_ref[...].astype(F32))
    out_ref[...] = (gmid_ref[...] + norm_pull(n, scale, row_of(bias_ref, GAIN_ONE), gh)).astype(BF)
    @pl.when(pl.program_id(0) == 0)
    def _():
        vec_ref[...] = jnp.zeros_like(vec_ref)
    vec_ref[0:1] += jnp.sum(gh * n, axis=0, keepdims=True)
    vec_ref[1:2] += jnp.sum(gh, axis=0, keepdims=True)

def final(x, parts, w, gmid, vec, rows=256):
    t, d = x.shape
    return pl.pallas_call(
        final_kernel,
        name="final",
        grid=(t // rows,),
        in_specs=[
            pl.BlockSpec((rows, d), lambda i: (i, 0)),
            whole(w.shape),
            pl.BlockSpec((rows, d), lambda i: (i, 0)),
            whole(vec.shape),
            *[pl.BlockSpec((3, rows, g.shape[2]), lambda i: (0, i, 0)) for g in parts],
        ],
        out_specs=[pl.BlockSpec((rows, d), lambda i: (i, 0)), whole((2, d))],
        out_shape=[jax.ShapeDtypeStruct((t, d), BF), jax.ShapeDtypeStruct((2, d), F32)],
        compiler_params=params(1, 32 << 20),
        cost_estimate=cost(6 * t * d * d, 15e6),
    )(x, w, gmid, vec, *parts)
def spread_matrix(size, width):
    row = lax.broadcasted_iota(jnp.int32, (128, width), 0).astype(F32)
    col = lax.broadcasted_iota(jnp.int32, (128, width), 1).astype(F32)
    inside = col - jnp.floor((col + 0.5) / size) * size
    return jnp.where(inside == row, 1.0, 0.0)

def own_columns(count, size, per, width):
    at = lax.broadcasted_iota(jnp.int32, (count, width), 0).astype(F32)
    at = at - jnp.floor((at + 0.5) / per) * per
    col = lax.broadcasted_iota(jnp.int32, (count, width), 1).astype(F32)
    return jnp.logical_and(col >= at * size, col < (at + 1) * size)


def unfold_vectors(rows_of, count, out_ref):
    d = out_ref.shape[1]
    out_ref[...] = jnp.zeros_like(out_ref)
    for rows, slots, first in ((1, range(6), 0), (2, (6,), BIAS_QKV), (4, (7,), BIAS_FC)):
        size, per = d * rows // count, count // rows
        spread = spread_matrix(size, d).astype(BF)
        mine = own_columns(count, size, per, d)
        for s in slots:
            got = jnp.where(mine, mm(rows_of(s), spread), 0.0)
            for r in range(rows):
                to = first + (s if rows == 1 else 2 * r if rows == 2 else r)
                out_ref[to : to + 1] = jnp.sum(got[r * per : (r + 1) * per], axis=0, keepdims=True)

def unfold_kernel(x_ref, out_ref):
    unfold_vectors(lambda s: x_ref[s], x_ref.shape[1], out_ref)

def unfold(x, d):
    return pl.pallas_call(
        unfold_kernel,
        name="unfold",
        in_specs=[pl.BlockSpec(memory_space=pltpu.VMEM)],
        out_shape=jax.ShapeDtypeStruct((VECTOR_ROWS, d), F32),
        compiler_params=params(0, 16 << 20),
        cost_estimate=cost(1e8, 1e6),
    )(x)

def unfold_pieces_kernel(n_src, place, *rest):
    sources, out_ref, x_ref = rest[:n_src], rest[n_src], rest[-1]
    r = sources[0].shape[1] // 2
    for s, source in enumerate(sources):
        for p in range(source.shape[0]):
            tile = source[p].astype(F32)
            for c in range(2):
                x_ref[2 * place[s, 1 + p] + c] = tile[c * r : c * r + 8]
    unfold_vectors(lambda s: x_ref[:, s, :].astype(BF), x_ref.shape[0], out_ref)

def unfold_pieces(place, sources, count, d):
    np_, r, wide = sources[0].shape
    return pl.pallas_call(
        functools.partial(unfold_pieces_kernel, len(sources)),
        name="unfold",
        grid_spec=pltpu.PrefetchScalarGridSpec(
            num_scalar_prefetch=1,
            grid=(1,),
            in_specs=[whole((np_, r, 128), (0, 0, wide // 128 - 1)) for _ in sources],
            out_specs=whole((VECTOR_ROWS, d)),
            scratch_shapes=[pltpu.VMEM((count, 8, 128), F32)],
        ),
        out_shape=jax.ShapeDtypeStruct((VECTOR_ROWS, d), F32),
        compiler_params=params(1, 16 << 20),
        cost_estimate=cost(1e8, 1e6),
    )(place, *sources)

def fold_kernel(first_ref, sums_ref, qkv_ref, fc_ref, out_ref):
    count, d = out_ref.shape[1], first_ref.shape[1]
    singles = [
        first_ref[0:1], first_ref[1:2], sums_ref[3:4], sums_ref[1:2], sums_ref[2:3], sums_ref[0:1],
    ]
    pairs = [[v] for v in singles] + [[qkv_ref[0:1], qkv_ref[2:3]], [fc_ref[r : r + 1] for r in range(4)]]
    for rows, slots in ((1, range(6)), (2, (6,)), (4, (7,))):
        size, per = d * rows // count, count // rows
        spread = spread_matrix(size, d)
        mine = own_columns(count, size, per, d)
        full = jnp.concatenate(
            [
                jnp.where(mine, jnp.concatenate([jnp.broadcast_to(v, (per, d)) for v in pairs[s]], 0), 0.0)
                for s in slots
            ],
            0,
        )
        got = lax.dot_general(
            full, spread, (((1,), (1,)), ((), ())), precision=lax.Precision.HIGHEST, preferred_element_type=F32
        )
        for i, s in enumerate(slots):
            out_ref[s] = got[i * count : (i + 1) * count]

def fold(first, sums, qkv, fc, count):
    return pl.pallas_call(
        fold_kernel,
        name="fold",
        in_specs=[pl.BlockSpec(memory_space=pltpu.VMEM)] * 4,
        out_shape=jax.ShapeDtypeStruct((8, count, 128), F32),
        compiler_params=params(0, 32 << 20),
        cost_estimate=cost(1e8, 1e6),
    )(first, sums, qkv, fc)


class Grid:
    order = (0, 2, 1, 3)

    def __init__(self, mesh, rows):
        wide, narrow = mesh.shape["wide"], mesh.shape["narrow"]
        self.count = wide * narrow
        self.paired = narrow == 4 and wide == 8 and rows % 8 == 0
        self.blocks = self.count // 2 if self.paired else 1
        self.z = wide // 2

    def index(self, z, x, y, c):
        return ((z * 2 + x) * 2 + y) * 2 + c

    def places(self):
        return [
            (z, x, y, c) for z in range(self.z) for x in range(2) for y in range(2) for c in range(2)
        ]

    def perm(self, target):
        return [(self.index(*at), self.index(*target(*at))) for at in self.places()]

    def here(self):
        w, n = lax.axis_index("wide"), lax.axis_index("narrow")
        return w // 2, w % 2, n // 2, n % 2

    def table(self):
        rows = []
        for z0, x0, y0, c0 in self.places():
            mine = []
            for half in (c0, 1 - c0):
                for ka, kb in ((0, 0), (1, 0), (0, 1), (1, 1)):
                    kx, ky = (ka, kb) if half == 0 else (kb, ka)
                    blocks = [
                        ((z0 ^ kz) * 2 + (x0 ^ kx)) * 2 + (y0 ^ ky) for kz in self.order
                    ]
                    mine.append([half] + blocks)
            rows.append(mine)
        return np.array(rows, np.int32)

    def wide_table(self):
        rows = []
        for z0, x0, y0, c0 in self.places():
            mine = []
            for half in (c0, 1 - c0):
                for kb in (0, 1):
                    line = [half]
                    for kz in self.order:
                        for ka in (0, 1):
                            kx, ky = (ka, kb) if half == 0 else (kb, ka)
                            line.append(((z0 ^ kz) * 2 + (x0 ^ kx)) * 2 + (y0 ^ ky))
                    mine.append(line)
            rows.append(mine)
        return np.array(rows, np.int32)

    def routes(self):
        near, far = [], []
        for z0, x0, y0, c0 in self.places():
            if c0 == 0:
                near.append([[1 - x0, 0], [1 - x0, 1]])
                far.append([[x0, 1 - y0, 1 - y0], [x0, y0, y0]])
            else:
                near.append([[0, 1 - y0], [1, 1 - y0]])
                far.append([[1 - x0, y0, 1 - x0], [x0, y0, x0]])
        return np.array(near, np.int32), np.array(far, np.int32)

    def send(self, value, target):
        return lax.ppermute(value, AXES, self.perm(target))

    def other_core(self, value):
        return self.send(value, lambda z, x, y, c: (z, x, y, 1 - c))

    def along(self, value, turn):
        return self.send(
            value,
            lambda z, x, y, c: (z, 1 - x, y, c) if c == turn else (z, x, 1 - y, c),
        )

    def up(self, value, k):
        return self.send(value, lambda z, x, y, c: (z ^ k, x, y, c))


def both(first, own, other, axis):
    return jnp.where(
        first, jnp.concatenate([own, other], axis), jnp.concatenate([other, own], axis)
    )


def pair_rows(grid, shard, extra=None):
    c = grid.here()[3]
    h = shard.shape[1] // 2
    mine = lax.dynamic_slice_in_dim(shard, c * h, h, 1)
    away = lax.dynamic_slice_in_dim(shard, (1 - c) * h, h, 1)
    if extra is not None:
        mine, away = jnp.concatenate([mine, extra], 1), jnp.concatenate([away, extra], 1)
    return both(c == 0, mine, grid.other_core(away), 0)


def spread_z(grid, pair):
    return jnp.stack([pair] + [grid.up(pair, k) for k in grid.order[1:]])


def with_other(grid, sources):
    return sources + [grid.other_core(s) for s in sources]


def stage(*values):
    return lax.optimization_barrier(values)


def after(value, *earlier):
    return lax.optimization_barrier((value, *earlier))[0]


def add(a, b):
    return (a.astype(F32) + b.astype(F32)).astype(BF)


def pick(v, at, axis):
    return lax.dynamic_index_in_dim(v, at, axis, keepdims=False)


class Sum:
    def __init__(self, grid, tables, sends, keeps, rows=False, split=False):
        self.grid, self.tables, self.rows_under, self.split = grid, tables, rows, split
        self.shape = (grid.z, 2, 2)
        self.keeps = keeps
        self.got = [grid.other_core(s) for s in sends]

    def core(self):
        block = lambda v: v.reshape(*self.shape, *v.shape[1:])
        self.keeps, self.got = [block(k) for k in self.keeps], [block(g) for g in self.got]
        self.away = route(self.tables[0], self.keeps, self.got, (), self.rows_under, self.split)
        return self.away

    def near(self):
        self.came = [self.grid.along(v, 0) for v in self.away]

    def middle(self):
        self.away, self.stay = route(self.tables[1], self.keeps, self.got, self.came, self.rows_under)
        return self.away

    def far(self):
        self.got = self.grid.along(self.away, 1)

    def last(self):
        self.own = add(self.stay, self.got)[0]
        return self.own

    def up(self):
        z = self.grid.here()[0]
        away = jnp.stack([pick(self.own, z ^ 1, 0), pick(self.own, z ^ 3, 0)])
        self.stay = jnp.stack([pick(self.own, z, 0), pick(self.own, z ^ 2, 0)])
        self.got = self.grid.up(away, 1)

    def across(self):
        self.stay = add(self.stay, self.got)
        self.got = self.grid.up(self.stay[1], 2)

    def rows(self):
        return self.stay[0].astype(F32) + self.got.astype(F32)


def own_rows(grid, total):
    c = grid.here()[3]
    r = total.shape[0] // 2
    other = grid.other_core(lax.dynamic_slice_in_dim(total, (1 - c) * r, r, 0))
    return both(c == 0, lax.dynamic_slice_in_dim(total, c * r, r, 0), other, 1)


def stack_small(vectors):
    total = jnp.zeros((8, 128), BF)
    for i, v in enumerate(vectors):
        total = total + jnp.pad(v.reshape(1, -1), ((i, 7 - i), (0, 128 - v.shape[0])))
    return total


def gather_small(count, vectors):
    flat = stack_small(vectors)
    return lax.all_to_all(jnp.broadcast_to(flat[:, None], (8, count, 128)), AXES, 1, 1, tiled=True)


def scatter_small(cut):
    return jnp.sum(lax.all_to_all(cut, AXES, 1, 1, tiled=True), axis=1)


def halves_of(weight):
    h = weight.shape[1] // 2
    return [weight[None, :, :h], weight[None, :, h:]]


def local(
    mesh,
    tokens,
    norm1_gain,
    norm1_bias,
    qkv_weight,
    qkv_bias,
    out_weight,
    out_bias,
    norm2_gain,
    norm2_bias,
    fc_weight,
    fc_bias,
    proj_weight,
    proj_bias,
    seq_lengths,
    out_cotangent,
):
    d = tokens.shape[1]
    grid = Grid(mesh, out_weight.shape[0])
    blocks = grid.blocks
    vectors = [norm1_gain, norm1_bias, out_bias, norm2_gain, norm2_bias, proj_bias, qkv_bias, fc_bias]
    if grid.paired:
        place = jnp.asarray(grid.table())[lax.axis_index(AXES)]
        wide_place = jnp.asarray(grid.wide_table())[lax.axis_index(AXES)]
        tables = [jnp.asarray(v)[lax.axis_index(AXES)] for v in grid.routes()]
        core = grid.here()[3].reshape(1).astype(jnp.int32)
        extra = jnp.pad(stack_small(vectors), ((0, qkv_weight.shape[0] - 8), (0, 0)))
        pair_qkv = pair_rows(grid, qkv_weight, extra)
        place, fc_shard, out_shard, proj_shard, pair_qkv = stage(
            place, fc_weight, out_weight, proj_weight, pair_qkv
        )
        stack_qkv = spread_z(grid, pair_qkv)
        first = jnp.concatenate([pair_rows(grid, fc_shard), pair_rows(grid, out_shard)], 1)
        second = pair_rows(grid, proj_shard)
        near_second = grid.along(second, 0)
        stack_qkv, first, second, near_second = stage(stack_qkv, first, second, near_second)
        two_second = jnp.stack([second, near_second])
        near_qkv, far_qkv = grid.along(stack_qkv, 0), grid.along(stack_qkv, 1)
        two_first = grid.up(first, 2)
        others = [grid.other_core(stack_qkv)]
        near_qkv, far_qkv, two_first, *others = stage(near_qkv, far_qkv, two_first, *others)
        last_qkv = grid.along(near_qkv, 1)
        two_first = jnp.stack([first, two_first])
        four_first = grid.up(two_first, 1)
        across_second = grid.up(two_second, 2)
        others += [grid.other_core(v) for v in (near_qkv, far_qkv)]
        last_qkv, across_second, two_first, four_first, *others = stage(
            last_qkv, across_second, two_first, four_first, *others
        )
        qkv_sources = [stack_qkv, near_qkv, far_qkv, last_qkv, *others, grid.other_core(last_qkv)]
        stack_first = jnp.concatenate([two_first, four_first])
        near_first, far_first = grid.along(stack_first, 0), grid.along(stack_first, 1)
        four_second = jnp.concatenate([two_second, across_second])
        beyond_second = grid.up(four_second, 1)
        others = [grid.other_core(stack_first)]
        *qkv_sources, stack_first = stage(*qkv_sources, stack_first)
        vec = unfold_pieces(place, qkv_sources[:4], grid.count, d)
    else:
        place = wide_place = jnp.asarray(np.array([[0, 0], [1, 0]], np.int32))
        core = jnp.zeros((1,), jnp.int32)
        full = lambda v: lax.all_gather(v, AXES, axis=0, tiled=True)
        qkv_sources = halves_of(full(qkv_weight))
        vec = unfold(gather_small(grid.count, vectors), d)
    qkv, low_one, qkv_full = project(
        place, tokens, vec, qkv_sources, blocks
    )
    if grid.paired:
        qkv, four_second, beyond_second, near_first, far_first, *others = stage(
            qkv, four_second, beyond_second, near_first, far_first, *others
        )
        stack_second = jnp.concatenate([four_second, beyond_second])
        last_first = grid.along(near_first, 1)
        far_second = grid.along(stack_second, 1)
        others += [grid.other_core(near_first), grid.other_core(far_first)]
    attended = [list(attend(seq_lengths, qkv, 4, 0, 512))]
    if grid.paired:
        attended[0][2], qkv, *others = stage(attended[0][2], qkv, *others)
        second_others = [grid.other_core(stack_second)]
    else:
        fcs = halves_of(full(fc_weight))
        outs, out_at = halves_of(full(out_weight)), 0
        projs = halves_of(full(proj_weight))
    attended.append(attend(seq_lengths, qkv, 2, 4, 512))
    mixed = [a[1] for a in attended]
    if grid.paired:
        mixed[1], last_first, *second_others = stage(mixed[1], last_first, *second_others)
        outs = [stack_first, near_first, far_first, last_first, *others, grid.other_core(last_first)]
        fcs, out_at = outs, 4
    middle, low_two, out_full = mix(
        place, mixed, tokens, vec, outs, blocks, out_at
    )
    if grid.paired:
        low_two, far_second = stage(low_two, far_second)
        projs = [stack_second, far_second, *second_others, grid.other_core(far_second)]
    (layer_out, grad_middle, grad_branch, fc_send, fc_keep, proj_send, proj_keep, fc_bias_term, sums) = mlp(
        core, place, wide_place, seq_lengths, middle, low_two, out_cotangent, vec,
        fcs, projs, blocks,
    )
    grad_mixed, out_send, out_keep = unmix(core, seq_lengths, grad_branch, mixed, out_full, blocks)
    if grid.paired:
        fc_sum = Sum(grid, tables, [fc_send], [fc_keep])
        proj_sum = Sum(grid, tables, [proj_send, out_send], [proj_keep, out_keep], True)
        grad_mixed, *fc_sum.away = stage(grad_mixed, *fc_sum.core())
        fc_sum.near()
        grad_mixed, *proj_sum.away = stage(grad_mixed, *proj_sum.core())
        proj_sum.near()
    grad_one = attend_grad(qkv, grad_mixed, attended[0][0], attended[0][2], 0)
    qkv_one = list(unproject(core, low_one, grad_one, blocks))
    if grid.paired:
        qkv_one[2], grad_mixed, fc_sum.came[0], proj_sum.came[0] = stage(
            qkv_one[2], grad_mixed, fc_sum.came[0], proj_sum.came[0]
        )
        fc_sum.middle()
        fc_sum.far()
        proj_sum.middle()
        grad_mixed, fc_sum.stay, proj_sum.away, proj_sum.stay = stage(
            grad_mixed, fc_sum.stay, proj_sum.away, proj_sum.stay
        )
        proj_sum.far()
    grad_two = attend_grad(qkv, grad_mixed, attended[1][0], attended[1][2], 4)
    if grid.paired:
        fc_sum.got, grad_two = stage(fc_sum.got, grad_two)
        fc_sum.last()
        fc_sum.up()
    grads = [grad_one, grad_two]
    qkv_two = unproject(core, low_one, grad_two, blocks)
    if grid.paired:
        qkv_sum = Sum(grid, tables, [qkv_one[0], qkv_two[0]], [qkv_one[1], qkv_two[1]])
        *qkv_sum.got, proj_sum.got = stage(*qkv_sum.got, proj_sum.got)
        grad_middle, *qkv_sum.away = stage(grad_middle, *qkv_sum.core())
        qkv_sum.near()
        grad_middle, proj_sum.own = stage(grad_middle, proj_sum.last())
        proj_sum.up()
    input_grad, first_sums = final(tokens, grads, qkv_full, grad_middle, vec)
    qkv_sums = jnp.concatenate([qkv_one[2], qkv_two[2]], 1)
    cut = fold(first_sums, sums, qkv_sums, fc_bias_term, grid.count)
    if grid.paired:
        cut, qkv_sum.came[0], proj_sum.got, fc_sum.got = stage(cut, qkv_sum.came[0], proj_sum.got, fc_sum.got)
        qkv_sum.middle()
        qkv_sum.far()
        fc_sum.across()
        proj_sum.stay = add(proj_sum.stay, proj_sum.got)
        cut, qkv_sum.got, fc_sum.got, proj_sum.stay = stage(cut, qkv_sum.got, fc_sum.got, proj_sum.stay)
        proj_sum.got = grid.up(proj_sum.stay[1], 2)
        qkv_sum.last()
        qkv_sum.up()
    little = scatter_small(cut)
    if grid.paired:
        qkv_sum.across()
        fc_sum.got, proj_sum.got, qkv_sum.stay = stage(fc_sum.got, proj_sum.got, qkv_sum.stay)
        fc_weight_grad = own_rows(grid, fc_sum.rows())
        total = proj_sum.rows()
        proj_rows = proj_keep.shape[1]
        proj_weight_grad = own_rows(grid, total[:proj_rows])
        out_weight_grad = own_rows(grid, total[proj_rows:])
        shards = [little[s, : vectors[s].shape[0]] for s in range(8)]
        fc_weight_grad, proj_weight_grad, out_weight_grad, qkv_sum.got, *shards = stage(
            fc_weight_grad, proj_weight_grad, out_weight_grad, qkv_sum.got, *shards
        )
        total = qkv_sum.rows()
        wide = qkv_one[1].shape[2]
        ends = [own_rows(grid, total[:, :wide]), own_rows(grid, total[:, wide:])]
    else:
        reduce = lambda v: lax.psum_scatter(v.astype(F32), AXES, scatter_dimension=0, tiled=True)
        side = lambda k, s: jnp.concatenate([k[0], s[0]], 1)
        fc_weight_grad = reduce(side(fc_keep, fc_send))
        out_weight_grad = reduce(side(out_keep, out_send))
        ends = [reduce(side(u[1], u[0])) for u in (qkv_one, qkv_two)]
        proj_weight_grad = reduce(side(proj_keep, proj_send))
        shards = [little[s, : vectors[s].shape[0]] for s in range(8)]
    third = lambda e, i: e[:, i * e.shape[1] // 3 : (i + 1) * e.shape[1] // 3]
    qkv_weight_grad = jnp.concatenate([third(e, i) for i in range(3) for e in ends], 1)
    shard = lambda s: shards[s]
    return (
        layer_out,
        input_grad,
        shard(0),
        shard(1),
        qkv_weight_grad,
        shard(6),
        out_weight_grad,
        shard(2),
        shard(3),
        shard(4),
        fc_weight_grad,
        shard(7),
        proj_weight_grad,
        shard(5),
    )


def solution(mesh):
    matrix, vector = P(AXES, None), P(AXES)
    ins = (
        matrix, vector, vector, matrix, vector, matrix, vector, vector,
        vector, matrix, vector, matrix, vector, vector, matrix,
    )
    outs = (
        matrix, matrix, vector, vector, matrix, vector, matrix, vector,
        vector, vector, matrix, vector, matrix, vector,
    )
    return jax.shard_map(
        functools.partial(local, mesh), mesh=mesh, in_specs=ins, out_specs=outs, check_vma=False
    )
```
